32 devices in a mesh: dp: 8 (over y, x, core), seq: 4 (over z).
Axes of the slice: x: 2, y: 2, z: 4, core: 2. Of those that a mesh axis runs over, the one named last changes fastest.
Arguments:
- block_input: bfloat16 [2, 8, 1024, 768], P(None, 'dp', 'seq'), may hold values from -6 to 6
- segments: int32 [2, 8, 1024], P(None, 'dp'), may hold values from 0 to 7, never falling along the last dimension, each value on 1 to 800 neighbouring positions
- cotangent: bfloat16 [2, 8, 1024, 768], P(None, 'dp', 'seq'), may hold values from -6 to 6
- ln1_gain: bfloat16 [768], P(('dp', 'seq')), may hold values from 0.5 to 1.5
- ln1_bias: bfloat16 [768], P(('dp', 'seq')), may hold values from -1.75 to 1.75
- w_qkv: bfloat16 [768, 2304], P(('dp', 'seq')), may hold values from -0.21875 to 0.21875
- b_qv: bfloat16 [1536], P(('dp', 'seq')), may hold values from -1.75 to 1.75
- w_out: bfloat16 [768, 768], P(('dp', 'seq')), may hold values from -6 to 6
- b_out: bfloat16 [768], P(('dp', 'seq')), may hold values from -12 to 12
- ln2_gain: bfloat16 [768], P(('dp', 'seq')), may hold values from 0.5 to 1.5
- ln2_bias: bfloat16 [768], P(('dp', 'seq')), may hold values from -1.75 to 1.75
- w_fc: bfloat16 [768, 3072], P(('dp', 'seq')), may hold values from -0.21875 to 0.21875
- b_fc: bfloat16 [3072], P(('dp', 'seq')), may hold values from -3 to 3
- w_proj: bfloat16 [3072, 768], P(('dp', 'seq')), may hold values from -3 to 3
- b_proj: bfloat16 [768], P(('dp', 'seq')), may hold values from -12 to 12
Outputs:
- block_output: bfloat16 [2, 8, 1024, 768], P(None, 'dp', 'seq')
- in_grad: bfloat16 [2, 8, 1024, 768], P(None, 'dp', 'seq')
- grad_ln1_gain: float32 [768], P(('dp', 'seq'))
- grad_ln1_bias: float32 [768], P(('dp', 'seq'))
- grad_w_qkv: float32 [768, 2304], P(('dp', 'seq'))
- grad_b_qv: float32 [1536], P(('dp', 'seq'))
- grad_w_out: float32 [768, 768], P(('dp', 'seq'))
- grad_b_out: float32 [768], P(('dp', 'seq'))
- grad_ln2_gain: float32 [768], P(('dp', 'seq'))
- grad_ln2_bias: float32 [768], P(('dp', 'seq'))
- grad_w_fc: float32 [768, 3072], P(('dp', 'seq'))
- grad_b_fc: float32 [3072], P(('dp', 'seq'))
- grad_w_proj: float32 [3072, 768], P(('dp', 'seq'))
- grad_b_proj: float32 [768], P(('dp', 'seq'))
The draws below stay inside these ranges and needn't reach their ends.
Inputs may be any that keep to these rules, and one draw needn't show every extreme that they name: `segments`: segment numbers never fall along a sequence; the tokens of one number in one sequence form a document of 1 to 800 tokens, and one document of each draw has exactly that many.
All inputs are finite; a program needn't handle non-finite values.
Results may differ from the reference program's by a relative error of at most 0.025.
Values may be sent and summed in bfloat16 or wider, within the bound.
A program may use at most 192 MiB of HBM per device.

```python
import math
import jax
import jax.numpy as jnp
import numpy as np
from jax import lax

D = 768
HEADS = 12
HEAD_DIM = 64
FF = 3072
L = 1024
MB = 2
SEQ_DP = 1
BATCH = 8
N_DP = 8


def steps_of(own_key, shape, pieces, low, high):
    loudness, own = 1.0, jax.random.fold_in(own_key, 6)
    for position, parts in pieces:
        draws = jnp.exp(jax.random.uniform(jax.random.fold_in(own, position), (parts,), jnp.float32, low / len(pieces), high / len(pieces)))
        loudness = loudness * jnp.repeat(draws, shape[position] // parts).reshape([-1 if axis == position else 1 for axis in range(len(shape))])
    return loudness


def split_up(amount, total, most, slope):
    weights = [(1 << 20) // math.isqrt(grade ** slope) + 1 for grade in range(2, amount + 1)]
    spare, counts = total - most - (amount - 1), [1] * (amount - 1)
    while spare > 0:
        movable = [i for i in range(amount - 1) if counts[i] < most]
        whole, budget = sum([weights[i] for i in movable]), spare
        for i in movable:
            addition = min(most - counts[i], max(1, budget * weights[i] // whole), spare)
            counts[i] = counts[i] + addition
            spare = spare - addition
    return np.array([most] + counts)


def uneven(own_key, count, total, reach, lean):
    if count == 2:
        one = jax.random.randint(own_key, (), max(1, total - reach), min(reach, total - 1) + 1)
        return jnp.stack([one, total - one])
    sizes = jnp.asarray(split_up(count, total, reach, lean), jnp.int32)
    pairs = (count - 1) // 2
    giver, receiver = sizes[1:1 + 2 * pairs:2], sizes[2:2 + 2 * pairs:2]
    slack = jnp.minimum(giver - 1, reach - receiver)
    moved = jax.random.randint(jax.random.fold_in(own_key, 1), (pairs,), 0, 1 << 20) % (slack + 1)
    sizes = sizes.at[1:1 + 2 * pairs:2].set(giver - moved).at[2:2 + 2 * pairs:2].set(receiver + moved)
    return sizes[jax.random.permutation(jax.random.fold_in(own_key, 2), count)]


def bell_draw(stream_key, dims, width, limit, pieces=(), kind=jnp.bfloat16):
    gain = steps_of(stream_key, dims, pieces, -0.22, 0.18) if pieces else 1.0
    entries = jax.random.normal(stream_key, dims, jnp.float32) * width * gain
    return jnp.minimum(jnp.maximum(entries, -limit), limit).astype(kind)


def setup_inputs(seed: int = 0) -> dict:
    key_of = jax.random.split(jax.random.key(seed), 16)
    return {
        "block_input": bell_draw(key_of[0], (MB, BATCH, L, D), 1.0, 6.0, ((1, 8), (2, 4))),
        "segments": jax.vmap(lambda own: jnp.searchsorted(jnp.cumsum(uneven(own, max(2, L // 128), L, L * 25 // 32, 1)), jnp.arange(L), side="right"))(jax.random.split(key_of[1], MB * BATCH)).reshape((MB, BATCH, L)).astype(jnp.int32),
        "cotangent": bell_draw(key_of[2], (MB, BATCH, L, D), 1.0, 6.0, ((1, 8), (2, 4))),
        "ln1_gain": jnp.clip(1.0 + 0.1 * jax.random.normal(key_of[3], (D,), jnp.float32), 0.5, 1.5).astype(jnp.bfloat16),
        "ln1_bias": bell_draw(key_of[4], (D,), 0.3, 1.75, ((0, 32),)),
        "w_qkv": bell_draw(key_of[5], (D, 3 * D), D ** -0.5, 0.21875, ((0, 32),)),
        "b_qv": bell_draw(key_of[6], (2 * D,), 0.3, 1.75, ((0, 32),)),
        "w_out": bell_draw(key_of[7], (D, D), 1.0, 6.0, ((0, 32),)),
        "b_out": bell_draw(key_of[8], (D,), 2.0, 12.0, ((0, 32),)),
        "ln2_gain": jnp.clip(1.0 + 0.1 * jax.random.normal(key_of[9], (D,), jnp.float32), 0.5, 1.5).astype(jnp.bfloat16),
        "ln2_bias": bell_draw(key_of[10], (D,), 0.3, 1.75, ((0, 32),)),
        "w_fc": bell_draw(key_of[11], (D, FF), D ** -0.5, 0.21875, ((0, 32),)),
        "b_fc": bell_draw(key_of[12], (FF,), 0.5, 3.0, ((0, 32),)),
        "w_proj": bell_draw(key_of[13], (FF, D), 0.2, 3.0, ((0, 32),)),
        "b_proj": bell_draw(key_of[14], (D,), 2.0, 12.0, ((0, 32),)),
    }


@jax.custom_vjp
def low(v):
    return lax.optimization_barrier(v.astype(jnp.bfloat16)).astype(jnp.float32)

@jax.custom_vjp
def low_back(v):
    return v

def low_keep(v):
    return (low(v), None)

def low_pass(kept, grad):
    return (grad,)

def back_keep(v):
    return (v, None)

def back_low(kept, grad):
    return (low(grad),)
low.defvjp(low_keep, low_pass)
low_back.defvjp(back_keep, back_low)
branch_scale = 48.0 ** (-0.5)
norm_eps = 1e-05
masked_score = -1e+30
gelu_coeff = 0.044715
gelu_root = (2.0 / 3.141592653589793) ** 0.5

def matmul(left_arr, right_arr):
    return jnp.dot(left_arr, right_arr, precision=lax.Precision.HIGHEST)

def layer_norm(tok_rows, gain_vec, bias_vec):
    center = tok_rows - lax.optimization_barrier(jnp.mean(tok_rows, -1, keepdims=True))
    inverse = lax.rsqrt(lax.optimization_barrier(jnp.mean(center * center, -1, keepdims=True)) + norm_eps)
    return center * inverse * gain_vec + bias_vec

def gelu_tanh(pre_act):
    tanh_val = jnp.tanh(gelu_root * (pre_act + gelu_coeff * pre_act * pre_act * pre_act))
    return 0.5 * pre_act * (1.0 + tanh_val)

def attend(operand):
    queries, key_rows, values, seg_ids = operand
    places = jnp.arange(seg_ids.shape[0], dtype=jnp.int32)
    visible = (seg_ids[:, None] == seg_ids[None, :]) & (places[:, None] >= places[None, :])
    scores = jnp.einsum('qhd,khd->hqk', queries, key_rows, precision=lax.Precision.HIGHEST) * HEAD_DIM ** (-0.5)
    scores = low_back(scores)
    scores = jnp.where(visible[None], scores, masked_score)
    row_top = lax.optimization_barrier(jnp.max(scores, -1, keepdims=True))
    exponent = jnp.exp(scores - row_top)
    attention_probability = low(exponent / lax.optimization_barrier(jnp.sum(exponent, -1, keepdims=True)))
    return jnp.einsum('hqk,khd->qhd', attention_probability, values, precision=lax.Precision.HIGHEST)

def forward(params, block_in, seg_ids):
    gain_one, bias_one, w_qkv, b_qv, w_out, b_out, gain_two, bias_two, w_fc, b_fc, w_proj, b_proj = params
    seq_count = block_in.shape[0]
    tok_rows = block_in.reshape(-1, D)
    act_one = low(layer_norm(tok_rows, gain_one, bias_one))
    bias_full = jnp.concatenate([b_qv[:D], jnp.zeros((D,), jnp.float32), b_qv[D:]])
    qkv = low(low_back(matmul(act_one, w_qkv) + bias_full))
    qkv_heads = qkv.reshape(seq_count, L, 3, HEADS, HEAD_DIM)
    mixed_out = lax.map(jax.checkpoint(attend), (qkv_heads[:, :, 0], qkv_heads[:, :, 1], qkv_heads[:, :, 2], seg_ids))
    mixed_out = low(low_back(mixed_out.reshape(-1, D)))
    resid_mid = tok_rows + branch_scale * low_back(matmul(mixed_out, w_out) + b_out)
    act_two = low(layer_norm(resid_mid, gain_two, bias_two))
    hidden = low_back(matmul(act_two, w_fc) + b_fc)
    act_three = low(gelu_tanh(hidden))
    result = resid_mid + branch_scale * low_back(matmul(act_three, w_proj) + b_proj)
    return result.reshape(seq_count, L, D)

def reference(block_input, segments, cotangent, ln1_gain, ln1_bias, w_qkv, b_qv, w_out, b_out, ln2_gain, ln2_bias, w_fc, b_fc, w_proj, b_proj):
    params = tuple((param.astype(jnp.float32) for param in (ln1_gain, ln1_bias, w_qkv, b_qv, w_out, b_out, ln2_gain, ln2_bias, w_fc, b_fc, w_proj, b_proj)))
    groups = MB * N_DP
    input_groups = block_input.astype(jnp.float32).reshape(groups, SEQ_DP, L, D)
    seg_groups = segments.reshape(groups, SEQ_DP, L)
    cot_groups = cotangent.astype(jnp.float32).reshape(groups, SEQ_DP, L, D)

    def scan_step(grad_total, operand):
        block_in, seg_ids, cot_block = operand
        result, pull_back = jax.vjp(lambda param_set, inputs: forward(param_set, inputs, seg_ids), params, block_in)
        grad_params, grad_input = pull_back(cot_block)
        grad_total = jax.tree.map(lambda left_arr, right_arr: left_arr + right_arr, grad_total, grad_params)
        return (grad_total, (result.astype(jnp.bfloat16), grad_input.astype(jnp.bfloat16)))
    zero_grads = jax.tree.map(jnp.zeros_like, params)
    grad_total, (result_all, input_grads) = lax.scan(scan_step, zero_grads, (input_groups, seg_groups, cot_groups))
    return (result_all.reshape(MB, BATCH, L, D), input_grads.reshape(MB, BATCH, L, D), grad_total[0], grad_total[1], grad_total[2], grad_total[3], grad_total[4], grad_total[5], grad_total[6], grad_total[7], grad_total[8], grad_total[9], grad_total[10], grad_total[11])
```

```python
import functools

import jax
import jax.numpy as jnp
from jax import lax
from jax.experimental import pallas as pl
from jax.experimental.pallas import tpu as pltpu
from jax.sharding import PartitionSpec as P

HEADS = 12
HEAD_DIM = 64
MESH = pl.DeviceIdType.MESH
PIECES = 4
ANY = pl.ANY

branch_scale = 48.0 ** (-0.5)
norm_eps = 1e-05
masked_score = -1e30
gelu_coeff = 0.044715
gelu_root = (2.0 / 3.141592653589793) ** 0.5


def layer_norm(tok_rows, gain_vec, bias_vec):
    center = tok_rows - jnp.mean(tok_rows, -1, keepdims=True)
    inverse = lax.rsqrt(jnp.mean(center * center, -1, keepdims=True) + norm_eps)
    normed = center * inverse
    return (normed * gain_vec + bias_vec, normed, inverse)


def norm_back(grad_in, normed, inverse, gain_vec):
    grad_gain = jnp.sum(grad_in * normed, 0)
    grad_bias = jnp.sum(grad_in, 0)
    scaled = grad_in * gain_vec
    spread = (
        scaled
        - jnp.mean(scaled, -1, keepdims=True)
        - normed * jnp.mean(scaled * normed, -1, keepdims=True)
    )
    return (inverse * spread, grad_gain, grad_bias)


def gelu_tanh(pre_act):
    tanh_val = jnp.tanh(gelu_root * (pre_act + gelu_coeff * pre_act * pre_act * pre_act))
    return 0.5 * pre_act * (1.0 + tanh_val)


def gelu_slope(pre_act):
    tanh_val = jnp.tanh(gelu_root * (pre_act + gelu_coeff * pre_act * pre_act * pre_act))
    inner_slope = gelu_root * (1.0 + 3.0 * gelu_coeff * pre_act * pre_act)
    return 0.5 * (1.0 + tanh_val) + 0.5 * pre_act * (1.0 - tanh_val * tanh_val) * inner_slope


def log2(n):
    k = n.bit_length() - 1
    assert 1 << k == n
    return k


class Place:
    def __init__(self, dp_n, seq_n):
        self.dp_n, self.seq_n = dp_n, seq_n
        self.dp, self.seq = lax.axis_index("dp"), lax.axis_index("seq")
        self.core = lax.rem(self.dp, 2)
        self.pair = lax.div(self.dp, 2)
        self.me = self.dp * seq_n + self.seq
        self.seqs = seq_n // 2
        self.parts = seq_n // 4
        self.quarter = lax.div(self.seq, self.parts)
        self.quarter_core = self.core_of(self.quarter)
        self.source_core = lax.div(self.seq, self.seqs)

    def core_of(self, quarter):
        return lax.rem(lax.div(quarter + 1, 2), 2)

    def bit(self, name):
        axis, k = name
        return lax.rem(lax.div(self.seq if axis == "seq" else self.dp, 1 << k), 2)

    def delta(self, name):
        axis, k = name
        return (1 - 2 * self.bit(name)) * ((1 << k) * (1 if axis == "seq" else self.seq_n))

    def partner(self, name):
        axis, k = name
        step = (1 - 2 * self.bit(name)) * (1 << k)
        if axis == "seq":
            return (self.dp, self.seq + step)
        return (self.dp + step, self.seq)

    def sibling(self):
        return self.partner(("dp", 0))

    def enter(self):
        barrier = pltpu.get_barrier_semaphore()
        count = 0
        for core_step in range(2):
            for seq_step in range(self.seq_n):
                if core_step == 0 and seq_step == 0:
                    continue
                other = (
                    self.pair * 2 + lax.rem(self.core + core_step, 2),
                    lax.rem(self.seq + seq_step, self.seq_n),
                )
                pl.semaphore_signal(barrier, inc=1, device_id=other, device_id_type=MESH)
                count += 1
        for k in range(1, log2(self.dp_n)):
            pl.semaphore_signal(barrier, inc=1, device_id=self.partner(("dp", k)), device_id_type=MESH)
            count += 1
        pl.semaphore_wait(barrier, count)


def orders_of(dp_n, seq_n):
    along = [("seq", k) for k in reversed(range(log2(seq_n)))]
    across = [("dp", k) for k in range(1, log2(dp_n))]
    back = across[::-1]
    return {
        "zxy": along + across,
        "zyx": along + back,
        "xyz": across + along,
        "yxz": back + along,
    }


def repeat(count, body):
    if count <= 16:
        for j in range(count):
            body(j)
    else:
        lax.fori_loop(0, count, lambda j, c: (body(j), c)[1], 0)


def spread(j, deltas):
    total = 0
    for i, delta in enumerate(deltas):
        if isinstance(j, int):
            if (j >> i) & 1:
                total = total + delta
        else:
            total = total + lax.rem(lax.div(j, 1 << i), 2) * delta
    return total


def resolve(shape, cut):
    axis, pieces, k = cut
    if axis == 1 and shape[1] % (8 * pieces):
        axis = 2
    unit = 8 if axis == 1 else 128
    units = shape[axis] // unit
    start, stop = units * k // pieces, units * (k + 1) // pieces
    return axis, start * unit, (stop - start) * unit


def piece_shape(shape, cut):
    axis, _, size = resolve(shape, cut)
    shape = list(shape)
    shape[axis] = size
    return tuple(shape[1:])


def piece_of(ref, lead, cut):
    axis, start, size = resolve(ref.shape, cut)
    where = [slice(None)] * 2
    where[axis - 1] = pl.ds(start, size)
    return ref.at[(lead, *where)]


GATHER = (
    (0, 2, 3, 0, "zxy", 0),
    (0, 2, 3, 1, "zyx", 0),
    (4, 2, 1, 0, "zyx", 0),
    (0, 2, 3, 2, "zxy", 1),
    (1, 2, 1, 0, "zyx", 1),
    (2, 2, 4, 0, "zxy", 2),
    (3, 1, 4, 0, "zyx", 2),
    (2, 2, 4, 1, "zxy", 3),
    (3, 1, 4, 1, "zyx", 3),
    (2, 2, 4, 2, "zxy", 4),
    (3, 1, 4, 2, "zyx", 4),
    (2, 2, 4, 3, "zxy", 5),
    (3, 1, 4, 3, "zyx", 5),
)
X_WAVE, COT_WAVE = 2, 5


def gather_kernel(dp_n, seq_n, major, x_ref, cot_ref, seg_ref, *refs):
    n_arr = 5
    shard = refs[:n_arr]
    x_out, cot_out, seg_out = refs[n_arr : n_arr + 3]
    full = refs[n_arr + 3 : n_arr + 3 + n_arr]
    (send_sem, recv_sem, side_send, side_recv, own_sem, tok_send, tok_recv, tok_own, seg_sem) = refs[
        2 * n_arr + 3 :
    ]
    at = Place(dp_n, seq_n)
    orders = orders_of(dp_n, seq_n)
    stages = len(orders["zxy"])
    at.enter()
    sibling = at.sibling()

    piece = piece_of

    def put(src, dst, s_sem, r_sem, device):
        pltpu.make_async_remote_copy(
            src_ref=src, dst_ref=dst, send_sem=s_sem, recv_sem=r_sem, device_id=device, device_id_type=MESH
        ).start()

    def place_of(a, idx, cut, count=None):
        if a in major:
            idx = idx + cut[2] * dp_n * seq_n
            return full[a].at[idx if count is None else pl.ds(idx, count)]
        return piece(full[a], idx if count is None else pl.ds(idx, count), cut)

    def group(a, cut, count, s_sem, r_sem, device):
        whole = place_of(a, 0, cut, count)
        return pltpu.make_async_remote_copy(
            src_ref=whole, dst_ref=whole, send_sem=s_sem, recv_sem=r_sem, device_id=device, device_id_type=MESH
        )

    def own_src(a, cut):
        return piece(shard[a], 0, cut)

    def stage(c, t):
        a, *cut, order, _ = GATHER[c]
        names = orders[order]
        deltas = [at.delta(n) for n in names]
        if t > 0:
            group(a, cut, 1 << (t - 1), send_sem.at[c, t - 1], recv_sem.at[c, t - 1], sibling).wait_recv()

            def pass_on(j):
                idx = at.me + deltas[t - 1] + spread(j, deltas[: t - 1])
                place = place_of(a, idx, cut)
                put(place, place, side_send.at[c, t], side_recv.at[c, t], sibling)

            if t < stages:
                partner = at.partner(names[t])

                def onward(j):
                    idx = at.me + spread(j, deltas[:t])
                    place = place_of(a, idx, cut)
                    put(own_src(a, cut) if isinstance(j, int) and j == 0 else place, place, send_sem.at[c, t], recv_sem.at[c, t], partner)

                onward(0)
                repeat((1 << t) - 1, lambda j: onward(j + 1))
            repeat(1 << (t - 1), pass_on)
        else:
            partner = at.partner(names[0])
            place = place_of(a, at.me, cut)
            put(own_src(a, cut), place, send_sem.at[c, 0], recv_sem.at[c, 0], partner)
            put(own_src(a, cut), place, side_send.at[c, 0], side_recv.at[c, 0], sibling)
            pltpu.make_async_copy(own_src(a, cut), place, own_sem.at[c]).start()

    slot = lax.div(at.quarter, 2) * at.parts + lax.rem(at.seq, at.parts)
    seg_copy = pltpu.make_async_remote_copy(
        src_ref=seg_ref,
        dst_ref=seg_out,
        send_sem=seg_sem.at[0],
        recv_sem=seg_sem.at[1],
        device_id=sibling,
        device_id_type=MESH,
    )

    def token_copies(which, src, dst, i):
        to_seq = at.core * at.seqs + i
        mine = (to_seq == at.seq) & (at.quarter_core == at.core)
        remote = pltpu.make_async_remote_copy(
            src_ref=src.at[i],
            dst_ref=dst.at[slot],
            send_sem=tok_send.at[which, i],
            recv_sem=tok_recv.at[which, at.seq],
            device_id=(at.pair * 2 + at.quarter_core, to_seq),
            device_id_type=MESH,
        )
        local = pltpu.make_async_copy(src.at[i], dst.at[slot], tok_own.at[which])
        return mine, remote, local

    def tokens_start(which, src, dst):
        for i in range(at.seqs):
            mine, remote, local = token_copies(which, src, dst, i)
            pl.when(jnp.logical_not(mine))(remote.start)
            pl.when(mine)(local.start)

    def tokens_wait(which, src, dst):
        for i in range(at.seqs):
            mine, remote, local = token_copies(which, src, dst, i)
            pl.when(jnp.logical_not(mine))(remote.wait_send)
            pl.when(mine)(local.wait)
        for z in range(seq_n):
            comes = (at.core_of(z // at.parts) == at.core) & jnp.logical_not(
                (at.seq == z) & (at.source_core == at.core)
            )
            arrival = pltpu.make_async_remote_copy(
                src_ref=src.at[0],
                dst_ref=dst.at[0],
                send_sem=tok_send.at[which, 0],
                recv_sem=tok_recv.at[which, z],
                device_id=sibling,
                device_id_type=MESH,
            )
            pl.when(comes)(arrival.wait_recv)

    seg_copy.start()
    waves = stages + 1 + max(c[5] for c in GATHER)
    for wave in range(waves):
        for c in range(len(GATHER)):
            t = wave - GATHER[c][5]
            if 0 <= t <= stages:
                stage(c, t)
        if wave == X_WAVE:
            tokens_start(0, x_ref, x_out)
        if wave == COT_WAVE:
            tokens_start(1, cot_ref, cot_out)
    for c in range(len(GATHER)):
        a, *cut, order, _ = GATHER[c]
        names = orders[order]
        for t in range(stages):
            group(a, cut, 1 << t, send_sem.at[c, t], recv_sem.at[c, t], at.partner(names[t])).wait_send()
        for t in range(stages + 1):
            one = group(a, cut, 1 << max(t - 1, 0), side_send.at[c, t], side_recv.at[c, t], sibling)
            one.wait_send()
            one.wait_recv()
        pltpu.make_async_copy(own_src(a, cut), place_of(a, at.me, cut), own_sem.at[c]).wait()
    tokens_wait(0, x_ref, x_out)
    tokens_wait(1, cot_ref, cot_out)
    seg_copy.wait()


def gather_all(mesh_shape, x, cot, seg, shards, major=()):
    dp_n, seq_n = mesh_shape
    seqs, blk, width = x.shape
    n_dev = dp_n * seq_n
    stages = log2(n_dev) - 1
    chunks = len(GATHER)
    vmem = pl.BlockSpec(memory_space=pltpu.VMEM)
    hbm = pl.BlockSpec(memory_space=ANY)
    token_shape = jax.ShapeDtypeStruct((seq_n // 2, blk, width), x.dtype)
    DMA = pltpu.SemaphoreType.DMA
    return pl.pallas_call(
        functools.partial(gather_kernel, dp_n, seq_n, major),
        out_shape=[token_shape, token_shape, jax.ShapeDtypeStruct(seg.shape, seg.dtype)]
        + [
            jax.ShapeDtypeStruct((PIECES * n_dev,) + piece_shape((1,) + s.shape, (2 if i == 2 else 1, PIECES, 0)), s.dtype)
            if i in major
            else jax.ShapeDtypeStruct((n_dev,) + s.shape, s.dtype)
            for i, s in enumerate(shards)
        ],
        in_specs=[vmem] * (3 + len(shards)),
        out_specs=[hbm] * 2 + [vmem] + [hbm] * len(shards),
        scratch_shapes=[
            DMA((chunks, stages)),
            DMA((chunks, stages)),
            DMA((chunks, stages + 1)),
            DMA((chunks, stages + 1)),
            DMA((chunks,)),
            DMA((2, seqs)),
            DMA((2, seq_n)),
            DMA((2,)),
            DMA((2,)),
        ],
        compiler_params=pltpu.CompilerParams(collective_id=0, has_side_effects=True),
        name="gather_all",
    )(x, cot, seg, *[s[None] for s in shards])


REDUCE = (
    (2, 2, 4, 0, "zxy", 0),
    (3, 1, 4, 0, "zyx", 0),
    (2, 2, 4, 1, "zxy", 1),
    (3, 1, 4, 1, "zyx", 1),
    (2, 2, 4, 2, "zxy", 2),
    (3, 1, 4, 2, "zyx", 2),
    (2, 2, 4, 3, "zxy", 3),
    (3, 1, 4, 3, "zyx", 3),
    (0, 2, 3, 2, "zxy", 4),
    (1, 2, 1, 0, "zyx", 4),
    (0, 2, 3, 0, "zxy", 5),
    (0, 2, 3, 1, "zyx", 5),
    (4, 2, 1, 0, "zyx", 5),
)


def reduce_kernel(dp_n, seq_n, *refs):
    n_arr, chunks = 5, len(REDUCE)
    tok_in, parts = refs[:2], refs[2 : 2 + n_arr]
    refs = refs[2 + n_arr :]
    tok_out, totals = refs[:2], refs[2 : 2 + n_arr]
    refs = refs[2 + n_arr :]
    at = Place(dp_n, seq_n)
    orders = orders_of(dp_n, seq_n)
    stages = len(orders["zxy"])
    buffers = [refs[c * (stages + 2) : (c + 1) * (stages + 2)] for c in range(chunks)]
    send_sem, recv_sem, own_sem, tok_send, tok_recv, tok_own = refs[chunks * (stages + 2) :]
    at.enter()
    sibling = at.sibling()

    def names_of(c):
        return orders[REDUCE[c][4]][::-1]

    def index_of(c, j, core):
        total = core * seq_n
        for s, (axis, k) in enumerate(names_of(c)):
            value = lax.rem(lax.div(j, 1 << (stages - 1 - s)), 2) if not isinstance(j, int) else (j >> (stages - 1 - s)) & 1
            total = total + value * ((1 << k) * (1 if axis == "seq" else seq_n))
        return total

    def hop(c, t, src):
        device = sibling if t == 0 else at.partner(names_of(c)[t - 1])
        return pltpu.make_async_remote_copy(
            src_ref=src,
            dst_ref=buffers[c][t + 1],
            send_sem=send_sem.at[c, t],
            recv_sem=recv_sem.at[c, t],
            device_id=device,
            device_id_type=MESH,
        )

    def first(c):
        a, *cut, _, _ = REDUCE[c]
        own, got = buffers[c][:2]

        def one(j):
            src = piece_of(parts[a], index_of(c, j, 1 - at.core), cut)
            pltpu.make_async_remote_copy(
                src_ref=src,
                dst_ref=got.at[j],
                send_sem=send_sem.at[c, 0],
                recv_sem=recv_sem.at[c, 0],
                device_id=sibling,
                device_id_type=MESH,
            ).start()
            pltpu.make_async_copy(
                piece_of(parts[a], index_of(c, j, at.core), cut), own.at[j], own_sem.at[c]
            ).start()

        repeat(1 << stages, one)

    def own_wait(c):
        a, *cut, _, _ = REDUCE[c]
        whole = piece_of(parts[a], pl.ds(0, 1 << stages), cut)
        pltpu.make_async_copy(whole, buffers[c][0], own_sem.at[c]).wait()

    def add(c, t, lo, count, kept):
        old, got = buffers[c][t], buffers[c][t + 1]

        def one(j, carry):
            total = old[kept + lo + j].astype(jnp.float32) + got[lo + j].astype(jnp.float32)
            got[lo + j] = total.astype(got.dtype)
            return carry

        lax.fori_loop(0, count, one, 0)

    def stage(c, t):
        if t == 0:
            first(c)
            return
        names = names_of(c)
        hop(c, t - 1, buffers[c][t]).wait_recv()
        if t == 1:
            own_wait(c)
            kept = 0
        else:
            kept = at.bit(names[t - 2]) * (1 << (stages - t + 1))
        if t <= stages:
            half = 1 << (stages - t)
            mine = at.bit(names[t - 1])
            add(c, t - 1, (1 - mine) * half, half, kept)
            hop(c, t, buffers[c][t].at[pl.ds((1 - mine) * half, half)]).start()
            add(c, t - 1, mine * half, half, kept)
        else:
            a, *cut, _, _ = REDUCE[c]
            old, got = buffers[c][t - 1], buffers[c][t]
            total = old[kept].astype(jnp.float32) + got[0].astype(jnp.float32)
            piece_of(totals[a], 0, cut)[...] = total

    def token_copies(which, j):
        slot, rest = j // at.parts, j % at.parts
        quarter = at.core + slot * (3 - 2 * at.core)
        to_seq = quarter * at.parts + rest
        mine = (to_seq == at.seq) & (at.source_core == at.core)
        src = tok_in[which].at[j]
        place = at.seq - at.source_core * at.seqs
        remote = pltpu.make_async_remote_copy(
            src_ref=src,
            dst_ref=tok_out[which].at[place],
            send_sem=tok_send.at[which, j],
            recv_sem=tok_recv.at[which, place],
            device_id=(at.pair * 2 + at.source_core, to_seq),
            device_id_type=MESH,
        )
        local = pltpu.make_async_copy(src, tok_out[which].at[place], tok_own.at[which])
        return mine, remote, local

    for which in range(2):
        for j in range(seq_n // 2):
            mine, remote, local = token_copies(which, j)
            pl.when(jnp.logical_not(mine))(remote.start)
            pl.when(mine)(local.start)
    for wave in range(stages + 2 + max(c[5] for c in REDUCE)):
        for c in range(chunks):
            t = wave - REDUCE[c][5]
            if 0 <= t <= stages + 1:
                stage(c, t)
    for c in range(chunks):
        for t in range(stages + 1):
            hop(c, t, buffers[c][t + 1]).wait_send()
    for which in range(2):
        for j in range(seq_n // 2):
            mine, remote, local = token_copies(which, j)
            pl.when(jnp.logical_not(mine))(remote.wait_send)
            pl.when(mine)(local.wait)
        for i in range(at.seqs):
            comes = jnp.logical_not((at.core * at.seqs + i == at.seq) & (at.quarter_core == at.core))
            arrival = pltpu.make_async_remote_copy(
                src_ref=tok_in[which].at[0],
                dst_ref=tok_out[which].at[i],
                send_sem=tok_send.at[which, 0],
                recv_sem=tok_recv.at[which, i],
                device_id=sibling,
                device_id_type=MESH,
            )
            pl.when(comes)(arrival.wait_recv)


def reduce_all(mesh_shape, tokens, parts):
    dp_n, seq_n = mesh_shape
    stages = log2(dp_n * seq_n) - 1
    _, blk, width = tokens[0].shape
    vmem = pl.BlockSpec(memory_space=pltpu.VMEM)
    hbm = pl.BlockSpec(memory_space=ANY)
    DMA = pltpu.SemaphoreType.DMA
    chunks = len(REDUCE)
    scratch = []
    for a, *cut, _, _ in REDUCE:
        shape = piece_shape(parts[a].shape, cut)
        for count in (1 << stages,) + tuple(1 << (stages - t) for t in range(stages + 1)):
            scratch.append(pltpu.VMEM((count,) + shape, parts[a].dtype))
    out = pl.pallas_call(
        functools.partial(reduce_kernel, dp_n, seq_n),
        out_shape=[jax.ShapeDtypeStruct((seq_n // 2, blk, width), t.dtype) for t in tokens]
        + [jax.ShapeDtypeStruct((1,) + p.shape[1:], jnp.float32) for p in parts],
        in_specs=[vmem] * 2 + [hbm] * len(parts),
        out_specs=[hbm] * 2 + [vmem] * len(parts),
        scratch_shapes=scratch
        + [
            DMA((chunks, stages + 1)),
            DMA((chunks, stages + 1)),
            DMA((chunks,)),
            DMA((2, seq_n // 2)),
            DMA((2, seq_n // 2)),
            DMA((2,)),
        ],
        compiler_params=pltpu.CompilerParams(
            collective_id=1, has_side_effects=True, vmem_limit_bytes=60 * 1024 * 1024
        ),
        name="reduce_all",
    )(*tokens, *parts)
    return out[:2], [g[0] for g in out[2:]]


def swap_kernel(dp_n, seq_n, cols, src_ref, out_ref, send_sem, recv_sem):
    at = Place(dp_n, seq_n)
    sibling = at.sibling()
    barrier = pltpu.get_barrier_semaphore()
    pl.semaphore_signal(barrier, inc=1, device_id=sibling, device_id_type=MESH)
    pl.semaphore_wait(barrier, 1)
    first, width = cols
    copy = pltpu.make_async_remote_copy(
        src_ref=src_ref.at[:, pl.ds(first, width)],
        dst_ref=out_ref,
        send_sem=send_sem,
        recv_sem=recv_sem,
        device_id=sibling,
        device_id_type=MESH,
    )
    copy.start()
    copy.wait()


def swap(mesh_shape, src, cols, which):
    hbm = pl.BlockSpec(memory_space=ANY)
    return pl.pallas_call(
        functools.partial(swap_kernel, *mesh_shape, cols),
        out_shape=jax.ShapeDtypeStruct((src.shape[0], cols[1]), src.dtype),
        in_specs=[hbm],
        out_specs=hbm,
        scratch_shapes=[pltpu.SemaphoreType.DMA, pltpu.SemaphoreType.DMA],
        compiler_params=pltpu.CompilerParams(collective_id=which, has_side_effects=True),
        name="swap",
    )(src)


NT = (((1,), (1,)), ((), ()))
NN = (((1,), (0,)), ((), ()))
TN = (((0,), (0,)), ((), ()))


def dot(a, b, dims):
    return lax.dot_general(a, b, dims, preferred_element_type=jnp.float32)


def woven(own, other):
    half = own.shape[0] // 2
    return jnp.concatenate([own[:half], other[:half], own[half:], other[half:]], 0)


def head_masks():
    lane = lax.broadcasted_iota(jnp.int32, (1, 2 * HEAD_DIM), 1)
    first = (lane < HEAD_DIM).astype(jnp.bfloat16)
    return first, 1 - first


def attend_kernel(q_ref, ko_ref, vo_ref, ks_ref, vs_ref, bias_ref, o_ref, lse_ref):
    rows = q_ref.shape[0]
    half = rows // 2
    keys = woven(ko_ref[...], ks_ref[...])
    values = woven(vo_ref[...], vs_ref[...])
    masks = head_masks()
    scale = jnp.bfloat16(HEAD_DIM ** (-0.5))
    for slot in range(2):
        seen = rows * (slot + 1)
        here = slice(slot * half, (slot + 1) * half)
        q = q_ref[here] * scale
        outs = []
        for head in range(2):
            s = dot(keys[:seen], q * masks[head], NT) + bias_ref[:seen, here]
            top = jnp.max(s, 0, keepdims=True)
            e = jnp.exp(s - top)
            total = jnp.sum(e, 0, keepdims=True)
            p = (e * (1.0 / total)).astype(jnp.bfloat16)
            mixed = dot(values[:seen], p, TN)
            outs.append(mixed[head * HEAD_DIM : (head + 1) * HEAD_DIM])
            lse_ref[0, head : head + 1, here] = top + jnp.log(total)
        o_ref[here] = jnp.concatenate(outs, 0).T.astype(jnp.bfloat16)


def attend(qkv, kv_other, bias):
    rows, wide = qkv.shape
    width = wide // 3
    pairs = width // (2 * HEAD_DIM)
    col = lambda first: pl.BlockSpec((rows, 2 * HEAD_DIM), lambda h, first=first: (0, first * pairs + h))
    return pl.pallas_call(
        attend_kernel,
        grid=(pairs,),
        out_shape=[
            jax.ShapeDtypeStruct((rows, width), jnp.bfloat16),
            jax.ShapeDtypeStruct((pairs, 2, rows), jnp.float32),
        ],
        in_specs=[col(0), col(1), col(2), col(0), col(1), pl.BlockSpec(bias.shape, lambda h: (0, 0))],
        out_specs=[col(0), pl.BlockSpec((1, 2, rows), lambda h: (h, 0, 0))],
        name="attend",
    )(qkv, qkv, qkv, kv_other, kv_other, bias)


def attend_back_kernel(
    q_ref, ko_ref, vo_ref, ks_ref, vs_ref, go_ref, bias_ref, lse_ref, gq_ref, gko_ref, gvo_ref, gks_ref, gvs_ref, gk_sum, gv_sum
):
    rows = q_ref.shape[0]
    half = rows // 2
    keys = woven(ko_ref[...], ks_ref[...])
    values = woven(vo_ref[...], vs_ref[...])
    masks = head_masks()
    scale = HEAD_DIM ** (-0.5)
    for slot in (1, 0):
        seen = rows * (slot + 1)
        here = slice(slot * half, (slot + 1) * half)
        q = q_ref[here] * jnp.bfloat16(scale)
        go = go_ref[here]
        gqs, gk, gv = [], None, None
        for head in range(2):
            q_h, go_h = q * masks[head], go * masks[head]
            s = dot(keys[:seen], q_h, NT) + bias_ref[:seen, here]
            p = jnp.exp(s - lse_ref[0, head : head + 1, here])
            gp = dot(values[:seen], go_h, NT)
            row_dot = jnp.sum(p * gp, 0, keepdims=True)
            gs = (p * (gp - row_dot)).astype(jnp.bfloat16)
            gv_h = dot(p.astype(jnp.bfloat16), go_h, NN)
            gk_h = dot(gs, q_h, NN)
            gk = gk_h if gk is None else gk + gk_h
            gv = gv_h if gv is None else gv + gv_h
            gq = dot(keys[:seen], gs, TN)
            gqs.append(gq[head * HEAD_DIM : (head + 1) * HEAD_DIM])
        gq_ref[here] = (jnp.concatenate(gqs, 0).T * scale).astype(gq_ref.dtype)
        if slot == 1:
            gk_sum[...] = gk
            gv_sum[...] = gv
        else:
            gk_sum[:seen] += gk
            gv_sum[:seen] += gv
    for total, own, other in ((gk_sum, gko_ref, gks_ref), (gv_sum, gvo_ref, gvs_ref)):
        for slot in range(2):
            here = slice(slot * half, (slot + 1) * half)
            own[here] = total[2 * slot * half : (2 * slot + 1) * half].astype(own.dtype)
            other[here] = total[(2 * slot + 1) * half : (2 * slot + 2) * half].astype(other.dtype)


def attend_back(qkv, kv_other, go, bias, lse):
    rows, wide = qkv.shape
    width = wide // 3
    pairs = width // (2 * HEAD_DIM)
    lanes = 2 * HEAD_DIM
    col = lambda first: pl.BlockSpec((rows, lanes), lambda h, first=first: (0, first * pairs + h))
    out = jax.ShapeDtypeStruct((rows, width), jnp.bfloat16)
    return pl.pallas_call(
        attend_back_kernel,
        grid=(pairs,),
        out_shape=[out] * 5,
        in_specs=[
            col(0),
            col(1),
            col(2),
            col(0),
            col(1),
            col(0),
            pl.BlockSpec(bias.shape, lambda h: (0, 0)),
            pl.BlockSpec((1, 2, rows), lambda h: (h, 0, 0)),
        ],
        out_specs=[col(0)] * 5,
        scratch_shapes=[pltpu.VMEM((2 * rows, lanes), jnp.float32)] * 2,
        name="attend_back",
    )(qkv, qkv, qkv, kv_other, kv_other, go, bias, lse)


def rows_at(start, size):
    return pl.ds(pl.multiple_of(start, 16), size)


class Reduction:
    def __init__(self, at, order, bufs, send, keep, sems, own):
        self.at, self.bufs, self.send, self.keep, self.own = at, bufs, send, keep, own
        self.send_sem, self.recv_sem = sems
        self.order = order
        self.names = order + [("seq", k) for k in reversed(range(log2(at.seq_n)))]
        self.last = len(self.names)
        self.dp_rows = bufs[0].shape[0] // (at.dp_n // 2)

    def dp_of(self, j, core):
        dp = core
        for i, (_, k) in enumerate(reversed(self.order)):
            bit = (j >> i) & 1 if isinstance(j, int) else lax.rem(lax.div(j, 1 << i), 2)
            dp = dp + bit * (1 << k)
        return dp

    def copy(self, t, src, dst=None):
        at = self.at
        return pltpu.make_async_remote_copy(
            src_ref=src,
            dst_ref=self.bufs[t] if dst is None else dst,
            send_sem=self.send_sem.at[t],
            recv_sem=self.recv_sem.at[t],
            device_id=at.sibling() if t == 0 else at.partner(self.names[t - 1]),
            device_id_type=MESH,
        )

    def start(self):
        for j in range(self.at.dp_n // 2):
            dst = self.bufs[0].at[pl.ds(j * self.dp_rows, self.dp_rows)]
            self.copy(0, self.own(self.dp_of(j, 1 - self.at.core)), dst).start()

    def fold(self, t, lo, size):
        got = self.bufs[t - 1]
        if t == 1:
            blocks = size // self.dp_rows
            first = lax.div(lo, self.dp_rows)
            step = self.dp_rows // 2
            for j in range(blocks):
                old = self.own(self.dp_of(first + j, self.at.core))

                def one(i, carry, old=old, j=j):
                    here = rows_at((first + j) * self.dp_rows + i * step, step)
                    total = old[pl.ds(i * step, step)].astype(jnp.float32) + got[here].astype(jnp.float32)
                    got[here] = total.astype(got.dtype)
                    return carry

                for i in range(2):
                    one(i, 0)
            return
        old = self.bufs[t - 2]
        kept = self.at.bit(self.names[t - 2]) * got.shape[0]
        step = self.bufs[self.last - 1].shape[0]

        def one(i, carry):
            here = rows_at(lo + i * step, step)
            total = old[rows_at(kept + lo + i * step, step)].astype(jnp.float32) + got[here].astype(jnp.float32)
            got[here] = total.astype(got.dtype)
            return carry

        lax.fori_loop(0, size // step, one, 0)

    def stage(self, t):
        self.copy(t - 1, self.bufs[t - 1]).wait_recv()
        got = self.bufs[t - 1]
        mine = self.at.bit(self.names[t - 1])
        half = got.shape[0] // 2
        if t < self.last:
            self.fold(t, (1 - mine) * half, half)
            self.copy(t, got.at[rows_at((1 - mine) * half, half)]).start()
            self.fold(t, mine * half, half)
        else:
            kept = self.at.bit(self.names[t - 2]) * got.shape[0]
            total = self.bufs[t - 2][rows_at(kept, 2 * half)].astype(jnp.float32) + got[...].astype(jnp.float32)
            low, high = total[:half], total[half:]
            self.send[...] = jnp.where(mine == 0, high, low).astype(self.send.dtype)
            self.copy(t, self.send).start()
            self.keep[...] = jnp.where(mine == 0, low, high)

    def finish(self):
        self.copy(self.last, self.bufs[self.last]).wait_recv()
        return self.keep[...] + self.bufs[self.last][...].astype(jnp.float32)

    def drain(self):
        for t in range(self.last + 1):
            self.copy(t, self.bufs[t]).wait_send()


GRADS = 2 * PIECES + 4


def back_kernel(dp_n, seq_n, *refs):
    (resid, cot, mixed, qkv, kv_other, lse, x_in, bias, vec, fc_hbm, proj_hbm, wqkv_hbm, wout_hbm) = refs[:13]
    result_out, input_out, fc_out, proj_out, qkv_out, wout_out, small_out = refs[13:20]
    (wbuf, gbuf, act, gm, a3, gh, resacc, gact, gqkv, away, back, tok, vecs, gk_sum, gv_sum) = refs[20:35]
    refs = refs[35:]
    at = Place(dp_n, seq_n)
    stages = log2(dp_n * seq_n)
    big, small_bufs = refs[: stages + 2], refs[stages + 2 : 2 * stages + 4]
    (small_src, big_send, big_recv, small_send, small_recv, w_sem, swap_sem, tok_send, tok_recv, tok_own) = refs[
        2 * stages + 4 :
    ]
    rows, width = resid.shape
    half = rows // 2
    shard = fc_out.shape[0]
    across = [("dp", k) for k in range(1, log2(dp_n))]
    at.enter()
    sibling = at.sibling()

    def own_rows(src):
        return lambda dp: src.at[pl.ds(pl.multiple_of(dp * (seq_n * shard), 16), seq_n * shard)]

    def reduction(kind, c):
        order = across[::-1] if kind == 0 else across
        where = lax.rem(c, gbuf.shape[0]) if not isinstance(c, int) else c % gbuf.shape[0]
        return Reduction(
            at,
            order,
            [b.at[c] for b in big[:stages]],
            big[stages].at[c],
            big[stages + 1].at[c],
            (big_send.at[c], big_recv.at[c]),
            own_rows(gbuf.at[where]),
        )

    def vector_reduction():
        return Reduction(
            at,
            across,
            list(small_bufs[:stages]),
            small_bufs[stages],
            small_bufs[stages + 1],
            (small_send, small_recv),
            own_rows(small_src),
        )

    def weight_copy(slot, src):
        return pltpu.make_async_copy(src, wbuf.at[slot], w_sem.at[slot])

    def load_piece(j):
        slot = 2 * lax.rem(j, 2)
        weight_copy(slot, fc_hbm.at[j]).start()
        weight_copy(slot + 1, proj_hbm.at[j]).start()

    load_piece(jnp.int32(0))

    resid_v = resid[...]
    normed, inverse = normalised(resid_v)
    act[...] = (normed * vec[3:4] + vec[4:5]).astype(jnp.bfloat16)
    grad_mlp = (branch_scale * cot[...].astype(jnp.float32)).astype(jnp.bfloat16)
    gm[...] = grad_mlp
    vecs[...] = jnp.zeros_like(vecs)
    vecs[5:6] = jnp.sum(grad_mlp.astype(jnp.float32), 0, keepdims=True)
    resacc[...] = jnp.zeros_like(resacc)
    gact[...] = jnp.zeros_like(gact)

    def wave(w):
        for t in range(stages, 0, -1):
            for kind in range(2):
                j = w - t

                def step(t=t, kind=kind, j=j):
                    red = reduction(kind, 2 * j + kind)
                    if t < stages:
                        red.stage(t)
                    elif kind == 0:
                        fc_out[:, pl.ds(pl.multiple_of(j * width, 128), width)] = red.finish()
                    else:
                        proj_out[pl.ds(pl.multiple_of(j * shard, 8), shard)] = red.finish()

                pl.when((j >= 0) & (j < PIECES))(step)

    def piece(j, carry):
        slot = 2 * lax.rem(j, 2)
        pl.when(j + 1 < PIECES)(lambda: load_piece(j + 1))
        weight_copy(slot, fc_hbm.at[j]).wait()
        weight_copy(slot + 1, proj_hbm.at[j]).wait()
        fc, proj = wbuf.at[slot], wbuf.at[slot + 1]
        bias_fc = vec[pl.ds(6 + j, 1)]

        def some(r, total):
            here = pl.ds(pl.multiple_of(r * half, 16), half)
            u = dot(act[here], fc[...], NN) + bias_fc
            bent = jnp.tanh(gelu_root * (u + gelu_coeff * u * u * u))
            hidden = (0.5 * u * (1.0 + bent)).astype(jnp.bfloat16)
            inner = gelu_root * (1.0 + 3.0 * gelu_coeff * u * u)
            slope = 0.5 * (1.0 + bent) + 0.5 * u * (1.0 - bent * bent) * inner
            a3[here] = hidden
            resacc[here] += dot(hidden, proj[...], NN)
            grad_u = (dot(gm[here], proj[...], NT) * slope).astype(jnp.bfloat16)
            gh[here] = grad_u
            gact[here] += dot(grad_u, fc[...], NT)
            return total + jnp.sum(grad_u.astype(jnp.float32), 0, keepdims=True)

        total = lax.fori_loop(0, 2, some, jnp.zeros((1, width), jnp.float32))
        vecs[pl.ds(6 + j, 1)] = total
        wave(j)
        for kind, (left, right) in enumerate(((act, gh), (a3, gm))):
            c = 2 * j + kind
            red = reduction(kind, c)
            pl.when(c >= gbuf.shape[0])(
                lambda red=red, c=c, kind=kind: reduction(kind, c - gbuf.shape[0]).copy(0, big[0].at[0]).wait_send()
            )
            gbuf[lax.rem(c, gbuf.shape[0])] = dot(left[...], right[...], TN).astype(jnp.bfloat16)
            red.start()
        return carry

    lax.fori_loop(0, PIECES, piece, 0)
    for slot in range(3):
        weight_copy(slot, wqkv_hbm.at[:, pl.ds(slot * width, width)]).start()
    weight_copy(3, wout_hbm).start()

    def token_copies(which, j):
        slot, rest = j // at.parts, j % at.parts
        quarter = at.core + slot * (3 - 2 * at.core)
        to_seq = quarter * at.parts + rest
        mine = (to_seq == at.seq) & (at.source_core == at.core)
        place = at.seq - at.source_core * at.seqs
        out = (result_out, input_out)[which]
        remote = pltpu.make_async_remote_copy(
            src_ref=tok.at[which, j],
            dst_ref=out.at[place],
            send_sem=tok_send.at[which, j],
            recv_sem=tok_recv.at[which, place],
            device_id=(at.pair * 2 + at.source_core, to_seq),
            device_id_type=MESH,
        )
        local = pltpu.make_async_copy(tok.at[which, j], out.at[place], tok_own.at[which])
        return mine, remote, local

    def tokens_start(which, value):
        tok[which] = value.astype(jnp.bfloat16).reshape(tok.shape[1:])
        for j in range(seq_n // 2):
            mine, remote, local = token_copies(which, j)
            pl.when(jnp.logical_not(mine))(remote.start)
            pl.when(mine)(local.start)

    def tokens_wait(which):
        for j in range(seq_n // 2):
            mine, remote, local = token_copies(which, j)
            pl.when(jnp.logical_not(mine))(remote.wait_send)
            pl.when(mine)(local.wait)
        for i in range(at.seqs):
            comes = jnp.logical_not((at.core * at.seqs + i == at.seq) & (at.quarter_core == at.core))
            arrival = pltpu.make_async_remote_copy(
                src_ref=tok.at[which, 0],
                dst_ref=(result_out, input_out)[which].at[i],
                send_sem=tok_send.at[which, 0],
                recv_sem=tok_recv.at[which, i],
                device_id=sibling,
                device_id_type=MESH,
            )
            pl.when(comes)(arrival.wait_recv)

    tokens_start(0, resid[...] + branch_scale * (resacc[...] + vec[5:6]))

    normed, inverse = normalised(resid[...])
    grad_two = gact[...]
    vecs[3:4] = jnp.sum(grad_two * normed, 0, keepdims=True)
    vecs[4:5] = jnp.sum(grad_two, 0, keepdims=True)
    grad_mid = cot[...].astype(jnp.float32) + norm_spread(grad_two, normed, inverse, vec[3:4])
    gact[...] = grad_mid
    grad_branch = (branch_scale * grad_mid).astype(jnp.bfloat16)
    act[...] = grad_branch
    vecs[2:3] = jnp.sum(grad_branch.astype(jnp.float32), 0, keepdims=True)
    wave(PIECES)

    c_out = 2 * PIECES
    reduction(0, c_out - gbuf.shape[0]).copy(0, big[0].at[0]).wait_send()
    gbuf[c_out % gbuf.shape[0]] = dot(mixed[...], grad_branch, TN).astype(jnp.bfloat16)
    reduction(1, c_out).start()
    weight_copy(3, wout_hbm).wait()
    gm[...] = dot(grad_branch, wbuf[3], NT).astype(jnp.bfloat16)

    pairs = width // (2 * HEAD_DIM)

    def heads(i, carry):
        at_q = pl.ds(pl.multiple_of(i * 128, 128), 128)
        at_k = pl.ds(pl.multiple_of(width + i * 128, 128), 128)
        at_v = pl.ds(pl.multiple_of(2 * width + i * 128, 128), 128)
        attend_back_kernel(
            qkv.at[:, at_q],
            qkv.at[:, at_k],
            qkv.at[:, at_v],
            kv_other.at[:, at_q],
            kv_other.at[:, at_k],
            gm.at[:, at_q],
            bias,
            lse.at[pl.ds(i, 1)],
            gqkv.at[:, at_q],
            gqkv.at[:, at_k],
            gqkv.at[:, at_v],
            away.at[:, at_q],
            away.at[:, at_k],
            gk_sum,
            gv_sum,
        )
        wave(PIECES + 1 + i)
        for t in range(1, stages + 1):

            def step(t=t):
                red = reduction(1, c_out)
                if t < stages:
                    red.stage(t)
                else:
                    wout_out[...] = red.finish()

            pl.when(i == t - 1)(step)
        return carry

    lax.fori_loop(0, pairs, heads, 0)

    exchange = pltpu.make_async_remote_copy(
        src_ref=away,
        dst_ref=back,
        send_sem=swap_sem.at[0],
        recv_sem=swap_sem.at[1],
        device_id=sibling,
        device_id_type=MESH,
    )
    exchange.start()
    normed, inverse = normalised(x_in[...].astype(jnp.float32))
    act[...] = (normed * vec[0:1] + vec[1:2]).astype(jnp.bfloat16)

    def grad_of(part):
        c = c_out + 1 + part
        kind = part % 2
        here = pl.ds(part * width, width)
        if part > 0:
            far = pl.ds((part - 1) * width, width)
            gqkv[:, here] = (gqkv[:, here].astype(jnp.float32) + back[:, far].astype(jnp.float32)).astype(jnp.bfloat16)
        reduction(kind, c - gbuf.shape[0]).copy(0, big[0].at[0]).wait_send()
        gbuf[c % gbuf.shape[0]] = dot(act[...], gqkv[:, here], TN).astype(jnp.bfloat16)
        reduction(kind, c).start()
        weight_copy(part, wqkv_hbm.at[:, here]).wait()

    def after(part, t):
        reduction(part % 2, c_out + 1 + part).stage(t)

    def column_sum(part):
        return jnp.sum(gqkv[:, pl.ds(part * width, width)].astype(jnp.float32), 0, keepdims=True)

    grad_of(0)
    exchange.wait()
    grad_of(1)
    after(0, 1)
    grad_of(2)
    after(1, 1)
    after(0, 2)
    first = column_sum(0)
    third = column_sum(2)
    for row, value in ((10, first), (11, first), (12, third), (13, third)):
        vecs[row : row + 1] = value
    grad_one = dot(gqkv[:, pl.ds(0, width)], wbuf[0], NT)
    after(2, 1)
    after(1, 2)
    after(0, 3)
    grad_one = grad_one + dot(gqkv[:, pl.ds(width, width)], wbuf[1], NT)
    grad_one = grad_one + dot(gqkv[:, pl.ds(2 * width, width)], wbuf[2], NT)
    after(2, 2)
    after(1, 3)
    after(0, 4)
    normed, inverse = normalised(x_in[...].astype(jnp.float32))
    vecs[0:1] = jnp.sum(grad_one * normed, 0, keepdims=True)
    vecs[1:2] = jnp.sum(grad_one, 0, keepdims=True)
    tokens_start(1, gact[...] + norm_spread(grad_one, normed, inverse, vec[0:1]))
    columns = vecs[...].T
    small_src[...] = columns
    lane = lax.broadcasted_iota(jnp.int32, (1, 128), 1)
    even, odd = (lane == 10) | (lane == 12), (lane == 11) | (lane == 13)
    n_dev = dp_n * seq_n
    for d in range(n_dev):
        start = 2 * shard * (d % (n_dev // 2))
        kept = columns[d * shard : (d + 1) * shard]
        kept = jnp.where(even, columns[start : start + shard], kept)
        kept = jnp.where(odd, columns[start + shard : start + 2 * shard], kept)
        small_src[d * shard : (d + 1) * shard] = kept
    vector = vector_reduction()
    vector.start()
    after(2, 3)
    after(1, 4)
    vector.stage(1)
    after(2, 4)
    vector.stage(2)
    vector.stage(3)
    vector.stage(4)
    for part in range(3):
        qkv_out[:, pl.ds(part * width, width)] = reduction(part % 2, c_out + 1 + part).finish()
    small_out[...] = vector.finish()
    for c in range(GRADS):
        red = reduction(0, c)
        for t in range(stages):
            waited = c < GRADS - gbuf.shape[0] and t == 0
            if not waited:
                red.copy(t, red.bufs[t]).wait_send()
    vector.drain()
    tokens_wait(0)
    tokens_wait(1)


def back_all(mesh_shape, shards, resid, cot, mixed, qkv, kv_other, lse, x_rows, bias, vec, fc, proj, wqkv, wout):
    dp_n, seq_n = mesh_shape
    rows, width = resid.shape
    stages = log2(dp_n * seq_n)
    blk = rows // (seq_n // 2)
    shard = width // (dp_n * seq_n)
    vmem = pl.BlockSpec(memory_space=pltpu.VMEM)
    hbm = pl.BlockSpec(memory_space=ANY)
    DMA = pltpu.SemaphoreType.DMA
    low, full = jnp.bfloat16, jnp.float32
    slots = 4

    def buffers(lead, cols, dtype):
        sizes = [width // 2 >> t for t in range(stages - 1)] + [shard, shard]
        return [pltpu.VMEM(lead + (size, cols), dtype) for size in sizes] + [pltpu.VMEM(lead + (shard, cols), full)]

    token = jax.ShapeDtypeStruct((seq_n // 2, blk, width), low)
    out = pl.pallas_call(
        functools.partial(back_kernel, dp_n, seq_n),
        out_shape=[token, token] + [jax.ShapeDtypeStruct(s, full) for s in shards + [(shard, 128)]],
        in_specs=[vmem] * 9 + [hbm] * 4,
        out_specs=[hbm] * 2 + [vmem] * 5,
        scratch_shapes=[
            pltpu.VMEM((4, width, width), low),
            pltpu.VMEM((slots, width, width), low),
            pltpu.VMEM((rows, width), low),
            pltpu.VMEM((rows, width), low),
            pltpu.VMEM((rows, width), low),
            pltpu.VMEM((rows, width), low),
            pltpu.VMEM((rows, width), full),
            pltpu.VMEM((rows, width), full),
            pltpu.VMEM((rows, 3 * width), low),
            pltpu.VMEM((rows, 2 * width), low),
            pltpu.VMEM((rows, 2 * width), low),
            pltpu.VMEM((2, seq_n // 2, blk, width), low),
            pltpu.VMEM((128, width), full),
            pltpu.VMEM((2 * rows, 128), full),
            pltpu.VMEM((2 * rows, 128), full),
        ]
        + buffers((GRADS,), width, low)
        + buffers((), 128, full)
        + [
            pltpu.VMEM((width, 128), full),
            DMA((GRADS, stages)),
            DMA((GRADS, stages)),
            DMA((stages,)),
            DMA((stages,)),
            DMA((4,)),
            DMA((2,)),
            DMA((2, seq_n // 2)),
            DMA((2, seq_n // 2)),
            DMA((2,)),
        ],
        compiler_params=pltpu.CompilerParams(
            collective_id=4, has_side_effects=True, vmem_limit_bytes=64 * 1024 * 1024 - 65536
        ),
        name="back_all",
    )(resid, cot, mixed, qkv, kv_other, lse, x_rows, bias, vec, fc, proj, wqkv, wout)
    return out[:2], out[2:]


def normalised(rows):
    center = rows - jnp.mean(rows, -1, keepdims=True)
    inverse = lax.rsqrt(jnp.mean(center * center, -1, keepdims=True) + norm_eps)
    return center * inverse, inverse


def norm_spread(grad_in, normed, inverse, gain):
    scaled = grad_in * gain
    return inverse * (
        scaled
        - jnp.mean(scaled, -1, keepdims=True)
        - normed * jnp.mean(scaled * normed, -1, keepdims=True)
    )


def packed(vectors, row_unit, dtype):
    flat = jnp.concatenate(vectors, -1)
    size = flat.shape[-1]
    rows = -(-size // (128 * row_unit)) * row_unit
    flat = jnp.pad(flat, [(0, 0)] * (flat.ndim - 1) + [(0, rows * 128 - size)])
    return flat.reshape(flat.shape[:-1] + (rows, 128)).astype(dtype)


def unpacked(rows, sizes):
    flat = rows.reshape(rows.shape[0], -1)
    out, first = [], 0
    for size in sizes:
        out.append(flat[:, first : first + size].reshape(-1))
        first += size
    return out


def block(mesh_shape, *args):
    (
        block_input,
        segments,
        cotangent,
        ln1_gain,
        ln1_bias,
        w_qkv,
        b_qv,
        w_out,
        b_out,
        ln2_gain,
        ln2_bias,
        w_fc,
        b_fc,
        w_proj,
        b_proj,
    ) = args
    dp_n, seq_n = mesh_shape
    n_dev = dp_n * seq_n
    micro_count, seq_count, stretch, width = block_input.shape
    seq_len = segments.shape[2]
    seqs = micro_count * seq_count
    assert 2 * seqs == seq_n and seq_n % 4 == 0
    at = Place(dp_n, seq_n)
    vectors = (ln1_gain, ln1_bias, b_qv, b_out, ln2_gain, ln2_bias, b_fc, b_proj)
    sizes = [v.shape[0] for v in vectors]
    gathered = gather_all(
        mesh_shape,
        block_input.reshape(seqs, stretch, width),
        cotangent.reshape(seqs, stretch, width),
        segments.reshape(seqs, seq_len),
        (w_qkv, w_out, w_fc, w_proj, packed(vectors, 16, jnp.bfloat16)),
    )
    x_rows, cot_rows, seg_other, weight_qkv, weight_out, weight_fc, weight_proj, small = gathered
    rows = seq_len // 2
    half = rows // 2
    x_rows = x_rows.reshape(rows, width).astype(jnp.float32)
    grad_out = cot_rows.reshape(rows, width).astype(jnp.float32)
    weight_qkv, weight_out, weight_fc, weight_proj = [
        w.reshape(-1, w.shape[-1]) for w in (weight_qkv, weight_out, weight_fc, weight_proj)
    ]
    gain_one, bias_one, bias_qv, bias_out, gain_two, bias_two, bias_fc, bias_proj = [
        v.astype(jnp.float32) for v in unpacked(small, sizes)
    ]

    seg_all = jnp.where(at.source_core == at.core, segments.reshape(seqs, seq_len), seg_other)
    seg = lax.dynamic_index_in_dim(seg_all, at.seq - at.source_core * seqs, 0, keepdims=False)
    quarter = jnp.arange(half, dtype=jnp.int32)
    own_first = [at.core * half, (3 - at.core) * half]
    other_first = [(1 - at.core) * half, (2 + at.core) * half]
    firsts = [own_first[0], other_first[0], own_first[1], other_first[1]]
    key_place = jnp.concatenate([f + quarter for f in firsts])
    key_seg = jnp.concatenate([lax.dynamic_slice_in_dim(seg, f, half, 0) for f in firsts])
    query_place = jnp.concatenate([key_place[:half], key_place[2 * half : 3 * half]])
    query_seg = jnp.concatenate([key_seg[:half], key_seg[2 * half : 3 * half]])
    visible = (key_seg[:, None] == query_seg[None, :]) & (key_place[:, None] <= query_place[None, :])
    bias = jnp.where(visible, 0.0, masked_score).astype(jnp.float32)

    normed_out, normed_one, inverse_one = layer_norm(x_rows, gain_one, bias_one)
    act_one = normed_out.astype(jnp.bfloat16)
    bias_full = jnp.concatenate([bias_qv[:width], jnp.zeros((width,), jnp.float32), bias_qv[width:]])
    qkv = (jnp.dot(act_one, weight_qkv, preferred_element_type=jnp.float32) + bias_full).astype(jnp.bfloat16)
    kv_other = swap(mesh_shape, qkv, (width, 2 * width), 2)
    mixed_out, lse = attend(qkv, kv_other, bias)
    resid_mid = x_rows + branch_scale * (
        jnp.dot(mixed_out, weight_out, preferred_element_type=jnp.float32) + bias_out
    )

    normed_out, normed_two, inverse_two = layer_norm(resid_mid, gain_two, bias_two)
    act_two = normed_out.astype(jnp.bfloat16)
    hidden = jnp.dot(act_two, weight_fc, preferred_element_type=jnp.float32) + bias_fc
    act_three = gelu_tanh(hidden).astype(jnp.bfloat16)
    result = resid_mid + branch_scale * (
        jnp.dot(act_three, weight_proj, preferred_element_type=jnp.float32) + bias_proj
    )
    grad_mlp = (branch_scale * grad_out).astype(jnp.bfloat16)
    grad_bproj = jnp.sum(grad_mlp.astype(jnp.float32), 0)
    grad_wproj = dot(act_three, grad_mlp, TN)
    grad_act3 = dot(grad_mlp, weight_proj, NT)
    grad_hidden = (grad_act3 * gelu_slope(hidden)).astype(jnp.bfloat16)
    grad_bfc = jnp.sum(grad_hidden.astype(jnp.float32), 0)
    grad_wfc = dot(act_two, grad_hidden, TN)
    grad_act2 = dot(grad_hidden, weight_fc, NT)
    grad_norm2, grad_gain2, grad_bias2 = norm_back(grad_act2, normed_two, inverse_two, gain_two)
    grad_mid = grad_out + grad_norm2

    grad_branch = (branch_scale * grad_mid).astype(jnp.bfloat16)
    grad_bout = jnp.sum(grad_branch.astype(jnp.float32), 0)
    grad_wout = dot(mixed_out, grad_branch, TN)
    grad_mixed = dot(grad_branch, weight_out, NT).astype(jnp.bfloat16)
    grad_q, grad_k, grad_v, away_k, away_v = attend_back(qkv, kv_other, grad_mixed, bias, lse)
    back = swap(mesh_shape, jnp.concatenate([away_k, away_v], 1), (0, 2 * width), 3)
    key_value = jnp.concatenate([grad_k, grad_v], 1).astype(jnp.float32) + back.astype(jnp.float32)
    grad_qkv = jnp.concatenate([grad_q, key_value.astype(jnp.bfloat16)], 1)
    grad_wide = grad_qkv.astype(jnp.float32)
    grad_bqv = jnp.concatenate([jnp.sum(grad_wide[:, :width], 0), jnp.sum(grad_wide[:, 2 * width :], 0)])
    grad_wqkv = dot(act_one, grad_qkv, TN)
    grad_act1 = dot(grad_qkv, weight_qkv, NT)
    grad_norm1, grad_gain1, grad_bias1 = norm_back(grad_act1, normed_one, inverse_one, gain_one)
    grad_input = grad_mid + grad_norm1

    vec_grads = (grad_gain1, grad_bias1, grad_bqv, grad_bout, grad_gain2, grad_bias2, grad_bfc, grad_bproj)
    token_block = (seq_n // 2, stretch, width)
    parts = [
        g.astype(jnp.bfloat16).reshape((n_dev, -1, g.shape[-1]))
        for g in (grad_wqkv, grad_wout, grad_wfc, grad_wproj)
    ] + [packed([v.reshape(n_dev, -1) for v in vec_grads], 8, jnp.float32)]
    (result, grad_input), totals = reduce_all(
        mesh_shape,
        [result.astype(jnp.bfloat16).reshape(token_block), grad_input.astype(jnp.bfloat16).reshape(token_block)],
        parts,
    )
    owned = unpacked(totals[4].reshape(1, -1), sizes)
    shape = block_input.shape
    return (
        result.reshape(shape),
        grad_input.reshape(shape),
        owned[0],
        owned[1],
        totals[0],
        owned[2],
        totals[1],
        owned[3],
        owned[4],
        owned[5],
        totals[2],
        owned[6],
        totals[3],
        owned[7],
    )


def mask_of(at, seqs, seg_own, seg_other, half):
    seg_all = jnp.where(at.source_core == at.core, seg_own, seg_other)
    seg = lax.dynamic_index_in_dim(seg_all, at.seq - at.source_core * seqs, 0, keepdims=False)
    quarter = jnp.arange(half, dtype=jnp.int32)
    firsts = [at.core * half, (1 - at.core) * half, (3 - at.core) * half, (2 + at.core) * half]
    key_place = jnp.concatenate([f + quarter for f in firsts])
    key_seg = jnp.concatenate([lax.dynamic_slice_in_dim(seg, f, half, 0) for f in firsts])
    query_place = jnp.concatenate([key_place[:half], key_place[2 * half : 3 * half]])
    query_seg = jnp.concatenate([key_seg[:half], key_seg[2 * half : 3 * half]])
    visible = (key_seg[:, None] == query_seg[None, :]) & (key_place[:, None] <= query_place[None, :])
    return jnp.where(visible, 0.0, masked_score).astype(jnp.float32)


def fused_block(mesh_shape, *args):
    (
        block_input,
        segments,
        cotangent,
        ln1_gain,
        ln1_bias,
        w_qkv,
        b_qv,
        w_out,
        b_out,
        ln2_gain,
        ln2_bias,
        w_fc,
        b_fc,
        w_proj,
        b_proj,
    ) = args
    dp_n, seq_n = mesh_shape
    n_dev = dp_n * seq_n
    micro_count, seq_count, stretch, width = block_input.shape
    seq_len = segments.shape[2]
    seqs = micro_count * seq_count
    assert 2 * seqs == seq_n and seq_n % 4 == 0 and w_fc.shape[1] == PIECES * width
    at = Place(dp_n, seq_n)
    shard = width // n_dev
    fc_cols = w_fc.reshape(shard, n_dev, PIECES, shard).transpose(0, 2, 1, 3).reshape(shard, -1)
    vectors = jnp.concatenate(
        [jnp.stack([ln1_gain, ln1_bias, b_out, ln2_gain, ln2_bias, b_proj]), b_fc.reshape(PIECES, shard), b_qv.reshape(2, shard)]
    )
    vectors = jnp.pad(vectors, ((0, 128 - vectors.shape[0]), (0, 0))).T
    gathered = gather_all(
        mesh_shape,
        block_input.reshape(seqs, stretch, width),
        cotangent.reshape(seqs, stretch, width),
        segments.reshape(seqs, seq_len),
        (w_qkv, w_out, fc_cols, w_proj, vectors),
        (2, 3),
    )
    x_low, cot_rows, seg_other, weight_qkv, weight_out, weight_fc, weight_proj, small = gathered
    rows = seq_len // 2
    half = rows // 2
    x_low, cot_rows = x_low.reshape(rows, width), cot_rows.reshape(rows, width)
    x_rows = x_low.astype(jnp.float32)
    weight_qkv, weight_out = [w.reshape(width, w.shape[-1]) for w in (weight_qkv, weight_out)]
    weight_fc, weight_proj = [w.reshape(PIECES, width, width) for w in (weight_fc, weight_proj)]
    vec = small.reshape(width, 128).T[:16].astype(jnp.float32)
    bias_qv = vec[10:12].reshape(2, n_dev, shard).transpose(1, 0, 2).reshape(-1)
    bias = mask_of(at, seqs, segments.reshape(seqs, seq_len), seg_other, half)

    normed, _ = normalised(x_rows)
    act_one = (normed * vec[0] + vec[1]).astype(jnp.bfloat16)
    bias_full = jnp.concatenate([bias_qv[:width], jnp.zeros((width,), jnp.float32), bias_qv[width:]])
    qkv = (jnp.dot(act_one, weight_qkv, preferred_element_type=jnp.float32) + bias_full).astype(jnp.bfloat16)
    kv_other = swap(mesh_shape, qkv, (width, 2 * width), 2)
    mixed_out, lse = attend(qkv, kv_other, bias)
    resid_mid = x_rows + branch_scale * (jnp.dot(mixed_out, weight_out, preferred_element_type=jnp.float32) + vec[2])
    shapes = [(shard, PIECES * width), (PIECES * shard, width), (shard, 3 * width), (shard, width)]
    (result, grad_input), (grad_fc, grad_proj, grad_qkv, grad_out, columns) = back_all(
        mesh_shape,
        shapes,
        resid_mid,
        cot_rows,
        mixed_out,
        qkv,
        kv_other,
        lse,
        x_low,
        bias,
        vec,
        weight_fc,
        weight_proj,
        weight_qkv,
        weight_out,
    )
    grad_fc = grad_fc.reshape(shard, PIECES, n_dev, shard).transpose(0, 2, 1, 3).reshape(shard, -1)
    lines = columns.T
    grad_bqv = jnp.where(at.me < n_dev // 2, lines[10:12], lines[12:14]).reshape(-1)
    shape = block_input.shape
    return (
        result.reshape(shape),
        grad_input.reshape(shape),
        lines[0],
        lines[1],
        grad_qkv,
        grad_bqv,
        grad_out,
        lines[2],
        lines[3],
        lines[4],
        grad_fc,
        lines[6:10].reshape(-1),
        grad_proj,
        lines[5],
    )


def whole_block(mesh_shape, *args):
    aligned = args[5].shape[0] % 8 == 0
    return (fused_block if aligned else block)(mesh_shape, *args)


def solution(mesh):
    both = ("dp", "seq")
    tokens, vector, matrix = P(None, "dp", "seq", None), P(both), P(both, None)
    return jax.shard_map(
        functools.partial(whole_block, (mesh.shape["dp"], mesh.shape["seq"])),
        mesh=mesh,
        in_specs=(
            tokens,
            P(None, "dp", None),
            tokens,
            vector,
            vector,
            matrix,
            vector,
            matrix,
            vector,
            vector,
            vector,
            matrix,
            vector,
            matrix,
            vector,
        ),
        out_specs=(
            tokens,
            tokens,
            vector,
            vector,
            matrix,
            vector,
            matrix,
            vector,
            vector,
            vector,
            matrix,
            vector,
            matrix,
            vector,
        ),
        check_vma=False,
    )
```

```python
import functools

import jax
import jax.numpy as jnp
from jax import lax
from jax.experimental import pallas as pl
from jax.experimental.pallas import tpu as pltpu
from jax.sharding import PartitionSpec as P

HEADS = 12
HEAD_DIM = 64
MESH = pl.DeviceIdType.MESH
PIECES = 4
ANY = pl.ANY

branch_scale = 48.0 ** (-0.5)
norm_eps = 1e-05
masked_score = -1e30
gelu_coeff = 0.044715
gelu_root = (2.0 / 3.141592653589793) ** 0.5


def layer_norm(tok_rows, gain_vec, bias_vec):
    center = tok_rows - jnp.mean(tok_rows, -1, keepdims=True)
    inverse = lax.rsqrt(jnp.mean(center * center, -1, keepdims=True) + norm_eps)
    normed = center * inverse
    return (normed * gain_vec + bias_vec, normed, inverse)


def norm_back(grad_in, normed, inverse, gain_vec):
    grad_gain = jnp.sum(grad_in * normed, 0)
    grad_bias = jnp.sum(grad_in, 0)
    scaled = grad_in * gain_vec
    spread = (
        scaled
        - jnp.mean(scaled, -1, keepdims=True)
        - normed * jnp.mean(scaled * normed, -1, keepdims=True)
    )
    return (inverse * spread, grad_gain, grad_bias)


def gelu_tanh(pre_act):
    tanh_val = jnp.tanh(gelu_root * (pre_act + gelu_coeff * pre_act * pre_act * pre_act))
    return 0.5 * pre_act * (1.0 + tanh_val)


def gelu_slope(pre_act):
    tanh_val = jnp.tanh(gelu_root * (pre_act + gelu_coeff * pre_act * pre_act * pre_act))
    inner_slope = gelu_root * (1.0 + 3.0 * gelu_coeff * pre_act * pre_act)
    return 0.5 * (1.0 + tanh_val) + 0.5 * pre_act * (1.0 - tanh_val * tanh_val) * inner_slope


def log2(n):
    k = n.bit_length() - 1
    assert 1 << k == n
    return k


class Place:
    def __init__(self, dp_n, seq_n):
        self.dp_n, self.seq_n = dp_n, seq_n
        self.dp, self.seq = lax.axis_index("dp"), lax.axis_index("seq")
        self.core = lax.rem(self.dp, 2)
        self.pair = lax.div(self.dp, 2)
        self.me = self.dp * seq_n + self.seq
        self.seqs = seq_n // 2
        self.parts = seq_n // 4
        self.quarter = lax.div(self.seq, self.parts)
        self.quarter_core = self.core_of(self.quarter)
        self.source_core = lax.div(self.seq, self.seqs)

    def core_of(self, quarter):
        return lax.rem(lax.div(quarter + 1, 2), 2)

    def bit(self, name):
        axis, k = name
        return lax.rem(lax.div(self.seq if axis == "seq" else self.dp, 1 << k), 2)

    def delta(self, name):
        axis, k = name
        return (1 - 2 * self.bit(name)) * ((1 << k) * (1 if axis == "seq" else self.seq_n))

    def partner(self, name):
        axis, k = name
        step = (1 - 2 * self.bit(name)) * (1 << k)
        if axis == "seq":
            return (self.dp, self.seq + step)
        return (self.dp + step, self.seq)

    def sibling(self):
        return self.partner(("dp", 0))

    def enter(self):
        barrier = pltpu.get_barrier_semaphore()
        count = 0
        for core_step in range(2):
            for seq_step in range(self.seq_n):
                if core_step == 0 and seq_step == 0:
                    continue
                other = (
                    self.pair * 2 + lax.rem(self.core + core_step, 2),
                    lax.rem(self.seq + seq_step, self.seq_n),
                )
                pl.semaphore_signal(barrier, inc=1, device_id=other, device_id_type=MESH)
                count += 1
        for k in range(1, log2(self.dp_n)):
            pl.semaphore_signal(barrier, inc=1, device_id=self.partner(("dp", k)), device_id_type=MESH)
            count += 1
        pl.semaphore_wait(barrier, count)


def orders_of(dp_n, seq_n):
    along = [("seq", k) for k in reversed(range(log2(seq_n)))]
    across = [("dp", k) for k in range(1, log2(dp_n))]
    back = across[::-1]
    return {
        "zxy": along + across,
        "zyx": along + back,
        "xyz": across + along,
        "yxz": back + along,
    }


def repeat(count, body):
    if count <= 16:
        for j in range(count):
            body(j)
    else:
        lax.fori_loop(0, count, lambda j, c: (body(j), c)[1], 0)


def spread(j, deltas):
    total = 0
    for i, delta in enumerate(deltas):
        if isinstance(j, int):
            if (j >> i) & 1:
                total = total + delta
        else:
            total = total + lax.rem(lax.div(j, 1 << i), 2) * delta
    return total


def resolve(shape, cut):
    axis, pieces, k = cut
    if axis == 1 and shape[1] % (8 * pieces):
        axis = 2
    unit = 8 if axis == 1 else 128
    units = shape[axis] // unit
    start, stop = units * k // pieces, units * (k + 1) // pieces
    return axis, start * unit, (stop - start) * unit


def piece_shape(shape, cut):
    axis, _, size = resolve(shape, cut)
    shape = list(shape)
    shape[axis] = size
    return tuple(shape[1:])


def piece_of(ref, lead, cut):
    axis, start, size = resolve(ref.shape, cut)
    where = [slice(None)] * 2
    where[axis - 1] = pl.ds(start, size)
    return ref.at[(lead, *where)]


GATHER = (
    (0, 2, 3, 0, "zxy", 0),
    (0, 2, 3, 1, "zyx", 0),
    (4, 2, 1, 0, "zyx", 0),
    (0, 2, 3, 2, "zxy", 1),
    (1, 2, 1, 0, "zyx", 1),
    (2, 2, 4, 0, "zxy", 2),
    (3, 1, 4, 0, "zyx", 2),
    (2, 2, 4, 1, "zxy", 3),
    (3, 1, 4, 1, "zyx", 3),
    (2, 2, 4, 2, "zxy", 4),
    (3, 1, 4, 2, "zyx", 4),
    (2, 2, 4, 3, "zxy", 5),
    (3, 1, 4, 3, "zyx", 5),
)
X_WAVE, COT_WAVE = 2, 5


def gather_kernel(dp_n, seq_n, major, x_ref, cot_ref, seg_ref, *refs):
    n_arr = 5
    shard = refs[:n_arr]
    x_out, cot_out, seg_out = refs[n_arr : n_arr + 3]
    full = refs[n_arr + 3 : n_arr + 3 + n_arr]
    (send_sem, recv_sem, side_send, side_recv, own_sem, tok_send, tok_recv, tok_own, seg_sem) = refs[
        2 * n_arr + 3 :
    ]
    at = Place(dp_n, seq_n)
    orders = orders_of(dp_n, seq_n)
    stages = len(orders["zxy"])
    at.enter()
    sibling = at.sibling()

    piece = piece_of

    def put(src, dst, s_sem, r_sem, device):
        pltpu.make_async_remote_copy(
            src_ref=src, dst_ref=dst, send_sem=s_sem, recv_sem=r_sem, device_id=device, device_id_type=MESH
        ).start()

    def place_of(a, idx, cut, count=None):
        if a in major:
            idx = idx + cut[2] * dp_n * seq_n
            return full[a].at[idx if count is None else pl.ds(idx, count)]
        return piece(full[a], idx if count is None else pl.ds(idx, count), cut)

    def group(a, cut, count, s_sem, r_sem, device):
        whole = place_of(a, 0, cut, count)
        return pltpu.make_async_remote_copy(
            src_ref=whole, dst_ref=whole, send_sem=s_sem, recv_sem=r_sem, device_id=device, device_id_type=MESH
        )

    def own_src(a, cut):
        return piece(shard[a], 0, cut)

    def stage(c, t):
        a, *cut, order, _ = GATHER[c]
        names = orders[order]
        deltas = [at.delta(n) for n in names]
        if t > 0:
            group(a, cut, 1 << (t - 1), send_sem.at[c, t - 1], recv_sem.at[c, t - 1], sibling).wait_recv()

            def pass_on(j):
                idx = at.me + deltas[t - 1] + spread(j, deltas[: t - 1])
                place = place_of(a, idx, cut)
                put(place, place, side_send.at[c, t], side_recv.at[c, t], sibling)

            if t < stages:
                partner = at.partner(names[t])

                def onward(j):
                    idx = at.me + spread(j, deltas[:t])
                    place = place_of(a, idx, cut)
                    put(own_src(a, cut) if isinstance(j, int) and j == 0 else place, place, send_sem.at[c, t], recv_sem.at[c, t], partner)

                onward(0)
                repeat((1 << t) - 1, lambda j: onward(j + 1))
            repeat(1 << (t - 1), pass_on)
        else:
            partner = at.partner(names[0])
            place = place_of(a, at.me, cut)
            put(own_src(a, cut), place, send_sem.at[c, 0], recv_sem.at[c, 0], partner)
            put(own_src(a, cut), place, side_send.at[c, 0], side_recv.at[c, 0], sibling)
            pltpu.make_async_copy(own_src(a, cut), place, own_sem.at[c]).start()

    slot = lax.div(at.quarter, 2) * at.parts + lax.rem(at.seq, at.parts)
    seg_copy = pltpu.make_async_remote_copy(
        src_ref=seg_ref,
        dst_ref=seg_out,
        send_sem=seg_sem.at[0],
        recv_sem=seg_sem.at[1],
        device_id=sibling,
        device_id_type=MESH,
    )

    def token_copies(which, src, dst, i):
        to_seq = at.core * at.seqs + i
        mine = (to_seq == at.seq) & (at.quarter_core == at.core)
        remote = pltpu.make_async_remote_copy(
            src_ref=src.at[i],
            dst_ref=dst.at[slot],
            send_sem=tok_send.at[which, i],
            recv_sem=tok_recv.at[which, at.seq],
            device_id=(at.pair * 2 + at.quarter_core, to_seq),
            device_id_type=MESH,
        )
        local = pltpu.make_async_copy(src.at[i], dst.at[slot], tok_own.at[which])
        return mine, remote, local

    def tokens_start(which, src, dst):
        for i in range(at.seqs):
            mine, remote, local = token_copies(which, src, dst, i)
            pl.when(jnp.logical_not(mine))(remote.start)
            pl.when(mine)(local.start)

    def tokens_wait(which, src, dst):
        for i in range(at.seqs):
            mine, remote, local = token_copies(which, src, dst, i)
            pl.when(jnp.logical_not(mine))(remote.wait_send)
            pl.when(mine)(local.wait)
        for z in range(seq_n):
            comes = (at.core_of(z // at.parts) == at.core) & jnp.logical_not(
                (at.seq == z) & (at.source_core == at.core)
            )
            arrival = pltpu.make_async_remote_copy(
                src_ref=src.at[0],
                dst_ref=dst.at[0],
                send_sem=tok_send.at[which, 0],
                recv_sem=tok_recv.at[which, z],
                device_id=sibling,
                device_id_type=MESH,
            )
            pl.when(comes)(arrival.wait_recv)

    seg_copy.start()
    waves = stages + 1 + max(c[5] for c in GATHER)
    for wave in range(waves):
        for c in range(len(GATHER)):
            t = wave - GATHER[c][5]
            if 0 <= t <= stages:
                stage(c, t)
        if wave == X_WAVE:
            tokens_start(0, x_ref, x_out)
        if wave == COT_WAVE:
            tokens_start(1, cot_ref, cot_out)
    for c in range(len(GATHER)):
        a, *cut, order, _ = GATHER[c]
        names = orders[order]
        for t in range(stages):
            group(a, cut, 1 << t, send_sem.at[c, t], recv_sem.at[c, t], at.partner(names[t])).wait_send()
        for t in range(stages + 1):
            one = group(a, cut, 1 << max(t - 1, 0), side_send.at[c, t], side_recv.at[c, t], sibling)
            one.wait_send()
            one.wait_recv()
        pltpu.make_async_copy(own_src(a, cut), place_of(a, at.me, cut), own_sem.at[c]).wait()
    tokens_wait(0, x_ref, x_out)
    tokens_wait(1, cot_ref, cot_out)
    seg_copy.wait()


def gather_all(mesh_shape, x, cot, seg, shards, major=()):
    dp_n, seq_n = mesh_shape
    seqs, blk, width = x.shape
    n_dev = dp_n * seq_n
    stages = log2(n_dev) - 1
    chunks = len(GATHER)
    vmem = pl.BlockSpec(memory_space=pltpu.VMEM)
    hbm = pl.BlockSpec(memory_space=ANY)
    token_shape = jax.ShapeDtypeStruct((seq_n // 2, blk, width), x.dtype)
    DMA = pltpu.SemaphoreType.DMA
    return pl.pallas_call(
        functools.partial(gather_kernel, dp_n, seq_n, major),
        out_shape=[token_shape, token_shape, jax.ShapeDtypeStruct(seg.shape, seg.dtype)]
        + [
            jax.ShapeDtypeStruct((PIECES * n_dev,) + piece_shape((1,) + s.shape, (2 if i == 2 else 1, PIECES, 0)), s.dtype)
            if i in major
            else jax.ShapeDtypeStruct((n_dev,) + s.shape, s.dtype)
            for i, s in enumerate(shards)
        ],
        in_specs=[vmem] * (3 + len(shards)),
        out_specs=[hbm] * 2 + [vmem] + [hbm] * len(shards),
        scratch_shapes=[
            DMA((chunks, stages)),
            DMA((chunks, stages)),
            DMA((chunks, stages + 1)),
            DMA((chunks, stages + 1)),
            DMA((chunks,)),
            DMA((2, seqs)),
            DMA((2, seq_n)),
            DMA((2,)),
            DMA((2,)),
        ],
        compiler_params=pltpu.CompilerParams(collective_id=0, has_side_effects=True),
        name="gather_all",
    )(x, cot, seg, *[s[None] for s in shards])


REDUCE = (
    (2, 2, 4, 0, "zxy", 0),
    (3, 1, 4, 0, "zyx", 0),
    (2, 2, 4, 1, "zxy", 1),
    (3, 1, 4, 1, "zyx", 1),
    (2, 2, 4, 2, "zxy", 2),
    (3, 1, 4, 2, "zyx", 2),
    (2, 2, 4, 3, "zxy", 3),
    (3, 1, 4, 3, "zyx", 3),
    (0, 2, 3, 2, "zxy", 4),
    (1, 2, 1, 0, "zyx", 4),
    (0, 2, 3, 0, "zxy", 5),
    (0, 2, 3, 1, "zyx", 5),
    (4, 2, 1, 0, "zyx", 5),
)


def reduce_kernel(dp_n, seq_n, *refs):
    n_arr, chunks = 5, len(REDUCE)
    tok_in, parts = refs[:2], refs[2 : 2 + n_arr]
    refs = refs[2 + n_arr :]
    tok_out, totals = refs[:2], refs[2 : 2 + n_arr]
    refs = refs[2 + n_arr :]
    at = Place(dp_n, seq_n)
    orders = orders_of(dp_n, seq_n)
    stages = len(orders["zxy"])
    buffers = [refs[c * (stages + 2) : (c + 1) * (stages + 2)] for c in range(chunks)]
    send_sem, recv_sem, own_sem, tok_send, tok_recv, tok_own = refs[chunks * (stages + 2) :]
    at.enter()
    sibling = at.sibling()

    def names_of(c):
        return orders[REDUCE[c][4]][::-1]

    def index_of(c, j, core):
        total = core * seq_n
        for s, (axis, k) in enumerate(names_of(c)):
            value = lax.rem(lax.div(j, 1 << (stages - 1 - s)), 2) if not isinstance(j, int) else (j >> (stages - 1 - s)) & 1
            total = total + value * ((1 << k) * (1 if axis == "seq" else seq_n))
        return total

    def hop(c, t, src):
        device = sibling if t == 0 else at.partner(names_of(c)[t - 1])
        return pltpu.make_async_remote_copy(
            src_ref=src,
            dst_ref=buffers[c][t + 1],
            send_sem=send_sem.at[c, t],
            recv_sem=recv_sem.at[c, t],
            device_id=device,
            device_id_type=MESH,
        )

    def first(c):
        a, *cut, _, _ = REDUCE[c]
        own, got = buffers[c][:2]

        def one(j):
            src = piece_of(parts[a], index_of(c, j, 1 - at.core), cut)
            pltpu.make_async_remote_copy(
                src_ref=src,
                dst_ref=got.at[j],
                send_sem=send_sem.at[c, 0],
                recv_sem=recv_sem.at[c, 0],
                device_id=sibling,
                device_id_type=MESH,
            ).start()
            pltpu.make_async_copy(
                piece_of(parts[a], index_of(c, j, at.core), cut), own.at[j], own_sem.at[c]
            ).start()

        repeat(1 << stages, one)

    def own_wait(c):
        a, *cut, _, _ = REDUCE[c]
        whole = piece_of(parts[a], pl.ds(0, 1 << stages), cut)
        pltpu.make_async_copy(whole, buffers[c][0], own_sem.at[c]).wait()

    def add(c, t, lo, count, kept):
        old, got = buffers[c][t], buffers[c][t + 1]

        def one(j, carry):
            total = old[kept + lo + j].astype(jnp.float32) + got[lo + j].astype(jnp.float32)
            got[lo + j] = total.astype(got.dtype)
            return carry

        lax.fori_loop(0, count, one, 0)

    def stage(c, t):
        if t == 0:
            first(c)
            return
        names = names_of(c)
        hop(c, t - 1, buffers[c][t]).wait_recv()
        if t == 1:
            own_wait(c)
            kept = 0
        else:
            kept = at.bit(names[t - 2]) * (1 << (stages - t + 1))
        if t <= stages:
            half = 1 << (stages - t)
            mine = at.bit(names[t - 1])
            add(c, t - 1, (1 - mine) * half, half, kept)
            hop(c, t, buffers[c][t].at[pl.ds((1 - mine) * half, half)]).start()
            add(c, t - 1, mine * half, half, kept)
        else:
            a, *cut, _, _ = REDUCE[c]
            old, got = buffers[c][t - 1], buffers[c][t]
            total = old[kept].astype(jnp.float32) + got[0].astype(jnp.float32)
            piece_of(totals[a], 0, cut)[...] = total

    def token_copies(which, j):
        slot, rest = j // at.parts, j % at.parts
        quarter = at.core + slot * (3 - 2 * at.core)
        to_seq = quarter * at.parts + rest
        mine = (to_seq == at.seq) & (at.source_core == at.core)
        src = tok_in[which].at[j]
        place = at.seq - at.source_core * at.seqs
        remote = pltpu.make_async_remote_copy(
            src_ref=src,
            dst_ref=tok_out[which].at[place],
            send_sem=tok_send.at[which, j],
            recv_sem=tok_recv.at[which, place],
            device_id=(at.pair * 2 + at.source_core, to_seq),
            device_id_type=MESH,
        )
        local = pltpu.make_async_copy(src, tok_out[which].at[place], tok_own.at[which])
        return mine, remote, local

    for which in range(2):
        for j in range(seq_n // 2):
            mine, remote, local = token_copies(which, j)
            pl.when(jnp.logical_not(mine))(remote.start)
            pl.when(mine)(local.start)
    for wave in range(stages + 2 + max(c[5] for c in REDUCE)):
        for c in range(chunks):
            t = wave - REDUCE[c][5]
            if 0 <= t <= stages + 1:
                stage(c, t)
    for c in range(chunks):
        for t in range(stages + 1):
            hop(c, t, buffers[c][t + 1]).wait_send()
    for which in range(2):
        for j in range(seq_n // 2):
            mine, remote, local = token_copies(which, j)
            pl.when(jnp.logical_not(mine))(remote.wait_send)
            pl.when(mine)(local.wait)
        for i in range(at.seqs):
            comes = jnp.logical_not((at.core * at.seqs + i == at.seq) & (at.quarter_core == at.core))
            arrival = pltpu.make_async_remote_copy(
                src_ref=tok_in[which].at[0],
                dst_ref=tok_out[which].at[i],
                send_sem=tok_send.at[which, 0],
                recv_sem=tok_recv.at[which, i],
                device_id=sibling,
                device_id_type=MESH,
            )
            pl.when(comes)(arrival.wait_recv)


def reduce_all(mesh_shape, tokens, parts):
    dp_n, seq_n = mesh_shape
    stages = log2(dp_n * seq_n) - 1
    _, blk, width = tokens[0].shape
    vmem = pl.BlockSpec(memory_space=pltpu.VMEM)
    hbm = pl.BlockSpec(memory_space=ANY)
    DMA = pltpu.SemaphoreType.DMA
    chunks = len(REDUCE)
    scratch = []
    for a, *cut, _, _ in REDUCE:
        shape = piece_shape(parts[a].shape, cut)
        for count in (1 << stages,) + tuple(1 << (stages - t) for t in range(stages + 1)):
            scratch.append(pltpu.VMEM((count,) + shape, parts[a].dtype))
    out = pl.pallas_call(
        functools.partial(reduce_kernel, dp_n, seq_n),
        out_shape=[jax.ShapeDtypeStruct((seq_n // 2, blk, width), t.dtype) for t in tokens]
        + [jax.ShapeDtypeStruct((1,) + p.shape[1:], jnp.float32) for p in parts],
        in_specs=[vmem] * 2 + [hbm] * len(parts),
        out_specs=[hbm] * 2 + [vmem] * len(parts),
        scratch_shapes=scratch
        + [
            DMA((chunks, stages + 1)),
            DMA((chunks, stages + 1)),
            DMA((chunks,)),
            DMA((2, seq_n // 2)),
            DMA((2, seq_n // 2)),
            DMA((2,)),
        ],
        compiler_params=pltpu.CompilerParams(
            collective_id=1, has_side_effects=True, vmem_limit_bytes=60 * 1024 * 1024
        ),
        name="reduce_all",
    )(*tokens, *parts)
    return out[:2], [g[0] for g in out[2:]]


def swap_kernel(dp_n, seq_n, cols, src_ref, out_ref, send_sem, recv_sem):
    at = Place(dp_n, seq_n)
    sibling = at.sibling()
    barrier = pltpu.get_barrier_semaphore()
    pl.semaphore_signal(barrier, inc=1, device_id=sibling, device_id_type=MESH)
    pl.semaphore_wait(barrier, 1)
    first, width = cols
    copy = pltpu.make_async_remote_copy(
        src_ref=src_ref.at[:, pl.ds(first, width)],
        dst_ref=out_ref,
        send_sem=send_sem,
        recv_sem=recv_sem,
        device_id=sibling,
        device_id_type=MESH,
    )
    copy.start()
    copy.wait()


def swap(mesh_shape, src, cols, which):
    hbm = pl.BlockSpec(memory_space=ANY)
    return pl.pallas_call(
        functools.partial(swap_kernel, *mesh_shape, cols),
        out_shape=jax.ShapeDtypeStruct((src.shape[0], cols[1]), src.dtype),
        in_specs=[hbm],
        out_specs=hbm,
        scratch_shapes=[pltpu.SemaphoreType.DMA, pltpu.SemaphoreType.DMA],
        compiler_params=pltpu.CompilerParams(collective_id=which, has_side_effects=True),
        name="swap",
    )(src)


NT = (((1,), (1,)), ((), ()))
NN = (((1,), (0,)), ((), ()))
TN = (((0,), (0,)), ((), ()))


def dot(a, b, dims):
    return lax.dot_general(a, b, dims, preferred_element_type=jnp.float32)


def woven(own, other):
    half = own.shape[0] // 2
    return jnp.concatenate([own[:half], other[:half], own[half:], other[half:]], 0)


def head_masks():
    lane = lax.broadcasted_iota(jnp.int32, (1, 2 * HEAD_DIM), 1)
    first = (lane < HEAD_DIM).astype(jnp.bfloat16)
    return first, 1 - first


def attend_kernel(q_ref, ko_ref, vo_ref, ks_ref, vs_ref, bias_ref, o_ref, lse_ref):
    rows = q_ref.shape[0]
    half = rows // 2
    keys = woven(ko_ref[...], ks_ref[...])
    values = woven(vo_ref[...], vs_ref[...])
    masks = head_masks()
    scale = jnp.bfloat16(HEAD_DIM ** (-0.5))
    for slot in range(2):
        seen = rows * (slot + 1)
        here = slice(slot * half, (slot + 1) * half)
        q = q_ref[here] * scale
        outs = []
        for head in range(2):
            s = dot(keys[:seen], q * masks[head], NT) + bias_ref[:seen, here]
            top = jnp.max(s, 0, keepdims=True)
            e = jnp.exp(s - top)
            total = jnp.sum(e, 0, keepdims=True)
            p = (e * (1.0 / total)).astype(jnp.bfloat16)
            mixed = dot(values[:seen], p, TN)
            outs.append(mixed[head * HEAD_DIM : (head + 1) * HEAD_DIM])
            lse_ref[0, head : head + 1, here] = top + jnp.log(total)
        o_ref[here] = jnp.concatenate(outs, 0).T.astype(jnp.bfloat16)


def attend(qkv, kv_other, bias):
    rows, wide = qkv.shape
    width = wide // 3
    pairs = width // (2 * HEAD_DIM)
    col = lambda first: pl.BlockSpec((rows, 2 * HEAD_DIM), lambda h, first=first: (0, first * pairs + h))
    return pl.pallas_call(
        attend_kernel,
        grid=(pairs,),
        out_shape=[
            jax.ShapeDtypeStruct((rows, width), jnp.bfloat16),
            jax.ShapeDtypeStruct((pairs, 2, rows), jnp.float32),
        ],
        in_specs=[col(0), col(1), col(2), col(0), col(1), pl.BlockSpec(bias.shape, lambda h: (0, 0))],
        out_specs=[col(0), pl.BlockSpec((1, 2, rows), lambda h: (h, 0, 0))],
        name="attend",
    )(qkv, qkv, qkv, kv_other, kv_other, bias)


def attend_back_kernel(
    q_ref, ko_ref, vo_ref, ks_ref, vs_ref, go_ref, bias_ref, lse_ref, gq_ref, gko_ref, gvo_ref, gks_ref, gvs_ref, gk_sum, gv_sum
):
    rows = q_ref.shape[0]
    half = rows // 2
    keys = woven(ko_ref[...], ks_ref[...])
    values = woven(vo_ref[...], vs_ref[...])
    masks = head_masks()
    scale = HEAD_DIM ** (-0.5)
    for slot in (1, 0):
        seen = rows * (slot + 1)
        here = slice(slot * half, (slot + 1) * half)
        q = q_ref[here] * jnp.bfloat16(scale)
        go = go_ref[here]
        gqs, gk, gv = [], None, None
        for head in range(2):
            q_h, go_h = q * masks[head], go * masks[head]
            s = dot(keys[:seen], q_h, NT) + bias_ref[:seen, here]
            p = jnp.exp(s - lse_ref[0, head : head + 1, here])
            gp = dot(values[:seen], go_h, NT)
            row_dot = jnp.sum(p * gp, 0, keepdims=True)
            gs = (p * (gp - row_dot)).astype(jnp.bfloat16)
            gv_h = dot(p.astype(jnp.bfloat16), go_h, NN)
            gk_h = dot(gs, q_h, NN)
            gk = gk_h if gk is None else gk + gk_h
            gv = gv_h if gv is None else gv + gv_h
            gq = dot(keys[:seen], gs, TN)
            gqs.append(gq[head * HEAD_DIM : (head + 1) * HEAD_DIM])
        gq_ref[here] = (jnp.concatenate(gqs, 0).T * scale).astype(gq_ref.dtype)
        if slot == 1:
            gk_sum[...] = gk
            gv_sum[...] = gv
        else:
            gk_sum[:seen] += gk
            gv_sum[:seen] += gv
    for total, own, other in ((gk_sum, gko_ref, gks_ref), (gv_sum, gvo_ref, gvs_ref)):
        for slot in range(2):
            here = slice(slot * half, (slot + 1) * half)
            own[here] = total[2 * slot * half : (2 * slot + 1) * half].astype(own.dtype)
            other[here] = total[(2 * slot + 1) * half : (2 * slot + 2) * half].astype(other.dtype)


def attend_back(qkv, kv_other, go, bias, lse):
    rows, wide = qkv.shape
    width = wide // 3
    pairs = width // (2 * HEAD_DIM)
    lanes = 2 * HEAD_DIM
    col = lambda first: pl.BlockSpec((rows, lanes), lambda h, first=first: (0, first * pairs + h))
    out = jax.ShapeDtypeStruct((rows, width), jnp.bfloat16)
    return pl.pallas_call(
        attend_back_kernel,
        grid=(pairs,),
        out_shape=[out] * 5,
        in_specs=[
            col(0),
            col(1),
            col(2),
            col(0),
            col(1),
            col(0),
            pl.BlockSpec(bias.shape, lambda h: (0, 0)),
            pl.BlockSpec((1, 2, rows), lambda h: (h, 0, 0)),
        ],
        out_specs=[col(0)] * 5,
        scratch_shapes=[pltpu.VMEM((2 * rows, lanes), jnp.float32)] * 2,
        name="attend_back",
    )(qkv, qkv, qkv, kv_other, kv_other, go, bias, lse)


def rows_at(start, size):
    return pl.ds(pl.multiple_of(start, 16), size)


class Reduction:
    def __init__(self, at, order, refs, sems, own):
        self.at, self.own = at, own
        self.blocks, self.sends, self.gets, self.keeps = refs
        self.send_sem, self.recv_sem = sems
        self.order = order
        self.turns = len(order)
        self.last = self.turns + len(self.sends)
        self.names = order + [("seq", k) for k in range(len(self.sends))]
        self.dp_rows = self.blocks[0].shape[0] // (at.dp_n // 2)
        self.shard = self.dp_rows // at.seq_n

    def dp_of(self, j, core):
        dp = core
        for i, (_, k) in enumerate(reversed(self.order)):
            bit = (j >> i) & 1 if isinstance(j, int) else lax.rem(lax.div(j, 1 << i), 2)
            dp = dp + bit * (1 << k)
        return dp

    def landing(self, t):
        return self.blocks[t] if t <= self.turns else self.gets[t - self.turns - 1]

    def copy(self, t, src=None, dst=None):
        at = self.at
        return pltpu.make_async_remote_copy(
            src_ref=self.landing(t) if src is None else src,
            dst_ref=self.landing(t) if dst is None else dst,
            send_sem=self.send_sem.at[t],
            recv_sem=self.recv_sem.at[t],
            device_id=at.sibling() if t == 0 else at.partner(self.names[t - 1]),
            device_id_type=MESH,
        )

    def start(self):
        for j in range(self.at.dp_n // 2):
            dst = self.blocks[0].at[pl.ds(j * self.dp_rows, self.dp_rows)]
            self.copy(0, self.own(self.dp_of(j, 1 - self.at.core)), dst).start()

    def fold(self, t, lo, size):
        got = self.blocks[t - 1]
        step = self.dp_rows // 2
        if t == 1:
            first = lax.div(lo, self.dp_rows)
            for j in range(size // self.dp_rows):
                old = self.own(self.dp_of(first + j, self.at.core))
                for i in range(2):
                    here = rows_at((first + j) * self.dp_rows + i * step, step)
                    total = old[pl.ds(i * step, step)].astype(jnp.float32) + got[here].astype(jnp.float32)
                    got[here] = total.astype(got.dtype)
            return
        old = self.blocks[t - 2]
        kept = self.at.bit(self.names[t - 2]) * got.shape[0]
        for i in range(size // step):
            here = rows_at(lo + i * step, step)
            total = old[rows_at(kept + lo + i * step, step)].astype(jnp.float32) + got[here].astype(jnp.float32)
            got[here] = total.astype(got.dtype)

    def shards_of(self, t):
        got = self.landing(t - 1)
        if t == self.turns + 1:
            kept = self.at.bit(self.names[t - 2]) * self.dp_rows
            total = self.blocks[t - 2][rows_at(kept, self.dp_rows)].astype(jnp.float32) + got[...].astype(jnp.float32)
            return [total[i * self.shard : (i + 1) * self.shard] for i in range(self.at.seq_n)]
        keep = self.keeps[t - self.turns - 2]
        return [keep[i] + got[i].astype(jnp.float32) for i in range(keep.shape[0])]

    def stage(self, t):
        self.copy(t - 1).wait_recv()
        mine = self.at.bit(self.names[t - 1])
        if t <= self.turns:
            got = self.blocks[t - 1]
            half = got.shape[0] // 2
            self.fold(t, (1 - mine) * half, half)
            self.copy(t, got.at[rows_at((1 - mine) * half, half)]).start()
            self.fold(t, mine * half, half)
            return
        held = self.shards_of(t)
        m = t - self.turns - 1
        send, keep = self.sends[m], self.keeps[m]
        for i in range(len(held) // 2):
            send[i] = jnp.where(mine == 0, held[2 * i + 1], held[2 * i]).astype(send.dtype)
        self.copy(t, send).start()
        for i in range(len(held) // 2):
            keep[i] = jnp.where(mine == 0, held[2 * i], held[2 * i + 1])

    def finish(self):
        self.copy(self.last).wait_recv()
        return self.shards_of(self.last + 1)[0]


GRADS = 2 * PIECES + 4

AFTER = {
    "M0": "",
    "M1": "f01 p01",
    "M2": "f11 p11",
    "M3": "f21 p21 f02 p02",
    "T": "f31 p31",
    "A": "f12 p12 f03 p03",
    "B": "o1",
    "H0": "f22 p22",
    "H1": "f04 p04 f13 p13",
    "H2": "f32 p32",
    "H3": "f05 p05 f14 p14 f23 p23",
    "H4": "o2 f33 p33 f15 p15",
    "H5": "f24 p24",
    "Q": "",
    "K": "f34 p34 q1 f25 p25",
    "V": "k1 o3",
    "G": "v1 f35 p35",
    "N": "q2 k2 s1 o4 v2 q3 s2 k3 v3 s3 o5 q4 k4 v4 s4 q5 k5 v5 s5",
}


def back_kernel(dp_n, seq_n, *refs):
    (resid, cot, mixed, qkv, kv_other, lse, x_in, bias, vec, fc_hbm, proj_hbm, wqkv_hbm, wout_hbm) = refs[:13]
    result_out, input_out, fc_out, proj_out, qkv_out, wout_out, small_out = refs[13:20]
    (wbuf, gbuf, act, gm, a3, gh, resacc, gact, gqkv, away, back, tok, vecs, gk_sum, gv_sum) = refs[20:35]
    refs = refs[35:]
    at = Place(dp_n, seq_n)
    stages = log2(dp_n * seq_n)
    turns, folds = log2(dp_n) - 1, log2(seq_n)
    sets = [turns + 1, folds, folds, folds]
    count = sum(sets)

    def grouped(some):
        groups, first = [], 0
        for size in sets:
            groups.append(some[first : first + size])
            first += size
        return groups

    big, small_bufs = refs[:count], refs[count : 2 * count]
    (small_src, big_send, big_recv, small_send, small_recv, w_sem, swap_sem, tok_send, tok_recv, tok_own) = refs[
        2 * count :
    ]
    rows, width = resid.shape
    half = rows // 2
    shard = fc_out.shape[0]
    across = [("dp", k) for k in range(1, log2(dp_n))]
    at.enter()
    sibling = at.sibling()

    def own_rows(src):
        return lambda dp: src.at[pl.ds(pl.multiple_of(dp * (seq_n * shard), 16), seq_n * shard)]

    def reduction(kind, c):
        order = across[::-1] if kind == 0 else across
        where = lax.rem(c, gbuf.shape[0]) if not isinstance(c, int) else c % gbuf.shape[0]
        return Reduction(
            at,
            order,
            grouped([b.at[c] for b in big]),
            (big_send.at[c], big_recv.at[c]),
            own_rows(gbuf.at[where]),
        )

    def vector_reduction():
        return Reduction(
            at,
            across,
            grouped(small_bufs),
            (small_send, small_recv),
            own_rows(small_src),
        )

    def weight_copy(slot, src):
        return pltpu.make_async_copy(src, wbuf.at[slot], w_sem.at[slot])

    def load_piece(j):
        slot = 2 * lax.rem(j, 2)
        weight_copy(slot, fc_hbm.at[j]).start()
        weight_copy(slot + 1, proj_hbm.at[j]).start()

    load_piece(jnp.int32(0))

    resid_v = resid[...]
    normed, inverse = normalised(resid_v)
    act[...] = (normed * vec[3:4] + vec[4:5]).astype(jnp.bfloat16)
    grad_mlp = (branch_scale * cot[...].astype(jnp.float32)).astype(jnp.bfloat16)
    gm[...] = grad_mlp
    vecs[...] = jnp.zeros_like(vecs)
    vecs[5:6] = jnp.sum(grad_mlp.astype(jnp.float32), 0, keepdims=True)
    resacc[...] = jnp.zeros_like(resacc)
    gact[...] = jnp.zeros_like(gact)

    def after(slot):
        for name in AFTER[slot].split():
            kind, t = name[0], int(name[-1])
            if kind == "s":
                red = vector_reduction()
            else:
                c = 2 * int(name[1]) + (kind == "p") if kind in "fp" else 2 * PIECES + "oqkv".index(kind)
                red = reduction(1 if kind in "pok" else 0, int(c))
            if t < stages:
                red.stage(t)
                continue
            total = red.finish()
            if kind == "f":
                fc_out[:, int(name[1]) * width : (int(name[1]) + 1) * width] = total
            elif kind == "p":
                proj_out[int(name[1]) * shard : (int(name[1]) + 1) * shard] = total
            elif kind == "o":
                wout_out[...] = total
            elif kind == "s":
                small_out[...] = total
            else:
                part = "qkv".index(kind)
                qkv_out[:, part * width : (part + 1) * width] = total

    def after_each(prefix, i, count):
        for k in range(count):
            pl.when(i == k)(functools.partial(after, f"{prefix}{k}"))

    def piece(j, carry):
        slot = 2 * lax.rem(j, 2)
        pl.when(j + 1 < PIECES)(lambda: load_piece(j + 1))
        weight_copy(slot, fc_hbm.at[j]).wait()
        weight_copy(slot + 1, proj_hbm.at[j]).wait()
        fc, proj = wbuf.at[slot], wbuf.at[slot + 1]
        bias_fc = vec[pl.ds(6 + j, 1)]

        def some(r, total):
            here = pl.ds(pl.multiple_of(r * half, 16), half)
            u = dot(act[here], fc[...], NN) + bias_fc
            bent = jnp.tanh(gelu_root * (u + gelu_coeff * u * u * u))
            hidden = (0.5 * u * (1.0 + bent)).astype(jnp.bfloat16)
            inner = gelu_root * (1.0 + 3.0 * gelu_coeff * u * u)
            slope = 0.5 * (1.0 + bent) + 0.5 * u * (1.0 - bent * bent) * inner
            a3[here] = hidden
            resacc[here] += dot(hidden, proj[...], NN)
            grad_u = (dot(gm[here], proj[...], NT) * slope).astype(jnp.bfloat16)
            gh[here] = grad_u
            gact[here] += dot(grad_u, fc[...], NT)
            return total + jnp.sum(grad_u.astype(jnp.float32), 0, keepdims=True)

        total = lax.fori_loop(0, 2, some, jnp.zeros((1, width), jnp.float32))
        vecs[pl.ds(6 + j, 1)] = total
        for kind, (left, right) in enumerate(((act, gh), (a3, gm))):
            c = 2 * j + kind
            red = reduction(kind, c)
            pl.when(c >= gbuf.shape[0])(
                lambda red=red, c=c, kind=kind: reduction(kind, c - gbuf.shape[0]).copy(0).wait_send()
            )
            gbuf[lax.rem(c, gbuf.shape[0])] = dot(left[...], right[...], TN).astype(jnp.bfloat16)
            red.start()
        after_each("M", j, PIECES)
        return carry

    lax.fori_loop(0, PIECES, piece, 0)
    for slot in range(3):
        weight_copy(slot, wqkv_hbm.at[:, pl.ds(slot * width, width)]).start()
    weight_copy(3, wout_hbm).start()

    def token_copies(which, j):
        slot, rest = j // at.parts, j % at.parts
        quarter = at.core + slot * (3 - 2 * at.core)
        to_seq = quarter * at.parts + rest
        mine = (to_seq == at.seq) & (at.source_core == at.core)
        place = at.seq - at.source_core * at.seqs
        out = (result_out, input_out)[which]
        remote = pltpu.make_async_remote_copy(
            src_ref=tok.at[which, j],
            dst_ref=out.at[place],
            send_sem=tok_send.at[which, j],
            recv_sem=tok_recv.at[which, place],
            device_id=(at.pair * 2 + at.source_core, to_seq),
            device_id_type=MESH,
        )
        local = pltpu.make_async_copy(tok.at[which, j], out.at[place], tok_own.at[which])
        return mine, remote, local

    def tokens_start(which, value):
        tok[which] = value.astype(jnp.bfloat16).reshape(tok.shape[1:])
        for j in range(seq_n // 2):
            mine, remote, local = token_copies(which, j)
            pl.when(jnp.logical_not(mine))(remote.start)
            pl.when(mine)(local.start)

    def tokens_wait(which):
        for j in range(seq_n // 2):
            mine, remote, local = token_copies(which, j)
            pl.when(jnp.logical_not(mine))(remote.wait_send)
            pl.when(mine)(local.wait)
        for i in range(at.seqs):
            comes = jnp.logical_not((at.core * at.seqs + i == at.seq) & (at.quarter_core == at.core))
            arrival = pltpu.make_async_remote_copy(
                src_ref=tok.at[which, 0],
                dst_ref=(result_out, input_out)[which].at[i],
                send_sem=tok_send.at[which, 0],
                recv_sem=tok_recv.at[which, i],
                device_id=sibling,
                device_id_type=MESH,
            )
            pl.when(comes)(arrival.wait_recv)

    tokens_start(0, resid[...] + branch_scale * (resacc[...] + vec[5:6]))
    after("T")

    normed, inverse = normalised(resid[...])
    grad_two = gact[...]
    vecs[3:4] = jnp.sum(grad_two * normed, 0, keepdims=True)
    vecs[4:5] = jnp.sum(grad_two, 0, keepdims=True)
    grad_mid = cot[...].astype(jnp.float32) + norm_spread(grad_two, normed, inverse, vec[3:4])
    gact[...] = grad_mid
    grad_branch = (branch_scale * grad_mid).astype(jnp.bfloat16)
    act[...] = grad_branch
    vecs[2:3] = jnp.sum(grad_branch.astype(jnp.float32), 0, keepdims=True)

    c_out = 2 * PIECES
    reduction(0, c_out - gbuf.shape[0]).copy(0).wait_send()
    gbuf[c_out % gbuf.shape[0]] = dot(mixed[...], grad_branch, TN).astype(jnp.bfloat16)
    reduction(1, c_out).start()
    after("A")
    weight_copy(3, wout_hbm).wait()
    gm[...] = dot(grad_branch, wbuf[3], NT).astype(jnp.bfloat16)
    after("B")

    pairs = width // (2 * HEAD_DIM)

    def heads(i, carry):
        at_q = pl.ds(pl.multiple_of(i * 128, 128), 128)
        at_k = pl.ds(pl.multiple_of(width + i * 128, 128), 128)
        at_v = pl.ds(pl.multiple_of(2 * width + i * 128, 128), 128)
        attend_back_kernel(
            qkv.at[:, at_q],
            qkv.at[:, at_k],
            qkv.at[:, at_v],
            kv_other.at[:, at_q],
            kv_other.at[:, at_k],
            gm.at[:, at_q],
            bias,
            lse.at[pl.ds(i, 1)],
            gqkv.at[:, at_q],
            gqkv.at[:, at_k],
            gqkv.at[:, at_v],
            away.at[:, at_q],
            away.at[:, at_k],
            gk_sum,
            gv_sum,
        )
        after_each("H", i, 6)
        return carry

    lax.fori_loop(0, pairs, heads, 0)

    exchange = pltpu.make_async_remote_copy(
        src_ref=away,
        dst_ref=back,
        send_sem=swap_sem.at[0],
        recv_sem=swap_sem.at[1],
        device_id=sibling,
        device_id_type=MESH,
    )
    exchange.start()
    normed, inverse = normalised(x_in[...].astype(jnp.float32))
    act[...] = (normed * vec[0:1] + vec[1:2]).astype(jnp.bfloat16)

    def grad_of(part):
        c = c_out + 1 + part
        kind = part % 2
        here = pl.ds(part * width, width)
        if part > 0:
            far = pl.ds((part - 1) * width, width)
            gqkv[:, here] = (gqkv[:, here].astype(jnp.float32) + back[:, far].astype(jnp.float32)).astype(jnp.bfloat16)
        reduction(kind, c - gbuf.shape[0]).copy(0).wait_send()
        gbuf[c % gbuf.shape[0]] = dot(act[...], gqkv[:, here], TN).astype(jnp.bfloat16)
        reduction(kind, c).start()
        weight_copy(part, wqkv_hbm.at[:, here]).wait()

    def column_sum(part):
        return jnp.sum(gqkv[:, pl.ds(part * width, width)].astype(jnp.float32), 0, keepdims=True)

    grad_of(0)
    after("Q")
    exchange.wait()
    grad_of(1)
    after("K")
    grad_of(2)
    after("V")
    first, third = column_sum(0), column_sum(2)
    for row, value in ((10, first), (11, first), (12, third), (13, third)):
        vecs[row : row + 1] = value
    grad_one = dot(gqkv[:, pl.ds(0, width)], wbuf[0], NT)
    grad_one = grad_one + dot(gqkv[:, pl.ds(width, width)], wbuf[1], NT)
    resacc[...] = grad_one + dot(gqkv[:, pl.ds(2 * width, width)], wbuf[2], NT)
    after("G")
    grad_one = resacc[...]
    normed, inverse = normalised(x_in[...].astype(jnp.float32))
    vecs[0:1] = jnp.sum(grad_one * normed, 0, keepdims=True)
    vecs[1:2] = jnp.sum(grad_one, 0, keepdims=True)
    tokens_start(1, gact[...] + norm_spread(grad_one, normed, inverse, vec[0:1]))
    columns = vecs[...].T
    small_src[...] = columns
    lane = lax.broadcasted_iota(jnp.int32, (1, 128), 1)
    even, odd = (lane == 10) | (lane == 12), (lane == 11) | (lane == 13)
    n_dev = dp_n * seq_n
    for d in range(n_dev):
        start = 2 * shard * (d % (n_dev // 2))
        kept = columns[d * shard : (d + 1) * shard]
        kept = jnp.where(even, columns[start : start + shard], kept)
        kept = jnp.where(odd, columns[start + shard : start + 2 * shard], kept)
        small_src[d * shard : (d + 1) * shard] = kept
    vector_reduction().start()
    after("N")
    for c in range(GRADS):
        red = reduction(0, c)
        for t in range(0 if c >= GRADS - gbuf.shape[0] else 1, stages):
            red.copy(t).wait_send()
    for t in range(stages):
        vector_reduction().copy(t).wait_send()
    tokens_wait(0)
    tokens_wait(1)


def back_all(mesh_shape, shards, resid, cot, mixed, qkv, kv_other, lse, x_rows, bias, vec, fc, proj, wqkv, wout):
    dp_n, seq_n = mesh_shape
    rows, width = resid.shape
    stages = log2(dp_n * seq_n)
    blk = rows // (seq_n // 2)
    shard = width // (dp_n * seq_n)
    vmem = pl.BlockSpec(memory_space=pltpu.VMEM)
    hbm = pl.BlockSpec(memory_space=ANY)
    DMA = pltpu.SemaphoreType.DMA
    low, full = jnp.bfloat16, jnp.float32
    slots = 4

    def buffers(lead, cols, dtype):
        turns, folds = log2(dp_n) - 1, log2(seq_n)
        parts = [(seq_n >> (m + 1), shard, cols) for m in range(folds)]
        return (
            [pltpu.VMEM(lead + (width // 2 >> t, cols), dtype) for t in range(turns + 1)]
            + [pltpu.VMEM(lead + p, dtype) for p in parts] * 2
            + [pltpu.VMEM(lead + p, full) for p in parts]
        )

    token = jax.ShapeDtypeStruct((seq_n // 2, blk, width), low)
    out = pl.pallas_call(
        functools.partial(back_kernel, dp_n, seq_n),
        out_shape=[token, token] + [jax.ShapeDtypeStruct(s, full) for s in shards + [(shard, 128)]],
        in_specs=[vmem] * 9 + [hbm] * 4,
        out_specs=[hbm] * 2 + [vmem] * 5,
        scratch_shapes=[
            pltpu.VMEM((4, width, width), low),
            pltpu.VMEM((slots, width, width), low),
            pltpu.VMEM((rows, width), low),
            pltpu.VMEM((rows, width), low),
            pltpu.VMEM((rows, width), low),
            pltpu.VMEM((rows, width), low),
            pltpu.VMEM((rows, width), full),
            pltpu.VMEM((rows, width), full),
            pltpu.VMEM((rows, 3 * width), low),
            pltpu.VMEM((rows, 2 * width), low),
            pltpu.VMEM((rows, 2 * width), low),
            pltpu.VMEM((2, seq_n // 2, blk, width), low),
            pltpu.VMEM((128, width), full),
            pltpu.VMEM((2 * rows, 128), full),
            pltpu.VMEM((2 * rows, 128), full),
        ]
        + buffers((GRADS,), width, low)
        + buffers((), 128, full)
        + [
            pltpu.VMEM((width, 128), full),
            DMA((GRADS, stages)),
            DMA((GRADS, stages)),
            DMA((stages,)),
            DMA((stages,)),
            DMA((4,)),
            DMA((2,)),
            DMA((2, seq_n // 2)),
            DMA((2, seq_n // 2)),
            DMA((2,)),
        ],
        compiler_params=pltpu.CompilerParams(
            collective_id=4, has_side_effects=True, vmem_limit_bytes=64 * 1024 * 1024 - 65536
        ),
        name="back_all",
    )(resid, cot, mixed, qkv, kv_other, lse, x_rows, bias, vec, fc, proj, wqkv, wout)
    return out[:2], out[2:]


def normalised(rows):
    center = rows - jnp.mean(rows, -1, keepdims=True)
    inverse = lax.rsqrt(jnp.mean(center * center, -1, keepdims=True) + norm_eps)
    return center * inverse, inverse


def norm_spread(grad_in, normed, inverse, gain):
    scaled = grad_in * gain
    return inverse * (
        scaled
        - jnp.mean(scaled, -1, keepdims=True)
        - normed * jnp.mean(scaled * normed, -1, keepdims=True)
    )


def packed(vectors, row_unit, dtype):
    flat = jnp.concatenate(vectors, -1)
    size = flat.shape[-1]
    rows = -(-size // (128 * row_unit)) * row_unit
    flat = jnp.pad(flat, [(0, 0)] * (flat.ndim - 1) + [(0, rows * 128 - size)])
    return flat.reshape(flat.shape[:-1] + (rows, 128)).astype(dtype)


def unpacked(rows, sizes):
    flat = rows.reshape(rows.shape[0], -1)
    out, first = [], 0
    for size in sizes:
        out.append(flat[:, first : first + size].reshape(-1))
        first += size
    return out


def block(mesh_shape, *args):
    (
        block_input,
        segments,
        cotangent,
        ln1_gain,
        ln1_bias,
        w_qkv,
        b_qv,
        w_out,
        b_out,
        ln2_gain,
        ln2_bias,
        w_fc,
        b_fc,
        w_proj,
        b_proj,
    ) = args
    dp_n, seq_n = mesh_shape
    n_dev = dp_n * seq_n
    micro_count, seq_count, stretch, width = block_input.shape
    seq_len = segments.shape[2]
    seqs = micro_count * seq_count
    assert 2 * seqs == seq_n and seq_n % 4 == 0
    at = Place(dp_n, seq_n)
    vectors = (ln1_gain, ln1_bias, b_qv, b_out, ln2_gain, ln2_bias, b_fc, b_proj)
    sizes = [v.shape[0] for v in vectors]
    gathered = gather_all(
        mesh_shape,
        block_input.reshape(seqs, stretch, width),
        cotangent.reshape(seqs, stretch, width),
        segments.reshape(seqs, seq_len),
        (w_qkv, w_out, w_fc, w_proj, packed(vectors, 16, jnp.bfloat16)),
    )
    x_rows, cot_rows, seg_other, weight_qkv, weight_out, weight_fc, weight_proj, small = gathered
    rows = seq_len // 2
    half = rows // 2
    x_rows = x_rows.reshape(rows, width).astype(jnp.float32)
    grad_out = cot_rows.reshape(rows, width).astype(jnp.float32)
    weight_qkv, weight_out, weight_fc, weight_proj = [
        w.reshape(-1, w.shape[-1]) for w in (weight_qkv, weight_out, weight_fc, weight_proj)
    ]
    gain_one, bias_one, bias_qv, bias_out, gain_two, bias_two, bias_fc, bias_proj = [
        v.astype(jnp.float32) for v in unpacked(small, sizes)
    ]

    seg_all = jnp.where(at.source_core == at.core, segments.reshape(seqs, seq_len), seg_other)
    seg = lax.dynamic_index_in_dim(seg_all, at.seq - at.source_core * seqs, 0, keepdims=False)
    quarter = jnp.arange(half, dtype=jnp.int32)
    own_first = [at.core * half, (3 - at.core) * half]
    other_first = [(1 - at.core) * half, (2 + at.core) * half]
    firsts = [own_first[0], other_first[0], own_first[1], other_first[1]]
    key_place = jnp.concatenate([f + quarter for f in firsts])
    key_seg = jnp.concatenate([lax.dynamic_slice_in_dim(seg, f, half, 0) for f in firsts])
    query_place = jnp.concatenate([key_place[:half], key_place[2 * half : 3 * half]])
    query_seg = jnp.concatenate([key_seg[:half], key_seg[2 * half : 3 * half]])
    visible = (key_seg[:, None] == query_seg[None, :]) & (key_place[:, None] <= query_place[None, :])
    bias = jnp.where(visible, 0.0, masked_score).astype(jnp.float32)

    normed_out, normed_one, inverse_one = layer_norm(x_rows, gain_one, bias_one)
    act_one = normed_out.astype(jnp.bfloat16)
    bias_full = jnp.concatenate([bias_qv[:width], jnp.zeros((width,), jnp.float32), bias_qv[width:]])
    qkv = (jnp.dot(act_one, weight_qkv, preferred_element_type=jnp.float32) + bias_full).astype(jnp.bfloat16)
    kv_other = swap(mesh_shape, qkv, (width, 2 * width), 2)
    mixed_out, lse = attend(qkv, kv_other, bias)
    resid_mid = x_rows + branch_scale * (
        jnp.dot(mixed_out, weight_out, preferred_element_type=jnp.float32) + bias_out
    )

    normed_out, normed_two, inverse_two = layer_norm(resid_mid, gain_two, bias_two)
    act_two = normed_out.astype(jnp.bfloat16)
    hidden = jnp.dot(act_two, weight_fc, preferred_element_type=jnp.float32) + bias_fc
    act_three = gelu_tanh(hidden).astype(jnp.bfloat16)
    result = resid_mid + branch_scale * (
        jnp.dot(act_three, weight_proj, preferred_element_type=jnp.float32) + bias_proj
    )
    grad_mlp = (branch_scale * grad_out).astype(jnp.bfloat16)
    grad_bproj = jnp.sum(grad_mlp.astype(jnp.float32), 0)
    grad_wproj = dot(act_three, grad_mlp, TN)
    grad_act3 = dot(grad_mlp, weight_proj, NT)
    grad_hidden = (grad_act3 * gelu_slope(hidden)).astype(jnp.bfloat16)
    grad_bfc = jnp.sum(grad_hidden.astype(jnp.float32), 0)
    grad_wfc = dot(act_two, grad_hidden, TN)
    grad_act2 = dot(grad_hidden, weight_fc, NT)
    grad_norm2, grad_gain2, grad_bias2 = norm_back(grad_act2, normed_two, inverse_two, gain_two)
    grad_mid = grad_out + grad_norm2

    grad_branch = (branch_scale * grad_mid).astype(jnp.bfloat16)
    grad_bout = jnp.sum(grad_branch.astype(jnp.float32), 0)
    grad_wout = dot(mixed_out, grad_branch, TN)
    grad_mixed = dot(grad_branch, weight_out, NT).astype(jnp.bfloat16)
    grad_q, grad_k, grad_v, away_k, away_v = attend_back(qkv, kv_other, grad_mixed, bias, lse)
    back = swap(mesh_shape, jnp.concatenate([away_k, away_v], 1), (0, 2 * width), 3)
    key_value = jnp.concatenate([grad_k, grad_v], 1).astype(jnp.float32) + back.astype(jnp.float32)
    grad_qkv = jnp.concatenate([grad_q, key_value.astype(jnp.bfloat16)], 1)
    grad_wide = grad_qkv.astype(jnp.float32)
    grad_bqv = jnp.concatenate([jnp.sum(grad_wide[:, :width], 0), jnp.sum(grad_wide[:, 2 * width :], 0)])
    grad_wqkv = dot(act_one, grad_qkv, TN)
    grad_act1 = dot(grad_qkv, weight_qkv, NT)
    grad_norm1, grad_gain1, grad_bias1 = norm_back(grad_act1, normed_one, inverse_one, gain_one)
    grad_input = grad_mid + grad_norm1

    vec_grads = (grad_gain1, grad_bias1, grad_bqv, grad_bout, grad_gain2, grad_bias2, grad_bfc, grad_bproj)
    token_block = (seq_n // 2, stretch, width)
    parts = [
        g.astype(jnp.bfloat16).reshape((n_dev, -1, g.shape[-1]))
        for g in (grad_wqkv, grad_wout, grad_wfc, grad_wproj)
    ] + [packed([v.reshape(n_dev, -1) for v in vec_grads], 8, jnp.float32)]
    (result, grad_input), totals = reduce_all(
        mesh_shape,
        [result.astype(jnp.bfloat16).reshape(token_block), grad_input.astype(jnp.bfloat16).reshape(token_block)],
        parts,
    )
    owned = unpacked(totals[4].reshape(1, -1), sizes)
    shape = block_input.shape
    return (
        result.reshape(shape),
        grad_input.reshape(shape),
        owned[0],
        owned[1],
        totals[0],
        owned[2],
        totals[1],
        owned[3],
        owned[4],
        owned[5],
        totals[2],
        owned[6],
        totals[3],
        owned[7],
    )


def mask_of(at, seqs, seg_own, seg_other, half):
    seg_all = jnp.where(at.source_core == at.core, seg_own, seg_other)
    seg = lax.dynamic_index_in_dim(seg_all, at.seq - at.source_core * seqs, 0, keepdims=False)
    quarter = jnp.arange(half, dtype=jnp.int32)
    firsts = [at.core * half, (1 - at.core) * half, (3 - at.core) * half, (2 + at.core) * half]
    key_place = jnp.concatenate([f + quarter for f in firsts])
    key_seg = jnp.concatenate([lax.dynamic_slice_in_dim(seg, f, half, 0) for f in firsts])
    query_place = jnp.concatenate([key_place[:half], key_place[2 * half : 3 * half]])
    query_seg = jnp.concatenate([key_seg[:half], key_seg[2 * half : 3 * half]])
    visible = (key_seg[:, None] == query_seg[None, :]) & (key_place[:, None] <= query_place[None, :])
    return jnp.where(visible, 0.0, masked_score).astype(jnp.float32)


def fused_block(mesh_shape, *args):
    (
        block_input,
        segments,
        cotangent,
        ln1_gain,
        ln1_bias,
        w_qkv,
        b_qv,
        w_out,
        b_out,
        ln2_gain,
        ln2_bias,
        w_fc,
        b_fc,
        w_proj,
        b_proj,
    ) = args
    dp_n, seq_n = mesh_shape
    n_dev = dp_n * seq_n
    micro_count, seq_count, stretch, width = block_input.shape
    seq_len = segments.shape[2]
    seqs = micro_count * seq_count
    assert 2 * seqs == seq_n and seq_n % 4 == 0 and w_fc.shape[1] == PIECES * width
    at = Place(dp_n, seq_n)
    shard = width // n_dev
    fc_cols = w_fc.reshape(shard, n_dev, PIECES, shard).transpose(0, 2, 1, 3).reshape(shard, -1)
    vectors = jnp.concatenate(
        [jnp.stack([ln1_gain, ln1_bias, b_out, ln2_gain, ln2_bias, b_proj]), b_fc.reshape(PIECES, shard), b_qv.reshape(2, shard)]
    )
    vectors = jnp.pad(vectors, ((0, 128 - vectors.shape[0]), (0, 0))).T
    gathered = gather_all(
        mesh_shape,
        block_input.reshape(seqs, stretch, width),
        cotangent.reshape(seqs, stretch, width),
        segments.reshape(seqs, seq_len),
        (w_qkv, w_out, fc_cols, w_proj, vectors),
        (2, 3),
    )
    x_low, cot_rows, seg_other, weight_qkv, weight_out, weight_fc, weight_proj, small = gathered
    rows = seq_len // 2
    half = rows // 2
    x_low, cot_rows = x_low.reshape(rows, width), cot_rows.reshape(rows, width)
    x_rows = x_low.astype(jnp.float32)
    weight_qkv, weight_out = [w.reshape(width, w.shape[-1]) for w in (weight_qkv, weight_out)]
    weight_fc, weight_proj = [w.reshape(PIECES, width, width) for w in (weight_fc, weight_proj)]
    vec = small.reshape(width, 128).T[:16].astype(jnp.float32)
    bias_qv = vec[10:12].reshape(2, n_dev, shard).transpose(1, 0, 2).reshape(-1)
    bias = mask_of(at, seqs, segments.reshape(seqs, seq_len), seg_other, half)

    normed, _ = normalised(x_rows)
    act_one = (normed * vec[0] + vec[1]).astype(jnp.bfloat16)
    bias_full = jnp.concatenate([bias_qv[:width], jnp.zeros((width,), jnp.float32), bias_qv[width:]])
    qkv = (jnp.dot(act_one, weight_qkv, preferred_element_type=jnp.float32) + bias_full).astype(jnp.bfloat16)
    kv_other = swap(mesh_shape, qkv, (width, 2 * width), 2)
    mixed_out, lse = attend(qkv, kv_other, bias)
    resid_mid = x_rows + branch_scale * (jnp.dot(mixed_out, weight_out, preferred_element_type=jnp.float32) + vec[2])
    shapes = [(shard, PIECES * width), (PIECES * shard, width), (shard, 3 * width), (shard, width)]
    (result, grad_input), (grad_fc, grad_proj, grad_qkv, grad_out, columns) = back_all(
        mesh_shape,
        shapes,
        resid_mid,
        cot_rows,
        mixed_out,
        qkv,
        kv_other,
        lse,
        x_low,
        bias,
        vec,
        weight_fc,
        weight_proj,
        weight_qkv,
        weight_out,
    )
    grad_fc = grad_fc.reshape(shard, PIECES, n_dev, shard).transpose(0, 2, 1, 3).reshape(shard, -1)
    lines = columns.T
    grad_bqv = jnp.where(at.me < n_dev // 2, lines[10:12], lines[12:14]).reshape(-1)
    shape = block_input.shape
    return (
        result.reshape(shape),
        grad_input.reshape(shape),
        lines[0],
        lines[1],
        grad_qkv,
        grad_bqv,
        grad_out,
        lines[2],
        lines[3],
        lines[4],
        grad_fc,
        lines[6:10].reshape(-1),
        grad_proj,
        lines[5],
    )


def whole_block(mesh_shape, *args):
    aligned = args[5].shape[0] % 8 == 0 and mesh_shape[1] == 4
    return (fused_block if aligned else block)(mesh_shape, *args)


def solution(mesh):
    both = ("dp", "seq")
    tokens, vector, matrix = P(None, "dp", "seq", None), P(both), P(both, None)
    return jax.shard_map(
        functools.partial(whole_block, (mesh.shape["dp"], mesh.shape["seq"])),
        mesh=mesh,
        in_specs=(
            tokens,
            P(None, "dp", None),
            tokens,
            vector,
            vector,
            matrix,
            vector,
            matrix,
            vector,
            vector,
            vector,
            matrix,
            vector,
            matrix,
            vector,
        ),
        out_specs=(
            tokens,
            tokens,
            vector,
            vector,
            matrix,
            vector,
            matrix,
            vector,
            vector,
            vector,
            matrix,
            vector,
            matrix,
            vector,
        ),
        check_vma=False,
    )
```

```python
import functools

import jax
import jax.numpy as jnp
from jax import lax
from jax.experimental import pallas as pl
from jax.experimental.pallas import tpu as pltpu
from jax.sharding import PartitionSpec as P

HEADS = 12
HEAD_DIM = 64
MESH = pl.DeviceIdType.MESH
PIECES = 4
ANY = pl.ANY

branch_scale = 48.0 ** (-0.5)
norm_eps = 1e-05
masked_score = -1e30
gelu_coeff = 0.044715
gelu_root = (2.0 / 3.141592653589793) ** 0.5


def layer_norm(tok_rows, gain_vec, bias_vec):
    center = tok_rows - jnp.mean(tok_rows, -1, keepdims=True)
    inverse = lax.rsqrt(jnp.mean(center * center, -1, keepdims=True) + norm_eps)
    normed = center * inverse
    return (normed * gain_vec + bias_vec, normed, inverse)


def norm_back(grad_in, normed, inverse, gain_vec):
    grad_gain = jnp.sum(grad_in * normed, 0)
    grad_bias = jnp.sum(grad_in, 0)
    scaled = grad_in * gain_vec
    spread = (
        scaled
        - jnp.mean(scaled, -1, keepdims=True)
        - normed * jnp.mean(scaled * normed, -1, keepdims=True)
    )
    return (inverse * spread, grad_gain, grad_bias)


def gelu_tanh(pre_act):
    tanh_val = jnp.tanh(gelu_root * (pre_act + gelu_coeff * pre_act * pre_act * pre_act))
    return 0.5 * pre_act * (1.0 + tanh_val)


def gelu_slope(pre_act):
    tanh_val = jnp.tanh(gelu_root * (pre_act + gelu_coeff * pre_act * pre_act * pre_act))
    inner_slope = gelu_root * (1.0 + 3.0 * gelu_coeff * pre_act * pre_act)
    return 0.5 * (1.0 + tanh_val) + 0.5 * pre_act * (1.0 - tanh_val * tanh_val) * inner_slope


def log2(n):
    k = n.bit_length() - 1
    assert 1 << k == n
    return k


class Place:
    def __init__(self, dp_n, seq_n):
        self.dp_n, self.seq_n = dp_n, seq_n
        self.dp, self.seq = lax.axis_index("dp"), lax.axis_index("seq")
        self.core = lax.rem(self.dp, 2)
        self.pair = lax.div(self.dp, 2)
        self.me = self.dp * seq_n + self.seq
        self.seqs = seq_n // 2
        self.parts = seq_n // 4
        self.quarter = lax.div(self.seq, self.parts)
        self.quarter_core = self.core_of(self.quarter)
        self.source_core = lax.div(self.seq, self.seqs)

    def core_of(self, quarter):
        return lax.rem(lax.div(quarter + 1, 2), 2)

    def bit(self, name):
        axis, k = name
        return lax.rem(lax.div(self.seq if axis == "seq" else self.dp, 1 << k), 2)

    def delta(self, name):
        axis, k = name
        return (1 - 2 * self.bit(name)) * ((1 << k) * (1 if axis == "seq" else self.seq_n))

    def partner(self, name):
        axis, k = name
        step = (1 - 2 * self.bit(name)) * (1 << k)
        if axis == "seq":
            return (self.dp, self.seq + step)
        return (self.dp + step, self.seq)

    def sibling(self):
        return self.partner(("dp", 0))

    def enter(self):
        barrier = pltpu.get_barrier_semaphore()
        count = 0
        for core_step in range(2):
            for seq_step in range(self.seq_n):
                if core_step == 0 and seq_step == 0:
                    continue
                other = (
                    self.pair * 2 + lax.rem(self.core + core_step, 2),
                    lax.rem(self.seq + seq_step, self.seq_n),
                )
                pl.semaphore_signal(barrier, inc=1, device_id=other, device_id_type=MESH)
                count += 1
        for k in range(1, log2(self.dp_n)):
            pl.semaphore_signal(barrier, inc=1, device_id=self.partner(("dp", k)), device_id_type=MESH)
            count += 1
        pl.semaphore_wait(barrier, count)


def orders_of(dp_n, seq_n):
    along = [("seq", k) for k in reversed(range(log2(seq_n)))]
    across = [("dp", k) for k in range(1, log2(dp_n))]
    back = across[::-1]
    return {
        "zxy": along + across,
        "zyx": along + back,
        "xyz": across + along,
        "yxz": back + along,
    }


def repeat(count, body):
    if count <= 16:
        for j in range(count):
            body(j)
    else:
        lax.fori_loop(0, count, lambda j, c: (body(j), c)[1], 0)


def spread(j, deltas):
    total = 0
    for i, delta in enumerate(deltas):
        if isinstance(j, int):
            if (j >> i) & 1:
                total = total + delta
        else:
            total = total + lax.rem(lax.div(j, 1 << i), 2) * delta
    return total


def resolve(shape, cut):
    axis, pieces, k = cut
    if axis == 1 and shape[1] % (8 * pieces):
        axis = 2
    unit = 8 if axis == 1 else 128
    units = shape[axis] // unit
    start, stop = units * k // pieces, units * (k + 1) // pieces
    return axis, start * unit, (stop - start) * unit


def piece_shape(shape, cut):
    axis, _, size = resolve(shape, cut)
    shape = list(shape)
    shape[axis] = size
    return tuple(shape[1:])


def piece_of(ref, lead, cut):
    axis, start, size = resolve(ref.shape, cut)
    where = [slice(None)] * 2
    where[axis - 1] = pl.ds(start, size)
    return ref.at[(lead, *where)]


GATHER = (
    (0, 2, 3, 0, "zxy", 0),
    (0, 2, 3, 1, "zyx", 0),
    (4, 2, 1, 0, "zyx", 0),
    (0, 2, 3, 2, "zxy", 1),
    (1, 2, 1, 0, "zyx", 1),
    (2, 2, 4, 0, "zxy", 2),
    (3, 1, 4, 0, "zyx", 2),
    (2, 2, 4, 1, "zxy", 3),
    (3, 1, 4, 1, "zyx", 3),
    (2, 2, 4, 2, "zxy", 4),
    (3, 1, 4, 2, "zyx", 4),
    (2, 2, 4, 3, "zxy", 5),
    (3, 1, 4, 3, "zyx", 5),
)
X_WAVE, COT_WAVE = 2, 5


def gather_kernel(dp_n, seq_n, major, x_ref, cot_ref, seg_ref, *refs):
    n_arr = 5
    shard = refs[:n_arr]
    x_out, cot_out, seg_out = refs[n_arr : n_arr + 3]
    full = refs[n_arr + 3 : n_arr + 3 + n_arr]
    (send_sem, recv_sem, side_send, side_recv, own_sem, tok_send, tok_recv, tok_own, seg_sem) = refs[
        2 * n_arr + 3 :
    ]
    at = Place(dp_n, seq_n)
    orders = orders_of(dp_n, seq_n)
    stages = len(orders["zxy"])
    at.enter()
    sibling = at.sibling()

    piece = piece_of

    def put(src, dst, s_sem, r_sem, device):
        pltpu.make_async_remote_copy(
            src_ref=src, dst_ref=dst, send_sem=s_sem, recv_sem=r_sem, device_id=device, device_id_type=MESH
        ).start()

    def place_of(a, idx, cut, count=None):
        if a in major:
            idx = idx + cut[2] * dp_n * seq_n
            return full[a].at[idx if count is None else pl.ds(idx, count)]
        return piece(full[a], idx if count is None else pl.ds(idx, count), cut)

    def group(a, cut, count, s_sem, r_sem, device):
        whole = place_of(a, 0, cut, count)
        return pltpu.make_async_remote_copy(
            src_ref=whole, dst_ref=whole, send_sem=s_sem, recv_sem=r_sem, device_id=device, device_id_type=MESH
        )

    def own_src(a, cut):
        return piece(shard[a], 0, cut)

    def stage(c, t):
        a, *cut, order, _ = GATHER[c]
        names = orders[order]
        deltas = [at.delta(n) for n in names]
        if t > 0:
            group(a, cut, 1 << (t - 1), send_sem.at[c, t - 1], recv_sem.at[c, t - 1], sibling).wait_recv()

            def pass_on(j):
                idx = at.me + deltas[t - 1] + spread(j, deltas[: t - 1])
                place = place_of(a, idx, cut)
                put(place, place, side_send.at[c, t], side_recv.at[c, t], sibling)

            if t < stages:
                partner = at.partner(names[t])

                def onward(j):
                    idx = at.me + spread(j, deltas[:t])
                    place = place_of(a, idx, cut)
                    put(own_src(a, cut) if isinstance(j, int) and j == 0 else place, place, send_sem.at[c, t], recv_sem.at[c, t], partner)

                onward(0)
                repeat((1 << t) - 1, lambda j: onward(j + 1))
            repeat(1 << (t - 1), pass_on)
        else:
            partner = at.partner(names[0])
            place = place_of(a, at.me, cut)
            put(own_src(a, cut), place, send_sem.at[c, 0], recv_sem.at[c, 0], partner)
            put(own_src(a, cut), place, side_send.at[c, 0], side_recv.at[c, 0], sibling)
            pltpu.make_async_copy(own_src(a, cut), place, own_sem.at[c]).start()

    slot = lax.div(at.quarter, 2) * at.parts + lax.rem(at.seq, at.parts)
    seg_copy = pltpu.make_async_remote_copy(
        src_ref=seg_ref,
        dst_ref=seg_out,
        send_sem=seg_sem.at[0],
        recv_sem=seg_sem.at[1],
        device_id=sibling,
        device_id_type=MESH,
    )

    def token_copies(which, src, dst, i):
        to_seq = at.core * at.seqs + i
        mine = (to_seq == at.seq) & (at.quarter_core == at.core)
        remote = pltpu.make_async_remote_copy(
            src_ref=src.at[i],
            dst_ref=dst.at[slot],
            send_sem=tok_send.at[which, i],
            recv_sem=tok_recv.at[which, at.seq],
            device_id=(at.pair * 2 + at.quarter_core, to_seq),
            device_id_type=MESH,
        )
        local = pltpu.make_async_copy(src.at[i], dst.at[slot], tok_own.at[which])
        return mine, remote, local

    def tokens_start(which, src, dst):
        for i in range(at.seqs):
            mine, remote, local = token_copies(which, src, dst, i)
            pl.when(jnp.logical_not(mine))(remote.start)
            pl.when(mine)(local.start)

    def tokens_wait(which, src, dst):
        for i in range(at.seqs):
            mine, remote, local = token_copies(which, src, dst, i)
            pl.when(jnp.logical_not(mine))(remote.wait_send)
            pl.when(mine)(local.wait)
        for z in range(seq_n):
            comes = (at.core_of(z // at.parts) == at.core) & jnp.logical_not(
                (at.seq == z) & (at.source_core == at.core)
            )
            arrival = pltpu.make_async_remote_copy(
                src_ref=src.at[0],
                dst_ref=dst.at[0],
                send_sem=tok_send.at[which, 0],
                recv_sem=tok_recv.at[which, z],
                device_id=sibling,
                device_id_type=MESH,
            )
            pl.when(comes)(arrival.wait_recv)

    seg_copy.start()
    waves = stages + 1 + max(c[5] for c in GATHER)
    for wave in range(waves):
        for c in range(len(GATHER)):
            t = wave - GATHER[c][5]
            if 0 <= t <= stages:
                stage(c, t)
        if wave == X_WAVE:
            tokens_start(0, x_ref, x_out)
        if wave == COT_WAVE:
            tokens_start(1, cot_ref, cot_out)
    for c in range(len(GATHER)):
        a, *cut, order, _ = GATHER[c]
        names = orders[order]
        for t in range(stages):
            group(a, cut, 1 << t, send_sem.at[c, t], recv_sem.at[c, t], at.partner(names[t])).wait_send()
        for t in range(stages + 1):
            one = group(a, cut, 1 << max(t - 1, 0), side_send.at[c, t], side_recv.at[c, t], sibling)
            one.wait_send()
            one.wait_recv()
        pltpu.make_async_copy(own_src(a, cut), place_of(a, at.me, cut), own_sem.at[c]).wait()
    tokens_wait(0, x_ref, x_out)
    tokens_wait(1, cot_ref, cot_out)
    seg_copy.wait()


def gather_all(mesh_shape, x, cot, seg, shards, major=()):
    dp_n, seq_n = mesh_shape
    seqs, blk, width = x.shape
    n_dev = dp_n * seq_n
    stages = log2(n_dev) - 1
    chunks = len(GATHER)
    vmem = pl.BlockSpec(memory_space=pltpu.VMEM)
    hbm = pl.BlockSpec(memory_space=ANY)
    token_shape = jax.ShapeDtypeStruct((seq_n // 2, blk, width), x.dtype)
    DMA = pltpu.SemaphoreType.DMA
    return pl.pallas_call(
        functools.partial(gather_kernel, dp_n, seq_n, major),
        out_shape=[token_shape, token_shape, jax.ShapeDtypeStruct(seg.shape, seg.dtype)]
        + [
            jax.ShapeDtypeStruct((PIECES * n_dev,) + piece_shape((1,) + s.shape, (2 if i == 2 else 1, PIECES, 0)), s.dtype)
            if i in major
            else jax.ShapeDtypeStruct((n_dev,) + s.shape, s.dtype)
            for i, s in enumerate(shards)
        ],
        in_specs=[vmem] * (3 + len(shards)),
        out_specs=[hbm] * 2 + [vmem] + [hbm] * len(shards),
        scratch_shapes=[
            DMA((chunks, stages)),
            DMA((chunks, stages)),
            DMA((chunks, stages + 1)),
            DMA((chunks, stages + 1)),
            DMA((chunks,)),
            DMA((2, seqs)),
            DMA((2, seq_n)),
            DMA((2,)),
            DMA((2,)),
        ],
        compiler_params=pltpu.CompilerParams(collective_id=0, has_side_effects=True),
        name="gather_all",
    )(x, cot, seg, *[s[None] for s in shards])


REDUCE = (
    (2, 2, 4, 0, "zxy", 0),
    (3, 1, 4, 0, "zyx", 0),
    (2, 2, 4, 1, "zxy", 1),
    (3, 1, 4, 1, "zyx", 1),
    (2, 2, 4, 2, "zxy", 2),
    (3, 1, 4, 2, "zyx", 2),
    (2, 2, 4, 3, "zxy", 3),
    (3, 1, 4, 3, "zyx", 3),
    (0, 2, 3, 2, "zxy", 4),
    (1, 2, 1, 0, "zyx", 4),
    (0, 2, 3, 0, "zxy", 5),
    (0, 2, 3, 1, "zyx", 5),
    (4, 2, 1, 0, "zyx", 5),
)


def reduce_kernel(dp_n, seq_n, *refs):
    n_arr, chunks = 5, len(REDUCE)
    tok_in, parts = refs[:2], refs[2 : 2 + n_arr]
    refs = refs[2 + n_arr :]
    tok_out, totals = refs[:2], refs[2 : 2 + n_arr]
    refs = refs[2 + n_arr :]
    at = Place(dp_n, seq_n)
    orders = orders_of(dp_n, seq_n)
    stages = len(orders["zxy"])
    buffers = [refs[c * (stages + 2) : (c + 1) * (stages + 2)] for c in range(chunks)]
    send_sem, recv_sem, own_sem, tok_send, tok_recv, tok_own = refs[chunks * (stages + 2) :]
    at.enter()
    sibling = at.sibling()

    def names_of(c):
        return orders[REDUCE[c][4]][::-1]

    def index_of(c, j, core):
        total = core * seq_n
        for s, (axis, k) in enumerate(names_of(c)):
            value = lax.rem(lax.div(j, 1 << (stages - 1 - s)), 2) if not isinstance(j, int) else (j >> (stages - 1 - s)) & 1
            total = total + value * ((1 << k) * (1 if axis == "seq" else seq_n))
        return total

    def hop(c, t, src):
        device = sibling if t == 0 else at.partner(names_of(c)[t - 1])
        return pltpu.make_async_remote_copy(
            src_ref=src,
            dst_ref=buffers[c][t + 1],
            send_sem=send_sem.at[c, t],
            recv_sem=recv_sem.at[c, t],
            device_id=device,
            device_id_type=MESH,
        )

    def first(c):
        a, *cut, _, _ = REDUCE[c]
        own, got = buffers[c][:2]

        def one(j):
            src = piece_of(parts[a], index_of(c, j, 1 - at.core), cut)
            pltpu.make_async_remote_copy(
                src_ref=src,
                dst_ref=got.at[j],
                send_sem=send_sem.at[c, 0],
                recv_sem=recv_sem.at[c, 0],
                device_id=sibling,
                device_id_type=MESH,
            ).start()
            pltpu.make_async_copy(
                piece_of(parts[a], index_of(c, j, at.core), cut), own.at[j], own_sem.at[c]
            ).start()

        repeat(1 << stages, one)

    def own_wait(c):
        a, *cut, _, _ = REDUCE[c]
        whole = piece_of(parts[a], pl.ds(0, 1 << stages), cut)
        pltpu.make_async_copy(whole, buffers[c][0], own_sem.at[c]).wait()

    def add(c, t, lo, count, kept):
        old, got = buffers[c][t], buffers[c][t + 1]

        def one(j, carry):
            total = old[kept + lo + j].astype(jnp.float32) + got[lo + j].astype(jnp.float32)
            got[lo + j] = total.astype(got.dtype)
            return carry

        lax.fori_loop(0, count, one, 0)

    def stage(c, t):
        if t == 0:
            first(c)
            return
        names = names_of(c)
        hop(c, t - 1, buffers[c][t]).wait_recv()
        if t == 1:
            own_wait(c)
            kept = 0
        else:
            kept = at.bit(names[t - 2]) * (1 << (stages - t + 1))
        if t <= stages:
            half = 1 << (stages - t)
            mine = at.bit(names[t - 1])
            add(c, t - 1, (1 - mine) * half, half, kept)
            hop(c, t, buffers[c][t].at[pl.ds((1 - mine) * half, half)]).start()
            add(c, t - 1, mine * half, half, kept)
        else:
            a, *cut, _, _ = REDUCE[c]
            old, got = buffers[c][t - 1], buffers[c][t]
            total = old[kept].astype(jnp.float32) + got[0].astype(jnp.float32)
            piece_of(totals[a], 0, cut)[...] = total

    def token_copies(which, j):
        slot, rest = j // at.parts, j % at.parts
        quarter = at.core + slot * (3 - 2 * at.core)
        to_seq = quarter * at.parts + rest
        mine = (to_seq == at.seq) & (at.source_core == at.core)
        src = tok_in[which].at[j]
        place = at.seq - at.source_core * at.seqs
        remote = pltpu.make_async_remote_copy(
            src_ref=src,
            dst_ref=tok_out[which].at[place],
            send_sem=tok_send.at[which, j],
            recv_sem=tok_recv.at[which, place],
            device_id=(at.pair * 2 + at.source_core, to_seq),
            device_id_type=MESH,
        )
        local = pltpu.make_async_copy(src, tok_out[which].at[place], tok_own.at[which])
        return mine, remote, local

    for which in range(2):
        for j in range(seq_n // 2):
            mine, remote, local = token_copies(which, j)
            pl.when(jnp.logical_not(mine))(remote.start)
            pl.when(mine)(local.start)
    for wave in range(stages + 2 + max(c[5] for c in REDUCE)):
        for c in range(chunks):
            t = wave - REDUCE[c][5]
            if 0 <= t <= stages + 1:
                stage(c, t)
    for c in range(chunks):
        for t in range(stages + 1):
            hop(c, t, buffers[c][t + 1]).wait_send()
    for which in range(2):
        for j in range(seq_n // 2):
            mine, remote, local = token_copies(which, j)
            pl.when(jnp.logical_not(mine))(remote.wait_send)
            pl.when(mine)(local.wait)
        for i in range(at.seqs):
            comes = jnp.logical_not((at.core * at.seqs + i == at.seq) & (at.quarter_core == at.core))
            arrival = pltpu.make_async_remote_copy(
                src_ref=tok_in[which].at[0],
                dst_ref=tok_out[which].at[i],
                send_sem=tok_send.at[which, 0],
                recv_sem=tok_recv.at[which, i],
                device_id=sibling,
                device_id_type=MESH,
            )
            pl.when(comes)(arrival.wait_recv)


def reduce_all(mesh_shape, tokens, parts):
    dp_n, seq_n = mesh_shape
    stages = log2(dp_n * seq_n) - 1
    _, blk, width = tokens[0].shape
    vmem = pl.BlockSpec(memory_space=pltpu.VMEM)
    hbm = pl.BlockSpec(memory_space=ANY)
    DMA = pltpu.SemaphoreType.DMA
    chunks = len(REDUCE)
    scratch = []
    for a, *cut, _, _ in REDUCE:
        shape = piece_shape(parts[a].shape, cut)
        for count in (1 << stages,) + tuple(1 << (stages - t) for t in range(stages + 1)):
            scratch.append(pltpu.VMEM((count,) + shape, parts[a].dtype))
    out = pl.pallas_call(
        functools.partial(reduce_kernel, dp_n, seq_n),
        out_shape=[jax.ShapeDtypeStruct((seq_n // 2, blk, width), t.dtype) for t in tokens]
        + [jax.ShapeDtypeStruct((1,) + p.shape[1:], jnp.float32) for p in parts],
        in_specs=[vmem] * 2 + [hbm] * len(parts),
        out_specs=[hbm] * 2 + [vmem] * len(parts),
        scratch_shapes=scratch
        + [
            DMA((chunks, stages + 1)),
            DMA((chunks, stages + 1)),
            DMA((chunks,)),
            DMA((2, seq_n // 2)),
            DMA((2, seq_n // 2)),
            DMA((2,)),
        ],
        compiler_params=pltpu.CompilerParams(
            collective_id=1, has_side_effects=True, vmem_limit_bytes=60 * 1024 * 1024
        ),
        name="reduce_all",
    )(*tokens, *parts)
    return out[:2], [g[0] for g in out[2:]]


def swap_kernel(dp_n, seq_n, cols, src_ref, out_ref, send_sem, recv_sem):
    at = Place(dp_n, seq_n)
    sibling = at.sibling()
    barrier = pltpu.get_barrier_semaphore()
    pl.semaphore_signal(barrier, inc=1, device_id=sibling, device_id_type=MESH)
    pl.semaphore_wait(barrier, 1)
    first, width = cols
    copy = pltpu.make_async_remote_copy(
        src_ref=src_ref.at[:, pl.ds(first, width)],
        dst_ref=out_ref,
        send_sem=send_sem,
        recv_sem=recv_sem,
        device_id=sibling,
        device_id_type=MESH,
    )
    copy.start()
    copy.wait()


def swap(mesh_shape, src, cols, which):
    hbm = pl.BlockSpec(memory_space=ANY)
    return pl.pallas_call(
        functools.partial(swap_kernel, *mesh_shape, cols),
        out_shape=jax.ShapeDtypeStruct((src.shape[0], cols[1]), src.dtype),
        in_specs=[hbm],
        out_specs=hbm,
        scratch_shapes=[pltpu.SemaphoreType.DMA, pltpu.SemaphoreType.DMA],
        compiler_params=pltpu.CompilerParams(collective_id=which, has_side_effects=True),
        name="swap",
    )(src)


NT = (((1,), (1,)), ((), ()))
NN = (((1,), (0,)), ((), ()))
TN = (((0,), (0,)), ((), ()))


def dot(a, b, dims):
    return lax.dot_general(a, b, dims, preferred_element_type=jnp.float32)


def woven(own, other):
    half = own.shape[0] // 2
    return jnp.concatenate([own[:half], other[:half], own[half:], other[half:]], 0)


def head_masks():
    lane = lax.broadcasted_iota(jnp.int32, (1, 2 * HEAD_DIM), 1)
    first = (lane < HEAD_DIM).astype(jnp.bfloat16)
    return first, 1 - first


def attend_kernel(q_ref, ko_ref, vo_ref, ks_ref, vs_ref, bias_ref, o_ref, lse_ref):
    rows = q_ref.shape[0]
    half = rows // 2
    keys = woven(ko_ref[...], ks_ref[...])
    values = woven(vo_ref[...], vs_ref[...])
    masks = head_masks()
    scale = jnp.bfloat16(HEAD_DIM ** (-0.5))
    for slot in range(2):
        seen = rows * (slot + 1)
        here = slice(slot * half, (slot + 1) * half)
        q = q_ref[here] * scale
        outs = []
        for head in range(2):
            s = dot(keys[:seen], q * masks[head], NT) + bias_ref[:seen, here]
            top = jnp.max(s, 0, keepdims=True)
            e = jnp.exp(s - top)
            total = jnp.sum(e, 0, keepdims=True)
            p = (e * (1.0 / total)).astype(jnp.bfloat16)
            mixed = dot(values[:seen], p, TN)
            outs.append(mixed[head * HEAD_DIM : (head + 1) * HEAD_DIM])
            lse_ref[0, head : head + 1, here] = top + jnp.log(total)
        o_ref[here] = jnp.concatenate(outs, 0).T.astype(jnp.bfloat16)


def attend(qkv, kv_other, bias):
    rows, wide = qkv.shape
    width = wide // 3
    pairs = width // (2 * HEAD_DIM)
    col = lambda first: pl.BlockSpec((rows, 2 * HEAD_DIM), lambda h, first=first: (0, first * pairs + h))
    return pl.pallas_call(
        attend_kernel,
        grid=(pairs,),
        out_shape=[
            jax.ShapeDtypeStruct((rows, width), jnp.bfloat16),
            jax.ShapeDtypeStruct((pairs, 2, rows), jnp.float32),
        ],
        in_specs=[col(0), col(1), col(2), col(0), col(1), pl.BlockSpec(bias.shape, lambda h: (0, 0))],
        out_specs=[col(0), pl.BlockSpec((1, 2, rows), lambda h: (h, 0, 0))],
        name="attend",
    )(qkv, qkv, qkv, kv_other, kv_other, bias)


def attend_back_kernel(
    q_ref, ko_ref, vo_ref, ks_ref, vs_ref, go_ref, bias_ref, lse_ref, gq_ref, gko_ref, gvo_ref, gks_ref, gvs_ref, gk_sum, gv_sum
):
    rows = q_ref.shape[0]
    half = rows // 2
    keys = woven(ko_ref[...], ks_ref[...])
    values = woven(vo_ref[...], vs_ref[...])
    masks = head_masks()
    scale = HEAD_DIM ** (-0.5)
    for slot in (1, 0):
        seen = rows * (slot + 1)
        here = slice(slot * half, (slot + 1) * half)
        q = q_ref[here] * jnp.bfloat16(scale)
        go = go_ref[here]
        gqs, gk, gv = [], None, None
        for head in range(2):
            q_h, go_h = q * masks[head], go * masks[head]
            s = dot(keys[:seen], q_h, NT) + bias_ref[:seen, here]
            p = jnp.exp(s - lse_ref[0, head : head + 1, here])
            gp = dot(values[:seen], go_h, NT)
            row_dot = jnp.sum(p * gp, 0, keepdims=True)
            gs = (p * (gp - row_dot)).astype(jnp.bfloat16)
            gv_h = dot(p.astype(jnp.bfloat16), go_h, NN)
            gk_h = dot(gs, q_h, NN)
            gk = gk_h if gk is None else gk + gk_h
            gv = gv_h if gv is None else gv + gv_h
            gq = dot(keys[:seen], gs, TN)
            gqs.append(gq[head * HEAD_DIM : (head + 1) * HEAD_DIM])
        gq_ref[here] = (jnp.concatenate(gqs, 0).T * scale).astype(gq_ref.dtype)
        if slot == 1:
            gk_sum[...] = gk
            gv_sum[...] = gv
        else:
            gk_sum[:seen] += gk
            gv_sum[:seen] += gv
    for total, own, other in ((gk_sum, gko_ref, gks_ref), (gv_sum, gvo_ref, gvs_ref)):
        for slot in range(2):
            here = slice(slot * half, (slot + 1) * half)
            own[here] = total[2 * slot * half : (2 * slot + 1) * half].astype(own.dtype)
            other[here] = total[(2 * slot + 1) * half : (2 * slot + 2) * half].astype(other.dtype)


def attend_back(qkv, kv_other, go, bias, lse):
    rows, wide = qkv.shape
    width = wide // 3
    pairs = width // (2 * HEAD_DIM)
    lanes = 2 * HEAD_DIM
    col = lambda first: pl.BlockSpec((rows, lanes), lambda h, first=first: (0, first * pairs + h))
    out = jax.ShapeDtypeStruct((rows, width), jnp.bfloat16)
    return pl.pallas_call(
        attend_back_kernel,
        grid=(pairs,),
        out_shape=[out] * 5,
        in_specs=[
            col(0),
            col(1),
            col(2),
            col(0),
            col(1),
            col(0),
            pl.BlockSpec(bias.shape, lambda h: (0, 0)),
            pl.BlockSpec((1, 2, rows), lambda h: (h, 0, 0)),
        ],
        out_specs=[col(0)] * 5,
        scratch_shapes=[pltpu.VMEM((2 * rows, lanes), jnp.float32)] * 2,
        name="attend_back",
    )(qkv, qkv, qkv, kv_other, kv_other, go, bias, lse)


def rows_at(start, size):
    return pl.ds(pl.multiple_of(start, 16), size)


class Reduction:
    def __init__(self, at, order, refs, sems, own):
        self.at, self.own = at, own
        self.blocks, self.sends, self.gets, self.keeps = refs
        self.send_sem, self.recv_sem = sems
        self.order = order
        self.turns = len(order)
        self.last = self.turns + len(self.sends)
        self.names = order + [("seq", k) for k in range(len(self.sends))]
        self.dp_rows = self.blocks[0].shape[0] // (at.dp_n // 2)
        self.shard = self.dp_rows // at.seq_n

    def dp_of(self, j, core):
        dp = core
        for i, (_, k) in enumerate(reversed(self.order)):
            bit = (j >> i) & 1 if isinstance(j, int) else lax.rem(lax.div(j, 1 << i), 2)
            dp = dp + bit * (1 << k)
        return dp

    def landing(self, t):
        return self.blocks[t] if t <= self.turns else self.gets[t - self.turns - 1]

    def copy(self, t, src=None, dst=None):
        at = self.at
        return pltpu.make_async_remote_copy(
            src_ref=self.landing(t) if src is None else src,
            dst_ref=self.landing(t) if dst is None else dst,
            send_sem=self.send_sem.at[t],
            recv_sem=self.recv_sem.at[t],
            device_id=at.sibling() if t == 0 else at.partner(self.names[t - 1]),
            device_id_type=MESH,
        )

    def start(self):
        for j in range(self.at.dp_n // 2):
            dst = self.blocks[0].at[pl.ds(j * self.dp_rows, self.dp_rows)]
            self.copy(0, self.own(self.dp_of(j, 1 - self.at.core)), dst).start()

    def fold(self, t, lo, size):
        got = self.blocks[t - 1]
        step = self.dp_rows // 2
        if t == 1:
            first = lax.div(lo, self.dp_rows)
            for j in range(size // self.dp_rows):
                old = self.own(self.dp_of(first + j, self.at.core))
                for i in range(2):
                    here = rows_at((first + j) * self.dp_rows + i * step, step)
                    total = old[pl.ds(i * step, step)].astype(jnp.float32) + got[here].astype(jnp.float32)
                    got[here] = total.astype(got.dtype)
            return
        old = self.blocks[t - 2]
        kept = self.at.bit(self.names[t - 2]) * got.shape[0]
        for i in range(size // step):
            here = rows_at(lo + i * step, step)
            total = old[rows_at(kept + lo + i * step, step)].astype(jnp.float32) + got[here].astype(jnp.float32)
            got[here] = total.astype(got.dtype)

    def shards_of(self, t):
        got = self.landing(t - 1)
        if t == self.turns + 1:
            kept = self.at.bit(self.names[t - 2]) * self.dp_rows
            total = self.blocks[t - 2][rows_at(kept, self.dp_rows)].astype(jnp.float32) + got[...].astype(jnp.float32)
            return [total[i * self.shard : (i + 1) * self.shard] for i in range(self.at.seq_n)]
        keep = self.keeps[t - self.turns - 2]
        return [keep[i] + got[i].astype(jnp.float32) for i in range(keep.shape[0])]

    def stage(self, t):
        self.copy(t - 1).wait_recv()
        mine = self.at.bit(self.names[t - 1])
        if t <= self.turns:
            got = self.blocks[t - 1]
            half = got.shape[0] // 2
            self.fold(t, (1 - mine) * half, half)
            self.copy(t, got.at[rows_at((1 - mine) * half, half)]).start()
            self.fold(t, mine * half, half)
            return
        held = self.shards_of(t)
        m = t - self.turns - 1
        send, keep = self.sends[m], self.keeps[m]
        for i in range(len(held) // 2):
            send[i] = jnp.where(mine == 0, held[2 * i + 1], held[2 * i]).astype(send.dtype)
        self.copy(t, send).start()
        for i in range(len(held) // 2):
            keep[i] = jnp.where(mine == 0, held[2 * i], held[2 * i + 1])

    def finish(self):
        self.copy(self.last).wait_recv()
        return self.shards_of(self.last + 1)[0]


GRADS = 2 * PIECES + 4

AFTER = {
    "start": (
        "gs0", "gk0", "gq0", "gv0", "go0",
    ),
    "B0": (),
    "B1": (
        "gs1", "gk1", "gq1", "gv1", "go1", "X", "gf00", "gp00", "gs2", "gk2", "gs3", "gq2", "gv2", "go2", "gs4",
        "gk3", "gf10", "gp10", "gf01",
    ),
    "L1": (
        "gq3", "gp01", "go3", "gf20", "gp20", "gf11", "gv3", "gf02", "gp11", "gp02", "gf30", "gp30", "gf21", "gp21",
        "gf12", "gk4", "gq4", "gp12",
    ),
    "FK": (
        "gf31", "gp31", "gf22", "gp22", "go4", "gv4", "gf32", "gf03",
    ),
    "FV": (
        "C", "gp03", "gp32",
    ),
    "FQ": (
        "gf13", "gp13", "gf23",
    ),
    "E0": (
        "gp23", "gf33",
    ),
    "E1": (),
    "E2": (
        "gf04", "gp04", "gp33",
    ),
    "E3": (),
    "E4": (
        "gf14", "gp14",
    ),
    "E5": (),
    "O": (
        "gf24", "gp24",
    ),
    "L2": (),
    "M0": (
        "gf34", "gp34",
    ),
    "M1": (
        "rf01", "rp01",
    ),
    "M2": (
        "rf11", "rp11",
    ),
    "M3": (
        "rf02", "rp02", "rf21", "rp21",
    ),
    "T": (
        "rf31",
    ),
    "A": (
        "rf12", "rp12", "rp31", "rp03", "rf03",
    ),
    "B": (),
    "H0": (
        "ro1",
    ),
    "H1": (
        "rf22", "rp22",
    ),
    "H2": (
        "rp04", "rf13", "rf32",
    ),
    "H3": (
        "rf04", "rp13", "rp32",
    ),
    "H4": (
        "rp05", "rf14", "rp23",
    ),
    "H5": (
        "rf05", "rp14", "rp33", "ro2",
    ),
    "Q": (
        "rf15", "rp24", "rf23",
    ),
    "K": (
        "rp15", "rp34", "rf33", "ro3", "rq1",
    ),
    "V": (
        "rp25", "rf24", "rk1",
    ),
    "G": (
        "rp35", "rf34", "ro4", "rv1", "rf25",
    ),
    "N": (
        "rq2", "rk2", "rf35", "rs1", "ro5", "rv2", "rq3", "rs2", "rk3", "rv3", "rs3", "rq4", "rk4", "rv4", "rs4",
        "rq5", "rk5", "rv5", "rs5",
    ),
}
ORDER_ONE = "kosp"


def whole_kernel(dp_n, seq_n, *refs):
    x_ref, cot_ref, start_ref = refs[:3]
    w_qkv, w_out, w_fc, w_proj, w_vec = refs[3:8]
    result_out, input_out, fc_out, proj_out, qkv_out, wout_out, small_out = refs[8:15]
    qkv_hbm, out_hbm, fc_hbm, proj_hbm, vec_hbm = refs[15:20]
    (wbuf, gbuf, act, gm, a3, gh, resacc, gact, gqkv, away, back, tok, vecs, gk_sum, gv_sum) = refs[20:35]
    (x_in, cot, start_other, resid, mixed, qkv, kv_other, lse, bias, vec_low, vec) = refs[35:46]
    refs = refs[46:]
    at = Place(dp_n, seq_n)
    stages = log2(dp_n * seq_n)
    turns, folds = log2(dp_n) - 1, log2(seq_n)
    sets = [turns + 1, folds, folds, folds]
    count = sum(sets)

    def grouped(some):
        groups, first = [], 0
        for size in sets:
            groups.append(some[first : first + size])
            first += size
        return groups

    big, small_bufs = refs[:count], refs[count : 2 * count]
    (small_src, big_send, big_recv, small_send, small_recv, w_sem, swap_sem, tok_send, tok_recv, tok_own) = refs[
        2 * count : 2 * count + 10
    ]
    (ask_send, ask_recv, side_send, side_recv, own_sem, in_send, in_recv, in_own, start_sem, kv_sem, vec_sem) = refs[
        2 * count + 10 :
    ]
    rows, width = resid.shape
    half = rows // 2
    shard = fc_out.shape[0]
    n_dev = dp_n * seq_n
    across = [("dp", k) for k in range(1, log2(dp_n))]
    at.enter()
    sibling = at.sibling()

    def own_rows(src):
        return lambda dp: src.at[pl.ds(pl.multiple_of(dp * (seq_n * shard), 16), seq_n * shard)]

    def reduction(kind, c):
        order = across[::-1] if kind == 0 else across
        where = lax.rem(c, gbuf.shape[0]) if not isinstance(c, int) else c % gbuf.shape[0]
        return Reduction(
            at,
            order,
            grouped([b.at[c] for b in big]),
            (big_send.at[c], big_recv.at[c]),
            own_rows(gbuf.at[where]),
        )

    def vector_reduction():
        return Reduction(
            at,
            across,
            grouped(small_bufs),
            (small_send, small_recv),
            own_rows(small_src),
        )

    def weight_copy(slot, src):
        return pltpu.make_async_copy(src, wbuf.at[slot], w_sem.at[slot])


    def array(name):
        if name in "qkv":
            part = "qkv".index(name)
            cols = pl.ds(part * width, width)
            return part, qkv_hbm.at[:, cols], w_qkv.at[:, cols]
        if name == "o":
            return 3, out_hbm, w_out
        if name == "s":
            return 4, vec_hbm, w_vec
        j = int(name[1])
        if name[0] == "f":
            return 5 + j, fc_hbm.at[j], w_fc.at[:, pl.ds(j * width, width)]
        return 5 + PIECES + j, proj_hbm.at[j], w_proj.at[pl.ds(j * shard, shard)]

    along = [("seq", k) for k in reversed(range(folds))]

    def shard_rows(full, d):
        return full.at[pl.ds(pl.multiple_of(d * shard, 8), shard)]

    def put(src, dst, s_sem, r_sem, device):
        return pltpu.make_async_remote_copy(
            src_ref=src, dst_ref=dst, send_sem=s_sem, recv_sem=r_sem, device_id=device, device_id_type=MESH
        )

    def gather_stage(name, t):
        n, full, own = array(name)
        names = along + (across[::-1] if name[0] in ORDER_ONE else across)
        deltas = [at.delta(x) for x in names]
        if t == 0:
            place = shard_rows(full, at.me)
            put(own, place, ask_send.at[n, 0], ask_recv.at[n, 0], at.partner(names[0])).start()
            put(own, place, side_send.at[n, 0], side_recv.at[n, 0], sibling).start()
            pltpu.make_async_copy(own, place, own_sem.at[n]).start()
            return
        some = full.at[pl.ds(0, shard << (t - 1))]
        put(some, some, ask_send.at[n, t - 1], ask_recv.at[n, t - 1], sibling).wait_recv()
        if t < len(names):
            for j in range(1 << t):
                place = shard_rows(full, at.me + spread(j, deltas[:t]))
                put(own if j == 0 else place, place, ask_send.at[n, t], ask_recv.at[n, t], at.partner(names[t])).start()
        for j in range(1 << (t - 1)):
            place = shard_rows(full, at.me + deltas[t - 1] + spread(j, deltas[: t - 1]))
            put(place, place, side_send.at[n, t], side_recv.at[n, t], sibling).start()

    def gathered(name):
        n, full, own = array(name)
        for t in range(stages):
            some = full.at[pl.ds(0, shard << max(t - 1, 0))]
            put(some, some, side_send.at[n, t], side_recv.at[n, t], sibling).wait_recv()
        pltpu.make_async_copy(own, shard_rows(full, at.me), own_sem.at[n]).wait()

    def gather_drain(name):
        n, full, own = array(name)
        for t in range(stages - 1):
            some = full.at[pl.ds(0, shard << t)]
            put(some, some, ask_send.at[n, t], ask_recv.at[n, t], sibling).wait_send()
        for t in range(stages):
            some = full.at[pl.ds(0, shard << max(t - 1, 0))]
            put(some, some, side_send.at[n, t], side_recv.at[n, t], sibling).wait_send()

    slot_here = lax.div(at.quarter, 2) * at.parts + lax.rem(at.seq, at.parts)

    def incoming(which, i):
        src, dst = ((x_ref, x_in), (cot_ref, cot))[which]
        to_seq = at.core * at.seqs + i
        mine = (to_seq == at.seq) & (at.quarter_core == at.core)
        remote = put(
            src.at[i],
            dst.at[slot_here],
            in_send.at[which, i],
            in_recv.at[which, at.seq],
            (at.pair * 2 + at.quarter_core, to_seq),
        )
        local = pltpu.make_async_copy(src.at[i], dst.at[slot_here], in_own.at[which])
        return mine, remote, local

    def incoming_start(which):
        for i in range(at.seqs):
            mine, remote, local = incoming(which, i)
            pl.when(jnp.logical_not(mine))(remote.start)
            pl.when(mine)(local.start)

    def incoming_wait(which):
        src, dst = ((x_ref, x_in), (cot_ref, cot))[which]
        for i in range(at.seqs):
            mine, remote, local = incoming(which, i)
            pl.when(jnp.logical_not(mine))(remote.wait_send)
            pl.when(mine)(local.wait)
        for z in range(seq_n):
            comes = (at.core_of(z // at.parts) == at.core) & jnp.logical_not(
                (at.seq == z) & (at.source_core == at.core)
            )
            arrival = put(src.at[0], dst.at[0], in_send.at[which, 0], in_recv.at[which, z], sibling)
            pl.when(comes)(arrival.wait_recv)

    def load_piece(j):
        slot = 2 * lax.rem(j, 2)
        for k in range(PIECES):

            def ready(k=k):
                gathered(f"f{k}")
                gathered(f"p{k}")

            pl.when(j == k)(ready)
        weight_copy(slot, fc_hbm.at[j]).start()
        weight_copy(slot + 1, proj_hbm.at[j]).start()

    def after(slot):
        for op in AFTER[slot]:
            if op in "XC":
                incoming_start("XC".index(op))
                continue
            if op[0] == "g":
                gather_stage(op[1:-1], int(op[-1]))
                continue
            name, kind, t = op[1:], op[1], int(op[-1])
            if kind == "s":
                red = vector_reduction()
            else:
                c = 2 * int(name[1]) + (kind == "p") if kind in "fp" else 2 * PIECES + "oqkv".index(kind)
                red = reduction(int(kind in ORDER_ONE), int(c))
            if t < stages:
                red.stage(t)
                continue
            total = red.finish()
            if kind == "f":
                fc_out[:, int(name[1]) * width : (int(name[1]) + 1) * width] = total
            elif kind == "p":
                proj_out[int(name[1]) * shard : (int(name[1]) + 1) * shard] = total
            elif kind == "o":
                wout_out[...] = total
            elif kind == "s":
                small_out[...] = total
            else:
                part = "qkv".index(kind)
                qkv_out[:, part * width : (part + 1) * width] = total

    def after_each(prefix, i, count):
        for k in range(count):
            pl.when(i == k)(functools.partial(after, f"{prefix}{k}"))

    after("start")
    ask_start = put(start_ref, start_other, start_sem.at[0], start_sem.at[1], sibling)
    ask_start.start()
    ask_start.wait()
    row = pl.ds(at.seq - at.source_core * at.seqs, 1)
    first_seen = jnp.where(at.source_core == at.core, start_ref[row], start_other[row])
    down = lax.broadcasted_iota(jnp.int32, (half, 1), 0)
    along_row = lax.broadcasted_iota(jnp.int32, (1, half), 1)
    key_firsts = [at.core * half, (1 - at.core) * half, (3 - at.core) * half, (2 + at.core) * half]
    for slot in range(2):
        low, high = [first_seen[:, k * half : (k + 1) * half] for k in ((0, 1), (3, 2))[slot]]
        seen_from = jnp.where(at.core == 0, low, high)
        place = key_firsts[2 * slot] + along_row
        for tile in range(2 * slot + 2):
            key = key_firsts[tile] + down
            bias[tile * half : (tile + 1) * half, slot * half : (slot + 1) * half] = jnp.where(
                (key >= seen_from) & (key <= place), 0.0, masked_score
            )
    after("B0")
    after("B1")

    def token_rows(ref):
        return ref[...].reshape(rows, width).astype(jnp.float32)

    incoming_wait(0)
    gathered("s")
    vec_copy = pltpu.make_async_copy(vec_hbm, vec_low, vec_sem)
    vec_copy.start()
    normed, _ = normalised(token_rows(x_in))
    vec_copy.wait()
    columns = vec_low[...].astype(jnp.float32)
    vec[...] = columns.T[:16]
    odd_shard = lax.rem(lax.div(lax.broadcasted_iota(jnp.int32, (1, width), 1), shard), 2) == 1
    for part in range(2):
        doubled = [columns[d * shard : (d + 1) * shard] for d in range(part * n_dev // 2, (part + 1) * n_dev // 2) for _ in range(2)]
        lines = jnp.concatenate(doubled, 0).T
        vec[14 + part : 15 + part] = jnp.where(odd_shard, lines[11:12], lines[10:11])
    act[...] = (normed * vec[0:1] + vec[1:2]).astype(jnp.bfloat16)
    after("L1")

    def weight_here(name, slot):
        gathered(name)
        copy = weight_copy(slot, array(name)[1])
        copy.start()
        copy.wait()

    weight_here("k", 1)
    qkv[:, width : 2 * width] = dot(act[...], wbuf[1], NN).astype(jnp.bfloat16)
    after("FK")
    weight_here("v", 2)
    qkv[:, 2 * width :] = (dot(act[...], wbuf[2], NN) + vec[15:16]).astype(jnp.bfloat16)
    exchange_kv = put(qkv.at[:, pl.ds(width, 2 * width)], kv_other, kv_sem.at[0], kv_sem.at[1], sibling)
    exchange_kv.start()
    after("FV")
    weight_here("q", 0)
    qkv[:, :width] = (dot(act[...], wbuf[0], NN) + vec[14:15]).astype(jnp.bfloat16)
    after("FQ")
    gathered("o")
    weight_copy(3, out_hbm).start()
    exchange_kv.wait()
    pairs = width // (2 * HEAD_DIM)

    def heads_forward(i, carry):
        at_q = pl.ds(pl.multiple_of(i * 128, 128), 128)
        at_k = pl.ds(pl.multiple_of(width + i * 128, 128), 128)
        at_v = pl.ds(pl.multiple_of(2 * width + i * 128, 128), 128)
        attend_kernel(
            qkv.at[:, at_q],
            qkv.at[:, at_k],
            qkv.at[:, at_v],
            kv_other.at[:, at_q],
            kv_other.at[:, at_k],
            bias,
            mixed.at[:, at_q],
            lse.at[pl.ds(i, 1)],
        )
        after_each("E", i, 6)
        return carry

    lax.fori_loop(0, pairs, heads_forward, 0)
    weight_copy(3, out_hbm).wait()
    resid[...] = token_rows(x_in) + branch_scale * (dot(mixed[...], wbuf[3], NN) + vec[2:3])
    after("O")
    load_piece(jnp.int32(0))
    incoming_wait(1)

    normed, _ = normalised(resid[...])
    act[...] = (normed * vec[3:4] + vec[4:5]).astype(jnp.bfloat16)
    grad_mlp = (branch_scale * token_rows(cot)).astype(jnp.bfloat16)
    gm[...] = grad_mlp
    vecs[...] = jnp.zeros_like(vecs)
    vecs[5:6] = jnp.sum(grad_mlp.astype(jnp.float32), 0, keepdims=True)
    resacc[...] = jnp.zeros_like(resacc)
    gact[...] = jnp.zeros_like(gact)
    after("L2")

    def piece(j, carry):
        slot = 2 * lax.rem(j, 2)
        pl.when(j + 1 < PIECES)(lambda: load_piece(j + 1))
        weight_copy(slot, fc_hbm.at[j]).wait()
        weight_copy(slot + 1, proj_hbm.at[j]).wait()
        fc, proj = wbuf.at[slot], wbuf.at[slot + 1]
        bias_fc = vec[pl.ds(6 + j, 1)]

        def some(r, total):
            here = pl.ds(pl.multiple_of(r * half, 16), half)
            u = dot(act[here], fc[...], NN) + bias_fc
            bent = jnp.tanh(gelu_root * (u + gelu_coeff * u * u * u))
            hidden = (0.5 * u * (1.0 + bent)).astype(jnp.bfloat16)
            inner = gelu_root * (1.0 + 3.0 * gelu_coeff * u * u)
            slope = 0.5 * (1.0 + bent) + 0.5 * u * (1.0 - bent * bent) * inner
            a3[here] = hidden
            resacc[here] += dot(hidden, proj[...], NN)
            grad_u = (dot(gm[here], proj[...], NT) * slope).astype(jnp.bfloat16)
            gh[here] = grad_u
            gact[here] += dot(grad_u, fc[...], NT)
            return total + jnp.sum(grad_u.astype(jnp.float32), 0, keepdims=True)

        total = lax.fori_loop(0, 2, some, jnp.zeros((1, width), jnp.float32))
        vecs[pl.ds(6 + j, 1)] = total
        for kind, (left, right) in enumerate(((act, gh), (a3, gm))):
            c = 2 * j + kind
            red = reduction(kind, c)
            pl.when(c >= gbuf.shape[0])(
                lambda red=red, c=c, kind=kind: reduction(kind, c - gbuf.shape[0]).copy(0).wait_send()
            )
            gbuf[lax.rem(c, gbuf.shape[0])] = dot(left[...], right[...], TN).astype(jnp.bfloat16)
            red.start()
        after_each("M", j, PIECES)
        return carry

    lax.fori_loop(0, PIECES, piece, 0)
    for slot in range(3):
        weight_copy(slot, qkv_hbm.at[:, pl.ds(slot * width, width)]).start()
    weight_copy(3, out_hbm).start()

    def token_copies(which, j):
        slot, rest = j // at.parts, j % at.parts
        quarter = at.core + slot * (3 - 2 * at.core)
        to_seq = quarter * at.parts + rest
        mine = (to_seq == at.seq) & (at.source_core == at.core)
        place = at.seq - at.source_core * at.seqs
        out = (result_out, input_out)[which]
        remote = pltpu.make_async_remote_copy(
            src_ref=tok.at[which, j],
            dst_ref=out.at[place],
            send_sem=tok_send.at[which, j],
            recv_sem=tok_recv.at[which, place],
            device_id=(at.pair * 2 + at.source_core, to_seq),
            device_id_type=MESH,
        )
        local = pltpu.make_async_copy(tok.at[which, j], out.at[place], tok_own.at[which])
        return mine, remote, local

    def tokens_start(which, value):
        tok[which] = value.astype(jnp.bfloat16).reshape(tok.shape[1:])
        for j in range(seq_n // 2):
            mine, remote, local = token_copies(which, j)
            pl.when(jnp.logical_not(mine))(remote.start)
            pl.when(mine)(local.start)

    def tokens_wait(which):
        for j in range(seq_n // 2):
            mine, remote, local = token_copies(which, j)
            pl.when(jnp.logical_not(mine))(remote.wait_send)
            pl.when(mine)(local.wait)
        for i in range(at.seqs):
            comes = jnp.logical_not((at.core * at.seqs + i == at.seq) & (at.quarter_core == at.core))
            arrival = pltpu.make_async_remote_copy(
                src_ref=tok.at[which, 0],
                dst_ref=(result_out, input_out)[which].at[i],
                send_sem=tok_send.at[which, 0],
                recv_sem=tok_recv.at[which, i],
                device_id=sibling,
                device_id_type=MESH,
            )
            pl.when(comes)(arrival.wait_recv)

    tokens_start(0, resid[...] + branch_scale * (resacc[...] + vec[5:6]))
    after("T")

    normed, inverse = normalised(resid[...])
    grad_two = gact[...]
    vecs[3:4] = jnp.sum(grad_two * normed, 0, keepdims=True)
    vecs[4:5] = jnp.sum(grad_two, 0, keepdims=True)
    grad_mid = token_rows(cot) + norm_spread(grad_two, normed, inverse, vec[3:4])
    gact[...] = grad_mid
    grad_branch = (branch_scale * grad_mid).astype(jnp.bfloat16)
    act[...] = grad_branch
    vecs[2:3] = jnp.sum(grad_branch.astype(jnp.float32), 0, keepdims=True)

    c_out = 2 * PIECES
    reduction(0, c_out - gbuf.shape[0]).copy(0).wait_send()
    gbuf[c_out % gbuf.shape[0]] = dot(mixed[...], grad_branch, TN).astype(jnp.bfloat16)
    reduction(1, c_out).start()
    after("A")
    weight_copy(3, out_hbm).wait()
    gm[...] = dot(grad_branch, wbuf[3], NT).astype(jnp.bfloat16)
    after("B")

    def heads(i, carry):
        at_q = pl.ds(pl.multiple_of(i * 128, 128), 128)
        at_k = pl.ds(pl.multiple_of(width + i * 128, 128), 128)
        at_v = pl.ds(pl.multiple_of(2 * width + i * 128, 128), 128)
        attend_back_kernel(
            qkv.at[:, at_q],
            qkv.at[:, at_k],
            qkv.at[:, at_v],
            kv_other.at[:, at_q],
            kv_other.at[:, at_k],
            gm.at[:, at_q],
            bias,
            lse.at[pl.ds(i, 1)],
            gqkv.at[:, at_q],
            gqkv.at[:, at_k],
            gqkv.at[:, at_v],
            away.at[:, at_q],
            away.at[:, at_k],
            gk_sum,
            gv_sum,
        )
        after_each("H", i, 6)
        return carry

    lax.fori_loop(0, pairs, heads, 0)

    exchange = pltpu.make_async_remote_copy(
        src_ref=away,
        dst_ref=back,
        send_sem=swap_sem.at[0],
        recv_sem=swap_sem.at[1],
        device_id=sibling,
        device_id_type=MESH,
    )
    exchange.start()
    normed, inverse = normalised(token_rows(x_in))
    act[...] = (normed * vec[0:1] + vec[1:2]).astype(jnp.bfloat16)

    def grad_of(part):
        c = c_out + 1 + part
        kind = part % 2
        here = pl.ds(part * width, width)
        if part > 0:
            far = pl.ds((part - 1) * width, width)
            gqkv[:, here] = (gqkv[:, here].astype(jnp.float32) + back[:, far].astype(jnp.float32)).astype(jnp.bfloat16)
        reduction(kind, c - gbuf.shape[0]).copy(0).wait_send()
        gbuf[c % gbuf.shape[0]] = dot(act[...], gqkv[:, here], TN).astype(jnp.bfloat16)
        reduction(kind, c).start()
        weight_copy(part, qkv_hbm.at[:, here]).wait()

    def column_sum(part):
        return jnp.sum(gqkv[:, pl.ds(part * width, width)].astype(jnp.float32), 0, keepdims=True)

    grad_of(0)
    after("Q")
    exchange.wait()
    grad_of(1)
    after("K")
    grad_of(2)
    after("V")
    first, third = column_sum(0), column_sum(2)
    for row, value in ((10, first), (11, first), (12, third), (13, third)):
        vecs[row : row + 1] = value
    grad_one = dot(gqkv[:, pl.ds(0, width)], wbuf[0], NT)
    grad_one = grad_one + dot(gqkv[:, pl.ds(width, width)], wbuf[1], NT)
    resacc[...] = grad_one + dot(gqkv[:, pl.ds(2 * width, width)], wbuf[2], NT)
    after("G")
    grad_one = resacc[...]
    normed, inverse = normalised(token_rows(x_in))
    vecs[0:1] = jnp.sum(grad_one * normed, 0, keepdims=True)
    vecs[1:2] = jnp.sum(grad_one, 0, keepdims=True)
    tokens_start(1, gact[...] + norm_spread(grad_one, normed, inverse, vec[0:1]))
    columns = vecs[...].T
    small_src[...] = columns
    lane = lax.broadcasted_iota(jnp.int32, (1, 128), 1)
    even, odd = (lane == 10) | (lane == 12), (lane == 11) | (lane == 13)
    for d in range(n_dev):
        start = 2 * shard * (d % (n_dev // 2))
        kept = columns[d * shard : (d + 1) * shard]
        kept = jnp.where(even, columns[start : start + shard], kept)
        kept = jnp.where(odd, columns[start + shard : start + 2 * shard], kept)
        small_src[d * shard : (d + 1) * shard] = kept
    vector_reduction().start()
    after("N")
    for c in range(GRADS):
        red = reduction(0, c)
        for t in range(0 if c >= GRADS - gbuf.shape[0] else 1, stages):
            red.copy(t).wait_send()
    for t in range(stages):
        vector_reduction().copy(t).wait_send()
    for name in ["s", "q", "k", "v", "o"] + [f"{x}{j}" for x in "fp" for j in range(PIECES)]:
        gather_drain(name)
    tokens_wait(0)
    tokens_wait(1)


def whole(mesh_shape, x, cot, start, shards):
    dp_n, seq_n = mesh_shape
    seqs, blk, width = x.shape
    rows = blk * (seq_n // 2)
    n_dev = dp_n * seq_n
    stages = log2(n_dev)
    shard = width // n_dev
    vmem = pl.BlockSpec(memory_space=pltpu.VMEM)
    hbm = pl.BlockSpec(memory_space=ANY)
    DMA = pltpu.SemaphoreType.DMA
    low, full = jnp.bfloat16, jnp.float32
    slots = 4
    arrays = 5 + 2 * PIECES

    def buffers(lead, cols, dtype):
        turns, folds = log2(dp_n) - 1, log2(seq_n)
        parts = [(seq_n >> (m + 1), shard, cols) for m in range(folds)]
        return (
            [pltpu.VMEM(lead + (width // 2 >> t, cols), dtype) for t in range(turns + 1)]
            + [pltpu.VMEM(lead + p, dtype) for p in parts] * 2
            + [pltpu.VMEM(lead + p, full) for p in parts]
        )

    token = jax.ShapeDtypeStruct((seq_n // 2, blk, width), low)
    grads = [(shard, PIECES * width), (PIECES * shard, width), (shard, 3 * width), (shard, width), (shard, 128)]
    gathers = [(width, 3 * width), (width, width), (PIECES, width, width), (PIECES, width, width), (width, 128)]
    out = pl.pallas_call(
        functools.partial(whole_kernel, dp_n, seq_n),
        out_shape=[token, token]
        + [jax.ShapeDtypeStruct(s, full) for s in grads]
        + [jax.ShapeDtypeStruct(s, low) for s in gathers],
        in_specs=[vmem] * 8,
        out_specs=[hbm] * 2 + [vmem] * 5 + [hbm] * 5,
        scratch_shapes=[
            pltpu.VMEM((4, width, width), low),
            pltpu.VMEM((slots, width, width), low),
            pltpu.VMEM((rows, width), low),
            pltpu.VMEM((rows, width), low),
            pltpu.VMEM((rows, width), low),
            pltpu.VMEM((rows, width), low),
            pltpu.VMEM((rows, width), full),
            pltpu.VMEM((rows, width), full),
            pltpu.VMEM((rows, 3 * width), low),
            pltpu.VMEM((rows, 2 * width), low),
            pltpu.VMEM((rows, 2 * width), low),
            pltpu.VMEM((2, seq_n // 2, blk, width), low),
            pltpu.VMEM((128, width), full),
            pltpu.VMEM((2 * rows, 128), full),
            pltpu.VMEM((2 * rows, 128), full),
            pltpu.VMEM((seq_n // 2, blk, width), low),
            pltpu.VMEM((seq_n // 2, blk, width), low),
            pltpu.VMEM(start.shape, start.dtype),
            pltpu.VMEM((rows, width), full),
            pltpu.VMEM((rows, width), low),
            pltpu.VMEM((rows, 3 * width), low),
            pltpu.VMEM((rows, 2 * width), low),
            pltpu.VMEM((width // 128, 2, rows), full),
            pltpu.VMEM((2 * rows, rows), full),
            pltpu.VMEM((width, 128), low),
            pltpu.VMEM((16, width), full),
        ]
        + buffers((GRADS,), width, low)
        + buffers((), 128, full)
        + [
            pltpu.VMEM((width, 128), full),
            DMA((GRADS, stages)),
            DMA((GRADS, stages)),
            DMA((stages,)),
            DMA((stages,)),
            DMA((4,)),
            DMA((2,)),
            DMA((2, seq_n // 2)),
            DMA((2, seq_n // 2)),
            DMA((2,)),
            DMA((arrays, stages - 1)),
            DMA((arrays, stages - 1)),
            DMA((arrays, stages)),
            DMA((arrays, stages)),
            DMA((arrays,)),
            DMA((2, seqs)),
            DMA((2, seq_n)),
            DMA((2,)),
            DMA((2,)),
            DMA((2,)),
            DMA,
        ],
        compiler_params=pltpu.CompilerParams(
            collective_id=4, has_side_effects=True, vmem_limit_bytes=64 * 1024 * 1024 - 65536
        ),
        name="whole",
    )(x, cot, start, *shards)
    return out[:7]


def normalised(rows):
    center = rows - jnp.mean(rows, -1, keepdims=True)
    inverse = lax.rsqrt(jnp.mean(center * center, -1, keepdims=True) + norm_eps)
    return center * inverse, inverse


def norm_spread(grad_in, normed, inverse, gain):
    scaled = grad_in * gain
    return inverse * (
        scaled
        - jnp.mean(scaled, -1, keepdims=True)
        - normed * jnp.mean(scaled * normed, -1, keepdims=True)
    )


def packed(vectors, row_unit, dtype):
    flat = jnp.concatenate(vectors, -1)
    size = flat.shape[-1]
    rows = -(-size // (128 * row_unit)) * row_unit
    flat = jnp.pad(flat, [(0, 0)] * (flat.ndim - 1) + [(0, rows * 128 - size)])
    return flat.reshape(flat.shape[:-1] + (rows, 128)).astype(dtype)


def unpacked(rows, sizes):
    flat = rows.reshape(rows.shape[0], -1)
    out, first = [], 0
    for size in sizes:
        out.append(flat[:, first : first + size].reshape(-1))
        first += size
    return out


def block(mesh_shape, *args):
    (
        block_input,
        segments,
        cotangent,
        ln1_gain,
        ln1_bias,
        w_qkv,
        b_qv,
        w_out,
        b_out,
        ln2_gain,
        ln2_bias,
        w_fc,
        b_fc,
        w_proj,
        b_proj,
    ) = args
    dp_n, seq_n = mesh_shape
    n_dev = dp_n * seq_n
    micro_count, seq_count, stretch, width = block_input.shape
    seq_len = segments.shape[2]
    seqs = micro_count * seq_count
    assert 2 * seqs == seq_n and seq_n % 4 == 0
    at = Place(dp_n, seq_n)
    vectors = (ln1_gain, ln1_bias, b_qv, b_out, ln2_gain, ln2_bias, b_fc, b_proj)
    sizes = [v.shape[0] for v in vectors]
    gathered = gather_all(
        mesh_shape,
        block_input.reshape(seqs, stretch, width),
        cotangent.reshape(seqs, stretch, width),
        segments.reshape(seqs, seq_len),
        (w_qkv, w_out, w_fc, w_proj, packed(vectors, 16, jnp.bfloat16)),
    )
    x_rows, cot_rows, seg_other, weight_qkv, weight_out, weight_fc, weight_proj, small = gathered
    rows = seq_len // 2
    half = rows // 2
    x_rows = x_rows.reshape(rows, width).astype(jnp.float32)
    grad_out = cot_rows.reshape(rows, width).astype(jnp.float32)
    weight_qkv, weight_out, weight_fc, weight_proj = [
        w.reshape(-1, w.shape[-1]) for w in (weight_qkv, weight_out, weight_fc, weight_proj)
    ]
    gain_one, bias_one, bias_qv, bias_out, gain_two, bias_two, bias_fc, bias_proj = [
        v.astype(jnp.float32) for v in unpacked(small, sizes)
    ]

    seg_all = jnp.where(at.source_core == at.core, segments.reshape(seqs, seq_len), seg_other)
    seg = lax.dynamic_index_in_dim(seg_all, at.seq - at.source_core * seqs, 0, keepdims=False)
    quarter = jnp.arange(half, dtype=jnp.int32)
    own_first = [at.core * half, (3 - at.core) * half]
    other_first = [(1 - at.core) * half, (2 + at.core) * half]
    firsts = [own_first[0], other_first[0], own_first[1], other_first[1]]
    key_place = jnp.concatenate([f + quarter for f in firsts])
    key_seg = jnp.concatenate([lax.dynamic_slice_in_dim(seg, f, half, 0) for f in firsts])
    query_place = jnp.concatenate([key_place[:half], key_place[2 * half : 3 * half]])
    query_seg = jnp.concatenate([key_seg[:half], key_seg[2 * half : 3 * half]])
    visible = (key_seg[:, None] == query_seg[None, :]) & (key_place[:, None] <= query_place[None, :])
    bias = jnp.where(visible, 0.0, masked_score).astype(jnp.float32)

    normed_out, normed_one, inverse_one = layer_norm(x_rows, gain_one, bias_one)
    act_one = normed_out.astype(jnp.bfloat16)
    bias_full = jnp.concatenate([bias_qv[:width], jnp.zeros((width,), jnp.float32), bias_qv[width:]])
    qkv = (jnp.dot(act_one, weight_qkv, preferred_element_type=jnp.float32) + bias_full).astype(jnp.bfloat16)
    kv_other = swap(mesh_shape, qkv, (width, 2 * width), 2)
    mixed_out, lse = attend(qkv, kv_other, bias)
    resid_mid = x_rows + branch_scale * (
        jnp.dot(mixed_out, weight_out, preferred_element_type=jnp.float32) + bias_out
    )

    normed_out, normed_two, inverse_two = layer_norm(resid_mid, gain_two, bias_two)
    act_two = normed_out.astype(jnp.bfloat16)
    hidden = jnp.dot(act_two, weight_fc, preferred_element_type=jnp.float32) + bias_fc
    act_three = gelu_tanh(hidden).astype(jnp.bfloat16)
    result = resid_mid + branch_scale * (
        jnp.dot(act_three, weight_proj, preferred_element_type=jnp.float32) + bias_proj
    )
    grad_mlp = (branch_scale * grad_out).astype(jnp.bfloat16)
    grad_bproj = jnp.sum(grad_mlp.astype(jnp.float32), 0)
    grad_wproj = dot(act_three, grad_mlp, TN)
    grad_act3 = dot(grad_mlp, weight_proj, NT)
    grad_hidden = (grad_act3 * gelu_slope(hidden)).astype(jnp.bfloat16)
    grad_bfc = jnp.sum(grad_hidden.astype(jnp.float32), 0)
    grad_wfc = dot(act_two, grad_hidden, TN)
    grad_act2 = dot(grad_hidden, weight_fc, NT)
    grad_norm2, grad_gain2, grad_bias2 = norm_back(grad_act2, normed_two, inverse_two, gain_two)
    grad_mid = grad_out + grad_norm2

    grad_branch = (branch_scale * grad_mid).astype(jnp.bfloat16)
    grad_bout = jnp.sum(grad_branch.astype(jnp.float32), 0)
    grad_wout = dot(mixed_out, grad_branch, TN)
    grad_mixed = dot(grad_branch, weight_out, NT).astype(jnp.bfloat16)
    grad_q, grad_k, grad_v, away_k, away_v = attend_back(qkv, kv_other, grad_mixed, bias, lse)
    back = swap(mesh_shape, jnp.concatenate([away_k, away_v], 1), (0, 2 * width), 3)
    key_value = jnp.concatenate([grad_k, grad_v], 1).astype(jnp.float32) + back.astype(jnp.float32)
    grad_qkv = jnp.concatenate([grad_q, key_value.astype(jnp.bfloat16)], 1)
    grad_wide = grad_qkv.astype(jnp.float32)
    grad_bqv = jnp.concatenate([jnp.sum(grad_wide[:, :width], 0), jnp.sum(grad_wide[:, 2 * width :], 0)])
    grad_wqkv = dot(act_one, grad_qkv, TN)
    grad_act1 = dot(grad_qkv, weight_qkv, NT)
    grad_norm1, grad_gain1, grad_bias1 = norm_back(grad_act1, normed_one, inverse_one, gain_one)
    grad_input = grad_mid + grad_norm1

    vec_grads = (grad_gain1, grad_bias1, grad_bqv, grad_bout, grad_gain2, grad_bias2, grad_bfc, grad_bproj)
    token_block = (seq_n // 2, stretch, width)
    parts = [
        g.astype(jnp.bfloat16).reshape((n_dev, -1, g.shape[-1]))
        for g in (grad_wqkv, grad_wout, grad_wfc, grad_wproj)
    ] + [packed([v.reshape(n_dev, -1) for v in vec_grads], 8, jnp.float32)]
    (result, grad_input), totals = reduce_all(
        mesh_shape,
        [result.astype(jnp.bfloat16).reshape(token_block), grad_input.astype(jnp.bfloat16).reshape(token_block)],
        parts,
    )
    owned = unpacked(totals[4].reshape(1, -1), sizes)
    shape = block_input.shape
    return (
        result.reshape(shape),
        grad_input.reshape(shape),
        owned[0],
        owned[1],
        totals[0],
        owned[2],
        totals[1],
        owned[3],
        owned[4],
        owned[5],
        totals[2],
        owned[6],
        totals[3],
        owned[7],
    )


def fused_block(mesh_shape, *args):
    (
        block_input,
        segments,
        cotangent,
        ln1_gain,
        ln1_bias,
        w_qkv,
        b_qv,
        w_out,
        b_out,
        ln2_gain,
        ln2_bias,
        w_fc,
        b_fc,
        w_proj,
        b_proj,
    ) = args
    dp_n, seq_n = mesh_shape
    n_dev = dp_n * seq_n
    micro_count, seq_count, stretch, width = block_input.shape
    seq_len = segments.shape[2]
    seqs = micro_count * seq_count
    assert 2 * seqs == seq_n and seq_n % 4 == 0 and w_fc.shape[1] == PIECES * width
    at = Place(dp_n, seq_n)
    shard = width // n_dev
    fc_cols = w_fc.reshape(shard, n_dev, PIECES, shard).transpose(0, 2, 1, 3).reshape(shard, -1)
    vectors = jnp.concatenate(
        [jnp.stack([ln1_gain, ln1_bias, b_out, ln2_gain, ln2_bias, b_proj]), b_fc.reshape(PIECES, shard), b_qv.reshape(2, shard)]
    )
    vectors = jnp.pad(vectors, ((0, 128 - vectors.shape[0]), (0, 0))).T
    seg = segments.reshape(seqs, seq_len)
    start = jnp.sum((seg[:, None, :] < seg[:, :, None]).astype(jnp.int32), 2)
    result, grad_input, grad_fc, grad_proj, grad_qkv, grad_out, columns = whole(
        mesh_shape,
        block_input.reshape(seqs, stretch, width),
        cotangent.reshape(seqs, stretch, width),
        start,
        (w_qkv, w_out, fc_cols, w_proj, vectors),
    )
    grad_fc = grad_fc.reshape(shard, PIECES, n_dev, shard).transpose(0, 2, 1, 3).reshape(shard, -1)
    lines = columns.T
    grad_bqv = jnp.where(at.me < n_dev // 2, lines[10:12], lines[12:14]).reshape(-1)
    shape = block_input.shape
    return (
        result.reshape(shape),
        grad_input.reshape(shape),
        lines[0],
        lines[1],
        grad_qkv,
        grad_bqv,
        grad_out,
        lines[2],
        lines[3],
        lines[4],
        grad_fc,
        lines[6:10].reshape(-1),
        grad_proj,
        lines[5],
    )


def whole_block(mesh_shape, *args):
    aligned = args[5].shape[0] % 8 == 0 and mesh_shape[1] == 4
    return (fused_block if aligned else block)(mesh_shape, *args)


def solution(mesh):
    both = ("dp", "seq")
    tokens, vector, matrix = P(None, "dp", "seq", None), P(both), P(both, None)
    return jax.shard_map(
        functools.partial(whole_block, (mesh.shape["dp"], mesh.shape["seq"])),
        mesh=mesh,
        in_specs=(
            tokens,
            P(None, "dp", None),
            tokens,
            vector,
            vector,
            matrix,
            vector,
            matrix,
            vector,
            vector,
            vector,
            matrix,
            vector,
            matrix,
            vector,
        ),
        out_specs=(
            tokens,
            tokens,
            vector,
            vector,
            matrix,
            vector,
            matrix,
            vector,
            vector,
            vector,
            matrix,
            vector,
            matrix,
            vector,
        ),
        check_vma=False,
    )
```

```python
import functools
import math

import jax
import jax.numpy as jnp
from jax import lax
from jax.experimental import pallas as pl
from jax.experimental.pallas import tpu as pltpu
from jax.sharding import PartitionSpec as P

HEADS = 12
HEAD_DIM = 64
MESH = pl.DeviceIdType.MESH
PIECES = 4
ANY = pl.ANY

branch_scale = 48.0 ** (-0.5)
norm_eps = 1e-05
masked_score = -1e30
gelu_coeff = 0.044715
gelu_root = (2.0 / 3.141592653589793) ** 0.5


def layer_norm(tok_rows, gain_vec, bias_vec):
    center = tok_rows - jnp.mean(tok_rows, -1, keepdims=True)
    inverse = lax.rsqrt(jnp.mean(center * center, -1, keepdims=True) + norm_eps)
    normed = center * inverse
    return (normed * gain_vec + bias_vec, normed, inverse)


def norm_back(grad_in, normed, inverse, gain_vec):
    grad_gain = jnp.sum(grad_in * normed, 0)
    grad_bias = jnp.sum(grad_in, 0)
    scaled = grad_in * gain_vec
    spread = (
        scaled
        - jnp.mean(scaled, -1, keepdims=True)
        - normed * jnp.mean(scaled * normed, -1, keepdims=True)
    )
    return (inverse * spread, grad_gain, grad_bias)


def gelu_tanh(pre_act):
    tanh_val = jnp.tanh(gelu_root * (pre_act + gelu_coeff * pre_act * pre_act * pre_act))
    return 0.5 * pre_act * (1.0 + tanh_val)


def gelu_slope(pre_act):
    tanh_val = jnp.tanh(gelu_root * (pre_act + gelu_coeff * pre_act * pre_act * pre_act))
    inner_slope = gelu_root * (1.0 + 3.0 * gelu_coeff * pre_act * pre_act)
    return 0.5 * (1.0 + tanh_val) + 0.5 * pre_act * (1.0 - tanh_val * tanh_val) * inner_slope


def log2(n):
    k = n.bit_length() - 1
    assert 1 << k == n
    return k


class Place:
    def __init__(self, dp_n, seq_n):
        self.dp_n, self.seq_n = dp_n, seq_n
        self.dp, self.seq = lax.axis_index("dp"), lax.axis_index("seq")
        self.core = lax.rem(self.dp, 2)
        self.pair = lax.div(self.dp, 2)
        self.me = self.dp * seq_n + self.seq
        self.seqs = seq_n // 2
        self.parts = seq_n // 4
        self.quarter = lax.div(self.seq, self.parts)
        self.quarter_core = self.core_of(self.quarter)
        self.source_core = lax.div(self.seq, self.seqs)

    def core_of(self, quarter):
        return lax.rem(lax.div(quarter + 1, 2), 2)

    def bit(self, name):
        axis, k = name
        return lax.rem(lax.div(self.seq if axis == "seq" else self.dp, 1 << k), 2)

    def delta(self, name):
        axis, k = name
        return (1 - 2 * self.bit(name)) * ((1 << k) * (1 if axis == "seq" else self.seq_n))

    def partner(self, name):
        axis, k = name
        step = (1 - 2 * self.bit(name)) * (1 << k)
        if axis == "seq":
            return (self.dp, self.seq + step)
        return (self.dp + step, self.seq)

    def sibling(self):
        return self.partner(("dp", 0))

    def enter(self):
        barrier = pltpu.get_barrier_semaphore()
        count = 0
        for core_step in range(2):
            for seq_step in range(self.seq_n):
                if core_step == 0 and seq_step == 0:
                    continue
                other = (
                    self.pair * 2 + lax.rem(self.core + core_step, 2),
                    lax.rem(self.seq + seq_step, self.seq_n),
                )
                pl.semaphore_signal(barrier, inc=1, device_id=other, device_id_type=MESH)
                count += 1
        for k in range(1, log2(self.dp_n)):
            pl.semaphore_signal(barrier, inc=1, device_id=self.partner(("dp", k)), device_id_type=MESH)
            count += 1
        pl.semaphore_wait(barrier, count)


def orders_of(dp_n, seq_n):
    along = [("seq", k) for k in reversed(range(log2(seq_n)))]
    across = [("dp", k) for k in range(1, log2(dp_n))]
    back = across[::-1]
    return {
        "zxy": along + across,
        "zyx": along + back,
        "xyz": across + along,
        "yxz": back + along,
    }


def repeat(count, body):
    if count <= 16:
        for j in range(count):
            body(j)
    else:
        lax.fori_loop(0, count, lambda j, c: (body(j), c)[1], 0)


def spread(j, deltas):
    total = 0
    for i, delta in enumerate(deltas):
        if isinstance(j, int):
            if (j >> i) & 1:
                total = total + delta
        else:
            total = total + lax.rem(lax.div(j, 1 << i), 2) * delta
    return total


def resolve(shape, cut):
    axis, pieces, k = cut
    if axis == 1 and shape[1] % (8 * pieces):
        axis = 2
    unit = 8 if axis == 1 else 128
    units = shape[axis] // unit
    start, stop = units * k // pieces, units * (k + 1) // pieces
    return axis, start * unit, (stop - start) * unit


def piece_shape(shape, cut):
    axis, _, size = resolve(shape, cut)
    shape = list(shape)
    shape[axis] = size
    return tuple(shape[1:])


def piece_of(ref, lead, cut):
    axis, start, size = resolve(ref.shape, cut)
    where = [slice(None)] * 2
    where[axis - 1] = pl.ds(start, size)
    return ref.at[(lead, *where)]


GATHER = (
    (0, 2, 3, 0, "zxy", 0),
    (0, 2, 3, 1, "zyx", 0),
    (4, 2, 1, 0, "zyx", 0),
    (0, 2, 3, 2, "zxy", 1),
    (1, 2, 1, 0, "zyx", 1),
    (2, 2, 4, 0, "zxy", 2),
    (3, 1, 4, 0, "zyx", 2),
    (2, 2, 4, 1, "zxy", 3),
    (3, 1, 4, 1, "zyx", 3),
    (2, 2, 4, 2, "zxy", 4),
    (3, 1, 4, 2, "zyx", 4),
    (2, 2, 4, 3, "zxy", 5),
    (3, 1, 4, 3, "zyx", 5),
)
X_WAVE, COT_WAVE = 2, 5


def gather_kernel(dp_n, seq_n, major, x_ref, cot_ref, seg_ref, *refs):
    n_arr = 5
    shard = refs[:n_arr]
    x_out, cot_out, seg_out = refs[n_arr : n_arr + 3]
    full = refs[n_arr + 3 : n_arr + 3 + n_arr]
    (send_sem, recv_sem, side_send, side_recv, own_sem, tok_send, tok_recv, tok_own, seg_sem) = refs[
        2 * n_arr + 3 :
    ]
    at = Place(dp_n, seq_n)
    orders = orders_of(dp_n, seq_n)
    stages = len(orders["zxy"])
    at.enter()
    sibling = at.sibling()

    piece = piece_of

    def put(src, dst, s_sem, r_sem, device):
        pltpu.make_async_remote_copy(
            src_ref=src, dst_ref=dst, send_sem=s_sem, recv_sem=r_sem, device_id=device, device_id_type=MESH
        ).start()

    def place_of(a, idx, cut, count=None):
        if a in major:
            idx = idx + cut[2] * dp_n * seq_n
            return full[a].at[idx if count is None else pl.ds(idx, count)]
        return piece(full[a], idx if count is None else pl.ds(idx, count), cut)

    def group(a, cut, count, s_sem, r_sem, device):
        whole = place_of(a, 0, cut, count)
        return pltpu.make_async_remote_copy(
            src_ref=whole, dst_ref=whole, send_sem=s_sem, recv_sem=r_sem, device_id=device, device_id_type=MESH
        )

    def own_src(a, cut):
        return piece(shard[a], 0, cut)

    def stage(c, t):
        a, *cut, order, _ = GATHER[c]
        names = orders[order]
        deltas = [at.delta(n) for n in names]
        if t > 0:
            group(a, cut, 1 << (t - 1), send_sem.at[c, t - 1], recv_sem.at[c, t - 1], sibling).wait_recv()

            def pass_on(j):
                idx = at.me + deltas[t - 1] + spread(j, deltas[: t - 1])
                place = place_of(a, idx, cut)
                put(place, place, side_send.at[c, t], side_recv.at[c, t], sibling)

            if t < stages:
                partner = at.partner(names[t])

                def onward(j):
                    idx = at.me + spread(j, deltas[:t])
                    place = place_of(a, idx, cut)
                    put(own_src(a, cut) if isinstance(j, int) and j == 0 else place, place, send_sem.at[c, t], recv_sem.at[c, t], partner)

                onward(0)
                repeat((1 << t) - 1, lambda j: onward(j + 1))
            repeat(1 << (t - 1), pass_on)
        else:
            partner = at.partner(names[0])
            place = place_of(a, at.me, cut)
            put(own_src(a, cut), place, send_sem.at[c, 0], recv_sem.at[c, 0], partner)
            put(own_src(a, cut), place, side_send.at[c, 0], side_recv.at[c, 0], sibling)
            pltpu.make_async_copy(own_src(a, cut), place, own_sem.at[c]).start()

    slot = lax.div(at.quarter, 2) * at.parts + lax.rem(at.seq, at.parts)
    seg_copy = pltpu.make_async_remote_copy(
        src_ref=seg_ref,
        dst_ref=seg_out,
        send_sem=seg_sem.at[0],
        recv_sem=seg_sem.at[1],
        device_id=sibling,
        device_id_type=MESH,
    )

    def token_copies(which, src, dst, i):
        to_seq = at.core * at.seqs + i
        mine = (to_seq == at.seq) & (at.quarter_core == at.core)
        remote = pltpu.make_async_remote_copy(
            src_ref=src.at[i],
            dst_ref=dst.at[slot],
            send_sem=tok_send.at[which, i],
            recv_sem=tok_recv.at[which, at.seq],
            device_id=(at.pair * 2 + at.quarter_core, to_seq),
            device_id_type=MESH,
        )
        local = pltpu.make_async_copy(src.at[i], dst.at[slot], tok_own.at[which])
        return mine, remote, local

    def tokens_start(which, src, dst):
        for i in range(at.seqs):
            mine, remote, local = token_copies(which, src, dst, i)
            pl.when(jnp.logical_not(mine))(remote.start)
            pl.when(mine)(local.start)

    def tokens_wait(which, src, dst):
        for i in range(at.seqs):
            mine, remote, local = token_copies(which, src, dst, i)
            pl.when(jnp.logical_not(mine))(remote.wait_send)
            pl.when(mine)(local.wait)
        for z in range(seq_n):
            comes = (at.core_of(z // at.parts) == at.core) & jnp.logical_not(
                (at.seq == z) & (at.source_core == at.core)
            )
            arrival = pltpu.make_async_remote_copy(
                src_ref=src.at[0],
                dst_ref=dst.at[0],
                send_sem=tok_send.at[which, 0],
                recv_sem=tok_recv.at[which, z],
                device_id=sibling,
                device_id_type=MESH,
            )
            pl.when(comes)(arrival.wait_recv)

    seg_copy.start()
    waves = stages + 1 + max(c[5] for c in GATHER)
    for wave in range(waves):
        for c in range(len(GATHER)):
            t = wave - GATHER[c][5]
            if 0 <= t <= stages:
                stage(c, t)
        if wave == X_WAVE:
            tokens_start(0, x_ref, x_out)
        if wave == COT_WAVE:
            tokens_start(1, cot_ref, cot_out)
    for c in range(len(GATHER)):
        a, *cut, order, _ = GATHER[c]
        names = orders[order]
        for t in range(stages):
            group(a, cut, 1 << t, send_sem.at[c, t], recv_sem.at[c, t], at.partner(names[t])).wait_send()
        for t in range(stages + 1):
            one = group(a, cut, 1 << max(t - 1, 0), side_send.at[c, t], side_recv.at[c, t], sibling)
            one.wait_send()
            one.wait_recv()
        pltpu.make_async_copy(own_src(a, cut), place_of(a, at.me, cut), own_sem.at[c]).wait()
    tokens_wait(0, x_ref, x_out)
    tokens_wait(1, cot_ref, cot_out)
    seg_copy.wait()


def gather_all(mesh_shape, x, cot, seg, shards, major=()):
    dp_n, seq_n = mesh_shape
    seqs, blk, width = x.shape
    n_dev = dp_n * seq_n
    stages = log2(n_dev) - 1
    chunks = len(GATHER)
    vmem = pl.BlockSpec(memory_space=pltpu.VMEM)
    hbm = pl.BlockSpec(memory_space=ANY)
    token_shape = jax.ShapeDtypeStruct((seq_n // 2, blk, width), x.dtype)
    DMA = pltpu.SemaphoreType.DMA
    return pl.pallas_call(
        functools.partial(gather_kernel, dp_n, seq_n, major),
        out_shape=[token_shape, token_shape, jax.ShapeDtypeStruct(seg.shape, seg.dtype)]
        + [
            jax.ShapeDtypeStruct((PIECES * n_dev,) + piece_shape((1,) + s.shape, (2 if i == 2 else 1, PIECES, 0)), s.dtype)
            if i in major
            else jax.ShapeDtypeStruct((n_dev,) + s.shape, s.dtype)
            for i, s in enumerate(shards)
        ],
        in_specs=[vmem] * (3 + len(shards)),
        out_specs=[hbm] * 2 + [vmem] + [hbm] * len(shards),
        scratch_shapes=[
            DMA((chunks, stages)),
            DMA((chunks, stages)),
            DMA((chunks, stages + 1)),
            DMA((chunks, stages + 1)),
            DMA((chunks,)),
            DMA((2, seqs)),
            DMA((2, seq_n)),
            DMA((2,)),
            DMA((2,)),
        ],
        compiler_params=pltpu.CompilerParams(collective_id=0, has_side_effects=True),
        name="gather_all",
    )(x, cot, seg, *[s[None] for s in shards])


REDUCE = (
    (2, 2, 4, 0, "zxy", 0),
    (3, 1, 4, 0, "zyx", 0),
    (2, 2, 4, 1, "zxy", 1),
    (3, 1, 4, 1, "zyx", 1),
    (2, 2, 4, 2, "zxy", 2),
    (3, 1, 4, 2, "zyx", 2),
    (2, 2, 4, 3, "zxy", 3),
    (3, 1, 4, 3, "zyx", 3),
    (0, 2, 3, 2, "zxy", 4),
    (1, 2, 1, 0, "zyx", 4),
    (0, 2, 3, 0, "zxy", 5),
    (0, 2, 3, 1, "zyx", 5),
    (4, 2, 1, 0, "zyx", 5),
)


def reduce_kernel(dp_n, seq_n, *refs):
    n_arr, chunks = 5, len(REDUCE)
    tok_in, parts = refs[:2], refs[2 : 2 + n_arr]
    refs = refs[2 + n_arr :]
    tok_out, totals = refs[:2], refs[2 : 2 + n_arr]
    refs = refs[2 + n_arr :]
    at = Place(dp_n, seq_n)
    orders = orders_of(dp_n, seq_n)
    stages = len(orders["zxy"])
    buffers = [refs[c * (stages + 2) : (c + 1) * (stages + 2)] for c in range(chunks)]
    send_sem, recv_sem, own_sem, tok_send, tok_recv, tok_own = refs[chunks * (stages + 2) :]
    at.enter()
    sibling = at.sibling()

    def names_of(c):
        return orders[REDUCE[c][4]][::-1]

    def index_of(c, j, core):
        total = core * seq_n
        for s, (axis, k) in enumerate(names_of(c)):
            value = lax.rem(lax.div(j, 1 << (stages - 1 - s)), 2) if not isinstance(j, int) else (j >> (stages - 1 - s)) & 1
            total = total + value * ((1 << k) * (1 if axis == "seq" else seq_n))
        return total

    def hop(c, t, src):
        device = sibling if t == 0 else at.partner(names_of(c)[t - 1])
        return pltpu.make_async_remote_copy(
            src_ref=src,
            dst_ref=buffers[c][t + 1],
            send_sem=send_sem.at[c, t],
            recv_sem=recv_sem.at[c, t],
            device_id=device,
            device_id_type=MESH,
        )

    def first(c):
        a, *cut, _, _ = REDUCE[c]
        own, got = buffers[c][:2]

        def one(j):
            src = piece_of(parts[a], index_of(c, j, 1 - at.core), cut)
            pltpu.make_async_remote_copy(
                src_ref=src,
                dst_ref=got.at[j],
                send_sem=send_sem.at[c, 0],
                recv_sem=recv_sem.at[c, 0],
                device_id=sibling,
                device_id_type=MESH,
            ).start()
            pltpu.make_async_copy(
                piece_of(parts[a], index_of(c, j, at.core), cut), own.at[j], own_sem.at[c]
            ).start()

        repeat(1 << stages, one)

    def own_wait(c):
        a, *cut, _, _ = REDUCE[c]
        whole = piece_of(parts[a], pl.ds(0, 1 << stages), cut)
        pltpu.make_async_copy(whole, buffers[c][0], own_sem.at[c]).wait()

    def add(c, t, lo, count, kept):
        old, got = buffers[c][t], buffers[c][t + 1]

        def one(j, carry):
            total = old[kept + lo + j].astype(jnp.float32) + got[lo + j].astype(jnp.float32)
            got[lo + j] = total.astype(got.dtype)
            return carry

        lax.fori_loop(0, count, one, 0)

    def stage(c, t):
        if t == 0:
            first(c)
            return
        names = names_of(c)
        hop(c, t - 1, buffers[c][t]).wait_recv()
        if t == 1:
            own_wait(c)
            kept = 0
        else:
            kept = at.bit(names[t - 2]) * (1 << (stages - t + 1))
        if t <= stages:
            half = 1 << (stages - t)
            mine = at.bit(names[t - 1])
            add(c, t - 1, (1 - mine) * half, half, kept)
            hop(c, t, buffers[c][t].at[pl.ds((1 - mine) * half, half)]).start()
            add(c, t - 1, mine * half, half, kept)
        else:
            a, *cut, _, _ = REDUCE[c]
            old, got = buffers[c][t - 1], buffers[c][t]
            total = old[kept].astype(jnp.float32) + got[0].astype(jnp.float32)
            piece_of(totals[a], 0, cut)[...] = total

    def token_copies(which, j):
        slot, rest = j // at.parts, j % at.parts
        quarter = at.core + slot * (3 - 2 * at.core)
        to_seq = quarter * at.parts + rest
        mine = (to_seq == at.seq) & (at.source_core == at.core)
        src = tok_in[which].at[j]
        place = at.seq - at.source_core * at.seqs
        remote = pltpu.make_async_remote_copy(
            src_ref=src,
            dst_ref=tok_out[which].at[place],
            send_sem=tok_send.at[which, j],
            recv_sem=tok_recv.at[which, place],
            device_id=(at.pair * 2 + at.source_core, to_seq),
            device_id_type=MESH,
        )
        local = pltpu.make_async_copy(src, tok_out[which].at[place], tok_own.at[which])
        return mine, remote, local

    for which in range(2):
        for j in range(seq_n // 2):
            mine, remote, local = token_copies(which, j)
            pl.when(jnp.logical_not(mine))(remote.start)
            pl.when(mine)(local.start)
    for wave in range(stages + 2 + max(c[5] for c in REDUCE)):
        for c in range(chunks):
            t = wave - REDUCE[c][5]
            if 0 <= t <= stages + 1:
                stage(c, t)
    for c in range(chunks):
        for t in range(stages + 1):
            hop(c, t, buffers[c][t + 1]).wait_send()
    for which in range(2):
        for j in range(seq_n // 2):
            mine, remote, local = token_copies(which, j)
            pl.when(jnp.logical_not(mine))(remote.wait_send)
            pl.when(mine)(local.wait)
        for i in range(at.seqs):
            comes = jnp.logical_not((at.core * at.seqs + i == at.seq) & (at.quarter_core == at.core))
            arrival = pltpu.make_async_remote_copy(
                src_ref=tok_in[which].at[0],
                dst_ref=tok_out[which].at[i],
                send_sem=tok_send.at[which, 0],
                recv_sem=tok_recv.at[which, i],
                device_id=sibling,
                device_id_type=MESH,
            )
            pl.when(comes)(arrival.wait_recv)


def reduce_all(mesh_shape, tokens, parts):
    dp_n, seq_n = mesh_shape
    stages = log2(dp_n * seq_n) - 1
    _, blk, width = tokens[0].shape
    vmem = pl.BlockSpec(memory_space=pltpu.VMEM)
    hbm = pl.BlockSpec(memory_space=ANY)
    DMA = pltpu.SemaphoreType.DMA
    chunks = len(REDUCE)
    scratch = []
    for a, *cut, _, _ in REDUCE:
        shape = piece_shape(parts[a].shape, cut)
        for count in (1 << stages,) + tuple(1 << (stages - t) for t in range(stages + 1)):
            scratch.append(pltpu.VMEM((count,) + shape, parts[a].dtype))
    out = pl.pallas_call(
        functools.partial(reduce_kernel, dp_n, seq_n),
        out_shape=[jax.ShapeDtypeStruct((seq_n // 2, blk, width), t.dtype) for t in tokens]
        + [jax.ShapeDtypeStruct((1,) + p.shape[1:], jnp.float32) for p in parts],
        in_specs=[vmem] * 2 + [hbm] * len(parts),
        out_specs=[hbm] * 2 + [vmem] * len(parts),
        scratch_shapes=scratch
        + [
            DMA((chunks, stages + 1)),
            DMA((chunks, stages + 1)),
            DMA((chunks,)),
            DMA((2, seq_n // 2)),
            DMA((2, seq_n // 2)),
            DMA((2,)),
        ],
        compiler_params=pltpu.CompilerParams(
            collective_id=1, has_side_effects=True, vmem_limit_bytes=60 * 1024 * 1024
        ),
        name="reduce_all",
    )(*tokens, *parts)
    return out[:2], [g[0] for g in out[2:]]


def swap_kernel(dp_n, seq_n, cols, src_ref, out_ref, send_sem, recv_sem):
    at = Place(dp_n, seq_n)
    sibling = at.sibling()
    barrier = pltpu.get_barrier_semaphore()
    pl.semaphore_signal(barrier, inc=1, device_id=sibling, device_id_type=MESH)
    pl.semaphore_wait(barrier, 1)
    first, width = cols
    copy = pltpu.make_async_remote_copy(
        src_ref=src_ref.at[:, pl.ds(first, width)],
        dst_ref=out_ref,
        send_sem=send_sem,
        recv_sem=recv_sem,
        device_id=sibling,
        device_id_type=MESH,
    )
    copy.start()
    copy.wait()


def swap(mesh_shape, src, cols, which):
    hbm = pl.BlockSpec(memory_space=ANY)
    return pl.pallas_call(
        functools.partial(swap_kernel, *mesh_shape, cols),
        out_shape=jax.ShapeDtypeStruct((src.shape[0], cols[1]), src.dtype),
        in_specs=[hbm],
        out_specs=hbm,
        scratch_shapes=[pltpu.SemaphoreType.DMA, pltpu.SemaphoreType.DMA],
        compiler_params=pltpu.CompilerParams(collective_id=which, has_side_effects=True),
        name="swap",
    )(src)


NT = (((1,), (1,)), ((), ()))
NN = (((1,), (0,)), ((), ()))
TN = (((0,), (0,)), ((), ()))


def dot(a, b, dims):
    return lax.dot_general(a, b, dims, preferred_element_type=jnp.float32)


def woven(own, other):
    half = own.shape[0] // 2
    return jnp.concatenate([own[:half], other[:half], own[half:], other[half:]], 0)


def head_masks():
    lane = lax.broadcasted_iota(jnp.int32, (1, 2 * HEAD_DIM), 1)
    first = (lane < HEAD_DIM).astype(jnp.bfloat16)
    return first, 1 - first


def attend_kernel(q_ref, ko_ref, vo_ref, ks_ref, vs_ref, bias_ref, o_ref, lse_ref):
    rows = q_ref.shape[0]
    half = rows // 2
    keys = woven(ko_ref[...], ks_ref[...])
    values = woven(vo_ref[...], vs_ref[...])
    masks = head_masks()
    scale = jnp.bfloat16(HEAD_DIM ** (-0.5))
    for slot in range(2):
        seen = rows * (slot + 1)
        here = slice(slot * half, (slot + 1) * half)
        q = q_ref[here] * scale
        outs = []
        for head in range(2):
            s = dot(keys[:seen], q * masks[head], NT) + bias_ref[:seen, here]
            top = jnp.max(s, 0, keepdims=True)
            e = jnp.exp(s - top)
            total = jnp.sum(e, 0, keepdims=True)
            p = (e * (1.0 / total)).astype(jnp.bfloat16)
            mixed = dot(values[:seen], p, TN)
            outs.append(mixed[head * HEAD_DIM : (head + 1) * HEAD_DIM])
            lse_ref[0, head : head + 1, here] = top + jnp.log(total)
        o_ref[here] = jnp.concatenate(outs, 0).T.astype(jnp.bfloat16)


def attend(qkv, kv_other, bias):
    rows, wide = qkv.shape
    width = wide // 3
    pairs = width // (2 * HEAD_DIM)
    col = lambda first: pl.BlockSpec((rows, 2 * HEAD_DIM), lambda h, first=first: (0, first * pairs + h))
    return pl.pallas_call(
        attend_kernel,
        grid=(pairs,),
        out_shape=[
            jax.ShapeDtypeStruct((rows, width), jnp.bfloat16),
            jax.ShapeDtypeStruct((pairs, 2, rows), jnp.float32),
        ],
        in_specs=[col(0), col(1), col(2), col(0), col(1), pl.BlockSpec(bias.shape, lambda h: (0, 0))],
        out_specs=[col(0), pl.BlockSpec((1, 2, rows), lambda h: (h, 0, 0))],
        name="attend",
    )(qkv, qkv, qkv, kv_other, kv_other, bias)


def attend_back_kernel(
    q_ref, ko_ref, vo_ref, ks_ref, vs_ref, go_ref, bias_ref, lse_ref, gq_ref, gko_ref, gvo_ref, gks_ref, gvs_ref, gk_sum, gv_sum
):
    rows = q_ref.shape[0]
    half = rows // 2
    keys = woven(ko_ref[...], ks_ref[...])
    values = woven(vo_ref[...], vs_ref[...])
    masks = head_masks()
    scale = HEAD_DIM ** (-0.5)
    for slot in (1, 0):
        seen = rows * (slot + 1)
        here = slice(slot * half, (slot + 1) * half)
        q = q_ref[here] * jnp.bfloat16(scale)
        go = go_ref[here]
        gqs, gk, gv = [], None, None
        for head in range(2):
            q_h, go_h = q * masks[head], go * masks[head]
            s = dot(keys[:seen], q_h, NT) + bias_ref[:seen, here]
            p = jnp.exp(s - lse_ref[0, head : head + 1, here])
            gp = dot(values[:seen], go_h, NT)
            row_dot = jnp.sum(p * gp, 0, keepdims=True)
            gs = (p * (gp - row_dot)).astype(jnp.bfloat16)
            gv_h = dot(p.astype(jnp.bfloat16), go_h, NN)
            gk_h = dot(gs, q_h, NN)
            gk = gk_h if gk is None else gk + gk_h
            gv = gv_h if gv is None else gv + gv_h
            gq = dot(keys[:seen], gs, TN)
            gqs.append(gq[head * HEAD_DIM : (head + 1) * HEAD_DIM])
        gq_ref[here] = (jnp.concatenate(gqs, 0).T * scale).astype(gq_ref.dtype)
        if slot == 1:
            gk_sum[...] = gk
            gv_sum[...] = gv
        else:
            gk_sum[:seen] += gk
            gv_sum[:seen] += gv
    for total, own, other in ((gk_sum, gko_ref, gks_ref), (gv_sum, gvo_ref, gvs_ref)):
        for slot in range(2):
            here = slice(slot * half, (slot + 1) * half)
            own[here] = total[2 * slot * half : (2 * slot + 1) * half].astype(own.dtype)
            other[here] = total[(2 * slot + 1) * half : (2 * slot + 2) * half].astype(other.dtype)


def attend_back(qkv, kv_other, go, bias, lse):
    rows, wide = qkv.shape
    width = wide // 3
    pairs = width // (2 * HEAD_DIM)
    lanes = 2 * HEAD_DIM
    col = lambda first: pl.BlockSpec((rows, lanes), lambda h, first=first: (0, first * pairs + h))
    out = jax.ShapeDtypeStruct((rows, width), jnp.bfloat16)
    return pl.pallas_call(
        attend_back_kernel,
        grid=(pairs,),
        out_shape=[out] * 5,
        in_specs=[
            col(0),
            col(1),
            col(2),
            col(0),
            col(1),
            col(0),
            pl.BlockSpec(bias.shape, lambda h: (0, 0)),
            pl.BlockSpec((1, 2, rows), lambda h: (h, 0, 0)),
        ],
        out_specs=[col(0)] * 5,
        scratch_shapes=[pltpu.VMEM((2 * rows, lanes), jnp.float32)] * 2,
        name="attend_back",
    )(qkv, qkv, qkv, kv_other, kv_other, go, bias, lse)


def rows_at(start, size):
    return pl.ds(pl.multiple_of(start, 16), size)


class Reduction:
    def __init__(self, at, order, refs, sems, own):
        self.at, self.own = at, own
        self.blocks, self.sends, self.gets, self.keeps = refs
        self.send_sem, self.recv_sem = sems
        self.order = order
        self.turns = len(order)
        self.last = self.turns + len(self.sends)
        self.names = order + [("seq", k) for k in range(len(self.sends))]
        self.dp_rows = self.blocks[0].shape[0] // (at.dp_n // 2)
        self.shard = self.dp_rows // at.seq_n

    def dp_of(self, j, core):
        dp = core
        for i, (_, k) in enumerate(reversed(self.order)):
            bit = (j >> i) & 1 if isinstance(j, int) else lax.rem(lax.div(j, 1 << i), 2)
            dp = dp + bit * (1 << k)
        return dp

    def landing(self, t):
        return self.blocks[t] if t <= self.turns else self.gets[t - self.turns - 1]

    def copy(self, t, src=None, dst=None):
        at = self.at
        return pltpu.make_async_remote_copy(
            src_ref=self.landing(t) if src is None else src,
            dst_ref=self.landing(t) if dst is None else dst,
            send_sem=self.send_sem.at[t],
            recv_sem=self.recv_sem.at[t],
            device_id=at.sibling() if t == 0 else at.partner(self.names[t - 1]),
            device_id_type=MESH,
        )

    def start(self):
        for j in range(self.at.dp_n // 2):
            dst = self.blocks[0].at[pl.ds(j * self.dp_rows, self.dp_rows)]
            self.copy(0, self.own(self.dp_of(j, 1 - self.at.core)), dst).start()

    def fold(self, t, lo, size):
        got = self.blocks[t - 1]
        step = self.dp_rows // 2

        def one(i, carry):
            row = lo + i * step
            here = rows_at(row, step)
            if t == 1:
                half = lax.rem(i, 2) * step
                old = self.own(self.dp_of(lax.div(row, self.dp_rows), self.at.core))[rows_at(half, step)]
            else:
                kept = self.at.bit(self.names[t - 2]) * got.shape[0]
                old = self.blocks[t - 2][rows_at(kept + row, step)]
            got[here] = (old.astype(jnp.float32) + got[here].astype(jnp.float32)).astype(got.dtype)
            return carry

        lax.fori_loop(0, size // step, one, 0)

    def shards_of(self, t):
        got = self.landing(t - 1)
        if t == self.turns + 1:
            kept = self.at.bit(self.names[t - 2]) * self.dp_rows
            total = self.blocks[t - 2][rows_at(kept, self.dp_rows)].astype(jnp.float32) + got[...].astype(jnp.float32)
            return [total[i * self.shard : (i + 1) * self.shard] for i in range(self.at.seq_n)]
        keep = self.keeps[t - self.turns - 2]
        return [keep[i] + got[i].astype(jnp.float32) for i in range(keep.shape[0])]

    def stage(self, t):
        self.copy(t - 1).wait_recv()
        mine = self.at.bit(self.names[t - 1])
        if t <= self.turns:
            got = self.blocks[t - 1]
            half = got.shape[0] // 2
            self.fold(t, (1 - mine) * half, half)
            self.copy(t, got.at[rows_at((1 - mine) * half, half)]).start()
            self.fold(t, mine * half, half)
            return
        held = self.shards_of(t)
        m = t - self.turns - 1
        send, keep = self.sends[m], self.keeps[m]
        for i in range(len(held) // 2):
            send[i] = jnp.where(mine == 0, held[2 * i + 1], held[2 * i]).astype(send.dtype)
        self.copy(t, send).start()
        for i in range(len(held) // 2):
            keep[i] = jnp.where(mine == 0, held[2 * i], held[2 * i + 1])

    def finish(self):
        self.copy(self.last).wait_recv()
        return self.shards_of(self.last + 1)[0]


GRADS = 2 * PIECES + 4

AFTER = {
    "start": (
        "gs0", "gk0", "gq0", "gv0", "go0",
    ),
    "B0": (),
    "B1": (
        "gs1", "gk1", "gq1", "gv1", "go1", "X", "gf00", "gp00", "gs2", "gk2", "gs3", "gq2", "gv2", "go2", "gs4",
        "gk3", "gf10", "gp10", "gf01",
    ),
    "L1": (
        "gq3", "gp01", "go3", "gf20", "gp20", "gf11", "gv3", "gf02", "gp11", "gp02", "gf30", "gp30", "gf21", "gp21",
        "gf12", "gk4", "gq4", "gp12",
    ),
    "FK": (
        "gf31", "gp31", "gf22", "gp22", "go4", "gv4", "gf32", "gf03",
    ),
    "FV": (
        "C", "gp03", "gp32",
    ),
    "FQ": (
        "gf13", "gp13", "gf23",
    ),
    "E0": (
        "gp23", "gf33",
    ),
    "E1": (),
    "E2": (
        "gf04", "gp04", "gp33",
    ),
    "E3": (),
    "E4": (
        "gf14", "gp14",
    ),
    "E5": (),
    "O": (
        "gf24", "gp24",
    ),
    "L2": (),
    "M0": (
        "gf34", "gp34",
    ),
    "M1": (
        "rf01", "rp01",
    ),
    "M2": (
        "rf11", "rp11",
    ),
    "M3": (
        "rf02", "rp02", "rf21", "rp21",
    ),
    "T": (
        "rf31",
    ),
    "A": (
        "rf12", "rp12", "rp31", "rp03", "rf03",
    ),
    "B": (),
    "H0": (
        "ro1",
    ),
    "H1": (
        "rf22", "rp22",
    ),
    "H2": (
        "rp04", "rf13", "rf32",
    ),
    "H3": (
        "rf04", "rp13", "rp32",
    ),
    "H4": (
        "rp05", "rf14", "rp23",
    ),
    "H5": (
        "rf05", "rp14", "rp33", "ro2",
    ),
    "Q": (
        "rf15", "rp24", "rf23",
    ),
    "K": (
        "rp15", "rp34", "rf33", "ro3", "rq1",
    ),
    "V": (
        "rp25", "rf24", "rk1",
    ),
    "G": (
        "rp35", "rf34", "ro4", "rv1", "rf25",
    ),
    "N": (
        "rq2", "rk2", "rf35", "rs1", "ro5", "rv2", "U", "rq3", "rs2", "rk3", "rv3", "rs3", "rq4", "rk4", "rv4", "rs4",
        "rq5", "rk5", "rv5", "rs5",
    ),
}
ORDER_ONE = "kosp"


def whole_kernel(dp_n, seq_n, *refs):
    x_ref, cot_ref, start_ref = refs[:3]
    w_qkv, w_out, w_fc, w_proj, w_vec = refs[3:8]
    result_out, input_out, fc_out, proj_out, qkv_out, wout_out, small_out = refs[8:15]
    qkv_hbm, out_hbm, fc_hbm, proj_hbm, vec_hbm = refs[15:20]
    (wbuf, gbuf, act, gm, a3, gh, resacc, gact, gqkv, away, back, tok, vecs, gk_sum, gv_sum) = refs[20:35]
    (x_in, cot, start_other, resid, mixed, qkv, kv_other, lse, bias, vec_low, vec, fc_own, fc_sum) = refs[35:48]
    refs = refs[48:]
    at = Place(dp_n, seq_n)
    stages = log2(dp_n * seq_n)
    turns, folds = log2(dp_n) - 1, log2(seq_n)
    sets = [turns + 1, folds, folds, folds]
    count = sum(sets)

    def grouped(some):
        groups, first = [], 0
        for size in sets:
            groups.append(some[first : first + size])
            first += size
        return groups

    big, small_bufs = refs[:count], refs[count : 2 * count]
    (small_src, big_send, big_recv, small_send, small_recv, w_sem, swap_sem, tok_send, tok_recv, tok_own) = refs[
        2 * count : 2 * count + 10
    ]
    (ask_send, ask_recv, side_send, side_recv, own_sem, in_send, in_recv, in_own, start_sem, kv_sem, vec_sem) = refs[
        2 * count + 10 :
    ]
    rows, width = resid.shape
    half = rows // 2
    shard = fc_out.shape[0]
    n_dev = dp_n * seq_n
    across = [("dp", k) for k in range(1, log2(dp_n))]
    at.enter()
    sibling = at.sibling()

    def own_rows(src):
        return lambda dp: src.at[pl.ds(pl.multiple_of(dp * (seq_n * shard), 16), seq_n * shard)]

    def reduction(kind, c):
        order = across[::-1] if kind == 0 else across
        where = lax.rem(c, gbuf.shape[0]) if not isinstance(c, int) else c % gbuf.shape[0]
        return Reduction(
            at,
            order,
            grouped([b.at[c] for b in big]),
            (big_send.at[c], big_recv.at[c]),
            own_rows(gbuf.at[where]),
        )

    def vector_reduction():
        return Reduction(
            at,
            across,
            grouped(small_bufs),
            (small_send, small_recv),
            own_rows(small_src),
        )

    def weight_copy(slot, src):
        return pltpu.make_async_copy(src, wbuf.at[slot], w_sem.at[slot])


    def array(name):
        if name in "qkv":
            part = "qkv".index(name)
            cols = pl.ds(part * width, width)
            return part, qkv_hbm.at[:, cols], w_qkv.at[:, cols]
        if name == "o":
            return 3, out_hbm, w_out
        if name == "s":
            return 4, vec_hbm, w_vec
        j = int(name[1])
        if name[0] == "f":
            return 5 + j, fc_hbm.at[j], fc_own.at[:, pl.ds(j * width, width)]
        return 5 + PIECES + j, proj_hbm.at[j], w_proj.at[pl.ds(j * shard, shard)]

    along = [("seq", k) for k in reversed(range(folds))]

    def shard_rows(full, d):
        return full.at[pl.ds(pl.multiple_of(d * shard, 8), shard)]

    def put(src, dst, s_sem, r_sem, device):
        return pltpu.make_async_remote_copy(
            src_ref=src, dst_ref=dst, send_sem=s_sem, recv_sem=r_sem, device_id=device, device_id_type=MESH
        )

    def gather_stage(name, t):
        n, full, own = array(name)
        names = along + (across[::-1] if name[0] in ORDER_ONE else across)
        deltas = [at.delta(x) for x in names]
        if t == 0:
            place = shard_rows(full, at.me)
            put(own, place, ask_send.at[n, 0], ask_recv.at[n, 0], at.partner(names[0])).start()
            put(own, place, side_send.at[n, 0], side_recv.at[n, 0], sibling).start()
            pltpu.make_async_copy(own, place, own_sem.at[n]).start()
            return
        some = full.at[pl.ds(0, shard << (t - 1))]
        put(some, some, ask_send.at[n, t - 1], ask_recv.at[n, t - 1], sibling).wait_recv()
        if t == folds:
            pltpu.make_async_copy(own, shard_rows(full, at.me), own_sem.at[n]).wait()

        def held(t, shift):
            if t < folds:
                return [shard_rows(full, at.me + shift + spread(j, deltas[:t])) for j in range(1 << t)]
            size = seq_n * shard
            return [
                full.at[pl.ds(pl.multiple_of((at.dp * seq_n + shift + spread(j, deltas[folds:t])) * shard, 8), size)]
                for j in range(1 << (t - folds))
            ]

        if t < len(names):
            for j, place in enumerate(held(t, 0)):
                src = own if j == 0 and t < folds else place
                put(src, place, ask_send.at[n, t], ask_recv.at[n, t], at.partner(names[t])).start()
        for place in held(t - 1, deltas[t - 1]):
            put(place, place, side_send.at[n, t], side_recv.at[n, t], sibling).start()

    def gathered(name):
        n, full, own = array(name)
        for t in range(stages):
            some = full.at[pl.ds(0, shard << max(t - 1, 0))]
            put(some, some, side_send.at[n, t], side_recv.at[n, t], sibling).wait_recv()

    def gather_drain(name):
        n, full, own = array(name)
        for t in range(stages - 1):
            some = full.at[pl.ds(0, shard << t)]
            put(some, some, ask_send.at[n, t], ask_recv.at[n, t], sibling).wait_send()
        for t in range(stages):
            some = full.at[pl.ds(0, shard << max(t - 1, 0))]
            put(some, some, side_send.at[n, t], side_recv.at[n, t], sibling).wait_send()

    slot_here = lax.div(at.quarter, 2) * at.parts + lax.rem(at.seq, at.parts)

    def incoming(which, i):
        src, dst = ((x_ref, x_in), (cot_ref, cot))[which]
        to_seq = at.core * at.seqs + i
        mine = (to_seq == at.seq) & (at.quarter_core == at.core)
        remote = put(
            src.at[i],
            dst.at[slot_here],
            in_send.at[which, i],
            in_recv.at[which, at.seq],
            (at.pair * 2 + at.quarter_core, to_seq),
        )
        local = pltpu.make_async_copy(src.at[i], dst.at[slot_here], in_own.at[which])
        return mine, remote, local

    def incoming_start(which):
        for i in range(at.seqs):
            mine, remote, local = incoming(which, i)
            pl.when(jnp.logical_not(mine))(remote.start)
            pl.when(mine)(local.start)

    def incoming_wait(which):
        src, dst = ((x_ref, x_in), (cot_ref, cot))[which]
        for i in range(at.seqs):
            mine, remote, local = incoming(which, i)
            pl.when(jnp.logical_not(mine))(remote.wait_send)
            pl.when(mine)(local.wait)
        for z in range(seq_n):
            comes = (at.core_of(z // at.parts) == at.core) & jnp.logical_not(
                (at.seq == z) & (at.source_core == at.core)
            )
            arrival = put(src.at[0], dst.at[0], in_send.at[which, 0], in_recv.at[which, z], sibling)
            pl.when(comes)(arrival.wait_recv)

    def load_piece(j):
        slot = 2 * lax.rem(j, 2)
        for k in range(PIECES):

            def ready(k=k):
                gathered(f"f{k}")
                gathered(f"p{k}")

            pl.when(j == k)(ready)
        weight_copy(slot, fc_hbm.at[j]).start()
        weight_copy(slot + 1, proj_hbm.at[j]).start()

    def after(slot):
        for op in AFTER[slot]:
            if op == "U":
                unsort_units()
                continue
            if op in "XC":
                incoming_start("XC".index(op))
                continue
            if op[0] == "g":
                gather_stage(op[1:-1], int(op[-1]))
                continue
            name, kind, t = op[1:], op[1], int(op[-1])
            if kind == "s":
                red = vector_reduction()
            else:
                c = 2 * int(name[1]) + (kind == "p") if kind in "fp" else 2 * PIECES + "oqkv".index(kind)
                red = reduction(int(kind in ORDER_ONE), int(c))
            if t < stages:
                red.stage(t)
                continue
            total = red.finish()
            if kind == "f":
                fc_sum[:, int(name[1]) * width : (int(name[1]) + 1) * width] = total
            elif kind == "p":
                proj_out[int(name[1]) * shard : (int(name[1]) + 1) * shard] = total
            elif kind == "o":
                wout_out[...] = total
            elif kind == "s":
                square = jnp.concatenate([total, jnp.zeros((128 - shard, 128), jnp.float32)], 0).T
                square = jnp.concatenate([square[:10], jnp.where(at.me < n_dev // 2, square[10:12], square[12:14]), square[12:16]], 0)
                small_out[...] = square
            else:
                part = "qkv".index(kind)
                qkv_out[:, part * width : (part + 1) * width] = total

    def after_each(prefix, i, count):
        for k in range(count):
            pl.when(i == k)(functools.partial(after, f"{prefix}{k}"))

    period = PIECES * shard
    group = period * 128 // math.gcd(period, 128)
    lane = lax.broadcasted_iota(jnp.int32, (1, PIECES * 128), 1)
    entry = lax.rem(lane, 128)
    source = lax.div(entry, shard) * period + lax.div(lane, 128) * shard + lax.rem(entry, shard)
    per_piece = group // PIECES
    source = jnp.where(entry < per_piece, source, -1)
    sorter = (lax.broadcasted_iota(jnp.int32, (group, 1), 0) == source).astype(jnp.float32)
    lane_one = lax.broadcasted_iota(jnp.int32, (1, 128), 1)
    groups = PIECES * width // group

    def sort_units():
        pieces = [[jnp.zeros((shard, 128), jnp.float32) for _ in range(width // 128)] for _ in range(PIECES)]
        for g in range(groups):
            moved = dot(w_fc[:, g * group : (g + 1) * group], sorter.astype(jnp.bfloat16), NN)
            block, shift = divmod(g * per_piece, 128)
            for j in range(PIECES):
                turned = moved[:, j * 128 : (j + 1) * 128]
                if shift:
                    turned = pltpu.roll(turned, shift, 1)
                    if shift + per_piece > 128:
                        pieces[j][block + 1] = pieces[j][block + 1] + jnp.where(lane_one < shift, turned, 0.0)
                    turned = jnp.where(lane_one >= shift, turned, 0.0)
                pieces[j][block] = pieces[j][block] + turned
        for j in range(PIECES):
            fc_own[:, j * width : (j + 1) * width] = jnp.concatenate(pieces[j], 1).astype(jnp.bfloat16)

    def unsort_units():
        stacked = []
        for g in range(groups):
            block, shift = divmod(g * per_piece, 128)
            parts = []
            for j in range(PIECES):
                first = j * width + block * 128
                part = fc_sum[:, first : first + 128]
                if shift:
                    part = pltpu.roll(part, 128 - shift, 1)
                    if shift + per_piece > 128:
                        beyond = pltpu.roll(fc_sum[:, first + 128 : first + 256], 128 - shift, 1)
                        part = jnp.where(lane_one < 128 - shift, part, beyond)
                parts.append(jnp.where(lane_one < per_piece, part, 0.0))
            stacked.append(jnp.concatenate(parts, 1))
        moved = lax.dot_general(
            jnp.concatenate(stacked, 0), sorter, NT, precision=lax.Precision.HIGHEST, preferred_element_type=jnp.float32
        )
        for g in range(groups):
            fc_out[:, g * group : (g + 1) * group] = moved[g * shard : (g + 1) * shard]

    after("start")
    ask_start = put(start_ref, start_other, start_sem.at[0], start_sem.at[1], sibling)
    ask_start.start()
    ask_start.wait()
    row = pl.ds(at.seq - at.source_core * at.seqs, 1)
    first_seen = jnp.where(at.source_core == at.core, start_ref[row], start_other[row])
    down = lax.broadcasted_iota(jnp.int32, (half, 1), 0)
    along_row = lax.broadcasted_iota(jnp.int32, (1, half), 1)
    key_firsts = [at.core * half, (1 - at.core) * half, (3 - at.core) * half, (2 + at.core) * half]
    for slot in range(2):
        low, high = [first_seen[:, k * half : (k + 1) * half] for k in ((0, 1), (3, 2))[slot]]
        seen_from = jnp.where(at.core == 0, low, high)
        place = key_firsts[2 * slot] + along_row
        for tile in range(2 * slot + 2):
            key = key_firsts[tile] + down
            bias[tile * half : (tile + 1) * half, slot * half : (slot + 1) * half] = jnp.where(
                (key >= seen_from) & (key <= place), 0.0, masked_score
            )
    sort_units()
    after("B0")
    after("B1")

    def token_rows(ref):
        return ref[...].reshape(rows, width).astype(jnp.float32)

    incoming_wait(0)
    gathered("s")
    vec_copy = pltpu.make_async_copy(vec_hbm, vec_low, vec_sem)
    vec_copy.start()
    normed, _ = normalised(token_rows(x_in))
    vec_copy.wait()
    columns = vec_low[...].astype(jnp.float32)
    vec[...] = columns.T[:16]
    odd_shard = lax.rem(lax.div(lax.broadcasted_iota(jnp.int32, (1, width), 1), shard), 2) == 1
    for part in range(2):
        doubled = [columns[d * shard : (d + 1) * shard] for d in range(part * n_dev // 2, (part + 1) * n_dev // 2) for _ in range(2)]
        lines = jnp.concatenate(doubled, 0).T
        vec[14 + part : 15 + part] = jnp.where(odd_shard, lines[11:12], lines[10:11])
    act[...] = (normed * vec[0:1] + vec[1:2]).astype(jnp.bfloat16)
    after("L1")

    def weight_here(name, slot):
        gathered(name)
        copy = weight_copy(slot, array(name)[1])
        copy.start()
        copy.wait()

    weight_here("k", 1)
    qkv[:, width : 2 * width] = dot(act[...], wbuf[1], NN).astype(jnp.bfloat16)
    after("FK")
    weight_here("v", 2)
    qkv[:, 2 * width :] = (dot(act[...], wbuf[2], NN) + vec[15:16]).astype(jnp.bfloat16)
    exchange_kv = put(qkv.at[:, pl.ds(width, 2 * width)], kv_other, kv_sem.at[0], kv_sem.at[1], sibling)
    exchange_kv.start()
    after("FV")
    weight_here("q", 0)
    qkv[:, :width] = (dot(act[...], wbuf[0], NN) + vec[14:15]).astype(jnp.bfloat16)
    after("FQ")
    gathered("o")
    weight_copy(3, out_hbm).start()
    exchange_kv.wait()
    pairs = width // (2 * HEAD_DIM)

    def heads_forward(i, carry):
        at_q = pl.ds(pl.multiple_of(i * 128, 128), 128)
        at_k = pl.ds(pl.multiple_of(width + i * 128, 128), 128)
        at_v = pl.ds(pl.multiple_of(2 * width + i * 128, 128), 128)
        attend_kernel(
            qkv.at[:, at_q],
            qkv.at[:, at_k],
            qkv.at[:, at_v],
            kv_other.at[:, at_q],
            kv_other.at[:, at_k],
            bias,
            mixed.at[:, at_q],
            lse.at[pl.ds(i, 1)],
        )
        after_each("E", i, 6)
        return carry

    lax.fori_loop(0, pairs, heads_forward, 0)
    weight_copy(3, out_hbm).wait()
    resid[...] = token_rows(x_in) + branch_scale * (dot(mixed[...], wbuf[3], NN) + vec[2:3])
    after("O")
    load_piece(jnp.int32(0))
    incoming_wait(1)

    normed, _ = normalised(resid[...])
    act[...] = (normed * vec[3:4] + vec[4:5]).astype(jnp.bfloat16)
    grad_mlp = (branch_scale * token_rows(cot)).astype(jnp.bfloat16)
    gm[...] = grad_mlp
    vecs[...] = jnp.zeros_like(vecs)
    vecs[5:6] = jnp.sum(grad_mlp.astype(jnp.float32), 0, keepdims=True)
    resacc[...] = jnp.zeros_like(resacc)
    gact[...] = jnp.zeros_like(gact)
    after("L2")

    def piece(j, carry):
        slot = 2 * lax.rem(j, 2)
        pl.when(j + 1 < PIECES)(lambda: load_piece(j + 1))
        weight_copy(slot, fc_hbm.at[j]).wait()
        weight_copy(slot + 1, proj_hbm.at[j]).wait()
        fc, proj = wbuf.at[slot], wbuf.at[slot + 1]
        bias_fc = vec[pl.ds(6 + j, 1)]

        def some(r, total):
            here = pl.ds(pl.multiple_of(r * half, 16), half)
            u = dot(act[here], fc[...], NN) + bias_fc
            bent = jnp.tanh(gelu_root * (u + gelu_coeff * u * u * u))
            hidden = (0.5 * u * (1.0 + bent)).astype(jnp.bfloat16)
            inner = gelu_root * (1.0 + 3.0 * gelu_coeff * u * u)
            slope = 0.5 * (1.0 + bent) + 0.5 * u * (1.0 - bent * bent) * inner
            a3[here] = hidden
            resacc[here] += dot(hidden, proj[...], NN)
            grad_u = (dot(gm[here], proj[...], NT) * slope).astype(jnp.bfloat16)
            gh[here] = grad_u
            gact[here] += dot(grad_u, fc[...], NT)
            return total + jnp.sum(grad_u.astype(jnp.float32), 0, keepdims=True)

        total = lax.fori_loop(0, 2, some, jnp.zeros((1, width), jnp.float32))
        vecs[pl.ds(6 + j, 1)] = total
        for kind, (left, right) in enumerate(((act, gh), (a3, gm))):
            c = 2 * j + kind
            red = reduction(kind, c)
            pl.when(c >= gbuf.shape[0])(
                lambda red=red, c=c, kind=kind: reduction(kind, c - gbuf.shape[0]).copy(0).wait_send()
            )
            gbuf[lax.rem(c, gbuf.shape[0])] = dot(left[...], right[...], TN).astype(jnp.bfloat16)
            red.start()
        after_each("M", j, PIECES)
        return carry

    lax.fori_loop(0, PIECES, piece, 0)
    for slot in range(3):
        weight_copy(slot, qkv_hbm.at[:, pl.ds(slot * width, width)]).start()
    weight_copy(3, out_hbm).start()

    def token_copies(which, j):
        slot, rest = j // at.parts, j % at.parts
        quarter = at.core + slot * (3 - 2 * at.core)
        to_seq = quarter * at.parts + rest
        mine = (to_seq == at.seq) & (at.source_core == at.core)
        place = at.seq - at.source_core * at.seqs
        out = (result_out, input_out)[which]
        remote = pltpu.make_async_remote_copy(
            src_ref=tok.at[which, j],
            dst_ref=out.at[place],
            send_sem=tok_send.at[which, j],
            recv_sem=tok_recv.at[which, place],
            device_id=(at.pair * 2 + at.source_core, to_seq),
            device_id_type=MESH,
        )
        local = pltpu.make_async_copy(tok.at[which, j], out.at[place], tok_own.at[which])
        return mine, remote, local

    def tokens_start(which, value):
        tok[which] = value.astype(jnp.bfloat16).reshape(tok.shape[1:])
        for j in range(seq_n // 2):
            mine, remote, local = token_copies(which, j)
            pl.when(jnp.logical_not(mine))(remote.start)
            pl.when(mine)(local.start)

    def tokens_wait(which):
        for j in range(seq_n // 2):
            mine, remote, local = token_copies(which, j)
            pl.when(jnp.logical_not(mine))(remote.wait_send)
            pl.when(mine)(local.wait)
        for i in range(at.seqs):
            comes = jnp.logical_not((at.core * at.seqs + i == at.seq) & (at.quarter_core == at.core))
            arrival = pltpu.make_async_remote_copy(
                src_ref=tok.at[which, 0],
                dst_ref=(result_out, input_out)[which].at[i],
                send_sem=tok_send.at[which, 0],
                recv_sem=tok_recv.at[which, i],
                device_id=sibling,
                device_id_type=MESH,
            )
            pl.when(comes)(arrival.wait_recv)

    tokens_start(0, resid[...] + branch_scale * (resacc[...] + vec[5:6]))
    after("T")

    normed, inverse = normalised(resid[...])
    grad_two = gact[...]
    vecs[3:4] = jnp.sum(grad_two * normed, 0, keepdims=True)
    vecs[4:5] = jnp.sum(grad_two, 0, keepdims=True)
    grad_mid = token_rows(cot) + norm_spread(grad_two, normed, inverse, vec[3:4])
    gact[...] = grad_mid
    grad_branch = (branch_scale * grad_mid).astype(jnp.bfloat16)
    act[...] = grad_branch
    vecs[2:3] = jnp.sum(grad_branch.astype(jnp.float32), 0, keepdims=True)

    c_out = 2 * PIECES
    reduction(0, c_out - gbuf.shape[0]).copy(0).wait_send()
    gbuf[c_out % gbuf.shape[0]] = dot(mixed[...], grad_branch, TN).astype(jnp.bfloat16)
    reduction(1, c_out).start()
    after("A")
    weight_copy(3, out_hbm).wait()
    gm[...] = dot(grad_branch, wbuf[3], NT).astype(jnp.bfloat16)
    after("B")

    def heads(i, carry):
        at_q = pl.ds(pl.multiple_of(i * 128, 128), 128)
        at_k = pl.ds(pl.multiple_of(width + i * 128, 128), 128)
        at_v = pl.ds(pl.multiple_of(2 * width + i * 128, 128), 128)
        attend_back_kernel(
            qkv.at[:, at_q],
            qkv.at[:, at_k],
            qkv.at[:, at_v],
            kv_other.at[:, at_q],
            kv_other.at[:, at_k],
            gm.at[:, at_q],
            bias,
            lse.at[pl.ds(i, 1)],
            gqkv.at[:, at_q],
            gqkv.at[:, at_k],
            gqkv.at[:, at_v],
            away.at[:, at_q],
            away.at[:, at_k],
            gk_sum,
            gv_sum,
        )
        after_each("H", i, 6)
        return carry

    lax.fori_loop(0, pairs, heads, 0)

    exchange = pltpu.make_async_remote_copy(
        src_ref=away,
        dst_ref=back,
        send_sem=swap_sem.at[0],
        recv_sem=swap_sem.at[1],
        device_id=sibling,
        device_id_type=MESH,
    )
    exchange.start()
    normed, inverse = normalised(token_rows(x_in))
    act[...] = (normed * vec[0:1] + vec[1:2]).astype(jnp.bfloat16)

    def grad_of(part):
        c = c_out + 1 + part
        kind = part % 2
        here = pl.ds(part * width, width)
        if part > 0:
            far = pl.ds((part - 1) * width, width)
            gqkv[:, here] = (gqkv[:, here].astype(jnp.float32) + back[:, far].astype(jnp.float32)).astype(jnp.bfloat16)
        reduction(kind, c - gbuf.shape[0]).copy(0).wait_send()
        gbuf[c % gbuf.shape[0]] = dot(act[...], gqkv[:, here], TN).astype(jnp.bfloat16)
        reduction(kind, c).start()
        weight_copy(part, qkv_hbm.at[:, here]).wait()

    def column_sum(part):
        return jnp.sum(gqkv[:, pl.ds(part * width, width)].astype(jnp.float32), 0, keepdims=True)

    grad_of(0)
    after("Q")
    exchange.wait()
    grad_of(1)
    after("K")
    grad_of(2)
    after("V")
    first, third = column_sum(0), column_sum(2)
    for row, value in ((10, first), (11, first), (12, third), (13, third)):
        vecs[row : row + 1] = value
    grad_one = dot(gqkv[:, pl.ds(0, width)], wbuf[0], NT)
    grad_one = grad_one + dot(gqkv[:, pl.ds(width, width)], wbuf[1], NT)
    resacc[...] = grad_one + dot(gqkv[:, pl.ds(2 * width, width)], wbuf[2], NT)
    after("G")
    grad_one = resacc[...]
    normed, inverse = normalised(token_rows(x_in))
    vecs[0:1] = jnp.sum(grad_one * normed, 0, keepdims=True)
    vecs[1:2] = jnp.sum(grad_one, 0, keepdims=True)
    tokens_start(1, gact[...] + norm_spread(grad_one, normed, inverse, vec[0:1]))
    columns = vecs[...].T
    small_src[...] = columns
    lane = lax.broadcasted_iota(jnp.int32, (1, 128), 1)
    even, odd = (lane == 10) | (lane == 12), (lane == 11) | (lane == 13)
    for d in range(n_dev):
        start = 2 * shard * (d % (n_dev // 2))
        kept = columns[d * shard : (d + 1) * shard]
        kept = jnp.where(even, columns[start : start + shard], kept)
        kept = jnp.where(odd, columns[start + shard : start + 2 * shard], kept)
        small_src[d * shard : (d + 1) * shard] = kept
    vector_reduction().start()
    after("N")
    for c in range(GRADS):
        red = reduction(0, c)
        for t in range(0 if c >= GRADS - gbuf.shape[0] else 1, stages):
            red.copy(t).wait_send()
    for t in range(stages):
        vector_reduction().copy(t).wait_send()
    for name in ["s", "q", "k", "v", "o"] + [f"{x}{j}" for x in "fp" for j in range(PIECES)]:
        gather_drain(name)
    tokens_wait(0)
    tokens_wait(1)


def whole(mesh_shape, x, cot, start, shards):
    dp_n, seq_n = mesh_shape
    seqs, blk, width = x.shape
    rows = blk * (seq_n // 2)
    n_dev = dp_n * seq_n
    stages = log2(n_dev)
    shard = width // n_dev
    vmem = pl.BlockSpec(memory_space=pltpu.VMEM)
    hbm = pl.BlockSpec(memory_space=ANY)
    DMA = pltpu.SemaphoreType.DMA
    low, full = jnp.bfloat16, jnp.float32
    slots = 4
    arrays = 5 + 2 * PIECES

    def buffers(lead, cols, dtype):
        turns, folds = log2(dp_n) - 1, log2(seq_n)
        parts = [(seq_n >> (m + 1), shard, cols) for m in range(folds)]
        return (
            [pltpu.VMEM(lead + (width // 2 >> t, cols), dtype) for t in range(turns + 1)]
            + [pltpu.VMEM(lead + p, dtype) for p in parts] * 2
            + [pltpu.VMEM(lead + p, full) for p in parts]
        )

    token = jax.ShapeDtypeStruct((seq_n // 2, blk, width), low)
    grads = [(shard, PIECES * width), (PIECES * shard, width), (shard, 3 * width), (shard, width), (16, 128)]
    gathers = [(width, 3 * width), (width, width), (PIECES, width, width), (PIECES, width, width), (width, 128)]
    out = pl.pallas_call(
        functools.partial(whole_kernel, dp_n, seq_n),
        out_shape=[token, token]
        + [jax.ShapeDtypeStruct(s, full) for s in grads]
        + [jax.ShapeDtypeStruct(s, low) for s in gathers],
        in_specs=[vmem] * 8,
        out_specs=[hbm] * 2 + [vmem] * 5 + [hbm] * 5,
        scratch_shapes=[
            pltpu.VMEM((4, width, width), low),
            pltpu.VMEM((slots, width, width), low),
            pltpu.VMEM((rows, width), low),
            pltpu.VMEM((rows, width), low),
            pltpu.VMEM((rows, width), low),
            pltpu.VMEM((rows, width), low),
            pltpu.VMEM((rows, width), full),
            pltpu.VMEM((rows, width), full),
            pltpu.VMEM((rows, 3 * width), low),
            pltpu.VMEM((rows, 2 * width), low),
            pltpu.VMEM((rows, 2 * width), low),
            pltpu.VMEM((2, seq_n // 2, blk, width), low),
            pltpu.VMEM((128, width), full),
            pltpu.VMEM((2 * rows, 128), full),
            pltpu.VMEM((2 * rows, 128), full),
            pltpu.VMEM((seq_n // 2, blk, width), low),
            pltpu.VMEM((seq_n // 2, blk, width), low),
            pltpu.VMEM(start.shape, start.dtype),
            pltpu.VMEM((rows, width), full),
            pltpu.VMEM((rows, width), low),
            pltpu.VMEM((rows, 3 * width), low),
            pltpu.VMEM((rows, 2 * width), low),
            pltpu.VMEM((width // 128, 2, rows), full),
            pltpu.VMEM((2 * rows, rows), full),
            pltpu.VMEM((width, 128), low),
            pltpu.VMEM((16, width), full),
            pltpu.VMEM((shard, PIECES * width), low),
            pltpu.VMEM((shard, PIECES * width), full),
        ]
        + buffers((GRADS,), width, low)
        + buffers((), 128, full)
        + [
            pltpu.VMEM((width, 128), full),
            DMA((GRADS, stages)),
            DMA((GRADS, stages)),
            DMA((stages,)),
            DMA((stages,)),
            DMA((4,)),
            DMA((2,)),
            DMA((2, seq_n // 2)),
            DMA((2, seq_n // 2)),
            DMA((2,)),
            DMA((arrays, stages - 1)),
            DMA((arrays, stages - 1)),
            DMA((arrays, stages)),
            DMA((arrays, stages)),
            DMA((arrays,)),
            DMA((2, seqs)),
            DMA((2, seq_n)),
            DMA((2,)),
            DMA((2,)),
            DMA((2,)),
            DMA,
        ],
        compiler_params=pltpu.CompilerParams(
            collective_id=4, has_side_effects=True, vmem_limit_bytes=64 * 1024 * 1024 - 65536
        ),
        name="whole",
    )(x, cot, start, *shards)
    return out[:7]


def normalised(rows):
    center = rows - jnp.mean(rows, -1, keepdims=True)
    inverse = lax.rsqrt(jnp.mean(center * center, -1, keepdims=True) + norm_eps)
    return center * inverse, inverse


def norm_spread(grad_in, normed, inverse, gain):
    scaled = grad_in * gain
    return inverse * (
        scaled
        - jnp.mean(scaled, -1, keepdims=True)
        - normed * jnp.mean(scaled * normed, -1, keepdims=True)
    )


def packed(vectors, row_unit, dtype):
    flat = jnp.concatenate(vectors, -1)
    size = flat.shape[-1]
    rows = -(-size // (128 * row_unit)) * row_unit
    flat = jnp.pad(flat, [(0, 0)] * (flat.ndim - 1) + [(0, rows * 128 - size)])
    return flat.reshape(flat.shape[:-1] + (rows, 128)).astype(dtype)


def unpacked(rows, sizes):
    flat = rows.reshape(rows.shape[0], -1)
    out, first = [], 0
    for size in sizes:
        out.append(flat[:, first : first + size].reshape(-1))
        first += size
    return out


def block(mesh_shape, *args):
    (
        block_input,
        segments,
        cotangent,
        ln1_gain,
        ln1_bias,
        w_qkv,
        b_qv,
        w_out,
        b_out,
        ln2_gain,
        ln2_bias,
        w_fc,
        b_fc,
        w_proj,
        b_proj,
    ) = args
    dp_n, seq_n = mesh_shape
    n_dev = dp_n * seq_n
    micro_count, seq_count, stretch, width = block_input.shape
    seq_len = segments.shape[2]
    seqs = micro_count * seq_count
    assert 2 * seqs == seq_n and seq_n % 4 == 0
    at = Place(dp_n, seq_n)
    vectors = (ln1_gain, ln1_bias, b_qv, b_out, ln2_gain, ln2_bias, b_fc, b_proj)
    sizes = [v.shape[0] for v in vectors]
    gathered = gather_all(
        mesh_shape,
        block_input.reshape(seqs, stretch, width),
        cotangent.reshape(seqs, stretch, width),
        segments.reshape(seqs, seq_len),
        (w_qkv, w_out, w_fc, w_proj, packed(vectors, 16, jnp.bfloat16)),
    )
    x_rows, cot_rows, seg_other, weight_qkv, weight_out, weight_fc, weight_proj, small = gathered
    rows = seq_len // 2
    half = rows // 2
    x_rows = x_rows.reshape(rows, width).astype(jnp.float32)
    grad_out = cot_rows.reshape(rows, width).astype(jnp.float32)
    weight_qkv, weight_out, weight_fc, weight_proj = [
        w.reshape(-1, w.shape[-1]) for w in (weight_qkv, weight_out, weight_fc, weight_proj)
    ]
    gain_one, bias_one, bias_qv, bias_out, gain_two, bias_two, bias_fc, bias_proj = [
        v.astype(jnp.float32) for v in unpacked(small, sizes)
    ]

    seg_all = jnp.where(at.source_core == at.core, segments.reshape(seqs, seq_len), seg_other)
    seg = lax.dynamic_index_in_dim(seg_all, at.seq - at.source_core * seqs, 0, keepdims=False)
    quarter = jnp.arange(half, dtype=jnp.int32)
    own_first = [at.core * half, (3 - at.core) * half]
    other_first = [(1 - at.core) * half, (2 + at.core) * half]
    firsts = [own_first[0], other_first[0], own_first[1], other_first[1]]
    key_place = jnp.concatenate([f + quarter for f in firsts])
    key_seg = jnp.concatenate([lax.dynamic_slice_in_dim(seg, f, half, 0) for f in firsts])
    query_place = jnp.concatenate([key_place[:half], key_place[2 * half : 3 * half]])
    query_seg = jnp.concatenate([key_seg[:half], key_seg[2 * half : 3 * half]])
    visible = (key_seg[:, None] == query_seg[None, :]) & (key_place[:, None] <= query_place[None, :])
    bias = jnp.where(visible, 0.0, masked_score).astype(jnp.float32)

    normed_out, normed_one, inverse_one = layer_norm(x_rows, gain_one, bias_one)
    act_one = normed_out.astype(jnp.bfloat16)
    bias_full = jnp.concatenate([bias_qv[:width], jnp.zeros((width,), jnp.float32), bias_qv[width:]])
    qkv = (jnp.dot(act_one, weight_qkv, preferred_element_type=jnp.float32) + bias_full).astype(jnp.bfloat16)
    kv_other = swap(mesh_shape, qkv, (width, 2 * width), 2)
    mixed_out, lse = attend(qkv, kv_other, bias)
    resid_mid = x_rows + branch_scale * (
        jnp.dot(mixed_out, weight_out, preferred_element_type=jnp.float32) + bias_out
    )

    normed_out, normed_two, inverse_two = layer_norm(resid_mid, gain_two, bias_two)
    act_two = normed_out.astype(jnp.bfloat16)
    hidden = jnp.dot(act_two, weight_fc, preferred_element_type=jnp.float32) + bias_fc
    act_three = gelu_tanh(hidden).astype(jnp.bfloat16)
    result = resid_mid + branch_scale * (
        jnp.dot(act_three, weight_proj, preferred_element_type=jnp.float32) + bias_proj
    )
    grad_mlp = (branch_scale * grad_out).astype(jnp.bfloat16)
    grad_bproj = jnp.sum(grad_mlp.astype(jnp.float32), 0)
    grad_wproj = dot(act_three, grad_mlp, TN)
    grad_act3 = dot(grad_mlp, weight_proj, NT)
    grad_hidden = (grad_act3 * gelu_slope(hidden)).astype(jnp.bfloat16)
    grad_bfc = jnp.sum(grad_hidden.astype(jnp.float32), 0)
    grad_wfc = dot(act_two, grad_hidden, TN)
    grad_act2 = dot(grad_hidden, weight_fc, NT)
    grad_norm2, grad_gain2, grad_bias2 = norm_back(grad_act2, normed_two, inverse_two, gain_two)
    grad_mid = grad_out + grad_norm2

    grad_branch = (branch_scale * grad_mid).astype(jnp.bfloat16)
    grad_bout = jnp.sum(grad_branch.astype(jnp.float32), 0)
    grad_wout = dot(mixed_out, grad_branch, TN)
    grad_mixed = dot(grad_branch, weight_out, NT).astype(jnp.bfloat16)
    grad_q, grad_k, grad_v, away_k, away_v = attend_back(qkv, kv_other, grad_mixed, bias, lse)
    back = swap(mesh_shape, jnp.concatenate([away_k, away_v], 1), (0, 2 * width), 3)
    key_value = jnp.concatenate([grad_k, grad_v], 1).astype(jnp.float32) + back.astype(jnp.float32)
    grad_qkv = jnp.concatenate([grad_q, key_value.astype(jnp.bfloat16)], 1)
    grad_wide = grad_qkv.astype(jnp.float32)
    grad_bqv = jnp.concatenate([jnp.sum(grad_wide[:, :width], 0), jnp.sum(grad_wide[:, 2 * width :], 0)])
    grad_wqkv = dot(act_one, grad_qkv, TN)
    grad_act1 = dot(grad_qkv, weight_qkv, NT)
    grad_norm1, grad_gain1, grad_bias1 = norm_back(grad_act1, normed_one, inverse_one, gain_one)
    grad_input = grad_mid + grad_norm1

    vec_grads = (grad_gain1, grad_bias1, grad_bqv, grad_bout, grad_gain2, grad_bias2, grad_bfc, grad_bproj)
    token_block = (seq_n // 2, stretch, width)
    parts = [
        g.astype(jnp.bfloat16).reshape((n_dev, -1, g.shape[-1]))
        for g in (grad_wqkv, grad_wout, grad_wfc, grad_wproj)
    ] + [packed([v.reshape(n_dev, -1) for v in vec_grads], 8, jnp.float32)]
    (result, grad_input), totals = reduce_all(
        mesh_shape,
        [result.astype(jnp.bfloat16).reshape(token_block), grad_input.astype(jnp.bfloat16).reshape(token_block)],
        parts,
    )
    owned = unpacked(totals[4].reshape(1, -1), sizes)
    shape = block_input.shape
    return (
        result.reshape(shape),
        grad_input.reshape(shape),
        owned[0],
        owned[1],
        totals[0],
        owned[2],
        totals[1],
        owned[3],
        owned[4],
        owned[5],
        totals[2],
        owned[6],
        totals[3],
        owned[7],
    )


def settle_kernel(*refs):
    half = len(refs) // 2
    for src, dst in zip(refs[:half], refs[half:]):
        dst[...] = src[...]


def settle(arrays):
    vmem = pl.BlockSpec(memory_space=pltpu.VMEM)
    return pl.pallas_call(
        settle_kernel,
        out_shape=[jax.ShapeDtypeStruct(a.shape, a.dtype) for a in arrays],
        in_specs=[vmem] * len(arrays),
        out_specs=[vmem] * len(arrays),
        name="settle",
    )(*arrays)


def fused_block(mesh_shape, *args):
    (
        block_input,
        segments,
        cotangent,
        ln1_gain,
        ln1_bias,
        w_qkv,
        b_qv,
        w_out,
        b_out,
        ln2_gain,
        ln2_bias,
        w_fc,
        b_fc,
        w_proj,
        b_proj,
    ) = args
    dp_n, seq_n = mesh_shape
    n_dev = dp_n * seq_n
    micro_count, seq_count, stretch, width = block_input.shape
    seq_len = segments.shape[2]
    seqs = micro_count * seq_count
    assert 2 * seqs == seq_n and seq_n % 4 == 0 and w_fc.shape[1] == PIECES * width
    at = Place(dp_n, seq_n)
    shard = width // n_dev
    vectors = [ln1_gain, ln1_bias, b_out, ln2_gain, ln2_bias, b_proj]
    vectors += [b_fc[j * shard : (j + 1) * shard] for j in range(PIECES)] + [b_qv[:shard], b_qv[shard:]]
    lane = lax.broadcasted_iota(jnp.int32, (shard, 128), 1)
    columns = jnp.zeros((shard, 128), jnp.bfloat16)
    for k, vector in enumerate(vectors):
        columns = jnp.where(lane == k, vector[:, None], columns)
    seg = segments.reshape(seqs, seq_len)
    start = jnp.sum((seg[:, None, :] < seg[:, :, None]).astype(jnp.int32), 2)
    result, grad_input, grad_fc, grad_proj, grad_qkv, grad_out, lines = whole(
        mesh_shape,
        block_input.reshape(seqs, stretch, width),
        cotangent.reshape(seqs, stretch, width),
        start,
        (w_qkv, w_out, w_fc, w_proj, columns),
    )
    result, grad_input, grad_fc, grad_proj, grad_qkv, grad_out = settle(
        (result, grad_input, grad_fc, grad_proj, grad_qkv, grad_out)
    )
    lines = lines[:, :shard]
    grad_bqv = lines[10:12].reshape(-1)
    shape = block_input.shape
    return (
        result.reshape(shape),
        grad_input.reshape(shape),
        lines[0],
        lines[1],
        grad_qkv,
        grad_bqv,
        grad_out,
        lines[2],
        lines[3],
        lines[4],
        grad_fc,
        lines[6:10].reshape(-1),
        grad_proj,
        lines[5],
    )


def whole_block(mesh_shape, *args):
    aligned = args[5].shape[0] % 8 == 0 and mesh_shape[1] == 4
    return (fused_block if aligned else block)(mesh_shape, *args)


def solution(mesh):
    both = ("dp", "seq")
    tokens, vector, matrix = P(None, "dp", "seq", None), P(both), P(both, None)
    return jax.shard_map(
        functools.partial(whole_block, (mesh.shape["dp"], mesh.shape["seq"])),
        mesh=mesh,
        in_specs=(
            tokens,
            P(None, "dp", None),
            tokens,
            vector,
            vector,
            matrix,
            vector,
            matrix,
            vector,
            vector,
            vector,
            matrix,
            vector,
            matrix,
            vector,
        ),
        out_specs=(
            tokens,
            tokens,
            vector,
            vector,
            matrix,
            vector,
            matrix,
            vector,
            vector,
            vector,
            matrix,
            vector,
            matrix,
            vector,
        ),
        check_vma=False,
    )
```

```python
import functools
import math

import jax
import jax.numpy as jnp
from jax import lax
from jax.experimental import pallas as pl
from jax.experimental.pallas import tpu as pltpu
from jax.sharding import PartitionSpec as P

HEADS = 12
HEAD_DIM = 64
MESH = pl.DeviceIdType.MESH
PIECES = 4
ANY = pl.ANY

branch_scale = 48.0 ** (-0.5)
norm_eps = 1e-05
masked_score = -1e30
gelu_coeff = 0.044715
gelu_root = (2.0 / 3.141592653589793) ** 0.5


def layer_norm(tok_rows, gain_vec, bias_vec):
    center = tok_rows - jnp.mean(tok_rows, -1, keepdims=True)
    inverse = lax.rsqrt(jnp.mean(center * center, -1, keepdims=True) + norm_eps)
    normed = center * inverse
    return (normed * gain_vec + bias_vec, normed, inverse)


def norm_back(grad_in, normed, inverse, gain_vec):
    grad_gain = jnp.sum(grad_in * normed, 0)
    grad_bias = jnp.sum(grad_in, 0)
    scaled = grad_in * gain_vec
    spread = (
        scaled
        - jnp.mean(scaled, -1, keepdims=True)
        - normed * jnp.mean(scaled * normed, -1, keepdims=True)
    )
    return (inverse * spread, grad_gain, grad_bias)


def gelu_tanh(pre_act):
    tanh_val = jnp.tanh(gelu_root * (pre_act + gelu_coeff * pre_act * pre_act * pre_act))
    return 0.5 * pre_act * (1.0 + tanh_val)


def gelu_slope(pre_act):
    tanh_val = jnp.tanh(gelu_root * (pre_act + gelu_coeff * pre_act * pre_act * pre_act))
    inner_slope = gelu_root * (1.0 + 3.0 * gelu_coeff * pre_act * pre_act)
    return 0.5 * (1.0 + tanh_val) + 0.5 * pre_act * (1.0 - tanh_val * tanh_val) * inner_slope


def log2(n):
    k = n.bit_length() - 1
    assert 1 << k == n
    return k


class Place:
    def __init__(self, dp_n, seq_n):
        self.dp_n, self.seq_n = dp_n, seq_n
        self.dp, self.seq = lax.axis_index("dp"), lax.axis_index("seq")
        self.core = lax.rem(self.dp, 2)
        self.pair = lax.div(self.dp, 2)
        self.me = self.dp * seq_n + self.seq
        self.seqs = seq_n // 2
        self.parts = seq_n // 4
        self.quarter = lax.div(self.seq, self.parts)
        self.quarter_core = self.core_of(self.quarter)
        self.source_core = lax.div(self.seq, self.seqs)

    def core_of(self, quarter):
        return lax.rem(lax.div(quarter + 1, 2), 2)

    def bit(self, name):
        axis, k = name
        return lax.rem(lax.div(self.seq if axis == "seq" else self.dp, 1 << k), 2)

    def delta(self, name):
        axis, k = name
        return (1 - 2 * self.bit(name)) * ((1 << k) * (1 if axis == "seq" else self.seq_n))

    def partner(self, name):
        axis, k = name
        step = (1 - 2 * self.bit(name)) * (1 << k)
        if axis == "seq":
            return (self.dp, self.seq + step)
        return (self.dp + step, self.seq)

    def sibling(self):
        return self.partner(("dp", 0))

    def enter(self):
        barrier = pltpu.get_barrier_semaphore()
        count = 0
        for core_step in range(2):
            for seq_step in range(self.seq_n):
                if core_step == 0 and seq_step == 0:
                    continue
                other = (
                    self.pair * 2 + lax.rem(self.core + core_step, 2),
                    lax.rem(self.seq + seq_step, self.seq_n),
                )
                pl.semaphore_signal(barrier, inc=1, device_id=other, device_id_type=MESH)
                count += 1
        for k in range(1, log2(self.dp_n)):
            pl.semaphore_signal(barrier, inc=1, device_id=self.partner(("dp", k)), device_id_type=MESH)
            count += 1
        pl.semaphore_wait(barrier, count)


def orders_of(dp_n, seq_n):
    along = [("seq", k) for k in reversed(range(log2(seq_n)))]
    across = [("dp", k) for k in range(1, log2(dp_n))]
    back = across[::-1]
    return {
        "zxy": along + across,
        "zyx": along + back,
        "xyz": across + along,
        "yxz": back + along,
    }


def repeat(count, body):
    if count <= 16:
        for j in range(count):
            body(j)
    else:
        lax.fori_loop(0, count, lambda j, c: (body(j), c)[1], 0)


def spread(j, deltas):
    total = 0
    for i, delta in enumerate(deltas):
        if isinstance(j, int):
            if (j >> i) & 1:
                total = total + delta
        else:
            total = total + lax.rem(lax.div(j, 1 << i), 2) * delta
    return total


def resolve(shape, cut):
    axis, pieces, k = cut
    if axis == 1 and shape[1] % (8 * pieces):
        axis = 2
    unit = 8 if axis == 1 else 128
    units = shape[axis] // unit
    start, stop = units * k // pieces, units * (k + 1) // pieces
    return axis, start * unit, (stop - start) * unit


def piece_shape(shape, cut):
    axis, _, size = resolve(shape, cut)
    shape = list(shape)
    shape[axis] = size
    return tuple(shape[1:])


def piece_of(ref, lead, cut):
    axis, start, size = resolve(ref.shape, cut)
    where = [slice(None)] * 2
    where[axis - 1] = pl.ds(start, size)
    return ref.at[(lead, *where)]


GATHER = (
    (0, 2, 3, 0, "zxy", 0),
    (0, 2, 3, 1, "zyx", 0),
    (4, 2, 1, 0, "zyx", 0),
    (0, 2, 3, 2, "zxy", 1),
    (1, 2, 1, 0, "zyx", 1),
    (2, 2, 4, 0, "zxy", 2),
    (3, 1, 4, 0, "zyx", 2),
    (2, 2, 4, 1, "zxy", 3),
    (3, 1, 4, 1, "zyx", 3),
    (2, 2, 4, 2, "zxy", 4),
    (3, 1, 4, 2, "zyx", 4),
    (2, 2, 4, 3, "zxy", 5),
    (3, 1, 4, 3, "zyx", 5),
)
X_WAVE, COT_WAVE = 2, 5


def gather_kernel(dp_n, seq_n, major, x_ref, cot_ref, seg_ref, *refs):
    n_arr = 5
    shard = refs[:n_arr]
    x_out, cot_out, seg_out = refs[n_arr : n_arr + 3]
    full = refs[n_arr + 3 : n_arr + 3 + n_arr]
    (send_sem, recv_sem, side_send, side_recv, own_sem, tok_send, tok_recv, tok_own, seg_sem) = refs[
        2 * n_arr + 3 :
    ]
    at = Place(dp_n, seq_n)
    orders = orders_of(dp_n, seq_n)
    stages = len(orders["zxy"])
    at.enter()
    sibling = at.sibling()

    piece = piece_of

    def put(src, dst, s_sem, r_sem, device):
        pltpu.make_async_remote_copy(
            src_ref=src, dst_ref=dst, send_sem=s_sem, recv_sem=r_sem, device_id=device, device_id_type=MESH
        ).start()

    def place_of(a, idx, cut, count=None):
        if a in major:
            idx = idx + cut[2] * dp_n * seq_n
            return full[a].at[idx if count is None else pl.ds(idx, count)]
        return piece(full[a], idx if count is None else pl.ds(idx, count), cut)

    def group(a, cut, count, s_sem, r_sem, device):
        whole = place_of(a, 0, cut, count)
        return pltpu.make_async_remote_copy(
            src_ref=whole, dst_ref=whole, send_sem=s_sem, recv_sem=r_sem, device_id=device, device_id_type=MESH
        )

    def own_src(a, cut):
        return piece(shard[a], 0, cut)

    def stage(c, t):
        a, *cut, order, _ = GATHER[c]
        names = orders[order]
        deltas = [at.delta(n) for n in names]
        if t > 0:
            group(a, cut, 1 << (t - 1), send_sem.at[c, t - 1], recv_sem.at[c, t - 1], sibling).wait_recv()

            def pass_on(j):
                idx = at.me + deltas[t - 1] + spread(j, deltas[: t - 1])
                place = place_of(a, idx, cut)
                put(place, place, side_send.at[c, t], side_recv.at[c, t], sibling)

            if t < stages:
                partner = at.partner(names[t])

                def onward(j):
                    idx = at.me + spread(j, deltas[:t])
                    place = place_of(a, idx, cut)
                    put(own_src(a, cut) if isinstance(j, int) and j == 0 else place, place, send_sem.at[c, t], recv_sem.at[c, t], partner)

                onward(0)
                repeat((1 << t) - 1, lambda j: onward(j + 1))
            repeat(1 << (t - 1), pass_on)
        else:
            partner = at.partner(names[0])
            place = place_of(a, at.me, cut)
            put(own_src(a, cut), place, send_sem.at[c, 0], recv_sem.at[c, 0], partner)
            put(own_src(a, cut), place, side_send.at[c, 0], side_recv.at[c, 0], sibling)
            pltpu.make_async_copy(own_src(a, cut), place, own_sem.at[c]).start()

    slot = lax.div(at.quarter, 2) * at.parts + lax.rem(at.seq, at.parts)
    seg_copy = pltpu.make_async_remote_copy(
        src_ref=seg_ref,
        dst_ref=seg_out,
        send_sem=seg_sem.at[0],
        recv_sem=seg_sem.at[1],
        device_id=sibling,
        device_id_type=MESH,
    )

    def token_copies(which, src, dst, i):
        to_seq = at.core * at.seqs + i
        mine = (to_seq == at.seq) & (at.quarter_core == at.core)
        remote = pltpu.make_async_remote_copy(
            src_ref=src.at[i],
            dst_ref=dst.at[slot],
            send_sem=tok_send.at[which, i],
            recv_sem=tok_recv.at[which, at.seq],
            device_id=(at.pair * 2 + at.quarter_core, to_seq),
            device_id_type=MESH,
        )
        local = pltpu.make_async_copy(src.at[i], dst.at[slot], tok_own.at[which])
        return mine, remote, local

    def tokens_start(which, src, dst):
        for i in range(at.seqs):
            mine, remote, local = token_copies(which, src, dst, i)
            pl.when(jnp.logical_not(mine))(remote.start)
            pl.when(mine)(local.start)

    def tokens_wait(which, src, dst):
        for i in range(at.seqs):
            mine, remote, local = token_copies(which, src, dst, i)
            pl.when(jnp.logical_not(mine))(remote.wait_send)
            pl.when(mine)(local.wait)
        for z in range(seq_n):
            comes = (at.core_of(z // at.parts) == at.core) & jnp.logical_not(
                (at.seq == z) & (at.source_core == at.core)
            )
            arrival = pltpu.make_async_remote_copy(
                src_ref=src.at[0],
                dst_ref=dst.at[0],
                send_sem=tok_send.at[which, 0],
                recv_sem=tok_recv.at[which, z],
                device_id=sibling,
                device_id_type=MESH,
            )
            pl.when(comes)(arrival.wait_recv)

    seg_copy.start()
    waves = stages + 1 + max(c[5] for c in GATHER)
    for wave in range(waves):
        for c in range(len(GATHER)):
            t = wave - GATHER[c][5]
            if 0 <= t <= stages:
                stage(c, t)
        if wave == X_WAVE:
            tokens_start(0, x_ref, x_out)
        if wave == COT_WAVE:
            tokens_start(1, cot_ref, cot_out)
    for c in range(len(GATHER)):
        a, *cut, order, _ = GATHER[c]
        names = orders[order]
        for t in range(stages):
            group(a, cut, 1 << t, send_sem.at[c, t], recv_sem.at[c, t], at.partner(names[t])).wait_send()
        for t in range(stages + 1):
            one = group(a, cut, 1 << max(t - 1, 0), side_send.at[c, t], side_recv.at[c, t], sibling)
            one.wait_send()
            one.wait_recv()
        pltpu.make_async_copy(own_src(a, cut), place_of(a, at.me, cut), own_sem.at[c]).wait()
    tokens_wait(0, x_ref, x_out)
    tokens_wait(1, cot_ref, cot_out)
    seg_copy.wait()


def gather_all(mesh_shape, x, cot, seg, shards, major=()):
    dp_n, seq_n = mesh_shape
    seqs, blk, width = x.shape
    n_dev = dp_n * seq_n
    stages = log2(n_dev) - 1
    chunks = len(GATHER)
    vmem = pl.BlockSpec(memory_space=pltpu.VMEM)
    hbm = pl.BlockSpec(memory_space=ANY)
    token_shape = jax.ShapeDtypeStruct((seq_n // 2, blk, width), x.dtype)
    DMA = pltpu.SemaphoreType.DMA
    return pl.pallas_call(
        functools.partial(gather_kernel, dp_n, seq_n, major),
        out_shape=[token_shape, token_shape, jax.ShapeDtypeStruct(seg.shape, seg.dtype)]
        + [
            jax.ShapeDtypeStruct((PIECES * n_dev,) + piece_shape((1,) + s.shape, (2 if i == 2 else 1, PIECES, 0)), s.dtype)
            if i in major
            else jax.ShapeDtypeStruct((n_dev,) + s.shape, s.dtype)
            for i, s in enumerate(shards)
        ],
        in_specs=[vmem] * (3 + len(shards)),
        out_specs=[hbm] * 2 + [vmem] + [hbm] * len(shards),
        scratch_shapes=[
            DMA((chunks, stages)),
            DMA((chunks, stages)),
            DMA((chunks, stages + 1)),
            DMA((chunks, stages + 1)),
            DMA((chunks,)),
            DMA((2, seqs)),
            DMA((2, seq_n)),
            DMA((2,)),
            DMA((2,)),
        ],
        compiler_params=pltpu.CompilerParams(collective_id=0, has_side_effects=True),
        name="gather_all",
    )(x, cot, seg, *[s[None] for s in shards])


REDUCE = (
    (2, 2, 4, 0, "zxy", 0),
    (3, 1, 4, 0, "zyx", 0),
    (2, 2, 4, 1, "zxy", 1),
    (3, 1, 4, 1, "zyx", 1),
    (2, 2, 4, 2, "zxy", 2),
    (3, 1, 4, 2, "zyx", 2),
    (2, 2, 4, 3, "zxy", 3),
    (3, 1, 4, 3, "zyx", 3),
    (0, 2, 3, 2, "zxy", 4),
    (1, 2, 1, 0, "zyx", 4),
    (0, 2, 3, 0, "zxy", 5),
    (0, 2, 3, 1, "zyx", 5),
    (4, 2, 1, 0, "zyx", 5),
)


def reduce_kernel(dp_n, seq_n, *refs):
    n_arr, chunks = 5, len(REDUCE)
    tok_in, parts = refs[:2], refs[2 : 2 + n_arr]
    refs = refs[2 + n_arr :]
    tok_out, totals = refs[:2], refs[2 : 2 + n_arr]
    refs = refs[2 + n_arr :]
    at = Place(dp_n, seq_n)
    orders = orders_of(dp_n, seq_n)
    stages = len(orders["zxy"])
    buffers = [refs[c * (stages + 2) : (c + 1) * (stages + 2)] for c in range(chunks)]
    send_sem, recv_sem, own_sem, tok_send, tok_recv, tok_own = refs[chunks * (stages + 2) :]
    at.enter()
    sibling = at.sibling()

    def names_of(c):
        return orders[REDUCE[c][4]][::-1]

    def index_of(c, j, core):
        total = core * seq_n
        for s, (axis, k) in enumerate(names_of(c)):
            value = lax.rem(lax.div(j, 1 << (stages - 1 - s)), 2) if not isinstance(j, int) else (j >> (stages - 1 - s)) & 1
            total = total + value * ((1 << k) * (1 if axis == "seq" else seq_n))
        return total

    def hop(c, t, src):
        device = sibling if t == 0 else at.partner(names_of(c)[t - 1])
        return pltpu.make_async_remote_copy(
            src_ref=src,
            dst_ref=buffers[c][t + 1],
            send_sem=send_sem.at[c, t],
            recv_sem=recv_sem.at[c, t],
            device_id=device,
            device_id_type=MESH,
        )

    def first(c):
        a, *cut, _, _ = REDUCE[c]
        own, got = buffers[c][:2]

        def one(j):
            src = piece_of(parts[a], index_of(c, j, 1 - at.core), cut)
            pltpu.make_async_remote_copy(
                src_ref=src,
                dst_ref=got.at[j],
                send_sem=send_sem.at[c, 0],
                recv_sem=recv_sem.at[c, 0],
                device_id=sibling,
                device_id_type=MESH,
            ).start()
            pltpu.make_async_copy(
                piece_of(parts[a], index_of(c, j, at.core), cut), own.at[j], own_sem.at[c]
            ).start()

        repeat(1 << stages, one)

    def own_wait(c):
        a, *cut, _, _ = REDUCE[c]
        whole = piece_of(parts[a], pl.ds(0, 1 << stages), cut)
        pltpu.make_async_copy(whole, buffers[c][0], own_sem.at[c]).wait()

    def add(c, t, lo, count, kept):
        old, got = buffers[c][t], buffers[c][t + 1]

        def one(j, carry):
            total = old[kept + lo + j].astype(jnp.float32) + got[lo + j].astype(jnp.float32)
            got[lo + j] = total.astype(got.dtype)
            return carry

        lax.fori_loop(0, count, one, 0)

    def stage(c, t):
        if t == 0:
            first(c)
            return
        names = names_of(c)
        hop(c, t - 1, buffers[c][t]).wait_recv()
        if t == 1:
            own_wait(c)
            kept = 0
        else:
            kept = at.bit(names[t - 2]) * (1 << (stages - t + 1))
        if t <= stages:
            half = 1 << (stages - t)
            mine = at.bit(names[t - 1])
            add(c, t - 1, (1 - mine) * half, half, kept)
            hop(c, t, buffers[c][t].at[pl.ds((1 - mine) * half, half)]).start()
            add(c, t - 1, mine * half, half, kept)
        else:
            a, *cut, _, _ = REDUCE[c]
            old, got = buffers[c][t - 1], buffers[c][t]
            total = old[kept].astype(jnp.float32) + got[0].astype(jnp.float32)
            piece_of(totals[a], 0, cut)[...] = total

    def token_copies(which, j):
        slot, rest = j // at.parts, j % at.parts
        quarter = at.core + slot * (3 - 2 * at.core)
        to_seq = quarter * at.parts + rest
        mine = (to_seq == at.seq) & (at.source_core == at.core)
        src = tok_in[which].at[j]
        place = at.seq - at.source_core * at.seqs
        remote = pltpu.make_async_remote_copy(
            src_ref=src,
            dst_ref=tok_out[which].at[place],
            send_sem=tok_send.at[which, j],
            recv_sem=tok_recv.at[which, place],
            device_id=(at.pair * 2 + at.source_core, to_seq),
            device_id_type=MESH,
        )
        local = pltpu.make_async_copy(src, tok_out[which].at[place], tok_own.at[which])
        return mine, remote, local

    for which in range(2):
        for j in range(seq_n // 2):
            mine, remote, local = token_copies(which, j)
            pl.when(jnp.logical_not(mine))(remote.start)
            pl.when(mine)(local.start)
    for wave in range(stages + 2 + max(c[5] for c in REDUCE)):
        for c in range(chunks):
            t = wave - REDUCE[c][5]
            if 0 <= t <= stages + 1:
                stage(c, t)
    for c in range(chunks):
        for t in range(stages + 1):
            hop(c, t, buffers[c][t + 1]).wait_send()
    for which in range(2):
        for j in range(seq_n // 2):
            mine, remote, local = token_copies(which, j)
            pl.when(jnp.logical_not(mine))(remote.wait_send)
            pl.when(mine)(local.wait)
        for i in range(at.seqs):
            comes = jnp.logical_not((at.core * at.seqs + i == at.seq) & (at.quarter_core == at.core))
            arrival = pltpu.make_async_remote_copy(
                src_ref=tok_in[which].at[0],
                dst_ref=tok_out[which].at[i],
                send_sem=tok_send.at[which, 0],
                recv_sem=tok_recv.at[which, i],
                device_id=sibling,
                device_id_type=MESH,
            )
            pl.when(comes)(arrival.wait_recv)


def reduce_all(mesh_shape, tokens, parts):
    dp_n, seq_n = mesh_shape
    stages = log2(dp_n * seq_n) - 1
    _, blk, width = tokens[0].shape
    vmem = pl.BlockSpec(memory_space=pltpu.VMEM)
    hbm = pl.BlockSpec(memory_space=ANY)
    DMA = pltpu.SemaphoreType.DMA
    chunks = len(REDUCE)
    scratch = []
    for a, *cut, _, _ in REDUCE:
        shape = piece_shape(parts[a].shape, cut)
        for count in (1 << stages,) + tuple(1 << (stages - t) for t in range(stages + 1)):
            scratch.append(pltpu.VMEM((count,) + shape, parts[a].dtype))
    out = pl.pallas_call(
        functools.partial(reduce_kernel, dp_n, seq_n),
        out_shape=[jax.ShapeDtypeStruct((seq_n // 2, blk, width), t.dtype) for t in tokens]
        + [jax.ShapeDtypeStruct((1,) + p.shape[1:], jnp.float32) for p in parts],
        in_specs=[vmem] * 2 + [hbm] * len(parts),
        out_specs=[hbm] * 2 + [vmem] * len(parts),
        scratch_shapes=scratch
        + [
            DMA((chunks, stages + 1)),
            DMA((chunks, stages + 1)),
            DMA((chunks,)),
            DMA((2, seq_n // 2)),
            DMA((2, seq_n // 2)),
            DMA((2,)),
        ],
        compiler_params=pltpu.CompilerParams(
            collective_id=1, has_side_effects=True, vmem_limit_bytes=60 * 1024 * 1024
        ),
        name="reduce_all",
    )(*tokens, *parts)
    return out[:2], [g[0] for g in out[2:]]


def swap_kernel(dp_n, seq_n, cols, src_ref, out_ref, send_sem, recv_sem):
    at = Place(dp_n, seq_n)
    sibling = at.sibling()
    barrier = pltpu.get_barrier_semaphore()
    pl.semaphore_signal(barrier, inc=1, device_id=sibling, device_id_type=MESH)
    pl.semaphore_wait(barrier, 1)
    first, width = cols
    copy = pltpu.make_async_remote_copy(
        src_ref=src_ref.at[:, pl.ds(first, width)],
        dst_ref=out_ref,
        send_sem=send_sem,
        recv_sem=recv_sem,
        device_id=sibling,
        device_id_type=MESH,
    )
    copy.start()
    copy.wait()


def swap(mesh_shape, src, cols, which):
    hbm = pl.BlockSpec(memory_space=ANY)
    return pl.pallas_call(
        functools.partial(swap_kernel, *mesh_shape, cols),
        out_shape=jax.ShapeDtypeStruct((src.shape[0], cols[1]), src.dtype),
        in_specs=[hbm],
        out_specs=hbm,
        scratch_shapes=[pltpu.SemaphoreType.DMA, pltpu.SemaphoreType.DMA],
        compiler_params=pltpu.CompilerParams(collective_id=which, has_side_effects=True),
        name="swap",
    )(src)


NT = (((1,), (1,)), ((), ()))
NN = (((1,), (0,)), ((), ()))
TN = (((0,), (0,)), ((), ()))


def dot(a, b, dims):
    return lax.dot_general(a, b, dims, preferred_element_type=jnp.float32)


def woven(own, other):
    half = own.shape[0] // 2
    return jnp.concatenate([own[:half], other[:half], own[half:], other[half:]], 0)


def head_masks():
    lane = lax.broadcasted_iota(jnp.int32, (1, 2 * HEAD_DIM), 1)
    first = (lane < HEAD_DIM).astype(jnp.bfloat16)
    return first, 1 - first


def attend_kernel(q_ref, ko_ref, vo_ref, ks_ref, vs_ref, bias_ref, o_ref, lse_ref, sees=None):
    rows = q_ref.shape[0]
    sees = sees or (rows, 2 * rows)
    half = rows // 2
    keys = woven(ko_ref[...], ks_ref[...])
    values = woven(vo_ref[...], vs_ref[...])
    masks = head_masks()
    scale = jnp.bfloat16(HEAD_DIM ** (-0.5))
    for slot in range(2):
        seen = sees[slot]
        here = slice(slot * half, (slot + 1) * half)
        q = q_ref[here] * scale
        outs = []
        for head in range(2):
            s = dot(keys[:seen], q * masks[head], NT) + bias_ref[:seen, here]
            top = jnp.max(s, 0, keepdims=True)
            e = jnp.exp(s - top)
            total = jnp.sum(e, 0, keepdims=True)
            p = (e * (1.0 / total)).astype(jnp.bfloat16)
            mixed = dot(values[:seen], p, TN)
            outs.append(mixed[head * HEAD_DIM : (head + 1) * HEAD_DIM])
            lse_ref[0, head : head + 1, here] = top + jnp.log(total)
        o_ref[here] = jnp.concatenate(outs, 0).T.astype(jnp.bfloat16)


def attend(qkv, kv_other, bias):
    rows, wide = qkv.shape
    width = wide // 3
    pairs = width // (2 * HEAD_DIM)
    col = lambda first: pl.BlockSpec((rows, 2 * HEAD_DIM), lambda h, first=first: (0, first * pairs + h))
    return pl.pallas_call(
        attend_kernel,
        grid=(pairs,),
        out_shape=[
            jax.ShapeDtypeStruct((rows, width), jnp.bfloat16),
            jax.ShapeDtypeStruct((pairs, 2, rows), jnp.float32),
        ],
        in_specs=[col(0), col(1), col(2), col(0), col(1), pl.BlockSpec(bias.shape, lambda h: (0, 0))],
        out_specs=[col(0), pl.BlockSpec((1, 2, rows), lambda h: (h, 0, 0))],
        name="attend",
    )(qkv, qkv, qkv, kv_other, kv_other, bias)


def attend_back_kernel(
    q_ref, ko_ref, vo_ref, ks_ref, vs_ref, go_ref, bias_ref, lse_ref, gq_ref, gko_ref, gvo_ref, gks_ref, gvs_ref, gk_sum, gv_sum, sees=None
):
    rows = q_ref.shape[0]
    sees = sees or (rows, 2 * rows)
    half = rows // 2
    keys = woven(ko_ref[...], ks_ref[...])
    values = woven(vo_ref[...], vs_ref[...])
    masks = head_masks()
    scale = HEAD_DIM ** (-0.5)
    for slot in (1, 0):
        seen = sees[slot]
        here = slice(slot * half, (slot + 1) * half)
        q = q_ref[here] * jnp.bfloat16(scale)
        go = go_ref[here]
        gqs, gk, gv = [], None, None
        for head in range(2):
            q_h, go_h = q * masks[head], go * masks[head]
            s = dot(keys[:seen], q_h, NT) + bias_ref[:seen, here]
            p = jnp.exp(s - lse_ref[0, head : head + 1, here])
            gp = dot(values[:seen], go_h, NT)
            row_dot = jnp.sum(p * gp, 0, keepdims=True)
            gs = (p * (gp - row_dot)).astype(jnp.bfloat16)
            gv_h = dot(p.astype(jnp.bfloat16), go_h, NN)
            gk_h = dot(gs, q_h, NN)
            gk = gk_h if gk is None else gk + gk_h
            gv = gv_h if gv is None else gv + gv_h
            gq = dot(keys[:seen], gs, TN)
            gqs.append(gq[head * HEAD_DIM : (head + 1) * HEAD_DIM])
        gq_ref[here] = (jnp.concatenate(gqs, 0).T * scale).astype(gq_ref.dtype)
        if slot == 1:
            gk_sum[:seen] = gk
            gv_sum[:seen] = gv
            if seen < 2 * rows:
                gk_sum[seen:] = jnp.zeros((2 * rows - seen, gk.shape[1]), jnp.float32)
                gv_sum[seen:] = jnp.zeros((2 * rows - seen, gv.shape[1]), jnp.float32)
        else:
            gk_sum[:seen] += gk
            gv_sum[:seen] += gv
    for total, own, other in ((gk_sum, gko_ref, gks_ref), (gv_sum, gvo_ref, gvs_ref)):
        for slot in range(2):
            here = slice(slot * half, (slot + 1) * half)
            own[here] = total[2 * slot * half : (2 * slot + 1) * half].astype(own.dtype)
            other[here] = total[(2 * slot + 1) * half : (2 * slot + 2) * half].astype(other.dtype)


def attend_back(qkv, kv_other, go, bias, lse):
    rows, wide = qkv.shape
    width = wide // 3
    pairs = width // (2 * HEAD_DIM)
    lanes = 2 * HEAD_DIM
    col = lambda first: pl.BlockSpec((rows, lanes), lambda h, first=first: (0, first * pairs + h))
    out = jax.ShapeDtypeStruct((rows, width), jnp.bfloat16)
    return pl.pallas_call(
        attend_back_kernel,
        grid=(pairs,),
        out_shape=[out] * 5,
        in_specs=[
            col(0),
            col(1),
            col(2),
            col(0),
            col(1),
            col(0),
            pl.BlockSpec(bias.shape, lambda h: (0, 0)),
            pl.BlockSpec((1, 2, rows), lambda h: (h, 0, 0)),
        ],
        out_specs=[col(0)] * 5,
        scratch_shapes=[pltpu.VMEM((2 * rows, lanes), jnp.float32)] * 2,
        name="attend_back",
    )(qkv, qkv, qkv, kv_other, kv_other, go, bias, lse)


def rows_at(start, size):
    return pl.ds(pl.multiple_of(start, 16), size)


class Reduction:
    def __init__(self, at, order, refs, sems, own):
        self.at, self.own = at, own
        self.blocks, self.sends, self.gets, self.keeps = refs
        self.send_sem, self.recv_sem = sems
        self.order = order
        self.turns = len(order)
        self.last = self.turns + len(self.sends)
        self.names = order + [("seq", k) for k in range(len(self.sends))]
        self.dp_rows = self.blocks[0].shape[0] // (at.dp_n // 2)
        self.shard = self.dp_rows // at.seq_n

    def dp_of(self, j, core):
        dp = core
        for i, (_, k) in enumerate(reversed(self.order)):
            bit = (j >> i) & 1 if isinstance(j, int) else lax.rem(lax.div(j, 1 << i), 2)
            dp = dp + bit * (1 << k)
        return dp

    def landing(self, t):
        return self.blocks[t] if t <= self.turns else self.gets[t - self.turns - 1]

    def copy(self, t, src=None, dst=None):
        at = self.at
        return pltpu.make_async_remote_copy(
            src_ref=self.landing(t) if src is None else src,
            dst_ref=self.landing(t) if dst is None else dst,
            send_sem=self.send_sem.at[t],
            recv_sem=self.recv_sem.at[t],
            device_id=at.sibling() if t == 0 else at.partner(self.names[t - 1]),
            device_id_type=MESH,
        )

    def start(self):
        for j in range(self.at.dp_n // 2):
            dst = self.blocks[0].at[pl.ds(j * self.dp_rows, self.dp_rows)]
            self.copy(0, self.own(self.dp_of(j, 1 - self.at.core)), dst).start()

    def fold(self, t, lo, size):
        got = self.blocks[t - 1]
        step = self.dp_rows // 2

        def one(i, carry):
            row = lo + i * step
            here = rows_at(row, step)
            if t == 1:
                half = lax.rem(i, 2) * step
                old = self.own(self.dp_of(lax.div(row, self.dp_rows), self.at.core))[rows_at(half, step)]
            else:
                kept = self.at.bit(self.names[t - 2]) * got.shape[0]
                old = self.blocks[t - 2][rows_at(kept + row, step)]
            got[here] = (old.astype(jnp.float32) + got[here].astype(jnp.float32)).astype(got.dtype)
            return carry

        lax.fori_loop(0, size // step, one, 0)

    def shards_of(self, t):
        got = self.landing(t - 1)
        if t == self.turns + 1:
            kept = self.at.bit(self.names[t - 2]) * self.dp_rows
            total = self.blocks[t - 2][rows_at(kept, self.dp_rows)].astype(jnp.float32) + got[...].astype(jnp.float32)
            return [total[i * self.shard : (i + 1) * self.shard] for i in range(self.at.seq_n)]
        keep = self.keeps[t - self.turns - 2]
        return [keep[i] + got[i].astype(jnp.float32) for i in range(keep.shape[0])]

    def stage(self, t):
        self.copy(t - 1).wait_recv()
        mine = self.at.bit(self.names[t - 1])
        if t <= self.turns:
            got = self.blocks[t - 1]
            half = got.shape[0] // 2
            self.fold(t, (1 - mine) * half, half)
            self.copy(t, got.at[rows_at((1 - mine) * half, half)]).start()
            self.fold(t, mine * half, half)
            return
        held = self.shards_of(t)
        m = t - self.turns - 1
        send, keep = self.sends[m], self.keeps[m]
        for i in range(len(held) // 2):
            send[i] = jnp.where(mine == 0, held[2 * i + 1], held[2 * i]).astype(send.dtype)
        self.copy(t, send).start()
        for i in range(len(held) // 2):
            keep[i] = jnp.where(mine == 0, held[2 * i], held[2 * i + 1])

    def finish(self):
        self.copy(self.last).wait_recv()
        return self.shards_of(self.last + 1)[0]


GRADS = 2 * PIECES + 4

AFTER = {
    "start": (
        "gs0", "gq0", "gk0", "go0", "gv0",
    ),
    "B0": (
        "gs1", "gq1",
    ),
    "B1": (
        "gk1", "gf00", "gp00", "gs2", "go1", "gq2", "gv1", "gs3", "gk2", "gf01", "gf10", "gp10", "gp01", "go2", "gq3",
        "gv2", "X", "gs4", "gk3", "gf02", "gf20", "gp20", "gf11", "go3", "gp11", "gp02", "gv3", "gq4", "gk4", "gp03",
        "gf03", "gv4",
    ),
    "L1": (
        "go4", "gf12", "gf21",
    ),
    "FK": (
        "gp12", "gp21", "gf30", "gp30",
    ),
    "FV": (
        "C", "gf04", "gf22",
    ),
    "FQ": (
        "gp04", "gp13", "gp22", "gf31", "gf13", "gp31",
    ),
    "E0": (
        "gf23",
    ),
    "E1": (
        "gp23",
    ),
    "E2": (
        "gp14",
    ),
    "E3": (
        "gf14",
    ),
    "E4": (
        "gf32", "gp32",
    ),
    "E5": (
        "gf24", "gp24",
    ),
    "O": (),
    "L2": (
        "gf33", "gp33",
    ),
    "M0": (),
    "D0": (),
    "M1": (
        "rf01", "gf34", "gp34",
    ),
    "D1": (
        "rp01",
    ),
    "M2": (
        "rf11",
    ),
    "D2": (
        "rp11",
    ),
    "M3": (
        "rf02", "rp02", "rf21", "rp21",
    ),
    "D3": (),
    "T": (
        "rf12",
    ),
    "A": (
        "rp03", "rp12", "rf31", "rp31",
    ),
    "B": (
        "rf03",
    ),
    "H0": (
        "ro1",
    ),
    "H1": (
        "rf22",
    ),
    "H2": (
        "rp13", "rp22",
    ),
    "H3": (
        "rp04", "rf13",
    ),
    "H4": (
        "rf04", "rp14", "rf32", "rp32",
    ),
    "H5": (
        "rp05", "rf14", "rp23",
    ),
    "Q": (
        "rf05", "rp15", "rp33", "ro2",
    ),
    "K": (
        "rf15", "rp24", "rp34", "rf23", "rq1",
    ),
    "V": (
        "ro3", "rf33", "rk1",
    ),
    "G": (
        "rp25", "rp35", "rf24", "ro4", "rv1",
    ),
    "N": (
        "rf34", "rq2", "rs1", "rf25", "rk2", "ro5", "rq3", "rv2", "rs2", "rk3", "rs3", "rv3", "rq4", "rk4", "rs4",
        "rv4", "rf35", "U", "rq5", "rk5", "rs5", "rv5",
    ),
}
ORDER_ONE = "kosp"


def whole_kernel(dp_n, seq_n, *refs):
    x_ref, cot_ref, start_ref = refs[:3]
    w_qkv, w_out, w_fc, w_proj, w_vec = refs[3:8]
    result_out, input_out, fc_out, proj_out, qkv_out, wout_out, small_out = refs[8:15]
    qkv_hbm, out_hbm, fc_hbm, proj_hbm, vec_hbm = refs[15:20]
    (wbuf, gbuf, act, gm, a3, gh, resacc, gact, gqkv, away, back, tok, vecs, gk_sum, gv_sum) = refs[20:35]
    (x_in, cot, start_other, resid, mixed, qkv, kv_other, lse, bias, vec_low, vec, fc_own, fc_sum) = refs[35:48]
    refs = refs[48:]
    at = Place(dp_n, seq_n)
    stages = log2(dp_n * seq_n)
    turns, folds = log2(dp_n) - 1, log2(seq_n)
    sets = [turns + 1, folds, folds, folds]
    count = sum(sets)

    def grouped(some):
        groups, first = [], 0
        for size in sets:
            groups.append(some[first : first + size])
            first += size
        return groups

    big, small_bufs = refs[:count], refs[count : 2 * count]
    (small_src, big_send, big_recv, small_send, small_recv, w_sem, swap_sem, tok_send, tok_recv, tok_own) = refs[
        2 * count : 2 * count + 10
    ]
    (ask_send, ask_recv, side_send, side_recv, own_sem, in_send, in_recv, in_own, start_sem, kv_sem, vec_sem) = refs[
        2 * count + 10 :
    ]
    rows, width = resid.shape
    half = rows // 2
    shard = fc_out.shape[0]
    n_dev = dp_n * seq_n
    across = [("dp", k) for k in range(1, log2(dp_n))]
    at.enter()
    sibling = at.sibling()

    def own_rows(src):
        return lambda dp: src.at[pl.ds(pl.multiple_of(dp * (seq_n * shard), 16), seq_n * shard)]

    def reduction(kind, c):
        order = across[::-1] if kind == 0 else across
        where = lax.rem(c, gbuf.shape[0]) if not isinstance(c, int) else c % gbuf.shape[0]
        return Reduction(
            at,
            order,
            grouped([b.at[c] for b in big]),
            (big_send.at[c], big_recv.at[c]),
            own_rows(gbuf.at[where]),
        )

    def vector_reduction():
        return Reduction(
            at,
            across,
            grouped(small_bufs),
            (small_send, small_recv),
            own_rows(small_src),
        )

    def weight_copy(slot, src):
        return pltpu.make_async_copy(src, wbuf.at[slot], w_sem.at[slot])

    def by_core(kernel, *some):
        for core, sees in ((0, (half, 4 * half)), (1, (2 * half, 3 * half))):
            pl.when(at.core == core)(functools.partial(kernel, *some, sees=sees))

    step = 64

    def by_rows(body, sums=0):
        zeros = [jnp.zeros((8, width), jnp.float32)] * sums
        totals = lax.fori_loop(
            0, rows // step, lambda i, t: body(pl.ds(pl.multiple_of(i * step, step), step), t), zeros
        )
        return [jnp.sum(t, 0, keepdims=True) for t in totals]

    def eights(value):
        return jnp.sum(value.reshape(step // 8, 8, width), 0)

    def token_block(ref, here):
        blk = ref.shape[1]
        start = here.start
        return ref[lax.div(start, blk), pl.ds(pl.multiple_of(lax.rem(start, blk), step), step)].astype(jnp.float32)


    def array(name):
        if name in "qkv":
            part = "qkv".index(name)
            cols = pl.ds(part * width, width)
            return part, qkv_hbm.at[:, cols], w_qkv.at[:, cols]
        if name == "o":
            return 3, out_hbm, w_out
        if name == "s":
            return 4, vec_hbm, w_vec
        j = int(name[1])
        if name[0] == "f":
            return 5 + j, fc_hbm.at[j], fc_own.at[:, pl.ds(j * width, width)]
        return 5 + PIECES + j, proj_hbm.at[j], w_proj.at[pl.ds(j * shard, shard)]

    along = [("seq", k) for k in reversed(range(folds))]

    def shard_rows(full, d):
        return full.at[pl.ds(pl.multiple_of(d * shard, 8), shard)]

    def put(src, dst, s_sem, r_sem, device):
        return pltpu.make_async_remote_copy(
            src_ref=src, dst_ref=dst, send_sem=s_sem, recv_sem=r_sem, device_id=device, device_id_type=MESH
        )

    def gather_stage(name, t):
        n, full, own = array(name)
        names = along + (across[::-1] if name[0] in ORDER_ONE else across)
        deltas = [at.delta(x) for x in names]
        if t == 0:
            place = shard_rows(full, at.me)
            put(own, place, ask_send.at[n, 0], ask_recv.at[n, 0], at.partner(names[0])).start()
            put(own, place, side_send.at[n, 0], side_recv.at[n, 0], sibling).start()
            pltpu.make_async_copy(own, place, own_sem.at[n]).start()
            return
        some = full.at[pl.ds(0, shard << (t - 1))]
        put(some, some, ask_send.at[n, t - 1], ask_recv.at[n, t - 1], sibling).wait_recv()
        if t == folds:
            pltpu.make_async_copy(own, shard_rows(full, at.me), own_sem.at[n]).wait()

        def held(t, shift):
            if t < folds:
                return [shard_rows(full, at.me + shift + spread(j, deltas[:t])) for j in range(1 << t)]
            size = seq_n * shard
            return [
                full.at[pl.ds(pl.multiple_of((at.dp * seq_n + shift + spread(j, deltas[folds:t])) * shard, 8), size)]
                for j in range(1 << (t - folds))
            ]

        if t < len(names):
            for j, place in enumerate(held(t, 0)):
                src = own if j == 0 and t < folds else place
                put(src, place, ask_send.at[n, t], ask_recv.at[n, t], at.partner(names[t])).start()
        for place in held(t - 1, deltas[t - 1]):
            put(place, place, side_send.at[n, t], side_recv.at[n, t], sibling).start()

    def gathered(name):
        n, full, own = array(name)
        for t in range(stages):
            some = full.at[pl.ds(0, shard << max(t - 1, 0))]
            put(some, some, side_send.at[n, t], side_recv.at[n, t], sibling).wait_recv()

    def gather_drain(name):
        n, full, own = array(name)
        for t in range(stages - 1):
            some = full.at[pl.ds(0, shard << t)]
            put(some, some, ask_send.at[n, t], ask_recv.at[n, t], sibling).wait_send()
        for t in range(stages):
            some = full.at[pl.ds(0, shard << max(t - 1, 0))]
            put(some, some, side_send.at[n, t], side_recv.at[n, t], sibling).wait_send()

    slot_here = lax.div(at.quarter, 2) * at.parts + lax.rem(at.seq, at.parts)

    def incoming(which, i):
        src, dst = ((x_ref, x_in), (cot_ref, cot))[which]
        to_seq = at.core * at.seqs + i
        mine = (to_seq == at.seq) & (at.quarter_core == at.core)
        remote = put(
            src.at[i],
            dst.at[slot_here],
            in_send.at[which, i],
            in_recv.at[which, at.seq],
            (at.pair * 2 + at.quarter_core, to_seq),
        )
        local = pltpu.make_async_copy(src.at[i], dst.at[slot_here], in_own.at[which])
        return mine, remote, local

    def incoming_start(which):
        for i in range(at.seqs):
            mine, remote, local = incoming(which, i)
            pl.when(jnp.logical_not(mine))(remote.start)
            pl.when(mine)(local.start)

    def incoming_wait(which):
        src, dst = ((x_ref, x_in), (cot_ref, cot))[which]
        for i in range(at.seqs):
            mine, remote, local = incoming(which, i)
            pl.when(jnp.logical_not(mine))(remote.wait_send)
            pl.when(mine)(local.wait)
        for z in range(seq_n):
            comes = (at.core_of(z // at.parts) == at.core) & jnp.logical_not(
                (at.seq == z) & (at.source_core == at.core)
            )
            arrival = put(src.at[0], dst.at[0], in_send.at[which, 0], in_recv.at[which, z], sibling)
            pl.when(comes)(arrival.wait_recv)

    def load_piece(j):
        slot = 2 * lax.rem(j, 2)
        for k in range(PIECES):

            def ready(k=k):
                gathered(f"f{k}")
                gathered(f"p{k}")

            pl.when(j == k)(ready)
        weight_copy(slot, fc_hbm.at[j]).start()
        weight_copy(slot + 1, proj_hbm.at[j]).start()

    def after(slot):
        for op in AFTER[slot]:
            if op == "U":
                unsort_units()
                continue
            if op in "XC":
                incoming_start("XC".index(op))
                continue
            if op[0] == "g":
                gather_stage(op[1:-1], int(op[-1]))
                continue
            name, kind, t = op[1:], op[1], int(op[-1])
            if kind == "s":
                red = vector_reduction()
            else:
                c = 2 * int(name[1]) + (kind == "p") if kind in "fp" else 2 * PIECES + "oqkv".index(kind)
                red = reduction(int(kind in ORDER_ONE), int(c))
            if t < stages:
                red.stage(t)
                continue
            total = red.finish()
            if kind == "f":
                fc_sum[:, int(name[1]) * width : (int(name[1]) + 1) * width] = total
            elif kind == "p":
                proj_out[int(name[1]) * shard : (int(name[1]) + 1) * shard] = total
            elif kind == "o":
                wout_out[...] = total
            elif kind == "s":
                square = jnp.concatenate([total, jnp.zeros((128 - shard, 128), jnp.float32)], 0).T
                square = jnp.concatenate([square[:10], jnp.where(at.me < n_dev // 2, square[10:12], square[12:14]), square[12:16]], 0)
                small_out[...] = square
            else:
                part = "qkv".index(kind)
                qkv_out[:, part * width : (part + 1) * width] = total

    def after_each(prefix, i, count):
        for k in range(count):
            pl.when(i == k)(functools.partial(after, f"{prefix}{k}"))

    period = PIECES * shard
    group = period * 128 // math.gcd(period, 128)
    lane = lax.broadcasted_iota(jnp.int32, (1, PIECES * 128), 1)
    entry = lax.rem(lane, 128)
    source = lax.div(entry, shard) * period + lax.div(lane, 128) * shard + lax.rem(entry, shard)
    per_piece = group // PIECES
    source = jnp.where(entry < per_piece, source, -1)
    sorter = (lax.broadcasted_iota(jnp.int32, (group, 1), 0) == source).astype(jnp.float32)
    lane_one = lax.broadcasted_iota(jnp.int32, (1, 128), 1)
    groups = PIECES * width // group

    def sort_units():
        pieces = [[jnp.zeros((shard, 128), jnp.float32) for _ in range(width // 128)] for _ in range(PIECES)]
        for g in range(groups):
            moved = dot(w_fc[:, g * group : (g + 1) * group], sorter.astype(jnp.bfloat16), NN)
            block, shift = divmod(g * per_piece, 128)
            for j in range(PIECES):
                turned = moved[:, j * 128 : (j + 1) * 128]
                if shift:
                    turned = pltpu.roll(turned, shift, 1)
                    if shift + per_piece > 128:
                        pieces[j][block + 1] = pieces[j][block + 1] + jnp.where(lane_one < shift, turned, 0.0)
                    turned = jnp.where(lane_one >= shift, turned, 0.0)
                pieces[j][block] = pieces[j][block] + turned
        for j in range(PIECES):
            fc_own[:, j * width : (j + 1) * width] = jnp.concatenate(pieces[j], 1).astype(jnp.bfloat16)

    def unsort_units():
        stacked = []
        for g in range(groups):
            block, shift = divmod(g * per_piece, 128)
            parts = []
            for j in range(PIECES):
                first = j * width + block * 128
                part = fc_sum[:, first : first + 128]
                if shift:
                    part = pltpu.roll(part, 128 - shift, 1)
                    if shift + per_piece > 128:
                        beyond = pltpu.roll(fc_sum[:, first + 128 : first + 256], 128 - shift, 1)
                        part = jnp.where(lane_one < 128 - shift, part, beyond)
                parts.append(jnp.where(lane_one < per_piece, part, 0.0))
            stacked.append(jnp.concatenate(parts, 1))
        moved = lax.dot_general(
            jnp.concatenate(stacked, 0), sorter, NT, precision=lax.Precision.HIGHEST, preferred_element_type=jnp.float32
        )
        for g in range(groups):
            fc_out[:, g * group : (g + 1) * group] = moved[g * shard : (g + 1) * shard]

    after("start")
    ask_start = put(start_ref, start_other, start_sem.at[0], start_sem.at[1], sibling)
    ask_start.start()
    ask_start.wait()
    row = pl.ds(at.seq - at.source_core * at.seqs, 1)
    first_seen = jnp.where(at.source_core == at.core, start_ref[row], start_other[row])
    down = lax.broadcasted_iota(jnp.int32, (half, 1), 0)
    along_row = lax.broadcasted_iota(jnp.int32, (1, half), 1)
    key_firsts = [at.core * half, (1 - at.core) * half, (3 - at.core) * half, (2 + at.core) * half]
    for slot in range(2):
        low, high = [first_seen[:, k * half : (k + 1) * half] for k in ((0, 1), (3, 2))[slot]]
        seen_from = jnp.where(at.core == 0, low, high)
        place = key_firsts[2 * slot] + along_row
        for tile in range(2 * slot + 2):
            key = key_firsts[tile] + down
            bias[tile * half : (tile + 1) * half, slot * half : (slot + 1) * half] = jnp.where(
                (key >= seen_from) & (key <= place), 0.0, masked_score
            )
    sort_units()
    vecs[...] = jnp.zeros_like(vecs)
    resacc[...] = jnp.zeros_like(resacc)
    gact[...] = jnp.zeros_like(gact)
    after("B0")
    after("B1")

    incoming_wait(0)
    gathered("s")
    vec_copy = pltpu.make_async_copy(vec_hbm, vec_low, vec_sem)
    vec_copy.start()
    vec_copy.wait()
    columns = vec_low[...].astype(jnp.float32)
    vec[...] = columns.T[:16]
    odd_shard = lax.rem(lax.div(lax.broadcasted_iota(jnp.int32, (1, width), 1), shard), 2) == 1
    for part in range(2):
        doubled = [columns[d * shard : (d + 1) * shard] for d in range(part * n_dev // 2, (part + 1) * n_dev // 2) for _ in range(2)]
        lines = jnp.concatenate(doubled, 0).T
        vec[14 + part : 15 + part] = jnp.where(odd_shard, lines[11:12], lines[10:11])

    def first_norm(here, totals):
        normed, _ = normalised(token_block(x_in, here))
        act[here] = (normed * vec[0:1] + vec[1:2]).astype(jnp.bfloat16)
        return totals

    by_rows(first_norm)
    after("L1")

    def weight_here(name, slot):
        gathered(name)
        copy = weight_copy(slot, array(name)[1])
        copy.start()
        copy.wait()

    weight_here("k", 1)
    qkv[:, width : 2 * width] = dot(act[...], wbuf[1], NN).astype(jnp.bfloat16)
    after("FK")
    weight_here("v", 2)
    qkv[:, 2 * width :] = (dot(act[...], wbuf[2], NN) + vec[15:16]).astype(jnp.bfloat16)
    exchange_kv = put(qkv.at[:, pl.ds(width, 2 * width)], kv_other, kv_sem.at[0], kv_sem.at[1], sibling)
    exchange_kv.start()
    after("FV")
    weight_here("q", 0)
    qkv[:, :width] = (dot(act[...], wbuf[0], NN) + vec[14:15]).astype(jnp.bfloat16)
    after("FQ")
    exchange_kv.wait()
    pairs = width // (2 * HEAD_DIM)

    def load_out():
        gathered("o")
        weight_copy(3, out_hbm).start()

    def heads_forward(i, carry):
        pl.when(i == pairs - 1)(load_out)
        at_q = pl.ds(pl.multiple_of(i * 128, 128), 128)
        at_k = pl.ds(pl.multiple_of(width + i * 128, 128), 128)
        at_v = pl.ds(pl.multiple_of(2 * width + i * 128, 128), 128)
        by_core(
            attend_kernel,
            qkv.at[:, at_q],
            qkv.at[:, at_k],
            qkv.at[:, at_v],
            kv_other.at[:, at_q],
            kv_other.at[:, at_k],
            bias,
            mixed.at[:, at_q],
            lse.at[pl.ds(i, 1)],
        )
        after_each("E", i, 6)
        return carry

    lax.fori_loop(0, pairs, heads_forward, 0)
    weight_copy(3, out_hbm).wait()
    resid[...] = dot(mixed[...], wbuf[3], NN)
    after("O")
    load_piece(jnp.int32(0))
    incoming_wait(1)

    def second_norm(here, totals):
        middle = token_block(x_in, here) + branch_scale * (resid[here] + vec[2:3])
        resid[here] = middle
        normed, _ = normalised(middle)
        act[here] = (normed * vec[3:4] + vec[4:5]).astype(jnp.bfloat16)
        grad_mlp = (branch_scale * token_block(cot, here)).astype(jnp.bfloat16)
        gm[here] = grad_mlp
        return [totals[0] + eights(grad_mlp.astype(jnp.float32))]

    (vecs[5:6],) = by_rows(second_norm, 1)
    after("L2")

    def piece(j, carry):
        slot = 2 * lax.rem(j, 2)
        weight_copy(slot, fc_hbm.at[j]).wait()
        weight_copy(slot + 1, proj_hbm.at[j]).wait()
        fc, proj = wbuf.at[slot], wbuf.at[slot + 1]
        bias_fc = vec[pl.ds(6 + j, 1)]

        def some(r, total):
            here = pl.ds(pl.multiple_of(r * half, 16), half)
            u = dot(act[here], fc[...], NN) + bias_fc
            bent = jnp.tanh(gelu_root * (u + gelu_coeff * u * u * u))
            hidden = (0.5 * u * (1.0 + bent)).astype(jnp.bfloat16)
            inner = gelu_root * (1.0 + 3.0 * gelu_coeff * u * u)
            slope = 0.5 * (1.0 + bent) + 0.5 * u * (1.0 - bent * bent) * inner
            a3[here] = hidden
            resacc[here] += dot(hidden, proj[...], NN)
            grad_u = (dot(gm[here], proj[...], NT) * slope).astype(jnp.bfloat16)
            gh[here] = grad_u
            gact[here] += dot(grad_u, fc[...], NT)
            return total + jnp.sum(grad_u.astype(jnp.float32), 0, keepdims=True)

        total = lax.fori_loop(0, 2, some, jnp.zeros((1, width), jnp.float32))
        vecs[pl.ds(6 + j, 1)] = total
        after_each("M", j, PIECES)
        pl.when(j + 1 < PIECES)(lambda: load_piece(j + 1))
        for kind, (left, right) in enumerate(((act, gh), (a3, gm))):
            c = 2 * j + kind
            red = reduction(kind, c)
            pl.when(c >= gbuf.shape[0])(
                lambda red=red, c=c, kind=kind: reduction(kind, c - gbuf.shape[0]).copy(0).wait_send()
            )
            gbuf[lax.rem(c, gbuf.shape[0])] = dot(left[...], right[...], TN).astype(jnp.bfloat16)
            red.start()
        after_each("D", j, PIECES)
        return carry

    lax.fori_loop(0, PIECES, piece, 0)
    for slot in range(3):
        weight_copy(slot, qkv_hbm.at[:, pl.ds(slot * width, width)]).start()
    weight_copy(3, out_hbm).start()

    def token_copies(which, j):
        slot, rest = j // at.parts, j % at.parts
        quarter = at.core + slot * (3 - 2 * at.core)
        to_seq = quarter * at.parts + rest
        mine = (to_seq == at.seq) & (at.source_core == at.core)
        place = at.seq - at.source_core * at.seqs
        out = (result_out, input_out)[which]
        remote = pltpu.make_async_remote_copy(
            src_ref=tok.at[which, j],
            dst_ref=out.at[place],
            send_sem=tok_send.at[which, j],
            recv_sem=tok_recv.at[which, place],
            device_id=(at.pair * 2 + at.source_core, to_seq),
            device_id_type=MESH,
        )
        local = pltpu.make_async_copy(tok.at[which, j], out.at[place], tok_own.at[which])
        return mine, remote, local

    def tokens_store(which, here, value):
        blk = tok.shape[2]
        place = pl.ds(pl.multiple_of(lax.rem(here.start, blk), step), step)
        tok[which, lax.div(here.start, blk), place] = value.astype(jnp.bfloat16)

    def tokens_start(which):
        for j in range(seq_n // 2):
            mine, remote, local = token_copies(which, j)
            pl.when(jnp.logical_not(mine))(remote.start)
            pl.when(mine)(local.start)

    def tokens_wait(which):
        for j in range(seq_n // 2):
            mine, remote, local = token_copies(which, j)
            pl.when(jnp.logical_not(mine))(remote.wait_send)
            pl.when(mine)(local.wait)
        for i in range(at.seqs):
            comes = jnp.logical_not((at.core * at.seqs + i == at.seq) & (at.quarter_core == at.core))
            arrival = pltpu.make_async_remote_copy(
                src_ref=tok.at[which, 0],
                dst_ref=(result_out, input_out)[which].at[i],
                send_sem=tok_send.at[which, 0],
                recv_sem=tok_recv.at[which, i],
                device_id=sibling,
                device_id_type=MESH,
            )
            pl.when(comes)(arrival.wait_recv)

    def result(here, totals):
        tokens_store(0, here, resid[here] + branch_scale * (resacc[here] + vec[5:6]))
        return totals

    by_rows(result)
    tokens_start(0)
    after("T")

    def second_back(here, totals):
        normed, inverse = normalised(resid[here])
        grad_two = gact[here]
        grad_mid = token_block(cot, here) + norm_spread(grad_two, normed, inverse, vec[3:4])
        gact[here] = grad_mid
        grad_branch = (branch_scale * grad_mid).astype(jnp.bfloat16)
        act[here] = grad_branch
        return [
            totals[0] + eights(grad_branch.astype(jnp.float32)),
            totals[1] + eights(grad_two * normed),
            totals[2] + eights(grad_two),
        ]

    vecs[2:3], vecs[3:4], vecs[4:5] = by_rows(second_back, 3)

    c_out = 2 * PIECES
    reduction(0, c_out - gbuf.shape[0]).copy(0).wait_send()
    gbuf[c_out % gbuf.shape[0]] = dot(mixed[...], act[...], TN).astype(jnp.bfloat16)
    reduction(1, c_out).start()
    after("A")
    weight_copy(3, out_hbm).wait()
    gm[...] = dot(act[...], wbuf[3], NT).astype(jnp.bfloat16)
    after("B")

    def heads(i, carry):
        at_q = pl.ds(pl.multiple_of(i * 128, 128), 128)
        at_k = pl.ds(pl.multiple_of(width + i * 128, 128), 128)
        at_v = pl.ds(pl.multiple_of(2 * width + i * 128, 128), 128)
        by_core(
            attend_back_kernel,
            qkv.at[:, at_q],
            qkv.at[:, at_k],
            qkv.at[:, at_v],
            kv_other.at[:, at_q],
            kv_other.at[:, at_k],
            gm.at[:, at_q],
            bias,
            lse.at[pl.ds(i, 1)],
            gqkv.at[:, at_q],
            gqkv.at[:, at_k],
            gqkv.at[:, at_v],
            away.at[:, at_q],
            away.at[:, at_k],
            gk_sum,
            gv_sum,
        )
        after_each("H", i, 6)
        return carry

    lax.fori_loop(0, pairs, heads, 0)

    exchange = pltpu.make_async_remote_copy(
        src_ref=away,
        dst_ref=back,
        send_sem=swap_sem.at[0],
        recv_sem=swap_sem.at[1],
        device_id=sibling,
        device_id_type=MESH,
    )
    exchange.start()
    by_rows(first_norm)

    def grad_of(part):
        c = c_out + 1 + part
        kind = part % 2
        here = pl.ds(part * width, width)
        if part > 0:
            far = pl.ds((part - 1) * width, width)
            gqkv[:, here] = (gqkv[:, here].astype(jnp.float32) + back[:, far].astype(jnp.float32)).astype(jnp.bfloat16)
        reduction(kind, c - gbuf.shape[0]).copy(0).wait_send()
        gbuf[c % gbuf.shape[0]] = dot(act[...], gqkv[:, here], TN).astype(jnp.bfloat16)
        reduction(kind, c).start()
        weight_copy(part, qkv_hbm.at[:, here]).wait()

    def column_sum(part):
        return jnp.sum(gqkv[:, pl.ds(part * width, width)].astype(jnp.float32), 0, keepdims=True)

    grad_of(0)
    after("Q")
    exchange.wait()
    grad_of(1)
    after("K")
    grad_of(2)
    after("V")
    first, third = column_sum(0), column_sum(2)
    for row, value in ((10, first), (11, first), (12, third), (13, third)):
        vecs[row : row + 1] = value
    grad_one = dot(gqkv[:, pl.ds(0, width)], wbuf[0], NT)
    grad_one = grad_one + dot(gqkv[:, pl.ds(width, width)], wbuf[1], NT)
    resacc[...] = grad_one + dot(gqkv[:, pl.ds(2 * width, width)], wbuf[2], NT)
    after("G")

    def first_back(here, totals):
        normed, inverse = normalised(token_block(x_in, here))
        grad_one = resacc[here]
        tokens_store(1, here, gact[here] + norm_spread(grad_one, normed, inverse, vec[0:1]))
        return [totals[0] + eights(grad_one * normed), totals[1] + eights(grad_one)]

    vecs[0:1], vecs[1:2] = by_rows(first_back, 2)
    tokens_start(1)
    columns = vecs[...].T
    small_src[...] = columns
    lane = lax.broadcasted_iota(jnp.int32, (1, 128), 1)
    even, odd = (lane == 10) | (lane == 12), (lane == 11) | (lane == 13)
    for d in range(n_dev):
        start = 2 * shard * (d % (n_dev // 2))
        kept = columns[d * shard : (d + 1) * shard]
        kept = jnp.where(even, columns[start : start + shard], kept)
        kept = jnp.where(odd, columns[start + shard : start + 2 * shard], kept)
        small_src[d * shard : (d + 1) * shard] = kept
    vector_reduction().start()
    after("N")
    for c in range(GRADS):
        red = reduction(0, c)
        for t in range(0 if c >= GRADS - gbuf.shape[0] else 1, stages):
            red.copy(t).wait_send()
    for t in range(stages):
        vector_reduction().copy(t).wait_send()
    for name in ["s", "q", "k", "v", "o"] + [f"{x}{j}" for x in "fp" for j in range(PIECES)]:
        gather_drain(name)
    tokens_wait(0)
    tokens_wait(1)


def whole(mesh_shape, x, cot, start, shards):
    dp_n, seq_n = mesh_shape
    seqs, blk, width = x.shape
    rows = blk * (seq_n // 2)
    n_dev = dp_n * seq_n
    stages = log2(n_dev)
    shard = width // n_dev
    vmem = pl.BlockSpec(memory_space=pltpu.VMEM)
    hbm = pl.BlockSpec(memory_space=ANY)
    DMA = pltpu.SemaphoreType.DMA
    low, full = jnp.bfloat16, jnp.float32
    slots = 4
    arrays = 5 + 2 * PIECES

    def buffers(lead, cols, dtype):
        turns, folds = log2(dp_n) - 1, log2(seq_n)
        parts = [(seq_n >> (m + 1), shard, cols) for m in range(folds)]
        return (
            [pltpu.VMEM(lead + (width // 2 >> t, cols), dtype) for t in range(turns + 1)]
            + [pltpu.VMEM(lead + p, dtype) for p in parts] * 2
            + [pltpu.VMEM(lead + p, full) for p in parts]
        )

    token = jax.ShapeDtypeStruct((seq_n // 2, blk, width), low)
    grads = [(shard, PIECES * width), (PIECES * shard, width), (shard, 3 * width), (shard, width), (16, 128)]
    gathers = [(width, 3 * width), (width, width), (PIECES, width, width), (PIECES, width, width), (width, 128)]
    out = pl.pallas_call(
        functools.partial(whole_kernel, dp_n, seq_n),
        out_shape=[token, token]
        + [jax.ShapeDtypeStruct(s, full) for s in grads]
        + [jax.ShapeDtypeStruct(s, low) for s in gathers],
        in_specs=[vmem] * 8,
        out_specs=[hbm] * 2 + [vmem] * 5 + [hbm] * 5,
        scratch_shapes=[
            pltpu.VMEM((4, width, width), low),
            pltpu.VMEM((slots, width, width), low),
            pltpu.VMEM((rows, width), low),
            pltpu.VMEM((rows, width), low),
            pltpu.VMEM((rows, width), low),
            pltpu.VMEM((rows, width), low),
            pltpu.VMEM((rows, width), full),
            pltpu.VMEM((rows, width), full),
            pltpu.VMEM((rows, 3 * width), low),
            pltpu.VMEM((rows, 2 * width), low),
            pltpu.VMEM((rows, 2 * width), low),
            pltpu.VMEM((2, seq_n // 2, blk, width), low),
            pltpu.VMEM((128, width), full),
            pltpu.VMEM((2 * rows, 128), full),
            pltpu.VMEM((2 * rows, 128), full),
            pltpu.VMEM((seq_n // 2, blk, width), low),
            pltpu.VMEM((seq_n // 2, blk, width), low),
            pltpu.VMEM(start.shape, start.dtype),
            pltpu.VMEM((rows, width), full),
            pltpu.VMEM((rows, width), low),
            pltpu.VMEM((rows, 3 * width), low),
            pltpu.VMEM((rows, 2 * width), low),
            pltpu.VMEM((width // 128, 2, rows), full),
            pltpu.VMEM((2 * rows, rows), full),
            pltpu.VMEM((width, 128), low),
            pltpu.VMEM((16, width), full),
            pltpu.VMEM((shard, PIECES * width), low),
            pltpu.VMEM((shard, PIECES * width), full),
        ]
        + buffers((GRADS,), width, low)
        + buffers((), 128, full)
        + [
            pltpu.VMEM((width, 128), full),
            DMA((GRADS, stages)),
            DMA((GRADS, stages)),
            DMA((stages,)),
            DMA((stages,)),
            DMA((4,)),
            DMA((2,)),
            DMA((2, seq_n // 2)),
            DMA((2, seq_n // 2)),
            DMA((2,)),
            DMA((arrays, stages - 1)),
            DMA((arrays, stages - 1)),
            DMA((arrays, stages)),
            DMA((arrays, stages)),
            DMA((arrays,)),
            DMA((2, seqs)),
            DMA((2, seq_n)),
            DMA((2,)),
            DMA((2,)),
            DMA((2,)),
            DMA,
        ],
        compiler_params=pltpu.CompilerParams(
            collective_id=4, has_side_effects=True, vmem_limit_bytes=64 * 1024 * 1024 - 65536
        ),
        name="whole",
    )(x, cot, start, *shards)
    return out[:7]


def normalised(rows):
    center = rows - jnp.mean(rows, -1, keepdims=True)
    inverse = lax.rsqrt(jnp.mean(center * center, -1, keepdims=True) + norm_eps)
    return center * inverse, inverse


def norm_spread(grad_in, normed, inverse, gain):
    scaled = grad_in * gain
    return inverse * (
        scaled
        - jnp.mean(scaled, -1, keepdims=True)
        - normed * jnp.mean(scaled * normed, -1, keepdims=True)
    )


def packed(vectors, row_unit, dtype):
    flat = jnp.concatenate(vectors, -1)
    size = flat.shape[-1]
    rows = -(-size // (128 * row_unit)) * row_unit
    flat = jnp.pad(flat, [(0, 0)] * (flat.ndim - 1) + [(0, rows * 128 - size)])
    return flat.reshape(flat.shape[:-1] + (rows, 128)).astype(dtype)


def unpacked(rows, sizes):
    flat = rows.reshape(rows.shape[0], -1)
    out, first = [], 0
    for size in sizes:
        out.append(flat[:, first : first + size].reshape(-1))
        first += size
    return out


def block(mesh_shape, *args):
    (
        block_input,
        segments,
        cotangent,
        ln1_gain,
        ln1_bias,
        w_qkv,
        b_qv,
        w_out,
        b_out,
        ln2_gain,
        ln2_bias,
        w_fc,
        b_fc,
        w_proj,
        b_proj,
    ) = args
    dp_n, seq_n = mesh_shape
    n_dev = dp_n * seq_n
    micro_count, seq_count, stretch, width = block_input.shape
    seq_len = segments.shape[2]
    seqs = micro_count * seq_count
    assert 2 * seqs == seq_n and seq_n % 4 == 0
    at = Place(dp_n, seq_n)
    vectors = (ln1_gain, ln1_bias, b_qv, b_out, ln2_gain, ln2_bias, b_fc, b_proj)
    sizes = [v.shape[0] for v in vectors]
    gathered = gather_all(
        mesh_shape,
        block_input.reshape(seqs, stretch, width),
        cotangent.reshape(seqs, stretch, width),
        segments.reshape(seqs, seq_len),
        (w_qkv, w_out, w_fc, w_proj, packed(vectors, 16, jnp.bfloat16)),
    )
    x_rows, cot_rows, seg_other, weight_qkv, weight_out, weight_fc, weight_proj, small = gathered
    rows = seq_len // 2
    half = rows // 2
    x_rows = x_rows.reshape(rows, width).astype(jnp.float32)
    grad_out = cot_rows.reshape(rows, width).astype(jnp.float32)
    weight_qkv, weight_out, weight_fc, weight_proj = [
        w.reshape(-1, w.shape[-1]) for w in (weight_qkv, weight_out, weight_fc, weight_proj)
    ]
    gain_one, bias_one, bias_qv, bias_out, gain_two, bias_two, bias_fc, bias_proj = [
        v.astype(jnp.float32) for v in unpacked(small, sizes)
    ]

    seg_all = jnp.where(at.source_core == at.core, segments.reshape(seqs, seq_len), seg_other)
    seg = lax.dynamic_index_in_dim(seg_all, at.seq - at.source_core * seqs, 0, keepdims=False)
    quarter = jnp.arange(half, dtype=jnp.int32)
    own_first = [at.core * half, (3 - at.core) * half]
    other_first = [(1 - at.core) * half, (2 + at.core) * half]
    firsts = [own_first[0], other_first[0], own_first[1], other_first[1]]
    key_place = jnp.concatenate([f + quarter for f in firsts])
    key_seg = jnp.concatenate([lax.dynamic_slice_in_dim(seg, f, half, 0) for f in firsts])
    query_place = jnp.concatenate([key_place[:half], key_place[2 * half : 3 * half]])
    query_seg = jnp.concatenate([key_seg[:half], key_seg[2 * half : 3 * half]])
    visible = (key_seg[:, None] == query_seg[None, :]) & (key_place[:, None] <= query_place[None, :])
    bias = jnp.where(visible, 0.0, masked_score).astype(jnp.float32)

    normed_out, normed_one, inverse_one = layer_norm(x_rows, gain_one, bias_one)
    act_one = normed_out.astype(jnp.bfloat16)
    bias_full = jnp.concatenate([bias_qv[:width], jnp.zeros((width,), jnp.float32), bias_qv[width:]])
    qkv = (jnp.dot(act_one, weight_qkv, preferred_element_type=jnp.float32) + bias_full).astype(jnp.bfloat16)
    kv_other = swap(mesh_shape, qkv, (width, 2 * width), 2)
    mixed_out, lse = attend(qkv, kv_other, bias)
    resid_mid = x_rows + branch_scale * (
        jnp.dot(mixed_out, weight_out, preferred_element_type=jnp.float32) + bias_out
    )

    normed_out, normed_two, inverse_two = layer_norm(resid_mid, gain_two, bias_two)
    act_two = normed_out.astype(jnp.bfloat16)
    hidden = jnp.dot(act_two, weight_fc, preferred_element_type=jnp.float32) + bias_fc
    act_three = gelu_tanh(hidden).astype(jnp.bfloat16)
    result = resid_mid + branch_scale * (
        jnp.dot(act_three, weight_proj, preferred_element_type=jnp.float32) + bias_proj
    )
    grad_mlp = (branch_scale * grad_out).astype(jnp.bfloat16)
    grad_bproj = jnp.sum(grad_mlp.astype(jnp.float32), 0)
    grad_wproj = dot(act_three, grad_mlp, TN)
    grad_act3 = dot(grad_mlp, weight_proj, NT)
    grad_hidden = (grad_act3 * gelu_slope(hidden)).astype(jnp.bfloat16)
    grad_bfc = jnp.sum(grad_hidden.astype(jnp.float32), 0)
    grad_wfc = dot(act_two, grad_hidden, TN)
    grad_act2 = dot(grad_hidden, weight_fc, NT)
    grad_norm2, grad_gain2, grad_bias2 = norm_back(grad_act2, normed_two, inverse_two, gain_two)
    grad_mid = grad_out + grad_norm2

    grad_branch = (branch_scale * grad_mid).astype(jnp.bfloat16)
    grad_bout = jnp.sum(grad_branch.astype(jnp.float32), 0)
    grad_wout = dot(mixed_out, grad_branch, TN)
    grad_mixed = dot(grad_branch, weight_out, NT).astype(jnp.bfloat16)
    grad_q, grad_k, grad_v, away_k, away_v = attend_back(qkv, kv_other, grad_mixed, bias, lse)
    back = swap(mesh_shape, jnp.concatenate([away_k, away_v], 1), (0, 2 * width), 3)
    key_value = jnp.concatenate([grad_k, grad_v], 1).astype(jnp.float32) + back.astype(jnp.float32)
    grad_qkv = jnp.concatenate([grad_q, key_value.astype(jnp.bfloat16)], 1)
    grad_wide = grad_qkv.astype(jnp.float32)
    grad_bqv = jnp.concatenate([jnp.sum(grad_wide[:, :width], 0), jnp.sum(grad_wide[:, 2 * width :], 0)])
    grad_wqkv = dot(act_one, grad_qkv, TN)
    grad_act1 = dot(grad_qkv, weight_qkv, NT)
    grad_norm1, grad_gain1, grad_bias1 = norm_back(grad_act1, normed_one, inverse_one, gain_one)
    grad_input = grad_mid + grad_norm1

    vec_grads = (grad_gain1, grad_bias1, grad_bqv, grad_bout, grad_gain2, grad_bias2, grad_bfc, grad_bproj)
    token_block = (seq_n // 2, stretch, width)
    parts = [
        g.astype(jnp.bfloat16).reshape((n_dev, -1, g.shape[-1]))
        for g in (grad_wqkv, grad_wout, grad_wfc, grad_wproj)
    ] + [packed([v.reshape(n_dev, -1) for v in vec_grads], 8, jnp.float32)]
    (result, grad_input), totals = reduce_all(
        mesh_shape,
        [result.astype(jnp.bfloat16).reshape(token_block), grad_input.astype(jnp.bfloat16).reshape(token_block)],
        parts,
    )
    owned = unpacked(totals[4].reshape(1, -1), sizes)
    shape = block_input.shape
    return (
        result.reshape(shape),
        grad_input.reshape(shape),
        owned[0],
        owned[1],
        totals[0],
        owned[2],
        totals[1],
        owned[3],
        owned[4],
        owned[5],
        totals[2],
        owned[6],
        totals[3],
        owned[7],
    )


def settle_kernel(*refs):
    half = len(refs) // 2
    for src, dst in zip(refs[:half], refs[half:]):
        dst[...] = src[...]


def settle(arrays):
    vmem = pl.BlockSpec(memory_space=pltpu.VMEM)
    return pl.pallas_call(
        settle_kernel,
        out_shape=[jax.ShapeDtypeStruct(a.shape, a.dtype) for a in arrays],
        in_specs=[vmem] * len(arrays),
        out_specs=[vmem] * len(arrays),
        name="settle",
    )(*arrays)


def fused_block(mesh_shape, *args):
    (
        block_input,
        segments,
        cotangent,
        ln1_gain,
        ln1_bias,
        w_qkv,
        b_qv,
        w_out,
        b_out,
        ln2_gain,
        ln2_bias,
        w_fc,
        b_fc,
        w_proj,
        b_proj,
    ) = args
    dp_n, seq_n = mesh_shape
    n_dev = dp_n * seq_n
    micro_count, seq_count, stretch, width = block_input.shape
    seq_len = segments.shape[2]
    seqs = micro_count * seq_count
    assert 2 * seqs == seq_n and seq_n % 4 == 0 and w_fc.shape[1] == PIECES * width
    at = Place(dp_n, seq_n)
    shard = width // n_dev
    vectors = [ln1_gain, ln1_bias, b_out, ln2_gain, ln2_bias, b_proj]
    vectors += [b_fc[j * shard : (j + 1) * shard] for j in range(PIECES)] + [b_qv[:shard], b_qv[shard:]]
    lane = lax.broadcasted_iota(jnp.int32, (shard, 128), 1)
    columns = jnp.zeros((shard, 128), jnp.bfloat16)
    for k, vector in enumerate(vectors):
        columns = jnp.where(lane == k, vector[:, None], columns)
    seg = segments.reshape(seqs, seq_len)
    start = jnp.sum((seg[:, None, :] < seg[:, :, None]).astype(jnp.int32), 2)
    result, grad_input, grad_fc, grad_proj, grad_qkv, grad_out, lines = whole(
        mesh_shape,
        block_input.reshape(seqs, stretch, width),
        cotangent.reshape(seqs, stretch, width),
        start,
        (w_qkv, w_out, w_fc, w_proj, columns),
    )
    result, grad_input, grad_fc, grad_proj, grad_qkv, grad_out = settle(
        (result, grad_input, grad_fc, grad_proj, grad_qkv, grad_out)
    )
    lines = lines[:, :shard]
    grad_bqv = lines[10:12].reshape(-1)
    shape = block_input.shape
    return (
        result.reshape(shape),
        grad_input.reshape(shape),
        lines[0],
        lines[1],
        grad_qkv,
        grad_bqv,
        grad_out,
        lines[2],
        lines[3],
        lines[4],
        grad_fc,
        lines[6:10].reshape(-1),
        grad_proj,
        lines[5],
    )


def whole_block(mesh_shape, *args):
    aligned = args[5].shape[0] % 8 == 0 and mesh_shape[1] == 4
    return (fused_block if aligned else block)(mesh_shape, *args)


def solution(mesh):
    both = ("dp", "seq")
    tokens, vector, matrix = P(None, "dp", "seq", None), P(both), P(both, None)
    return jax.shard_map(
        functools.partial(whole_block, (mesh.shape["dp"], mesh.shape["seq"])),
        mesh=mesh,
        in_specs=(
            tokens,
            P(None, "dp", None),
            tokens,
            vector,
            vector,
            matrix,
            vector,
            matrix,
            vector,
            vector,
            vector,
            matrix,
            vector,
            matrix,
            vector,
        ),
        out_specs=(
            tokens,
            tokens,
            vector,
            vector,
            matrix,
            vector,
            matrix,
            vector,
            vector,
            vector,
            matrix,
            vector,
            matrix,
            vector,
        ),
        check_vma=False,
    )
```

```python
import functools
import math

import jax
import jax.numpy as jnp
from jax import lax
from jax.experimental import pallas as pl
from jax.experimental.pallas import tpu as pltpu
from jax.sharding import PartitionSpec as P

HEADS = 12
HEAD_DIM = 64
MESH = pl.DeviceIdType.MESH
PIECES = 4
ANY = pl.ANY

branch_scale = 48.0 ** (-0.5)
norm_eps = 1e-05
masked_score = -1e30
gelu_coeff = 0.044715
gelu_root = (2.0 / 3.141592653589793) ** 0.5


def layer_norm(tok_rows, gain_vec, bias_vec):
    center = tok_rows - jnp.mean(tok_rows, -1, keepdims=True)
    inverse = lax.rsqrt(jnp.mean(center * center, -1, keepdims=True) + norm_eps)
    normed = center * inverse
    return (normed * gain_vec + bias_vec, normed, inverse)


def norm_back(grad_in, normed, inverse, gain_vec):
    grad_gain = jnp.sum(grad_in * normed, 0)
    grad_bias = jnp.sum(grad_in, 0)
    scaled = grad_in * gain_vec
    spread = (
        scaled
        - jnp.mean(scaled, -1, keepdims=True)
        - normed * jnp.mean(scaled * normed, -1, keepdims=True)
    )
    return (inverse * spread, grad_gain, grad_bias)


def gelu_tanh(pre_act):
    tanh_val = jnp.tanh(gelu_root * (pre_act + gelu_coeff * pre_act * pre_act * pre_act))
    return 0.5 * pre_act * (1.0 + tanh_val)


def gelu_slope(pre_act):
    tanh_val = jnp.tanh(gelu_root * (pre_act + gelu_coeff * pre_act * pre_act * pre_act))
    inner_slope = gelu_root * (1.0 + 3.0 * gelu_coeff * pre_act * pre_act)
    return 0.5 * (1.0 + tanh_val) + 0.5 * pre_act * (1.0 - tanh_val * tanh_val) * inner_slope


def log2(n):
    k = n.bit_length() - 1
    assert 1 << k == n
    return k


class Place:
    def __init__(self, dp_n, seq_n):
        self.dp_n, self.seq_n = dp_n, seq_n
        self.dp, self.seq = lax.axis_index("dp"), lax.axis_index("seq")
        self.core = lax.rem(self.dp, 2)
        self.pair = lax.div(self.dp, 2)
        self.me = self.dp * seq_n + self.seq
        self.seqs = seq_n // 2
        self.parts = seq_n // 4
        self.quarter = lax.div(self.seq, self.parts)
        self.quarter_core = self.core_of(self.quarter)
        self.source_core = lax.div(self.seq, self.seqs)

    def core_of(self, quarter):
        return lax.rem(lax.div(quarter + 1, 2), 2)

    def bit(self, name):
        axis, k = name
        return lax.rem(lax.div(self.seq if axis == "seq" else self.dp, 1 << k), 2)

    def delta(self, name):
        axis, k = name
        return (1 - 2 * self.bit(name)) * ((1 << k) * (1 if axis == "seq" else self.seq_n))

    def partner(self, name):
        axis, k = name
        step = (1 - 2 * self.bit(name)) * (1 << k)
        if axis == "seq":
            return (self.dp, self.seq + step)
        return (self.dp + step, self.seq)

    def sibling(self):
        return self.partner(("dp", 0))

    def enter(self):
        barrier = pltpu.get_barrier_semaphore()
        count = 0
        for core_step in range(2):
            for seq_step in range(self.seq_n):
                if core_step == 0 and seq_step == 0:
                    continue
                other = (
                    self.pair * 2 + lax.rem(self.core + core_step, 2),
                    lax.rem(self.seq + seq_step, self.seq_n),
                )
                pl.semaphore_signal(barrier, inc=1, device_id=other, device_id_type=MESH)
                count += 1
        for k in range(1, log2(self.dp_n)):
            pl.semaphore_signal(barrier, inc=1, device_id=self.partner(("dp", k)), device_id_type=MESH)
            count += 1
        pl.semaphore_wait(barrier, count)


def orders_of(dp_n, seq_n):
    along = [("seq", k) for k in reversed(range(log2(seq_n)))]
    across = [("dp", k) for k in range(1, log2(dp_n))]
    back = across[::-1]
    return {
        "zxy": along + across,
        "zyx": along + back,
        "xyz": across + along,
        "yxz": back + along,
    }


def repeat(count, body):
    if count <= 16:
        for j in range(count):
            body(j)
    else:
        lax.fori_loop(0, count, lambda j, c: (body(j), c)[1], 0)


def spread(j, deltas):
    total = 0
    for i, delta in enumerate(deltas):
        if isinstance(j, int):
            if (j >> i) & 1:
                total = total + delta
        else:
            total = total + lax.rem(lax.div(j, 1 << i), 2) * delta
    return total


def resolve(shape, cut):
    axis, pieces, k = cut
    if axis == 1 and shape[1] % (8 * pieces):
        axis = 2
    unit = 8 if axis == 1 else 128
    units = shape[axis] // unit
    start, stop = units * k // pieces, units * (k + 1) // pieces
    return axis, start * unit, (stop - start) * unit


def piece_shape(shape, cut):
    axis, _, size = resolve(shape, cut)
    shape = list(shape)
    shape[axis] = size
    return tuple(shape[1:])


def piece_of(ref, lead, cut):
    axis, start, size = resolve(ref.shape, cut)
    where = [slice(None)] * 2
    where[axis - 1] = pl.ds(start, size)
    return ref.at[(lead, *where)]


GATHER = (
    (0, 2, 3, 0, "zxy", 0),
    (0, 2, 3, 1, "zyx", 0),
    (4, 2, 1, 0, "zyx", 0),
    (0, 2, 3, 2, "zxy", 1),
    (1, 2, 1, 0, "zyx", 1),
    (2, 2, 4, 0, "zxy", 2),
    (3, 1, 4, 0, "zyx", 2),
    (2, 2, 4, 1, "zxy", 3),
    (3, 1, 4, 1, "zyx", 3),
    (2, 2, 4, 2, "zxy", 4),
    (3, 1, 4, 2, "zyx", 4),
    (2, 2, 4, 3, "zxy", 5),
    (3, 1, 4, 3, "zyx", 5),
)
X_WAVE, COT_WAVE = 2, 5


def gather_kernel(dp_n, seq_n, major, x_ref, cot_ref, seg_ref, *refs):
    n_arr = 5
    shard = refs[:n_arr]
    x_out, cot_out, seg_out = refs[n_arr : n_arr + 3]
    full = refs[n_arr + 3 : n_arr + 3 + n_arr]
    (send_sem, recv_sem, side_send, side_recv, own_sem, tok_send, tok_recv, tok_own, seg_sem) = refs[
        2 * n_arr + 3 :
    ]
    at = Place(dp_n, seq_n)
    orders = orders_of(dp_n, seq_n)
    stages = len(orders["zxy"])
    at.enter()
    sibling = at.sibling()

    piece = piece_of

    def put(src, dst, s_sem, r_sem, device):
        pltpu.make_async_remote_copy(
            src_ref=src, dst_ref=dst, send_sem=s_sem, recv_sem=r_sem, device_id=device, device_id_type=MESH
        ).start()

    def place_of(a, idx, cut, count=None):
        if a in major:
            idx = idx + cut[2] * dp_n * seq_n
            return full[a].at[idx if count is None else pl.ds(idx, count)]
        return piece(full[a], idx if count is None else pl.ds(idx, count), cut)

    def group(a, cut, count, s_sem, r_sem, device):
        whole = place_of(a, 0, cut, count)
        return pltpu.make_async_remote_copy(
            src_ref=whole, dst_ref=whole, send_sem=s_sem, recv_sem=r_sem, device_id=device, device_id_type=MESH
        )

    def own_src(a, cut):
        return piece(shard[a], 0, cut)

    def stage(c, t):
        a, *cut, order, _ = GATHER[c]
        names = orders[order]
        deltas = [at.delta(n) for n in names]
        if t > 0:
            group(a, cut, 1 << (t - 1), send_sem.at[c, t - 1], recv_sem.at[c, t - 1], sibling).wait_recv()

            def pass_on(j):
                idx = at.me + deltas[t - 1] + spread(j, deltas[: t - 1])
                place = place_of(a, idx, cut)
                put(place, place, side_send.at[c, t], side_recv.at[c, t], sibling)

            if t < stages:
                partner = at.partner(names[t])

                def onward(j):
                    idx = at.me + spread(j, deltas[:t])
                    place = place_of(a, idx, cut)
                    put(own_src(a, cut) if isinstance(j, int) and j == 0 else place, place, send_sem.at[c, t], recv_sem.at[c, t], partner)

                onward(0)
                repeat((1 << t) - 1, lambda j: onward(j + 1))
            repeat(1 << (t - 1), pass_on)
        else:
            partner = at.partner(names[0])
            place = place_of(a, at.me, cut)
            put(own_src(a, cut), place, send_sem.at[c, 0], recv_sem.at[c, 0], partner)
            put(own_src(a, cut), place, side_send.at[c, 0], side_recv.at[c, 0], sibling)
            pltpu.make_async_copy(own_src(a, cut), place, own_sem.at[c]).start()

    slot = lax.div(at.quarter, 2) * at.parts + lax.rem(at.seq, at.parts)
    seg_copy = pltpu.make_async_remote_copy(
        src_ref=seg_ref,
        dst_ref=seg_out,
        send_sem=seg_sem.at[0],
        recv_sem=seg_sem.at[1],
        device_id=sibling,
        device_id_type=MESH,
    )

    def token_copies(which, src, dst, i):
        to_seq = at.core * at.seqs + i
        mine = (to_seq == at.seq) & (at.quarter_core == at.core)
        remote = pltpu.make_async_remote_copy(
            src_ref=src.at[i],
            dst_ref=dst.at[slot],
            send_sem=tok_send.at[which, i],
            recv_sem=tok_recv.at[which, at.seq],
            device_id=(at.pair * 2 + at.quarter_core, to_seq),
            device_id_type=MESH,
        )
        local = pltpu.make_async_copy(src.at[i], dst.at[slot], tok_own.at[which])
        return mine, remote, local

    def tokens_start(which, src, dst):
        for i in range(at.seqs):
            mine, remote, local = token_copies(which, src, dst, i)
            pl.when(jnp.logical_not(mine))(remote.start)
            pl.when(mine)(local.start)

    def tokens_wait(which, src, dst):
        for i in range(at.seqs):
            mine, remote, local = token_copies(which, src, dst, i)
            pl.when(jnp.logical_not(mine))(remote.wait_send)
            pl.when(mine)(local.wait)
        for z in range(seq_n):
            comes = (at.core_of(z // at.parts) == at.core) & jnp.logical_not(
                (at.seq == z) & (at.source_core == at.core)
            )
            arrival = pltpu.make_async_remote_copy(
                src_ref=src.at[0],
                dst_ref=dst.at[0],
                send_sem=tok_send.at[which, 0],
                recv_sem=tok_recv.at[which, z],
                device_id=sibling,
                device_id_type=MESH,
            )
            pl.when(comes)(arrival.wait_recv)

    seg_copy.start()
    waves = stages + 1 + max(c[5] for c in GATHER)
    for wave in range(waves):
        for c in range(len(GATHER)):
            t = wave - GATHER[c][5]
            if 0 <= t <= stages:
                stage(c, t)
        if wave == X_WAVE:
            tokens_start(0, x_ref, x_out)
        if wave == COT_WAVE:
            tokens_start(1, cot_ref, cot_out)
    for c in range(len(GATHER)):
        a, *cut, order, _ = GATHER[c]
        names = orders[order]
        for t in range(stages):
            group(a, cut, 1 << t, send_sem.at[c, t], recv_sem.at[c, t], at.partner(names[t])).wait_send()
        for t in range(stages + 1):
            one = group(a, cut, 1 << max(t - 1, 0), side_send.at[c, t], side_recv.at[c, t], sibling)
            one.wait_send()
            one.wait_recv()
        pltpu.make_async_copy(own_src(a, cut), place_of(a, at.me, cut), own_sem.at[c]).wait()
    tokens_wait(0, x_ref, x_out)
    tokens_wait(1, cot_ref, cot_out)
    seg_copy.wait()


def gather_all(mesh_shape, x, cot, seg, shards, major=()):
    dp_n, seq_n = mesh_shape
    seqs, blk, width = x.shape
    n_dev = dp_n * seq_n
    stages = log2(n_dev) - 1
    chunks = len(GATHER)
    vmem = pl.BlockSpec(memory_space=pltpu.VMEM)
    hbm = pl.BlockSpec(memory_space=ANY)
    token_shape = jax.ShapeDtypeStruct((seq_n // 2, blk, width), x.dtype)
    DMA = pltpu.SemaphoreType.DMA
    return pl.pallas_call(
        functools.partial(gather_kernel, dp_n, seq_n, major),
        out_shape=[token_shape, token_shape, jax.ShapeDtypeStruct(seg.shape, seg.dtype)]
        + [
            jax.ShapeDtypeStruct((PIECES * n_dev,) + piece_shape((1,) + s.shape, (2 if i == 2 else 1, PIECES, 0)), s.dtype)
            if i in major
            else jax.ShapeDtypeStruct((n_dev,) + s.shape, s.dtype)
            for i, s in enumerate(shards)
        ],
        in_specs=[vmem] * (3 + len(shards)),
        out_specs=[hbm] * 2 + [vmem] + [hbm] * len(shards),
        scratch_shapes=[
            DMA((chunks, stages)),
            DMA((chunks, stages)),
            DMA((chunks, stages + 1)),
            DMA((chunks, stages + 1)),
            DMA((chunks,)),
            DMA((2, seqs)),
            DMA((2, seq_n)),
            DMA((2,)),
            DMA((2,)),
        ],
        compiler_params=pltpu.CompilerParams(collective_id=0, has_side_effects=True),
        name="gather_all",
    )(x, cot, seg, *[s[None] for s in shards])


REDUCE = (
    (2, 2, 4, 0, "zxy", 0),
    (3, 1, 4, 0, "zyx", 0),
    (2, 2, 4, 1, "zxy", 1),
    (3, 1, 4, 1, "zyx", 1),
    (2, 2, 4, 2, "zxy", 2),
    (3, 1, 4, 2, "zyx", 2),
    (2, 2, 4, 3, "zxy", 3),
    (3, 1, 4, 3, "zyx", 3),
    (0, 2, 3, 2, "zxy", 4),
    (1, 2, 1, 0, "zyx", 4),
    (0, 2, 3, 0, "zxy", 5),
    (0, 2, 3, 1, "zyx", 5),
    (4, 2, 1, 0, "zyx", 5),
)


def reduce_kernel(dp_n, seq_n, *refs):
    n_arr, chunks = 5, len(REDUCE)
    tok_in, parts = refs[:2], refs[2 : 2 + n_arr]
    refs = refs[2 + n_arr :]
    tok_out, totals = refs[:2], refs[2 : 2 + n_arr]
    refs = refs[2 + n_arr :]
    at = Place(dp_n, seq_n)
    orders = orders_of(dp_n, seq_n)
    stages = len(orders["zxy"])
    buffers = [refs[c * (stages + 2) : (c + 1) * (stages + 2)] for c in range(chunks)]
    send_sem, recv_sem, own_sem, tok_send, tok_recv, tok_own = refs[chunks * (stages + 2) :]
    at.enter()
    sibling = at.sibling()

    def names_of(c):
        return orders[REDUCE[c][4]][::-1]

    def index_of(c, j, core):
        total = core * seq_n
        for s, (axis, k) in enumerate(names_of(c)):
            value = lax.rem(lax.div(j, 1 << (stages - 1 - s)), 2) if not isinstance(j, int) else (j >> (stages - 1 - s)) & 1
            total = total + value * ((1 << k) * (1 if axis == "seq" else seq_n))
        return total

    def hop(c, t, src):
        device = sibling if t == 0 else at.partner(names_of(c)[t - 1])
        return pltpu.make_async_remote_copy(
            src_ref=src,
            dst_ref=buffers[c][t + 1],
            send_sem=send_sem.at[c, t],
            recv_sem=recv_sem.at[c, t],
            device_id=device,
            device_id_type=MESH,
        )

    def first(c):
        a, *cut, _, _ = REDUCE[c]
        own, got = buffers[c][:2]

        def one(j):
            src = piece_of(parts[a], index_of(c, j, 1 - at.core), cut)
            pltpu.make_async_remote_copy(
                src_ref=src,
                dst_ref=got.at[j],
                send_sem=send_sem.at[c, 0],
                recv_sem=recv_sem.at[c, 0],
                device_id=sibling,
                device_id_type=MESH,
            ).start()
            pltpu.make_async_copy(
                piece_of(parts[a], index_of(c, j, at.core), cut), own.at[j], own_sem.at[c]
            ).start()

        repeat(1 << stages, one)

    def own_wait(c):
        a, *cut, _, _ = REDUCE[c]
        whole = piece_of(parts[a], pl.ds(0, 1 << stages), cut)
        pltpu.make_async_copy(whole, buffers[c][0], own_sem.at[c]).wait()

    def add(c, t, lo, count, kept):
        old, got = buffers[c][t], buffers[c][t + 1]

        def one(j, carry):
            total = old[kept + lo + j].astype(jnp.float32) + got[lo + j].astype(jnp.float32)
            got[lo + j] = total.astype(got.dtype)
            return carry

        lax.fori_loop(0, count, one, 0)

    def stage(c, t):
        if t == 0:
            first(c)
            return
        names = names_of(c)
        hop(c, t - 1, buffers[c][t]).wait_recv()
        if t == 1:
            own_wait(c)
            kept = 0
        else:
            kept = at.bit(names[t - 2]) * (1 << (stages - t + 1))
        if t <= stages:
            half = 1 << (stages - t)
            mine = at.bit(names[t - 1])
            add(c, t - 1, (1 - mine) * half, half, kept)
            hop(c, t, buffers[c][t].at[pl.ds((1 - mine) * half, half)]).start()
            add(c, t - 1, mine * half, half, kept)
        else:
            a, *cut, _, _ = REDUCE[c]
            old, got = buffers[c][t - 1], buffers[c][t]
            total = old[kept].astype(jnp.float32) + got[0].astype(jnp.float32)
            piece_of(totals[a], 0, cut)[...] = total

    def token_copies(which, j):
        slot, rest = j // at.parts, j % at.parts
        quarter = at.core + slot * (3 - 2 * at.core)
        to_seq = quarter * at.parts + rest
        mine = (to_seq == at.seq) & (at.source_core == at.core)
        src = tok_in[which].at[j]
        place = at.seq - at.source_core * at.seqs
        remote = pltpu.make_async_remote_copy(
            src_ref=src,
            dst_ref=tok_out[which].at[place],
            send_sem=tok_send.at[which, j],
            recv_sem=tok_recv.at[which, place],
            device_id=(at.pair * 2 + at.source_core, to_seq),
            device_id_type=MESH,
        )
        local = pltpu.make_async_copy(src, tok_out[which].at[place], tok_own.at[which])
        return mine, remote, local

    for which in range(2):
        for j in range(seq_n // 2):
            mine, remote, local = token_copies(which, j)
            pl.when(jnp.logical_not(mine))(remote.start)
            pl.when(mine)(local.start)
    for wave in range(stages + 2 + max(c[5] for c in REDUCE)):
        for c in range(chunks):
            t = wave - REDUCE[c][5]
            if 0 <= t <= stages + 1:
                stage(c, t)
    for c in range(chunks):
        for t in range(stages + 1):
            hop(c, t, buffers[c][t + 1]).wait_send()
    for which in range(2):
        for j in range(seq_n // 2):
            mine, remote, local = token_copies(which, j)
            pl.when(jnp.logical_not(mine))(remote.wait_send)
            pl.when(mine)(local.wait)
        for i in range(at.seqs):
            comes = jnp.logical_not((at.core * at.seqs + i == at.seq) & (at.quarter_core == at.core))
            arrival = pltpu.make_async_remote_copy(
                src_ref=tok_in[which].at[0],
                dst_ref=tok_out[which].at[i],
                send_sem=tok_send.at[which, 0],
                recv_sem=tok_recv.at[which, i],
                device_id=sibling,
                device_id_type=MESH,
            )
            pl.when(comes)(arrival.wait_recv)


def reduce_all(mesh_shape, tokens, parts):
    dp_n, seq_n = mesh_shape
    stages = log2(dp_n * seq_n) - 1
    _, blk, width = tokens[0].shape
    vmem = pl.BlockSpec(memory_space=pltpu.VMEM)
    hbm = pl.BlockSpec(memory_space=ANY)
    DMA = pltpu.SemaphoreType.DMA
    chunks = len(REDUCE)
    scratch = []
    for a, *cut, _, _ in REDUCE:
        shape = piece_shape(parts[a].shape, cut)
        for count in (1 << stages,) + tuple(1 << (stages - t) for t in range(stages + 1)):
            scratch.append(pltpu.VMEM((count,) + shape, parts[a].dtype))
    out = pl.pallas_call(
        functools.partial(reduce_kernel, dp_n, seq_n),
        out_shape=[jax.ShapeDtypeStruct((seq_n // 2, blk, width), t.dtype) for t in tokens]
        + [jax.ShapeDtypeStruct((1,) + p.shape[1:], jnp.float32) for p in parts],
        in_specs=[vmem] * 2 + [hbm] * len(parts),
        out_specs=[hbm] * 2 + [vmem] * len(parts),
        scratch_shapes=scratch
        + [
            DMA((chunks, stages + 1)),
            DMA((chunks, stages + 1)),
            DMA((chunks,)),
            DMA((2, seq_n // 2)),
            DMA((2, seq_n // 2)),
            DMA((2,)),
        ],
        compiler_params=pltpu.CompilerParams(
            collective_id=1, has_side_effects=True, vmem_limit_bytes=60 * 1024 * 1024
        ),
        name="reduce_all",
    )(*tokens, *parts)
    return out[:2], [g[0] for g in out[2:]]


def swap_kernel(dp_n, seq_n, cols, src_ref, out_ref, send_sem, recv_sem):
    at = Place(dp_n, seq_n)
    sibling = at.sibling()
    barrier = pltpu.get_barrier_semaphore()
    pl.semaphore_signal(barrier, inc=1, device_id=sibling, device_id_type=MESH)
    pl.semaphore_wait(barrier, 1)
    first, width = cols
    copy = pltpu.make_async_remote_copy(
        src_ref=src_ref.at[:, pl.ds(first, width)],
        dst_ref=out_ref,
        send_sem=send_sem,
        recv_sem=recv_sem,
        device_id=sibling,
        device_id_type=MESH,
    )
    copy.start()
    copy.wait()


def swap(mesh_shape, src, cols, which):
    hbm = pl.BlockSpec(memory_space=ANY)
    return pl.pallas_call(
        functools.partial(swap_kernel, *mesh_shape, cols),
        out_shape=jax.ShapeDtypeStruct((src.shape[0], cols[1]), src.dtype),
        in_specs=[hbm],
        out_specs=hbm,
        scratch_shapes=[pltpu.SemaphoreType.DMA, pltpu.SemaphoreType.DMA],
        compiler_params=pltpu.CompilerParams(collective_id=which, has_side_effects=True),
        name="swap",
    )(src)


NT = (((1,), (1,)), ((), ()))
NN = (((1,), (0,)), ((), ()))
TN = (((0,), (0,)), ((), ()))


def dot(a, b, dims):
    return lax.dot_general(a, b, dims, preferred_element_type=jnp.float32)


def woven(own, other):
    half = own.shape[0] // 2
    return jnp.concatenate([own[:half], other[:half], own[half:], other[half:]], 0)


def head_masks():
    lane = lax.broadcasted_iota(jnp.int32, (1, 2 * HEAD_DIM), 1)
    first = (lane < HEAD_DIM).astype(jnp.bfloat16)
    return first, 1 - first


def attend_kernel(q_ref, ko_ref, vo_ref, ks_ref, vs_ref, bias_ref, o_ref, lse_ref, sees=None):
    rows = q_ref.shape[0]
    sees = sees or (rows, 2 * rows)
    half = rows // 2
    keys = woven(ko_ref[...], ks_ref[...])
    values = woven(vo_ref[...], vs_ref[...])
    masks = head_masks()
    scale = jnp.bfloat16(HEAD_DIM ** (-0.5))
    for slot in range(2):
        seen = sees[slot]
        here = slice(slot * half, (slot + 1) * half)
        q = q_ref[here] * scale
        outs = []
        for head in range(2):
            s = dot(keys[:seen], q * masks[head], NT) + bias_ref[:seen, here]
            top = jnp.max(s, 0, keepdims=True)
            e = jnp.exp(s - top)
            total = jnp.sum(e, 0, keepdims=True)
            p = (e * (1.0 / total)).astype(jnp.bfloat16)
            mixed = dot(values[:seen], p, TN)
            outs.append(mixed[head * HEAD_DIM : (head + 1) * HEAD_DIM])
            lse_ref[0, head : head + 1, here] = top + jnp.log(total)
        o_ref[here] = jnp.concatenate(outs, 0).T.astype(jnp.bfloat16)


def attend(qkv, kv_other, bias):
    rows, wide = qkv.shape
    width = wide // 3
    pairs = width // (2 * HEAD_DIM)
    col = lambda first: pl.BlockSpec((rows, 2 * HEAD_DIM), lambda h, first=first: (0, first * pairs + h))
    return pl.pallas_call(
        attend_kernel,
        grid=(pairs,),
        out_shape=[
            jax.ShapeDtypeStruct((rows, width), jnp.bfloat16),
            jax.ShapeDtypeStruct((pairs, 2, rows), jnp.float32),
        ],
        in_specs=[col(0), col(1), col(2), col(0), col(1), pl.BlockSpec(bias.shape, lambda h: (0, 0))],
        out_specs=[col(0), pl.BlockSpec((1, 2, rows), lambda h: (h, 0, 0))],
        name="attend",
    )(qkv, qkv, qkv, kv_other, kv_other, bias)


def attend_back_kernel(
    q_ref, ko_ref, vo_ref, ks_ref, vs_ref, go_ref, bias_ref, lse_ref, gq_ref, gko_ref, gvo_ref, gks_ref, gvs_ref, gk_sum, gv_sum, sees=None
):
    rows = q_ref.shape[0]
    sees = sees or (rows, 2 * rows)
    half = rows // 2
    keys = woven(ko_ref[...], ks_ref[...])
    values = woven(vo_ref[...], vs_ref[...])
    masks = head_masks()
    scale = HEAD_DIM ** (-0.5)
    for slot in (1, 0):
        seen = sees[slot]
        here = slice(slot * half, (slot + 1) * half)
        q = q_ref[here] * jnp.bfloat16(scale)
        go = go_ref[here]
        gqs, gk, gv = [], None, None
        for head in range(2):
            q_h, go_h = q * masks[head], go * masks[head]
            s = dot(keys[:seen], q_h, NT) + bias_ref[:seen, here]
            p = jnp.exp(s - lse_ref[0, head : head + 1, here])
            gp = dot(values[:seen], go_h, NT)
            row_dot = jnp.sum(p * gp, 0, keepdims=True)
            gs = (p * (gp - row_dot)).astype(jnp.bfloat16)
            gv_h = dot(p.astype(jnp.bfloat16), go_h, NN)
            gk_h = dot(gs, q_h, NN)
            gk = gk_h if gk is None else gk + gk_h
            gv = gv_h if gv is None else gv + gv_h
            gq = dot(keys[:seen], gs, TN)
            gqs.append(gq[head * HEAD_DIM : (head + 1) * HEAD_DIM])
        gq_ref[here] = (jnp.concatenate(gqs, 0).T * scale).astype(gq_ref.dtype)
        if slot == 1:
            gk_sum[:seen] = gk
            gv_sum[:seen] = gv
            if seen < 2 * rows:
                gk_sum[seen:] = jnp.zeros((2 * rows - seen, gk.shape[1]), jnp.float32)
                gv_sum[seen:] = jnp.zeros((2 * rows - seen, gv.shape[1]), jnp.float32)
        else:
            gk_sum[:seen] += gk
            gv_sum[:seen] += gv
    for total, own, other in ((gk_sum, gko_ref, gks_ref), (gv_sum, gvo_ref, gvs_ref)):
        for slot in range(2):
            here = slice(slot * half, (slot + 1) * half)
            own[here] = total[2 * slot * half : (2 * slot + 1) * half].astype(own.dtype)
            other[here] = total[(2 * slot + 1) * half : (2 * slot + 2) * half].astype(other.dtype)


def attend_back(qkv, kv_other, go, bias, lse):
    rows, wide = qkv.shape
    width = wide // 3
    pairs = width // (2 * HEAD_DIM)
    lanes = 2 * HEAD_DIM
    col = lambda first: pl.BlockSpec((rows, lanes), lambda h, first=first: (0, first * pairs + h))
    out = jax.ShapeDtypeStruct((rows, width), jnp.bfloat16)
    return pl.pallas_call(
        attend_back_kernel,
        grid=(pairs,),
        out_shape=[out] * 5,
        in_specs=[
            col(0),
            col(1),
            col(2),
            col(0),
            col(1),
            col(0),
            pl.BlockSpec(bias.shape, lambda h: (0, 0)),
            pl.BlockSpec((1, 2, rows), lambda h: (h, 0, 0)),
        ],
        out_specs=[col(0)] * 5,
        scratch_shapes=[pltpu.VMEM((2 * rows, lanes), jnp.float32)] * 2,
        name="attend_back",
    )(qkv, qkv, qkv, kv_other, kv_other, go, bias, lse)


def rows_at(start, size):
    return pl.ds(pl.multiple_of(start, 16), size)


class Reduction:
    def __init__(self, at, order, refs, sems, own):
        self.at, self.own = at, own
        self.blocks, self.sends, self.gets, self.keeps = refs
        self.send_sem, self.recv_sem = sems
        self.order = order
        self.turns = len(order)
        self.last = self.turns + len(self.sends)
        self.names = order + [("seq", k) for k in range(len(self.sends))]
        self.dp_rows = self.blocks[0].shape[0] // (at.dp_n // 2)
        self.shard = self.dp_rows // at.seq_n

    def dp_of(self, j, core):
        dp = core
        for i, (_, k) in enumerate(reversed(self.order)):
            bit = (j >> i) & 1 if isinstance(j, int) else lax.rem(lax.div(j, 1 << i), 2)
            dp = dp + bit * (1 << k)
        return dp

    def landing(self, t):
        return self.blocks[t] if t <= self.turns else self.gets[t - self.turns - 1]

    def copy(self, t, src=None, dst=None):
        at = self.at
        return pltpu.make_async_remote_copy(
            src_ref=self.landing(t) if src is None else src,
            dst_ref=self.landing(t) if dst is None else dst,
            send_sem=self.send_sem.at[t],
            recv_sem=self.recv_sem.at[t],
            device_id=at.sibling() if t == 0 else at.partner(self.names[t - 1]),
            device_id_type=MESH,
        )

    def start(self):
        for j in range(self.at.dp_n // 2):
            dst = self.blocks[0].at[pl.ds(j * self.dp_rows, self.dp_rows)]
            self.copy(0, self.own(self.dp_of(j, 1 - self.at.core)), dst).start()

    def fold(self, t, lo, size):
        got = self.blocks[t - 1]
        step = self.dp_rows // 2

        def one(i, carry):
            row = lo + i * step
            here = rows_at(row, step)
            if t == 1:
                half = lax.rem(i, 2) * step
                old = self.own(self.dp_of(lax.div(row, self.dp_rows), self.at.core))[rows_at(half, step)]
            else:
                kept = self.at.bit(self.names[t - 2]) * got.shape[0]
                old = self.blocks[t - 2][rows_at(kept + row, step)]
            got[here] = (old.astype(jnp.float32) + got[here].astype(jnp.float32)).astype(got.dtype)
            return carry

        lax.fori_loop(0, size // step, one, 0)

    def shards_of(self, t):
        got = self.landing(t - 1)
        if t == self.turns + 1:
            kept = self.at.bit(self.names[t - 2]) * self.dp_rows
            total = self.blocks[t - 2][rows_at(kept, self.dp_rows)].astype(jnp.float32) + got[...].astype(jnp.float32)
            return [total[i * self.shard : (i + 1) * self.shard] for i in range(self.at.seq_n)]
        keep = self.keeps[t - self.turns - 2]
        return [keep[i] + got[i].astype(jnp.float32) for i in range(keep.shape[0])]

    def stage(self, t):
        self.copy(t - 1).wait_recv()
        mine = self.at.bit(self.names[t - 1])
        if t <= self.turns:
            got = self.blocks[t - 1]
            half = got.shape[0] // 2
            self.fold(t, (1 - mine) * half, half)
            self.copy(t, got.at[rows_at((1 - mine) * half, half)]).start()
            self.fold(t, mine * half, half)
            return
        held = self.shards_of(t)
        m = t - self.turns - 1
        send, keep = self.sends[m], self.keeps[m]
        for i in range(len(held) // 2):
            send[i] = jnp.where(mine == 0, held[2 * i + 1], held[2 * i]).astype(send.dtype)
        self.copy(t, send).start()
        for i in range(len(held) // 2):
            keep[i] = jnp.where(mine == 0, held[2 * i], held[2 * i + 1])

    def finish(self):
        self.copy(self.last).wait_recv()
        return self.shards_of(self.last + 1)[0]


GRADS = 2 * PIECES + 4

AFTER = {
    "start": (
        "gs0", "gq0", "gk0", "go0", "gv0",
    ),
    "B0": (
        "gs1",
    ),
    "B1": (
        "gq1", "gk1", "gf00", "gp00", "gs2", "go1", "gq2", "gv1", "gs3", "gk2", "gf01", "gf10", "gp10", "gp01", "go2",
        "gq3", "gv2", "X", "gs4", "gk3", "gf02", "gf20", "gp20", "gf11", "go3", "gp11", "gp02", "gv3", "gq4", "gk4",
        "gp03", "gf03", "gv4",
    ),
    "L1": (
        "go4", "gf12", "gp12", "gf21", "gp21", "gf30", "gp30",
    ),
    "FK": (),
    "FV": (
        "C", "gp04", "gf04", "gf22",
    ),
    "FQ": (
        "gp13", "gp22", "gf31", "gf13", "gp31",
    ),
    "E0": (
        "gf23",
    ),
    "E1": (
        "gp23",
    ),
    "E2": (
        "gp14",
    ),
    "E3": (
        "gf14",
    ),
    "E4": (
        "gf32", "gp32",
    ),
    "E5": (
        "gf24", "gp24",
    ),
    "O": (),
    "L2": (
        "gf33", "gp33",
    ),
    "M0": (),
    "D0": (),
    "M1": (
        "rf01", "gf34", "gp34",
    ),
    "D1": (
        "rp01",
    ),
    "M2": (
        "rf11",
    ),
    "D2": (
        "rp11",
    ),
    "M3": (
        "rf02", "rp02", "rf21", "rp21",
    ),
    "D3": (),
    "T": (
        "rf12",
    ),
    "A": (
        "rp03", "rp12", "rf31", "rp31",
    ),
    "B": (
        "rf03",
    ),
    "H0": (
        "ro1",
    ),
    "H1": (
        "rf22", "rp22",
    ),
    "H2": (
        "rp13", "rf13",
    ),
    "H3": (
        "rp04",
    ),
    "H4": (
        "rf04", "rp14", "rf32", "rp32",
    ),
    "H5": (
        "rp05", "rf14", "rp23",
    ),
    "Q": (
        "rf05", "rp15", "rp33", "ro2",
    ),
    "G": (
        "rf15", "rp24", "rp34", "rf23", "rq1",
    ),
    "N": (
        "rf33", "ro3",
    ),
    "K": (
        "rp25",
    ),
    "V": (
        "rf24", "rp35", "rs1", "rk1", "rv1", "rq2", "rs2", "rv2", "rk2", "rs3", "rf34", "rq3", "ro4", "rs4", "rk3",
        "rv3", "rf25", "rq4", "rf35", "U", "rk4", "ro5", "rs5", "rv4", "rq5", "rk5", "rv5",
    ),
}
ORDER_ONE = "kosp"


def whole_kernel(dp_n, seq_n, *refs):
    x_ref, cot_ref, start_ref = refs[:3]
    w_qkv, w_out, w_fc, w_proj, w_vec = refs[3:8]
    result_out, input_out, fc_out, proj_out, qkv_out, wout_out, small_out = refs[8:15]
    qkv_hbm, out_hbm, fc_hbm, proj_hbm, vec_hbm = refs[15:20]
    (wbuf, gbuf, act, gm, a3, gh, resacc, gact, gqkv, away, back, tok, vecs, gk_sum, gv_sum) = refs[20:35]
    (x_in, cot, start_other, resid, mixed, qkv, kv_other, lse, bias, vec_low, vec, fc_own, fc_sum) = refs[35:48]
    refs = refs[48:]
    at = Place(dp_n, seq_n)
    stages = log2(dp_n * seq_n)
    turns, folds = log2(dp_n) - 1, log2(seq_n)
    sets = [turns + 1, folds, folds, folds]
    count = sum(sets)

    def grouped(some):
        groups, first = [], 0
        for size in sets:
            groups.append(some[first : first + size])
            first += size
        return groups

    big, small_bufs = refs[:count], refs[count : 2 * count]
    (small_src, big_send, big_recv, small_send, small_recv, w_sem, swap_sem, tok_send, tok_recv, tok_own) = refs[
        2 * count : 2 * count + 10
    ]
    (ask_send, ask_recv, side_send, side_recv, own_sem, in_send, in_recv, in_own, start_sem, kv_sem, vec_sem) = refs[
        2 * count + 10 :
    ]
    rows, width = resid.shape
    half = rows // 2
    shard = fc_out.shape[0]
    n_dev = dp_n * seq_n
    across = [("dp", k) for k in range(1, log2(dp_n))]
    at.enter()
    sibling = at.sibling()

    def own_rows(src):
        return lambda dp: src.at[pl.ds(pl.multiple_of(dp * (seq_n * shard), 16), seq_n * shard)]

    def reduction(kind, c):
        order = across[::-1] if kind == 0 else across
        where = lax.rem(c, gbuf.shape[0]) if not isinstance(c, int) else c % gbuf.shape[0]
        return Reduction(
            at,
            order,
            grouped([b.at[c] for b in big]),
            (big_send.at[c], big_recv.at[c]),
            own_rows(gbuf.at[where]),
        )

    def vector_reduction():
        return Reduction(
            at,
            across,
            grouped(small_bufs),
            (small_send, small_recv),
            own_rows(small_src),
        )

    def weight_copy(slot, src):
        return pltpu.make_async_copy(src, wbuf.at[slot], w_sem.at[slot])

    def by_core(kernel, *some):
        for core, sees in ((0, (half, 4 * half)), (1, (2 * half, 3 * half))):
            pl.when(at.core == core)(functools.partial(kernel, *some, sees=sees))

    step = 64

    def by_rows(body, sums=0):
        zeros = [jnp.zeros((8, width), jnp.float32)] * sums
        totals = lax.fori_loop(
            0, rows // step, lambda i, t: body(pl.ds(pl.multiple_of(i * step, step), step), t), zeros
        )
        return [jnp.sum(t, 0, keepdims=True) for t in totals]

    def eights(value):
        return jnp.sum(value.reshape(step // 8, 8, width), 0)

    def token_block(ref, here):
        blk = ref.shape[1]
        start = here.start
        return ref[lax.div(start, blk), pl.ds(pl.multiple_of(lax.rem(start, blk), step), step)].astype(jnp.float32)


    def array(name):
        if name in "qkv":
            part = "qkv".index(name)
            cols = pl.ds(part * width, width)
            return part, qkv_hbm.at[:, cols], w_qkv.at[:, cols]
        if name == "o":
            return 3, out_hbm, w_out
        if name == "s":
            return 4, vec_hbm, w_vec
        j = int(name[1])
        if name[0] == "f":
            return 5 + j, fc_hbm.at[j], fc_own.at[:, pl.ds(j * width, width)]
        return 5 + PIECES + j, proj_hbm.at[j], w_proj.at[pl.ds(j * shard, shard)]

    along = [("seq", k) for k in reversed(range(folds))]

    def shard_rows(full, d):
        return full.at[pl.ds(pl.multiple_of(d * shard, 8), shard)]

    def put(src, dst, s_sem, r_sem, device):
        return pltpu.make_async_remote_copy(
            src_ref=src, dst_ref=dst, send_sem=s_sem, recv_sem=r_sem, device_id=device, device_id_type=MESH
        )

    def gather_stage(name, t):
        n, full, own = array(name)
        names = along + (across[::-1] if name[0] in ORDER_ONE else across)
        deltas = [at.delta(x) for x in names]
        if t == 0:
            place = shard_rows(full, at.me)
            put(own, place, ask_send.at[n, 0], ask_recv.at[n, 0], at.partner(names[0])).start()
            put(own, place, side_send.at[n, 0], side_recv.at[n, 0], sibling).start()
            pltpu.make_async_copy(own, place, own_sem.at[n]).start()
            return
        some = full.at[pl.ds(0, shard << (t - 1))]
        put(some, some, ask_send.at[n, t - 1], ask_recv.at[n, t - 1], sibling).wait_recv()
        if t == folds:
            pltpu.make_async_copy(own, shard_rows(full, at.me), own_sem.at[n]).wait()

        def held(t, shift):
            if t < folds:
                return [shard_rows(full, at.me + shift + spread(j, deltas[:t])) for j in range(1 << t)]
            size = seq_n * shard
            return [
                full.at[pl.ds(pl.multiple_of((at.dp * seq_n + shift + spread(j, deltas[folds:t])) * shard, 8), size)]
                for j in range(1 << (t - folds))
            ]

        if t < len(names):
            for j, place in enumerate(held(t, 0)):
                src = own if j == 0 and t < folds else place
                put(src, place, ask_send.at[n, t], ask_recv.at[n, t], at.partner(names[t])).start()
        for place in held(t - 1, deltas[t - 1]):
            put(place, place, side_send.at[n, t], side_recv.at[n, t], sibling).start()

    def gathered(name):
        n, full, own = array(name)
        for t in range(stages):
            some = full.at[pl.ds(0, shard << max(t - 1, 0))]
            put(some, some, side_send.at[n, t], side_recv.at[n, t], sibling).wait_recv()

    def gather_drain(name):
        n, full, own = array(name)
        for t in range(stages - 1):
            some = full.at[pl.ds(0, shard << t)]
            put(some, some, ask_send.at[n, t], ask_recv.at[n, t], sibling).wait_send()
        for t in range(stages):
            some = full.at[pl.ds(0, shard << max(t - 1, 0))]
            put(some, some, side_send.at[n, t], side_recv.at[n, t], sibling).wait_send()

    slot_here = lax.div(at.quarter, 2) * at.parts + lax.rem(at.seq, at.parts)

    def incoming(which, i):
        src, dst = ((x_ref, x_in), (cot_ref, cot))[which]
        to_seq = at.core * at.seqs + i
        mine = (to_seq == at.seq) & (at.quarter_core == at.core)
        remote = put(
            src.at[i],
            dst.at[slot_here],
            in_send.at[which, i],
            in_recv.at[which, at.seq],
            (at.pair * 2 + at.quarter_core, to_seq),
        )
        local = pltpu.make_async_copy(src.at[i], dst.at[slot_here], in_own.at[which])
        return mine, remote, local

    def incoming_start(which):
        for i in range(at.seqs):
            mine, remote, local = incoming(which, i)
            pl.when(jnp.logical_not(mine))(remote.start)
            pl.when(mine)(local.start)

    def incoming_wait(which):
        src, dst = ((x_ref, x_in), (cot_ref, cot))[which]
        for i in range(at.seqs):
            mine, remote, local = incoming(which, i)
            pl.when(jnp.logical_not(mine))(remote.wait_send)
            pl.when(mine)(local.wait)
        for z in range(seq_n):
            comes = (at.core_of(z // at.parts) == at.core) & jnp.logical_not(
                (at.seq == z) & (at.source_core == at.core)
            )
            arrival = put(src.at[0], dst.at[0], in_send.at[which, 0], in_recv.at[which, z], sibling)
            pl.when(comes)(arrival.wait_recv)

    def load_piece(j):
        slot = 2 * lax.rem(j, 2)
        for k in range(PIECES):

            def ready(k=k):
                gathered(f"f{k}")
                gathered(f"p{k}")

            pl.when(j == k)(ready)
        weight_copy(slot, fc_hbm.at[j]).start()
        weight_copy(slot + 1, proj_hbm.at[j]).start()

    def after(slot):
        for op in AFTER[slot]:
            if op == "U":
                unsort_units()
                continue
            if op in "XC":
                incoming_start("XC".index(op))
                continue
            if op[0] == "g":
                gather_stage(op[1:-1], int(op[-1]))
                continue
            name, kind, t = op[1:], op[1], int(op[-1])
            if kind == "s":
                red = vector_reduction()
            else:
                c = 2 * int(name[1]) + (kind == "p") if kind in "fp" else 2 * PIECES + "oqkv".index(kind)
                red = reduction(int(kind in ORDER_ONE), int(c))
            if t < stages:
                red.stage(t)
                continue
            total = red.finish()
            if kind == "f":
                fc_sum[:, int(name[1]) * width : (int(name[1]) + 1) * width] = total
            elif kind == "p":
                proj_out[int(name[1]) * shard : (int(name[1]) + 1) * shard] = total
            elif kind == "o":
                wout_out[...] = total
            elif kind == "s":
                square = jnp.concatenate([total, jnp.zeros((128 - shard, 128), jnp.float32)], 0).T
                pairs_qv = jnp.where(at.me < n_dev // 2, square[10:12], square[12:14])
                line_fc, line_qv = square[6:7], pairs_qv[:1]
                for j in range(1, PIECES):
                    line_fc = line_fc + pltpu.roll(square[6 + j : 7 + j], j * shard, 1)
                line_qv = line_qv + pltpu.roll(pairs_qv[1:2], shard, 1)
                small_out[...] = jnp.concatenate([square[:6], line_fc, line_qv], 0)
            else:
                part = "qkv".index(kind)
                qkv_out[:, part * width : (part + 1) * width] = total

    def after_each(prefix, i, count):
        for k in range(count):
            pl.when(i == k)(functools.partial(after, f"{prefix}{k}"))

    period = PIECES * shard
    group = period * 128 // math.gcd(period, 128)
    lane = lax.broadcasted_iota(jnp.int32, (1, PIECES * 128), 1)
    entry = lax.rem(lane, 128)
    source = lax.div(entry, shard) * period + lax.div(lane, 128) * shard + lax.rem(entry, shard)
    per_piece = group // PIECES
    source = jnp.where(entry < per_piece, source, -1)
    sorter = (lax.broadcasted_iota(jnp.int32, (group, 1), 0) == source).astype(jnp.float32)
    lane_one = lax.broadcasted_iota(jnp.int32, (1, 128), 1)
    groups = PIECES * width // group

    def sort_units():
        pieces = [[jnp.zeros((shard, 128), jnp.float32) for _ in range(width // 128)] for _ in range(PIECES)]
        for g in range(groups):
            moved = dot(w_fc[:, g * group : (g + 1) * group], sorter.astype(jnp.bfloat16), NN)
            block, shift = divmod(g * per_piece, 128)
            for j in range(PIECES):
                turned = moved[:, j * 128 : (j + 1) * 128]
                if shift:
                    turned = pltpu.roll(turned, shift, 1)
                    if shift + per_piece > 128:
                        pieces[j][block + 1] = pieces[j][block + 1] + jnp.where(lane_one < shift, turned, 0.0)
                    turned = jnp.where(lane_one >= shift, turned, 0.0)
                pieces[j][block] = pieces[j][block] + turned
        for j in range(PIECES):
            fc_own[:, j * width : (j + 1) * width] = jnp.concatenate(pieces[j], 1).astype(jnp.bfloat16)

    def unsort_units():
        stacked = []
        for g in range(groups):
            block, shift = divmod(g * per_piece, 128)
            parts = []
            for j in range(PIECES):
                first = j * width + block * 128
                part = fc_sum[:, first : first + 128]
                if shift:
                    part = pltpu.roll(part, 128 - shift, 1)
                    if shift + per_piece > 128:
                        beyond = pltpu.roll(fc_sum[:, first + 128 : first + 256], 128 - shift, 1)
                        part = jnp.where(lane_one < 128 - shift, part, beyond)
                parts.append(jnp.where(lane_one < per_piece, part, 0.0))
            stacked.append(jnp.concatenate(parts, 1))
        moved = lax.dot_general(
            jnp.concatenate(stacked, 0), sorter, NT, precision=lax.Precision.HIGHEST, preferred_element_type=jnp.float32
        )
        for g in range(groups):
            fc_out[:, g * group : (g + 1) * group] = moved[g * shard : (g + 1) * shard]

    after("start")
    ask_start = put(start_ref, start_other, start_sem.at[0], start_sem.at[1], sibling)
    ask_start.start()
    ask_start.wait()
    seq_here = at.seq - at.source_core * at.seqs
    numbers = jnp.where(at.source_core == at.core, start_ref[seq_here], start_other[seq_here])
    spot = lax.broadcasted_iota(jnp.int32, numbers.shape, 1)
    first_seen = jnp.where((spot > 0) & (numbers == pltpu.roll(numbers, 1, 1)), 0, spot)
    for k in range(log2(numbers.shape[1])):
        earlier = pltpu.roll(first_seen, 1 << k, 1)
        first_seen = jnp.maximum(first_seen, jnp.where(spot >= 1 << k, earlier, 0))
    down = lax.broadcasted_iota(jnp.int32, (half, 1), 0)
    along_row = lax.broadcasted_iota(jnp.int32, (1, half), 1)
    key_firsts = [at.core * half, (1 - at.core) * half, (3 - at.core) * half, (2 + at.core) * half]
    for slot in range(2):
        low, high = [first_seen[:, k * half : (k + 1) * half] for k in ((0, 1), (3, 2))[slot]]
        seen_from = jnp.where(at.core == 0, low, high)
        place = key_firsts[2 * slot] + along_row
        for tile in range(2 * slot + 2):
            key = key_firsts[tile] + down
            bias[tile * half : (tile + 1) * half, slot * half : (slot + 1) * half] = jnp.where(
                (key >= seen_from) & (key <= place), 0.0, masked_score
            )
    sort_units()
    vecs[...] = jnp.zeros_like(vecs)
    resacc[...] = jnp.zeros_like(resacc)
    gact[...] = jnp.zeros_like(gact)
    after("B0")
    after("B1")

    incoming_wait(0)
    gathered("s")
    vec_copy = pltpu.make_async_copy(vec_hbm, vec_low, vec_sem)
    vec_copy.start()
    vec_copy.wait()
    columns = vec_low[...].astype(jnp.float32)
    vec[...] = columns.T[:16]
    odd_shard = lax.rem(lax.div(lax.broadcasted_iota(jnp.int32, (1, width), 1), shard), 2) == 1
    for part in range(2):
        doubled = [columns[d * shard : (d + 1) * shard] for d in range(part * n_dev // 2, (part + 1) * n_dev // 2) for _ in range(2)]
        lines = jnp.concatenate(doubled, 0).T
        vec[14 + part : 15 + part] = jnp.where(odd_shard, lines[11:12], lines[10:11])

    def first_norm(here, totals):
        normed, _ = normalised(token_block(x_in, here))
        act[here] = (normed * vec[0:1] + vec[1:2]).astype(jnp.bfloat16)
        return totals

    by_rows(first_norm)
    after("L1")

    def weight_here(name, slot):
        gathered(name)
        copy = weight_copy(slot, array(name)[1])
        copy.start()
        copy.wait()

    weight_here("k", 1)
    qkv[:, width : 2 * width] = dot(act[...], wbuf[1], NN).astype(jnp.bfloat16)
    after("FK")
    weight_here("v", 2)
    qkv[:, 2 * width :] = (dot(act[...], wbuf[2], NN) + vec[15:16]).astype(jnp.bfloat16)
    exchange_kv = put(qkv.at[:, pl.ds(width, 2 * width)], kv_other, kv_sem.at[0], kv_sem.at[1], sibling)
    exchange_kv.start()
    after("FV")
    weight_here("q", 0)
    qkv[:, :width] = (dot(act[...], wbuf[0], NN) + vec[14:15]).astype(jnp.bfloat16)
    after("FQ")
    exchange_kv.wait()
    pairs = width // (2 * HEAD_DIM)

    def load_out():
        gathered("o")
        weight_copy(3, out_hbm).start()

    def heads_forward(i, carry):
        pl.when(i == pairs - 1)(load_out)
        at_q = pl.ds(pl.multiple_of(i * 128, 128), 128)
        at_k = pl.ds(pl.multiple_of(width + i * 128, 128), 128)
        at_v = pl.ds(pl.multiple_of(2 * width + i * 128, 128), 128)
        by_core(
            attend_kernel,
            qkv.at[:, at_q],
            qkv.at[:, at_k],
            qkv.at[:, at_v],
            kv_other.at[:, at_q],
            kv_other.at[:, at_k],
            bias,
            mixed.at[:, at_q],
            lse.at[pl.ds(i, 1)],
        )
        after_each("E", i, 6)
        return carry

    lax.fori_loop(0, pairs, heads_forward, 0)
    weight_copy(3, out_hbm).wait()
    resid[...] = dot(mixed[...], wbuf[3], NN)
    after("O")
    load_piece(jnp.int32(0))
    incoming_wait(1)

    def second_norm(here, totals):
        middle = token_block(x_in, here) + branch_scale * (resid[here] + vec[2:3])
        resid[here] = middle
        normed, _ = normalised(middle)
        act[here] = (normed * vec[3:4] + vec[4:5]).astype(jnp.bfloat16)
        grad_mlp = (branch_scale * token_block(cot, here)).astype(jnp.bfloat16)
        gm[here] = grad_mlp
        return [totals[0] + eights(grad_mlp.astype(jnp.float32))]

    (vecs[5:6],) = by_rows(second_norm, 1)
    after("L2")

    def piece(j, carry):
        slot = 2 * lax.rem(j, 2)
        weight_copy(slot, fc_hbm.at[j]).wait()
        weight_copy(slot + 1, proj_hbm.at[j]).wait()
        fc, proj = wbuf.at[slot], wbuf.at[slot + 1]
        bias_fc = vec[pl.ds(6 + j, 1)]

        def some(r, total):
            here = pl.ds(pl.multiple_of(r * half, 16), half)
            u = dot(act[here], fc[...], NN) + bias_fc
            bent = jnp.tanh(gelu_root * (u + gelu_coeff * u * u * u))
            hidden = (0.5 * u * (1.0 + bent)).astype(jnp.bfloat16)
            inner = gelu_root * (1.0 + 3.0 * gelu_coeff * u * u)
            slope = 0.5 * (1.0 + bent) + 0.5 * u * (1.0 - bent * bent) * inner
            a3[here] = hidden
            resacc[here] += dot(hidden, proj[...], NN)
            grad_u = (dot(gm[here], proj[...], NT) * slope).astype(jnp.bfloat16)
            gh[here] = grad_u
            gact[here] += dot(grad_u, fc[...], NT)
            return total + jnp.sum(grad_u.astype(jnp.float32), 0, keepdims=True)

        total = lax.fori_loop(0, 2, some, jnp.zeros((1, width), jnp.float32))
        vecs[pl.ds(6 + j, 1)] = total
        after_each("M", j, PIECES)
        pl.when(j + 1 < PIECES)(lambda: load_piece(j + 1))
        for kind, (left, right) in enumerate(((act, gh), (a3, gm))):
            c = 2 * j + kind
            red = reduction(kind, c)
            pl.when(c >= gbuf.shape[0])(
                lambda red=red, c=c, kind=kind: reduction(kind, c - gbuf.shape[0]).copy(0).wait_send()
            )
            gbuf[lax.rem(c, gbuf.shape[0])] = dot(left[...], right[...], TN).astype(jnp.bfloat16)
            red.start()
        after_each("D", j, PIECES)
        return carry

    lax.fori_loop(0, PIECES, piece, 0)
    for slot in range(3):
        weight_copy(slot, qkv_hbm.at[:, pl.ds(slot * width, width)]).start()
    weight_copy(3, out_hbm).start()

    def token_copies(which, j):
        slot, rest = j // at.parts, j % at.parts
        quarter = at.core + slot * (3 - 2 * at.core)
        to_seq = quarter * at.parts + rest
        mine = (to_seq == at.seq) & (at.source_core == at.core)
        place = at.seq - at.source_core * at.seqs
        out = (result_out, input_out)[which]
        remote = pltpu.make_async_remote_copy(
            src_ref=tok.at[which, j],
            dst_ref=out.at[place],
            send_sem=tok_send.at[which, j],
            recv_sem=tok_recv.at[which, place],
            device_id=(at.pair * 2 + at.source_core, to_seq),
            device_id_type=MESH,
        )
        local = pltpu.make_async_copy(tok.at[which, j], out.at[place], tok_own.at[which])
        return mine, remote, local

    def tokens_store(which, here, value):
        blk = tok.shape[2]
        place = pl.ds(pl.multiple_of(lax.rem(here.start, blk), step), step)
        tok[which, lax.div(here.start, blk), place] = value.astype(jnp.bfloat16)

    def tokens_start(which):
        for j in range(seq_n // 2):
            mine, remote, local = token_copies(which, j)
            pl.when(jnp.logical_not(mine))(remote.start)
            pl.when(mine)(local.start)

    def tokens_wait(which):
        for j in range(seq_n // 2):
            mine, remote, local = token_copies(which, j)
            pl.when(jnp.logical_not(mine))(remote.wait_send)
            pl.when(mine)(local.wait)
        for i in range(at.seqs):
            comes = jnp.logical_not((at.core * at.seqs + i == at.seq) & (at.quarter_core == at.core))
            arrival = pltpu.make_async_remote_copy(
                src_ref=tok.at[which, 0],
                dst_ref=(result_out, input_out)[which].at[i],
                send_sem=tok_send.at[which, 0],
                recv_sem=tok_recv.at[which, i],
                device_id=sibling,
                device_id_type=MESH,
            )
            pl.when(comes)(arrival.wait_recv)

    def result(here, totals):
        tokens_store(0, here, resid[here] + branch_scale * (resacc[here] + vec[5:6]))
        return totals

    by_rows(result)
    tokens_start(0)
    after("T")

    def second_back(here, totals):
        normed, inverse = normalised(resid[here])
        grad_two = gact[here]
        grad_mid = token_block(cot, here) + norm_spread(grad_two, normed, inverse, vec[3:4])
        gact[here] = grad_mid
        grad_branch = (branch_scale * grad_mid).astype(jnp.bfloat16)
        act[here] = grad_branch
        return [
            totals[0] + eights(grad_branch.astype(jnp.float32)),
            totals[1] + eights(grad_two * normed),
            totals[2] + eights(grad_two),
        ]

    vecs[2:3], vecs[3:4], vecs[4:5] = by_rows(second_back, 3)

    c_out = 2 * PIECES
    reduction(0, c_out - gbuf.shape[0]).copy(0).wait_send()
    gbuf[c_out % gbuf.shape[0]] = dot(mixed[...], act[...], TN).astype(jnp.bfloat16)
    reduction(1, c_out).start()
    after("A")
    weight_copy(3, out_hbm).wait()
    gm[...] = dot(act[...], wbuf[3], NT).astype(jnp.bfloat16)
    after("B")

    def heads(i, carry):
        at_q = pl.ds(pl.multiple_of(i * 128, 128), 128)
        at_k = pl.ds(pl.multiple_of(width + i * 128, 128), 128)
        at_v = pl.ds(pl.multiple_of(2 * width + i * 128, 128), 128)
        by_core(
            attend_back_kernel,
            qkv.at[:, at_q],
            qkv.at[:, at_k],
            qkv.at[:, at_v],
            kv_other.at[:, at_q],
            kv_other.at[:, at_k],
            gm.at[:, at_q],
            bias,
            lse.at[pl.ds(i, 1)],
            gqkv.at[:, at_q],
            gqkv.at[:, at_k],
            gqkv.at[:, at_v],
            away.at[:, at_q],
            away.at[:, at_k],
            gk_sum,
            gv_sum,
        )
        after_each("H", i, 6)
        return carry

    lax.fori_loop(0, pairs, heads, 0)

    exchange = pltpu.make_async_remote_copy(
        src_ref=away,
        dst_ref=back,
        send_sem=swap_sem.at[0],
        recv_sem=swap_sem.at[1],
        device_id=sibling,
        device_id_type=MESH,
    )
    exchange.start()
    by_rows(first_norm)

    def grad_of(part):
        c = c_out + 1 + part
        kind = part % 2
        here = pl.ds(part * width, width)
        reduction(kind, c - gbuf.shape[0]).copy(0).wait_send()
        gbuf[c % gbuf.shape[0]] = dot(act[...], gqkv[:, here], TN).astype(jnp.bfloat16)
        reduction(kind, c).start()

    grad_of(0)
    after("Q")
    exchange.wait()

    def meet(here, totals):
        for part in (1, 2):
            near, far = pl.ds(part * width, width), pl.ds((part - 1) * width, width)
            gqkv[here, near] = (gqkv[here, near].astype(jnp.float32) + back[here, far].astype(jnp.float32)).astype(
                jnp.bfloat16
            )
        return [
            totals[0] + eights(gqkv[here, pl.ds(0, width)].astype(jnp.float32)),
            totals[1] + eights(gqkv[here, pl.ds(2 * width, width)].astype(jnp.float32)),
        ]

    first, third = by_rows(meet, 2)
    for row, value in ((10, first), (11, first), (12, third), (13, third)):
        vecs[row : row + 1] = value
    for part in range(3):
        weight_copy(part, qkv_hbm.at[:, pl.ds(part * width, width)]).wait()
    grad_one = dot(gqkv[:, pl.ds(0, width)], wbuf[0], NT)
    grad_one = grad_one + dot(gqkv[:, pl.ds(width, width)], wbuf[1], NT)
    resacc[...] = grad_one + dot(gqkv[:, pl.ds(2 * width, width)], wbuf[2], NT)
    after("G")

    def first_back(here, totals):
        normed, inverse = normalised(token_block(x_in, here))
        grad_one = resacc[here]
        tokens_store(1, here, gact[here] + norm_spread(grad_one, normed, inverse, vec[0:1]))
        return [totals[0] + eights(grad_one * normed), totals[1] + eights(grad_one)]

    vecs[0:1], vecs[1:2] = by_rows(first_back, 2)
    tokens_start(1)
    columns = vecs[...].T
    small_src[...] = columns
    lane = lax.broadcasted_iota(jnp.int32, (1, 128), 1)
    even, odd = (lane == 10) | (lane == 12), (lane == 11) | (lane == 13)
    for d in range(n_dev):
        start = 2 * shard * (d % (n_dev // 2))
        kept = columns[d * shard : (d + 1) * shard]
        kept = jnp.where(even, columns[start : start + shard], kept)
        kept = jnp.where(odd, columns[start + shard : start + 2 * shard], kept)
        small_src[d * shard : (d + 1) * shard] = kept
    vector_reduction().start()
    after("N")
    grad_of(1)
    after("K")
    grad_of(2)
    after("V")
    for c in range(GRADS):
        red = reduction(0, c)
        for t in range(0 if c >= GRADS - gbuf.shape[0] else 1, stages):
            red.copy(t).wait_send()
    for t in range(stages):
        vector_reduction().copy(t).wait_send()
    for name in ["s", "q", "k", "v", "o"] + [f"{x}{j}" for x in "fp" for j in range(PIECES)]:
        gather_drain(name)
    tokens_wait(0)
    tokens_wait(1)


def whole(mesh_shape, x, cot, start, shards):
    dp_n, seq_n = mesh_shape
    seqs, blk, width = x.shape
    rows = blk * (seq_n // 2)
    n_dev = dp_n * seq_n
    stages = log2(n_dev)
    shard = width // n_dev
    vmem = pl.BlockSpec(memory_space=pltpu.VMEM)
    hbm = pl.BlockSpec(memory_space=ANY)
    DMA = pltpu.SemaphoreType.DMA
    low, full = jnp.bfloat16, jnp.float32
    slots = 4
    arrays = 5 + 2 * PIECES

    def buffers(lead, cols, dtype):
        turns, folds = log2(dp_n) - 1, log2(seq_n)
        parts = [(seq_n >> (m + 1), shard, cols) for m in range(folds)]
        return (
            [pltpu.VMEM(lead + (width // 2 >> t, cols), dtype) for t in range(turns + 1)]
            + [pltpu.VMEM(lead + p, dtype) for p in parts] * 2
            + [pltpu.VMEM(lead + p, full) for p in parts]
        )

    token = jax.ShapeDtypeStruct((seq_n // 2, blk, width), low)
    grads = [(shard, PIECES * width), (PIECES * shard, width), (shard, 3 * width), (shard, width), (8, 128)]
    gathers = [(width, 3 * width), (width, width), (PIECES, width, width), (PIECES, width, width), (width, 128)]
    out = pl.pallas_call(
        functools.partial(whole_kernel, dp_n, seq_n),
        out_shape=[token, token]
        + [jax.ShapeDtypeStruct(s, full) for s in grads]
        + [jax.ShapeDtypeStruct(s, low) for s in gathers],
        in_specs=[hbm] * 2 + [vmem] * 6,
        out_specs=[hbm] * 2 + [vmem] * 5 + [hbm] * 5,
        scratch_shapes=[
            pltpu.VMEM((4, width, width), low),
            pltpu.VMEM((slots, width, width), low),
            pltpu.VMEM((rows, width), low),
            pltpu.VMEM((rows, width), low),
            pltpu.VMEM((rows, width), low),
            pltpu.VMEM((rows, width), low),
            pltpu.VMEM((rows, width), full),
            pltpu.VMEM((rows, width), full),
            pltpu.VMEM((rows, 3 * width), low),
            pltpu.VMEM((rows, 2 * width), low),
            pltpu.VMEM((rows, 2 * width), low),
            pltpu.VMEM((2, seq_n // 2, blk, width), low),
            pltpu.VMEM((128, width), full),
            pltpu.VMEM((2 * rows, 128), full),
            pltpu.VMEM((2 * rows, 128), full),
            pltpu.VMEM((seq_n // 2, blk, width), low),
            pltpu.VMEM((seq_n // 2, blk, width), low),
            pltpu.VMEM(start.shape, start.dtype),
            pltpu.VMEM((rows, width), full),
            pltpu.VMEM((rows, width), low),
            pltpu.VMEM((rows, 3 * width), low),
            pltpu.VMEM((rows, 2 * width), low),
            pltpu.VMEM((width // 128, 2, rows), full),
            pltpu.VMEM((2 * rows, rows), full),
            pltpu.VMEM((width, 128), low),
            pltpu.VMEM((16, width), full),
            pltpu.VMEM((shard, PIECES * width), low),
            pltpu.VMEM((shard, PIECES * width), full),
        ]
        + buffers((GRADS,), width, low)
        + buffers((), 128, full)
        + [
            pltpu.VMEM((width, 128), full),
            DMA((GRADS, stages)),
            DMA((GRADS, stages)),
            DMA((stages,)),
            DMA((stages,)),
            DMA((4,)),
            DMA((2,)),
            DMA((2, seq_n // 2)),
            DMA((2, seq_n // 2)),
            DMA((2,)),
            DMA((arrays, stages - 1)),
            DMA((arrays, stages - 1)),
            DMA((arrays, stages)),
            DMA((arrays, stages)),
            DMA((arrays,)),
            DMA((2, seqs)),
            DMA((2, seq_n)),
            DMA((2,)),
            DMA((2,)),
            DMA((2,)),
            DMA,
        ],
        compiler_params=pltpu.CompilerParams(
            collective_id=4, has_side_effects=True, vmem_limit_bytes=64 * 1024 * 1024 - 65536
        ),
        name="whole",
    )(x, cot, start, *shards)
    return out[:7]


def normalised(rows):
    center = rows - jnp.mean(rows, -1, keepdims=True)
    inverse = lax.rsqrt(jnp.mean(center * center, -1, keepdims=True) + norm_eps)
    return center * inverse, inverse


def norm_spread(grad_in, normed, inverse, gain):
    scaled = grad_in * gain
    return inverse * (
        scaled
        - jnp.mean(scaled, -1, keepdims=True)
        - normed * jnp.mean(scaled * normed, -1, keepdims=True)
    )


def packed(vectors, row_unit, dtype):
    flat = jnp.concatenate(vectors, -1)
    size = flat.shape[-1]
    rows = -(-size // (128 * row_unit)) * row_unit
    flat = jnp.pad(flat, [(0, 0)] * (flat.ndim - 1) + [(0, rows * 128 - size)])
    return flat.reshape(flat.shape[:-1] + (rows, 128)).astype(dtype)


def unpacked(rows, sizes):
    flat = rows.reshape(rows.shape[0], -1)
    out, first = [], 0
    for size in sizes:
        out.append(flat[:, first : first + size].reshape(-1))
        first += size
    return out


def block(mesh_shape, *args):
    (
        block_input,
        segments,
        cotangent,
        ln1_gain,
        ln1_bias,
        w_qkv,
        b_qv,
        w_out,
        b_out,
        ln2_gain,
        ln2_bias,
        w_fc,
        b_fc,
        w_proj,
        b_proj,
    ) = args
    dp_n, seq_n = mesh_shape
    n_dev = dp_n * seq_n
    micro_count, seq_count, stretch, width = block_input.shape
    seq_len = segments.shape[2]
    seqs = micro_count * seq_count
    assert 2 * seqs == seq_n and seq_n % 4 == 0
    at = Place(dp_n, seq_n)
    vectors = (ln1_gain, ln1_bias, b_qv, b_out, ln2_gain, ln2_bias, b_fc, b_proj)
    sizes = [v.shape[0] for v in vectors]
    gathered = gather_all(
        mesh_shape,
        block_input.reshape(seqs, stretch, width),
        cotangent.reshape(seqs, stretch, width),
        segments.reshape(seqs, seq_len),
        (w_qkv, w_out, w_fc, w_proj, packed(vectors, 16, jnp.bfloat16)),
    )
    x_rows, cot_rows, seg_other, weight_qkv, weight_out, weight_fc, weight_proj, small = gathered
    rows = seq_len // 2
    half = rows // 2
    x_rows = x_rows.reshape(rows, width).astype(jnp.float32)
    grad_out = cot_rows.reshape(rows, width).astype(jnp.float32)
    weight_qkv, weight_out, weight_fc, weight_proj = [
        w.reshape(-1, w.shape[-1]) for w in (weight_qkv, weight_out, weight_fc, weight_proj)
    ]
    gain_one, bias_one, bias_qv, bias_out, gain_two, bias_two, bias_fc, bias_proj = [
        v.astype(jnp.float32) for v in unpacked(small, sizes)
    ]

    seg_all = jnp.where(at.source_core == at.core, segments.reshape(seqs, seq_len), seg_other)
    seg = lax.dynamic_index_in_dim(seg_all, at.seq - at.source_core * seqs, 0, keepdims=False)
    quarter = jnp.arange(half, dtype=jnp.int32)
    own_first = [at.core * half, (3 - at.core) * half]
    other_first = [(1 - at.core) * half, (2 + at.core) * half]
    firsts = [own_first[0], other_first[0], own_first[1], other_first[1]]
    key_place = jnp.concatenate([f + quarter for f in firsts])
    key_seg = jnp.concatenate([lax.dynamic_slice_in_dim(seg, f, half, 0) for f in firsts])
    query_place = jnp.concatenate([key_place[:half], key_place[2 * half : 3 * half]])
    query_seg = jnp.concatenate([key_seg[:half], key_seg[2 * half : 3 * half]])
    visible = (key_seg[:, None] == query_seg[None, :]) & (key_place[:, None] <= query_place[None, :])
    bias = jnp.where(visible, 0.0, masked_score).astype(jnp.float32)

    normed_out, normed_one, inverse_one = layer_norm(x_rows, gain_one, bias_one)
    act_one = normed_out.astype(jnp.bfloat16)
    bias_full = jnp.concatenate([bias_qv[:width], jnp.zeros((width,), jnp.float32), bias_qv[width:]])
    qkv = (jnp.dot(act_one, weight_qkv, preferred_element_type=jnp.float32) + bias_full).astype(jnp.bfloat16)
    kv_other = swap(mesh_shape, qkv, (width, 2 * width), 2)
    mixed_out, lse = attend(qkv, kv_other, bias)
    resid_mid = x_rows + branch_scale * (
        jnp.dot(mixed_out, weight_out, preferred_element_type=jnp.float32) + bias_out
    )

    normed_out, normed_two, inverse_two = layer_norm(resid_mid, gain_two, bias_two)
    act_two = normed_out.astype(jnp.bfloat16)
    hidden = jnp.dot(act_two, weight_fc, preferred_element_type=jnp.float32) + bias_fc
    act_three = gelu_tanh(hidden).astype(jnp.bfloat16)
    result = resid_mid + branch_scale * (
        jnp.dot(act_three, weight_proj, preferred_element_type=jnp.float32) + bias_proj
    )
    grad_mlp = (branch_scale * grad_out).astype(jnp.bfloat16)
    grad_bproj = jnp.sum(grad_mlp.astype(jnp.float32), 0)
    grad_wproj = dot(act_three, grad_mlp, TN)
    grad_act3 = dot(grad_mlp, weight_proj, NT)
    grad_hidden = (grad_act3 * gelu_slope(hidden)).astype(jnp.bfloat16)
    grad_bfc = jnp.sum(grad_hidden.astype(jnp.float32), 0)
    grad_wfc = dot(act_two, grad_hidden, TN)
    grad_act2 = dot(grad_hidden, weight_fc, NT)
    grad_norm2, grad_gain2, grad_bias2 = norm_back(grad_act2, normed_two, inverse_two, gain_two)
    grad_mid = grad_out + grad_norm2

    grad_branch = (branch_scale * grad_mid).astype(jnp.bfloat16)
    grad_bout = jnp.sum(grad_branch.astype(jnp.float32), 0)
    grad_wout = dot(mixed_out, grad_branch, TN)
    grad_mixed = dot(grad_branch, weight_out, NT).astype(jnp.bfloat16)
    grad_q, grad_k, grad_v, away_k, away_v = attend_back(qkv, kv_other, grad_mixed, bias, lse)
    back = swap(mesh_shape, jnp.concatenate([away_k, away_v], 1), (0, 2 * width), 3)
    key_value = jnp.concatenate([grad_k, grad_v], 1).astype(jnp.float32) + back.astype(jnp.float32)
    grad_qkv = jnp.concatenate([grad_q, key_value.astype(jnp.bfloat16)], 1)
    grad_wide = grad_qkv.astype(jnp.float32)
    grad_bqv = jnp.concatenate([jnp.sum(grad_wide[:, :width], 0), jnp.sum(grad_wide[:, 2 * width :], 0)])
    grad_wqkv = dot(act_one, grad_qkv, TN)
    grad_act1 = dot(grad_qkv, weight_qkv, NT)
    grad_norm1, grad_gain1, grad_bias1 = norm_back(grad_act1, normed_one, inverse_one, gain_one)
    grad_input = grad_mid + grad_norm1

    vec_grads = (grad_gain1, grad_bias1, grad_bqv, grad_bout, grad_gain2, grad_bias2, grad_bfc, grad_bproj)
    token_block = (seq_n // 2, stretch, width)
    parts = [
        g.astype(jnp.bfloat16).reshape((n_dev, -1, g.shape[-1]))
        for g in (grad_wqkv, grad_wout, grad_wfc, grad_wproj)
    ] + [packed([v.reshape(n_dev, -1) for v in vec_grads], 8, jnp.float32)]
    (result, grad_input), totals = reduce_all(
        mesh_shape,
        [result.astype(jnp.bfloat16).reshape(token_block), grad_input.astype(jnp.bfloat16).reshape(token_block)],
        parts,
    )
    owned = unpacked(totals[4].reshape(1, -1), sizes)
    shape = block_input.shape
    return (
        result.reshape(shape),
        grad_input.reshape(shape),
        owned[0],
        owned[1],
        totals[0],
        owned[2],
        totals[1],
        owned[3],
        owned[4],
        owned[5],
        totals[2],
        owned[6],
        totals[3],
        owned[7],
    )


def settle_kernel(*refs):
    half = len(refs) // 2
    for src, dst in zip(refs[:half], refs[half:]):
        dst[...] = src[...]


def settle(arrays):
    vmem = pl.BlockSpec(memory_space=pltpu.VMEM)
    return pl.pallas_call(
        settle_kernel,
        out_shape=[jax.ShapeDtypeStruct(a.shape, a.dtype) for a in arrays],
        in_specs=[vmem] * len(arrays),
        out_specs=[vmem] * len(arrays),
        name="settle",
    )(*arrays)


def fused_block(mesh_shape, *args):
    (
        block_input,
        segments,
        cotangent,
        ln1_gain,
        ln1_bias,
        w_qkv,
        b_qv,
        w_out,
        b_out,
        ln2_gain,
        ln2_bias,
        w_fc,
        b_fc,
        w_proj,
        b_proj,
    ) = args
    dp_n, seq_n = mesh_shape
    n_dev = dp_n * seq_n
    micro_count, seq_count, stretch, width = block_input.shape
    seq_len = segments.shape[2]
    seqs = micro_count * seq_count
    assert 2 * seqs == seq_n and seq_n % 4 == 0 and w_fc.shape[1] == PIECES * width
    at = Place(dp_n, seq_n)
    shard = width // n_dev
    vectors = [ln1_gain, ln1_bias, b_out, ln2_gain, ln2_bias, b_proj]
    vectors += [b_fc[j * shard : (j + 1) * shard] for j in range(PIECES)] + [b_qv[:shard], b_qv[shard:]]
    lane = lax.broadcasted_iota(jnp.int32, (shard, 128), 1)
    columns = jnp.zeros((shard, 128), jnp.bfloat16)
    for k, vector in enumerate(vectors):
        columns = jnp.where(lane == k, vector[:, None], columns)
    result, grad_input, grad_fc, grad_proj, grad_qkv, grad_out, lines = whole(
        mesh_shape,
        block_input.reshape(seqs, stretch, width),
        cotangent.reshape(seqs, stretch, width),
        segments.reshape(seqs, 1, seq_len),
        (w_qkv, w_out, w_fc, w_proj, columns),
    )
    result, grad_input, grad_fc, grad_proj, grad_qkv, grad_out = settle(
        (result, grad_input, grad_fc, grad_proj, grad_qkv, grad_out)
    )
    shape = block_input.shape
    return (
        result.reshape(shape),
        grad_input.reshape(shape),
        lines[0, :shard],
        lines[1, :shard],
        grad_qkv,
        lines[7, : 2 * shard],
        grad_out,
        lines[2, :shard],
        lines[3, :shard],
        lines[4, :shard],
        grad_fc,
        lines[6, : PIECES * shard],
        grad_proj,
        lines[5, :shard],
    )


def whole_block(mesh_shape, *args):
    aligned = args[5].shape[0] % 8 == 0 and mesh_shape[1] == 4
    return (fused_block if aligned else block)(mesh_shape, *args)


def solution(mesh):
    both = ("dp", "seq")
    tokens, vector, matrix = P(None, "dp", "seq", None), P(both), P(both, None)
    return jax.shard_map(
        functools.partial(whole_block, (mesh.shape["dp"], mesh.shape["seq"])),
        mesh=mesh,
        in_specs=(
            tokens,
            P(None, "dp", None),
            tokens,
            vector,
            vector,
            matrix,
            vector,
            matrix,
            vector,
            vector,
            vector,
            matrix,
            vector,
            matrix,
            vector,
        ),
        out_specs=(
            tokens,
            tokens,
            vector,
            vector,
            matrix,
            vector,
            matrix,
            vector,
            vector,
            vector,
            matrix,
            vector,
            matrix,
            vector,
        ),
        check_vma=False,
    )
```

```python
import functools
import math

import jax
import jax.numpy as jnp
from jax import lax
from jax.experimental import pallas as pl
from jax.experimental.pallas import tpu as pltpu
from jax.sharding import PartitionSpec as P

HEADS = 12
HEAD_DIM = 64
MESH = pl.DeviceIdType.MESH
PIECES = 4
ANY = pl.ANY

branch_scale = 48.0 ** (-0.5)
norm_eps = 1e-05
masked_score = -1e30
gelu_coeff = 0.044715
gelu_root = (2.0 / 3.141592653589793) ** 0.5


def layer_norm(tok_rows, gain_vec, bias_vec):
    center = tok_rows - jnp.mean(tok_rows, -1, keepdims=True)
    inverse = lax.rsqrt(jnp.mean(center * center, -1, keepdims=True) + norm_eps)
    normed = center * inverse
    return (normed * gain_vec + bias_vec, normed, inverse)


def norm_back(grad_in, normed, inverse, gain_vec):
    grad_gain = jnp.sum(grad_in * normed, 0)
    grad_bias = jnp.sum(grad_in, 0)
    scaled = grad_in * gain_vec
    spread = (
        scaled
        - jnp.mean(scaled, -1, keepdims=True)
        - normed * jnp.mean(scaled * normed, -1, keepdims=True)
    )
    return (inverse * spread, grad_gain, grad_bias)


def gelu_tanh(pre_act):
    tanh_val = jnp.tanh(gelu_root * (pre_act + gelu_coeff * pre_act * pre_act * pre_act))
    return 0.5 * pre_act * (1.0 + tanh_val)


def gelu_slope(pre_act):
    tanh_val = jnp.tanh(gelu_root * (pre_act + gelu_coeff * pre_act * pre_act * pre_act))
    inner_slope = gelu_root * (1.0 + 3.0 * gelu_coeff * pre_act * pre_act)
    return 0.5 * (1.0 + tanh_val) + 0.5 * pre_act * (1.0 - tanh_val * tanh_val) * inner_slope


def log2(n):
    k = n.bit_length() - 1
    assert 1 << k == n
    return k


class Place:
    def __init__(self, dp_n, seq_n):
        self.dp_n, self.seq_n = dp_n, seq_n
        self.dp, self.seq = lax.axis_index("dp"), lax.axis_index("seq")
        self.core = lax.rem(self.dp, 2)
        self.pair = lax.div(self.dp, 2)
        self.me = self.dp * seq_n + self.seq
        self.seqs = seq_n // 2
        self.parts = seq_n // 4
        self.quarter = lax.div(self.seq, self.parts)
        self.quarter_core = self.core_of(self.quarter)
        self.source_core = lax.div(self.seq, self.seqs)

    def core_of(self, quarter):
        return lax.rem(lax.div(quarter + 1, 2), 2)

    def bit(self, name):
        axis, k = name
        return lax.rem(lax.div(self.seq if axis == "seq" else self.dp, 1 << k), 2)

    def delta(self, name):
        axis, k = name
        return (1 - 2 * self.bit(name)) * ((1 << k) * (1 if axis == "seq" else self.seq_n))

    def partner(self, name):
        axis, k = name
        step = (1 - 2 * self.bit(name)) * (1 << k)
        if axis == "seq":
            return (self.dp, self.seq + step)
        return (self.dp + step, self.seq)

    def sibling(self):
        return self.partner(("dp", 0))

    def enter(self):
        barrier = pltpu.get_barrier_semaphore()
        count = 0
        for core_step in range(2):
            for seq_step in range(self.seq_n):
                if core_step == 0 and seq_step == 0:
                    continue
                other = (
                    self.pair * 2 + lax.rem(self.core + core_step, 2),
                    lax.rem(self.seq + seq_step, self.seq_n),
                )
                pl.semaphore_signal(barrier, inc=1, device_id=other, device_id_type=MESH)
                count += 1
        for k in range(1, log2(self.dp_n)):
            pl.semaphore_signal(barrier, inc=1, device_id=self.partner(("dp", k)), device_id_type=MESH)
            count += 1
        pl.semaphore_wait(barrier, count)


def orders_of(dp_n, seq_n):
    along = [("seq", k) for k in reversed(range(log2(seq_n)))]
    across = [("dp", k) for k in range(1, log2(dp_n))]
    back = across[::-1]
    return {
        "zxy": along + across,
        "zyx": along + back,
        "xyz": across + along,
        "yxz": back + along,
    }


def repeat(count, body):
    if count <= 16:
        for j in range(count):
            body(j)
    else:
        lax.fori_loop(0, count, lambda j, c: (body(j), c)[1], 0)


def spread(j, deltas):
    total = 0
    for i, delta in enumerate(deltas):
        if isinstance(j, int):
            if (j >> i) & 1:
                total = total + delta
        else:
            total = total + lax.rem(lax.div(j, 1 << i), 2) * delta
    return total


def resolve(shape, cut):
    axis, pieces, k = cut
    if axis == 1 and shape[1] % (8 * pieces):
        axis = 2
    unit = 8 if axis == 1 else 128
    units = shape[axis] // unit
    start, stop = units * k // pieces, units * (k + 1) // pieces
    return axis, start * unit, (stop - start) * unit


def piece_shape(shape, cut):
    axis, _, size = resolve(shape, cut)
    shape = list(shape)
    shape[axis] = size
    return tuple(shape[1:])


def piece_of(ref, lead, cut):
    axis, start, size = resolve(ref.shape, cut)
    where = [slice(None)] * 2
    where[axis - 1] = pl.ds(start, size)
    return ref.at[(lead, *where)]


GATHER = (
    (0, 2, 3, 0, "zxy", 0),
    (0, 2, 3, 1, "zyx", 0),
    (4, 2, 1, 0, "zyx", 0),
    (0, 2, 3, 2, "zxy", 1),
    (1, 2, 1, 0, "zyx", 1),
    (2, 2, 4, 0, "zxy", 2),
    (3, 1, 4, 0, "zyx", 2),
    (2, 2, 4, 1, "zxy", 3),
    (3, 1, 4, 1, "zyx", 3),
    (2, 2, 4, 2, "zxy", 4),
    (3, 1, 4, 2, "zyx", 4),
    (2, 2, 4, 3, "zxy", 5),
    (3, 1, 4, 3, "zyx", 5),
)
X_WAVE, COT_WAVE = 2, 5


def gather_kernel(dp_n, seq_n, major, x_ref, cot_ref, seg_ref, *refs):
    n_arr = 5
    shard = refs[:n_arr]
    x_out, cot_out, seg_out = refs[n_arr : n_arr + 3]
    full = refs[n_arr + 3 : n_arr + 3 + n_arr]
    (send_sem, recv_sem, side_send, side_recv, own_sem, tok_send, tok_recv, tok_own, seg_sem) = refs[
        2 * n_arr + 3 :
    ]
    at = Place(dp_n, seq_n)
    orders = orders_of(dp_n, seq_n)
    stages = len(orders["zxy"])
    at.enter()
    sibling = at.sibling()

    piece = piece_of

    def put(src, dst, s_sem, r_sem, device):
        pltpu.make_async_remote_copy(
            src_ref=src, dst_ref=dst, send_sem=s_sem, recv_sem=r_sem, device_id=device, device_id_type=MESH
        ).start()

    def place_of(a, idx, cut, count=None):
        if a in major:
            idx = idx + cut[2] * dp_n * seq_n
            return full[a].at[idx if count is None else pl.ds(idx, count)]
        return piece(full[a], idx if count is None else pl.ds(idx, count), cut)

    def group(a, cut, count, s_sem, r_sem, device):
        whole = place_of(a, 0, cut, count)
        return pltpu.make_async_remote_copy(
            src_ref=whole, dst_ref=whole, send_sem=s_sem, recv_sem=r_sem, device_id=device, device_id_type=MESH
        )

    def own_src(a, cut):
        return piece(shard[a], 0, cut)

    def stage(c, t):
        a, *cut, order, _ = GATHER[c]
        names = orders[order]
        deltas = [at.delta(n) for n in names]
        if t > 0:
            group(a, cut, 1 << (t - 1), send_sem.at[c, t - 1], recv_sem.at[c, t - 1], sibling).wait_recv()

            def pass_on(j):
                idx = at.me + deltas[t - 1] + spread(j, deltas[: t - 1])
                place = place_of(a, idx, cut)
                put(place, place, side_send.at[c, t], side_recv.at[c, t], sibling)

            if t < stages:
                partner = at.partner(names[t])

                def onward(j):
                    idx = at.me + spread(j, deltas[:t])
                    place = place_of(a, idx, cut)
                    put(own_src(a, cut) if isinstance(j, int) and j == 0 else place, place, send_sem.at[c, t], recv_sem.at[c, t], partner)

                onward(0)
                repeat((1 << t) - 1, lambda j: onward(j + 1))
            repeat(1 << (t - 1), pass_on)
        else:
            partner = at.partner(names[0])
            place = place_of(a, at.me, cut)
            put(own_src(a, cut), place, send_sem.at[c, 0], recv_sem.at[c, 0], partner)
            put(own_src(a, cut), place, side_send.at[c, 0], side_recv.at[c, 0], sibling)
            pltpu.make_async_copy(own_src(a, cut), place, own_sem.at[c]).start()

    slot = lax.div(at.quarter, 2) * at.parts + lax.rem(at.seq, at.parts)
    seg_copy = pltpu.make_async_remote_copy(
        src_ref=seg_ref,
        dst_ref=seg_out,
        send_sem=seg_sem.at[0],
        recv_sem=seg_sem.at[1],
        device_id=sibling,
        device_id_type=MESH,
    )

    def token_copies(which, src, dst, i):
        to_seq = at.core * at.seqs + i
        mine = (to_seq == at.seq) & (at.quarter_core == at.core)
        remote = pltpu.make_async_remote_copy(
            src_ref=src.at[i],
            dst_ref=dst.at[slot],
            send_sem=tok_send.at[which, i],
            recv_sem=tok_recv.at[which, at.seq],
            device_id=(at.pair * 2 + at.quarter_core, to_seq),
            device_id_type=MESH,
        )
        local = pltpu.make_async_copy(src.at[i], dst.at[slot], tok_own.at[which])
        return mine, remote, local

    def tokens_start(which, src, dst):
        for i in range(at.seqs):
            mine, remote, local = token_copies(which, src, dst, i)
            pl.when(jnp.logical_not(mine))(remote.start)
            pl.when(mine)(local.start)

    def tokens_wait(which, src, dst):
        for i in range(at.seqs):
            mine, remote, local = token_copies(which, src, dst, i)
            pl.when(jnp.logical_not(mine))(remote.wait_send)
            pl.when(mine)(local.wait)
        for z in range(seq_n):
            comes = (at.core_of(z // at.parts) == at.core) & jnp.logical_not(
                (at.seq == z) & (at.source_core == at.core)
            )
            arrival = pltpu.make_async_remote_copy(
                src_ref=src.at[0],
                dst_ref=dst.at[0],
                send_sem=tok_send.at[which, 0],
                recv_sem=tok_recv.at[which, z],
                device_id=sibling,
                device_id_type=MESH,
            )
            pl.when(comes)(arrival.wait_recv)

    seg_copy.start()
    waves = stages + 1 + max(c[5] for c in GATHER)
    for wave in range(waves):
        for c in range(len(GATHER)):
            t = wave - GATHER[c][5]
            if 0 <= t <= stages:
                stage(c, t)
        if wave == X_WAVE:
            tokens_start(0, x_ref, x_out)
        if wave == COT_WAVE:
            tokens_start(1, cot_ref, cot_out)
    for c in range(len(GATHER)):
        a, *cut, order, _ = GATHER[c]
        names = orders[order]
        for t in range(stages):
            group(a, cut, 1 << t, send_sem.at[c, t], recv_sem.at[c, t], at.partner(names[t])).wait_send()
        for t in range(stages + 1):
            one = group(a, cut, 1 << max(t - 1, 0), side_send.at[c, t], side_recv.at[c, t], sibling)
            one.wait_send()
            one.wait_recv()
        pltpu.make_async_copy(own_src(a, cut), place_of(a, at.me, cut), own_sem.at[c]).wait()
    tokens_wait(0, x_ref, x_out)
    tokens_wait(1, cot_ref, cot_out)
    seg_copy.wait()


def gather_all(mesh_shape, x, cot, seg, shards, major=()):
    dp_n, seq_n = mesh_shape
    seqs, blk, width = x.shape
    n_dev = dp_n * seq_n
    stages = log2(n_dev) - 1
    chunks = len(GATHER)
    vmem = pl.BlockSpec(memory_space=pltpu.VMEM)
    hbm = pl.BlockSpec(memory_space=ANY)
    token_shape = jax.ShapeDtypeStruct((seq_n // 2, blk, width), x.dtype)
    DMA = pltpu.SemaphoreType.DMA
    return pl.pallas_call(
        functools.partial(gather_kernel, dp_n, seq_n, major),
        out_shape=[token_shape, token_shape, jax.ShapeDtypeStruct(seg.shape, seg.dtype)]
        + [
            jax.ShapeDtypeStruct((PIECES * n_dev,) + piece_shape((1,) + s.shape, (2 if i == 2 else 1, PIECES, 0)), s.dtype)
            if i in major
            else jax.ShapeDtypeStruct((n_dev,) + s.shape, s.dtype)
            for i, s in enumerate(shards)
        ],
        in_specs=[vmem] * (3 + len(shards)),
        out_specs=[hbm] * 2 + [vmem] + [hbm] * len(shards),
        scratch_shapes=[
            DMA((chunks, stages)),
            DMA((chunks, stages)),
            DMA((chunks, stages + 1)),
            DMA((chunks, stages + 1)),
            DMA((chunks,)),
            DMA((2, seqs)),
            DMA((2, seq_n)),
            DMA((2,)),
            DMA((2,)),
        ],
        compiler_params=pltpu.CompilerParams(collective_id=0, has_side_effects=True),
        name="gather_all",
    )(x, cot, seg, *[s[None] for s in shards])


REDUCE = (
    (2, 2, 4, 0, "zxy", 0),
    (3, 1, 4, 0, "zyx", 0),
    (2, 2, 4, 1, "zxy", 1),
    (3, 1, 4, 1, "zyx", 1),
    (2, 2, 4, 2, "zxy", 2),
    (3, 1, 4, 2, "zyx", 2),
    (2, 2, 4, 3, "zxy", 3),
    (3, 1, 4, 3, "zyx", 3),
    (0, 2, 3, 2, "zxy", 4),
    (1, 2, 1, 0, "zyx", 4),
    (0, 2, 3, 0, "zxy", 5),
    (0, 2, 3, 1, "zyx", 5),
    (4, 2, 1, 0, "zyx", 5),
)


def reduce_kernel(dp_n, seq_n, *refs):
    n_arr, chunks = 5, len(REDUCE)
    tok_in, parts = refs[:2], refs[2 : 2 + n_arr]
    refs = refs[2 + n_arr :]
    tok_out, totals = refs[:2], refs[2 : 2 + n_arr]
    refs = refs[2 + n_arr :]
    at = Place(dp_n, seq_n)
    orders = orders_of(dp_n, seq_n)
    stages = len(orders["zxy"])
    buffers = [refs[c * (stages + 2) : (c + 1) * (stages + 2)] for c in range(chunks)]
    send_sem, recv_sem, own_sem, tok_send, tok_recv, tok_own = refs[chunks * (stages + 2) :]
    at.enter()
    sibling = at.sibling()

    def names_of(c):
        return orders[REDUCE[c][4]][::-1]

    def index_of(c, j, core):
        total = core * seq_n
        for s, (axis, k) in enumerate(names_of(c)):
            value = lax.rem(lax.div(j, 1 << (stages - 1 - s)), 2) if not isinstance(j, int) else (j >> (stages - 1 - s)) & 1
            total = total + value * ((1 << k) * (1 if axis == "seq" else seq_n))
        return total

    def hop(c, t, src):
        device = sibling if t == 0 else at.partner(names_of(c)[t - 1])
        return pltpu.make_async_remote_copy(
            src_ref=src,
            dst_ref=buffers[c][t + 1],
            send_sem=send_sem.at[c, t],
            recv_sem=recv_sem.at[c, t],
            device_id=device,
            device_id_type=MESH,
        )

    def first(c):
        a, *cut, _, _ = REDUCE[c]
        own, got = buffers[c][:2]

        def one(j):
            src = piece_of(parts[a], index_of(c, j, 1 - at.core), cut)
            pltpu.make_async_remote_copy(
                src_ref=src,
                dst_ref=got.at[j],
                send_sem=send_sem.at[c, 0],
                recv_sem=recv_sem.at[c, 0],
                device_id=sibling,
                device_id_type=MESH,
            ).start()
            pltpu.make_async_copy(
                piece_of(parts[a], index_of(c, j, at.core), cut), own.at[j], own_sem.at[c]
            ).start()

        repeat(1 << stages, one)

    def own_wait(c):
        a, *cut, _, _ = REDUCE[c]
        whole = piece_of(parts[a], pl.ds(0, 1 << stages), cut)
        pltpu.make_async_copy(whole, buffers[c][0], own_sem.at[c]).wait()

    def add(c, t, lo, count, kept):
        old, got = buffers[c][t], buffers[c][t + 1]

        def one(j, carry):
            total = old[kept + lo + j].astype(jnp.float32) + got[lo + j].astype(jnp.float32)
            got[lo + j] = total.astype(got.dtype)
            return carry

        lax.fori_loop(0, count, one, 0)

    def stage(c, t):
        if t == 0:
            first(c)
            return
        names = names_of(c)
        hop(c, t - 1, buffers[c][t]).wait_recv()
        if t == 1:
            own_wait(c)
            kept = 0
        else:
            kept = at.bit(names[t - 2]) * (1 << (stages - t + 1))
        if t <= stages:
            half = 1 << (stages - t)
            mine = at.bit(names[t - 1])
            add(c, t - 1, (1 - mine) * half, half, kept)
            hop(c, t, buffers[c][t].at[pl.ds((1 - mine) * half, half)]).start()
            add(c, t - 1, mine * half, half, kept)
        else:
            a, *cut, _, _ = REDUCE[c]
            old, got = buffers[c][t - 1], buffers[c][t]
            total = old[kept].astype(jnp.float32) + got[0].astype(jnp.float32)
            piece_of(totals[a], 0, cut)[...] = total

    def token_copies(which, j):
        slot, rest = j // at.parts, j % at.parts
        quarter = at.core + slot * (3 - 2 * at.core)
        to_seq = quarter * at.parts + rest
        mine = (to_seq == at.seq) & (at.source_core == at.core)
        src = tok_in[which].at[j]
        place = at.seq - at.source_core * at.seqs
        remote = pltpu.make_async_remote_copy(
            src_ref=src,
            dst_ref=tok_out[which].at[place],
            send_sem=tok_send.at[which, j],
            recv_sem=tok_recv.at[which, place],
            device_id=(at.pair * 2 + at.source_core, to_seq),
            device_id_type=MESH,
        )
        local = pltpu.make_async_copy(src, tok_out[which].at[place], tok_own.at[which])
        return mine, remote, local

    for which in range(2):
        for j in range(seq_n // 2):
            mine, remote, local = token_copies(which, j)
            pl.when(jnp.logical_not(mine))(remote.start)
            pl.when(mine)(local.start)
    for wave in range(stages + 2 + max(c[5] for c in REDUCE)):
        for c in range(chunks):
            t = wave - REDUCE[c][5]
            if 0 <= t <= stages + 1:
                stage(c, t)
    for c in range(chunks):
        for t in range(stages + 1):
            hop(c, t, buffers[c][t + 1]).wait_send()
    for which in range(2):
        for j in range(seq_n // 2):
            mine, remote, local = token_copies(which, j)
            pl.when(jnp.logical_not(mine))(remote.wait_send)
            pl.when(mine)(local.wait)
        for i in range(at.seqs):
            comes = jnp.logical_not((at.core * at.seqs + i == at.seq) & (at.quarter_core == at.core))
            arrival = pltpu.make_async_remote_copy(
                src_ref=tok_in[which].at[0],
                dst_ref=tok_out[which].at[i],
                send_sem=tok_send.at[which, 0],
                recv_sem=tok_recv.at[which, i],
                device_id=sibling,
                device_id_type=MESH,
            )
            pl.when(comes)(arrival.wait_recv)


def reduce_all(mesh_shape, tokens, parts):
    dp_n, seq_n = mesh_shape
    stages = log2(dp_n * seq_n) - 1
    _, blk, width = tokens[0].shape
    vmem = pl.BlockSpec(memory_space=pltpu.VMEM)
    hbm = pl.BlockSpec(memory_space=ANY)
    DMA = pltpu.SemaphoreType.DMA
    chunks = len(REDUCE)
    scratch = []
    for a, *cut, _, _ in REDUCE:
        shape = piece_shape(parts[a].shape, cut)
        for count in (1 << stages,) + tuple(1 << (stages - t) for t in range(stages + 1)):
            scratch.append(pltpu.VMEM((count,) + shape, parts[a].dtype))
    out = pl.pallas_call(
        functools.partial(reduce_kernel, dp_n, seq_n),
        out_shape=[jax.ShapeDtypeStruct((seq_n // 2, blk, width), t.dtype) for t in tokens]
        + [jax.ShapeDtypeStruct((1,) + p.shape[1:], jnp.float32) for p in parts],
        in_specs=[vmem] * 2 + [hbm] * len(parts),
        out_specs=[hbm] * 2 + [vmem] * len(parts),
        scratch_shapes=scratch
        + [
            DMA((chunks, stages + 1)),
            DMA((chunks, stages + 1)),
            DMA((chunks,)),
            DMA((2, seq_n // 2)),
            DMA((2, seq_n // 2)),
            DMA((2,)),
        ],
        compiler_params=pltpu.CompilerParams(
            collective_id=1, has_side_effects=True, vmem_limit_bytes=60 * 1024 * 1024
        ),
        name="reduce_all",
    )(*tokens, *parts)
    return out[:2], [g[0] for g in out[2:]]


def swap_kernel(dp_n, seq_n, cols, src_ref, out_ref, send_sem, recv_sem):
    at = Place(dp_n, seq_n)
    sibling = at.sibling()
    barrier = pltpu.get_barrier_semaphore()
    pl.semaphore_signal(barrier, inc=1, device_id=sibling, device_id_type=MESH)
    pl.semaphore_wait(barrier, 1)
    first, width = cols
    copy = pltpu.make_async_remote_copy(
        src_ref=src_ref.at[:, pl.ds(first, width)],
        dst_ref=out_ref,
        send_sem=send_sem,
        recv_sem=recv_sem,
        device_id=sibling,
        device_id_type=MESH,
    )
    copy.start()
    copy.wait()


def swap(mesh_shape, src, cols, which):
    hbm = pl.BlockSpec(memory_space=ANY)
    return pl.pallas_call(
        functools.partial(swap_kernel, *mesh_shape, cols),
        out_shape=jax.ShapeDtypeStruct((src.shape[0], cols[1]), src.dtype),
        in_specs=[hbm],
        out_specs=hbm,
        scratch_shapes=[pltpu.SemaphoreType.DMA, pltpu.SemaphoreType.DMA],
        compiler_params=pltpu.CompilerParams(collective_id=which, has_side_effects=True),
        name="swap",
    )(src)


NT = (((1,), (1,)), ((), ()))
NN = (((1,), (0,)), ((), ()))
TN = (((0,), (0,)), ((), ()))


def dot(a, b, dims):
    return lax.dot_general(a, b, dims, preferred_element_type=jnp.float32)


def woven(own, other):
    half = own.shape[0] // 2
    return jnp.concatenate([own[:half], other[:half], own[half:], other[half:]], 0)


def head_masks():
    lane = lax.broadcasted_iota(jnp.int32, (1, 2 * HEAD_DIM), 1)
    first = (lane < HEAD_DIM).astype(jnp.bfloat16)
    return first, 1 - first


def attend_kernel(q_ref, ko_ref, vo_ref, ks_ref, vs_ref, bias_ref, o_ref, lse_ref, sees=None):
    rows = q_ref.shape[0]
    sees = sees or (rows, 2 * rows)
    half = rows // 2
    keys = woven(ko_ref[...], ks_ref[...])
    values = woven(vo_ref[...], vs_ref[...])
    masks = head_masks()
    scale = jnp.bfloat16(HEAD_DIM ** (-0.5))
    for slot in range(2):
        seen = sees[slot]
        here = slice(slot * half, (slot + 1) * half)
        q = q_ref[here] * scale
        outs = []
        for head in range(2):
            s = dot(keys[:seen], q * masks[head], NT) + bias_ref[:seen, here]
            top = jnp.max(s, 0, keepdims=True)
            e = jnp.exp(s - top)
            total = jnp.sum(e, 0, keepdims=True)
            p = (e * (1.0 / total)).astype(jnp.bfloat16)
            mixed = dot(values[:seen], p, TN)
            outs.append(mixed[head * HEAD_DIM : (head + 1) * HEAD_DIM])
            lse_ref[0, head : head + 1, here] = top + jnp.log(total)
        o_ref[here] = jnp.concatenate(outs, 0).T.astype(jnp.bfloat16)


def attend(qkv, kv_other, bias):
    rows, wide = qkv.shape
    width = wide // 3
    pairs = width // (2 * HEAD_DIM)
    col = lambda first: pl.BlockSpec((rows, 2 * HEAD_DIM), lambda h, first=first: (0, first * pairs + h))
    return pl.pallas_call(
        attend_kernel,
        grid=(pairs,),
        out_shape=[
            jax.ShapeDtypeStruct((rows, width), jnp.bfloat16),
            jax.ShapeDtypeStruct((pairs, 2, rows), jnp.float32),
        ],
        in_specs=[col(0), col(1), col(2), col(0), col(1), pl.BlockSpec(bias.shape, lambda h: (0, 0))],
        out_specs=[col(0), pl.BlockSpec((1, 2, rows), lambda h: (h, 0, 0))],
        name="attend",
    )(qkv, qkv, qkv, kv_other, kv_other, bias)


def attend_back_kernel(
    q_ref, ko_ref, vo_ref, ks_ref, vs_ref, go_ref, bias_ref, lse_ref, gq_ref, gko_ref, gvo_ref, gks_ref, gvs_ref, gk_sum, gv_sum, sees=None
):
    rows = q_ref.shape[0]
    sees = sees or (rows, 2 * rows)
    half = rows // 2
    keys = woven(ko_ref[...], ks_ref[...])
    values = woven(vo_ref[...], vs_ref[...])
    masks = head_masks()
    scale = HEAD_DIM ** (-0.5)
    for slot in (1, 0):
        seen = sees[slot]
        here = slice(slot * half, (slot + 1) * half)
        q = q_ref[here] * jnp.bfloat16(scale)
        go = go_ref[here]
        gqs, gk, gv = [], None, None
        for head in range(2):
            q_h, go_h = q * masks[head], go * masks[head]
            s = dot(keys[:seen], q_h, NT) + bias_ref[:seen, here]
            p = jnp.exp(s - lse_ref[0, head : head + 1, here])
            gp = dot(values[:seen], go_h, NT)
            row_dot = jnp.sum(p * gp, 0, keepdims=True)
            gs = (p * (gp - row_dot)).astype(jnp.bfloat16)
            gv_h = dot(p.astype(jnp.bfloat16), go_h, NN)
            gk_h = dot(gs, q_h, NN)
            gk = gk_h if gk is None else gk + gk_h
            gv = gv_h if gv is None else gv + gv_h
            gq = dot(keys[:seen], gs, TN)
            gqs.append(gq[head * HEAD_DIM : (head + 1) * HEAD_DIM])
        gq_ref[here] = (jnp.concatenate(gqs, 0).T * scale).astype(gq_ref.dtype)
        if slot == 1:
            gk_sum[:seen] = gk
            gv_sum[:seen] = gv
            if seen < 2 * rows:
                gk_sum[seen:] = jnp.zeros((2 * rows - seen, gk.shape[1]), jnp.float32)
                gv_sum[seen:] = jnp.zeros((2 * rows - seen, gv.shape[1]), jnp.float32)
        else:
            gk_sum[:seen] += gk
            gv_sum[:seen] += gv
    for total, own, other in ((gk_sum, gko_ref, gks_ref), (gv_sum, gvo_ref, gvs_ref)):
        for slot in range(2):
            here = slice(slot * half, (slot + 1) * half)
            own[here] = total[2 * slot * half : (2 * slot + 1) * half].astype(own.dtype)
            other[here] = total[(2 * slot + 1) * half : (2 * slot + 2) * half].astype(other.dtype)


def attend_back(qkv, kv_other, go, bias, lse):
    rows, wide = qkv.shape
    width = wide // 3
    pairs = width // (2 * HEAD_DIM)
    lanes = 2 * HEAD_DIM
    col = lambda first: pl.BlockSpec((rows, lanes), lambda h, first=first: (0, first * pairs + h))
    out = jax.ShapeDtypeStruct((rows, width), jnp.bfloat16)
    return pl.pallas_call(
        attend_back_kernel,
        grid=(pairs,),
        out_shape=[out] * 5,
        in_specs=[
            col(0),
            col(1),
            col(2),
            col(0),
            col(1),
            col(0),
            pl.BlockSpec(bias.shape, lambda h: (0, 0)),
            pl.BlockSpec((1, 2, rows), lambda h: (h, 0, 0)),
        ],
        out_specs=[col(0)] * 5,
        scratch_shapes=[pltpu.VMEM((2 * rows, lanes), jnp.float32)] * 2,
        name="attend_back",
    )(qkv, qkv, qkv, kv_other, kv_other, go, bias, lse)


def rows_at(start, size):
    return pl.ds(pl.multiple_of(start, 16), size)


class Reduction:
    def __init__(self, at, order, refs, sems, own):
        self.at, self.own = at, own
        self.blocks, self.sends, self.gets, self.keeps = refs
        self.send_sem, self.recv_sem = sems
        self.order = order
        self.turns = len(order)
        self.last = self.turns + len(self.sends)
        self.names = order + [("seq", k) for k in range(len(self.sends))]
        self.dp_rows = self.blocks[0].shape[0] // (at.dp_n // 2)
        self.shard = self.dp_rows // at.seq_n

    def dp_of(self, j, core):
        dp = core
        for i, (_, k) in enumerate(reversed(self.order)):
            bit = (j >> i) & 1 if isinstance(j, int) else lax.rem(lax.div(j, 1 << i), 2)
            dp = dp + bit * (1 << k)
        return dp

    def landing(self, t):
        return self.blocks[t] if t <= self.turns else self.gets[t - self.turns - 1]

    def copy(self, t, src=None, dst=None):
        at = self.at
        return pltpu.make_async_remote_copy(
            src_ref=self.landing(t) if src is None else src,
            dst_ref=self.landing(t) if dst is None else dst,
            send_sem=self.send_sem.at[t],
            recv_sem=self.recv_sem.at[t],
            device_id=at.sibling() if t == 0 else at.partner(self.names[t - 1]),
            device_id_type=MESH,
        )

    def start(self):
        for j in range(self.at.dp_n // 2):
            dst = self.blocks[0].at[pl.ds(j * self.dp_rows, self.dp_rows)]
            self.copy(0, self.own(self.dp_of(j, 1 - self.at.core)), dst).start()

    def fold(self, t, lo, size):
        got = self.blocks[t - 1]
        step = self.dp_rows // 2

        def one(i, carry):
            row = lo + i * step
            here = rows_at(row, step)
            if t == 1:
                half = lax.rem(i, 2) * step
                old = self.own(self.dp_of(lax.div(row, self.dp_rows), self.at.core))[rows_at(half, step)]
            else:
                kept = self.at.bit(self.names[t - 2]) * got.shape[0]
                old = self.blocks[t - 2][rows_at(kept + row, step)]
            got[here] = (old.astype(jnp.float32) + got[here].astype(jnp.float32)).astype(got.dtype)
            return carry

        lax.fori_loop(0, size // step, one, 0)

    def shards_of(self, t):
        got = self.landing(t - 1)
        if t == self.turns + 1:
            kept = self.at.bit(self.names[t - 2]) * self.dp_rows
            total = self.blocks[t - 2][rows_at(kept, self.dp_rows)].astype(jnp.float32) + got[...].astype(jnp.float32)
            return [total[i * self.shard : (i + 1) * self.shard] for i in range(self.at.seq_n)]
        keep = self.keeps[t - self.turns - 2]
        return [keep[i] + got[i].astype(jnp.float32) for i in range(keep.shape[0])]

    def stage(self, t):
        self.copy(t - 1).wait_recv()
        mine = self.at.bit(self.names[t - 1])
        if t <= self.turns:
            got = self.blocks[t - 1]
            half = got.shape[0] // 2
            self.fold(t, (1 - mine) * half, half)
            self.copy(t, got.at[rows_at((1 - mine) * half, half)]).start()
            self.fold(t, mine * half, half)
            return
        held = self.shards_of(t)
        m = t - self.turns - 1
        send, keep = self.sends[m], self.keeps[m]
        for i in range(len(held) // 2):
            send[i] = jnp.where(mine == 0, held[2 * i + 1], held[2 * i]).astype(send.dtype)
        self.copy(t, send).start()
        for i in range(len(held) // 2):
            keep[i] = jnp.where(mine == 0, held[2 * i], held[2 * i + 1])

    def finish(self):
        self.copy(self.last).wait_recv()
        return self.shards_of(self.last + 1)[0]


GRADS = 2 * PIECES + 4

AFTER = {
    "start": (
        "gq0", "gs0", "gk0", "gv0", "go0",
    ),
    "B0": (
        "gq1", "gs1",
    ),
    "B1": (
        "gk1", "gf00", "gp00", "gv1", "gq2", "gs2", "go1", "gk2", "gs3", "gf01", "gf10", "gp10", "gp01", "gv2", "X",
        "gq3", "gs4", "go2", "gk3", "gf02", "gf20", "gp20", "gf11", "gv3", "gp11", "gp02", "gq4", "gk4", "go3",
        "gf03", "gv4", "go4", "gp03",
    ),
    "L1": (
        "gf12", "gp12", "gf21", "gp21", "gf30", "gp30",
    ),
    "FK": (),
    "FV": (
        "C", "gf04", "gp04", "gf22",
    ),
    "FQ": (
        "gp13", "gp22", "gf31", "gp31", "gf13",
    ),
    "E0": (
        "gf23",
    ),
    "E1": (
        "gp23",
    ),
    "E2": (
        "gp14",
    ),
    "E3": (
        "gf14",
    ),
    "E4": (
        "gf32", "gp32",
    ),
    "E5": (
        "gf24", "gp24",
    ),
    "O": (),
    "L2": (
        "gf33", "gp33",
    ),
    "M0": (),
    "D0": (),
    "M1": (
        "rf01", "gf34", "rp01", "gp34",
    ),
    "D1": (),
    "M2": (
        "rf11",
    ),
    "D2": (
        "rp11", "rf02",
    ),
    "M3": (
        "rp02", "rf21", "rp21",
    ),
    "D3": (
        "rf12",
    ),
    "T": (),
    "A": (
        "rp03", "rp12", "rf31", "rf03", "rp31",
    ),
    "B": (),
    "H0": (
        "ro1",
    ),
    "H1": (
        "rf22", "rp22",
    ),
    "H2": (
        "rf13", "rp13",
    ),
    "H3": (
        "rp04",
    ),
    "H4": (
        "rf04", "rf14", "rf32", "rp32",
    ),
    "H5": (
        "rp05", "rp14", "rp23",
    ),
    "Q": (
        "rf05", "rf15", "rp33", "ro2",
    ),
    "K": (
        "rp15", "rp24", "rf23", "rq1",
    ),
    "V": (
        "rp34",
    ),
    "G": (
        "rp25", "rf24", "rf33", "rk1", "rv1", "ro3",
    ),
    "N": (
        "rp35", "rq2", "rf25", "rf34", "rs1", "ro4", "rk2", "rv2", "rq3", "rk3", "rs2", "rv3", "rs3", "rq4", "rk4",
        "rf35", "U", "rv4", "rs4", "ro5", "rq5", "rk5", "rv5", "rs5",
    ),
}
ORDER_ONE = "kosp"


def whole_kernel(dp_n, seq_n, *refs):
    x_ref, cot_ref, start_ref = refs[:3]
    w_qkv, w_out, w_fc, w_proj, w_vec = refs[3:8]
    result_out, input_out, fc_out, proj_out, qkv_out, wout_out, small_out = refs[8:15]
    qkv_hbm, out_hbm, fc_hbm, proj_hbm, vec_hbm = refs[15:20]
    (wbuf, gbuf, act, gm, a3, gh, resacc, gact, gqkv, away, back, tok, vecs, gk_sum, gv_sum) = refs[20:35]
    (x_in, cot, start_other, resid, mixed, qkv, kv_other, lse, bias, vec_low, vec, fc_own, fc_sum) = refs[35:48]
    refs = refs[48:]
    at = Place(dp_n, seq_n)
    stages = log2(dp_n * seq_n)
    turns, folds = log2(dp_n) - 1, log2(seq_n)
    sets = [turns + 1, folds, folds, folds]
    count = sum(sets)

    def grouped(some):
        groups, first = [], 0
        for size in sets:
            groups.append(some[first : first + size])
            first += size
        return groups

    big, small_bufs = refs[:count], refs[count : 2 * count]
    (small_src, big_send, big_recv, small_send, small_recv, w_sem, swap_sem, tok_send, tok_recv, tok_own) = refs[
        2 * count : 2 * count + 10
    ]
    (ask_send, ask_recv, side_send, side_recv, own_sem, in_send, in_recv, in_own, start_sem, kv_sem, vec_sem) = refs[
        2 * count + 10 :
    ]
    rows, width = resid.shape
    half = rows // 2
    shard = fc_out.shape[0]
    n_dev = dp_n * seq_n
    across = [("dp", k) for k in range(1, log2(dp_n))]
    at.enter()
    sibling = at.sibling()

    def own_rows(src):
        return lambda dp: src.at[pl.ds(pl.multiple_of(dp * (seq_n * shard), 16), seq_n * shard)]

    def reduction(kind, c):
        order = across[::-1] if kind == 0 else across
        where = lax.rem(c, gbuf.shape[0]) if not isinstance(c, int) else c % gbuf.shape[0]
        return Reduction(
            at,
            order,
            grouped([b.at[c] for b in big]),
            (big_send.at[c], big_recv.at[c]),
            own_rows(gbuf.at[where]),
        )

    def vector_reduction():
        return Reduction(
            at,
            across,
            grouped(small_bufs),
            (small_send, small_recv),
            own_rows(small_src),
        )

    def weight_copy(slot, src):
        return pltpu.make_async_copy(src, wbuf.at[slot], w_sem.at[slot])

    def by_core(kernel, *some):
        for core, sees in ((0, (half, 4 * half)), (1, (2 * half, 3 * half))):
            pl.when(at.core == core)(functools.partial(kernel, *some, sees=sees))

    step = 64

    def by_rows(body, sums=0):
        zeros = [jnp.zeros((8, width), jnp.float32)] * sums
        totals = lax.fori_loop(
            0, rows // step, lambda i, t: body(pl.ds(pl.multiple_of(i * step, step), step), t), zeros
        )
        return [jnp.sum(t, 0, keepdims=True) for t in totals]

    def eights(value):
        return jnp.sum(value.reshape(step // 8, 8, width), 0)

    def token_block(ref, here):
        blk = ref.shape[1]
        start = here.start
        return ref[lax.div(start, blk), pl.ds(pl.multiple_of(lax.rem(start, blk), step), step)].astype(jnp.float32)


    def array(name):
        if name in "qkv":
            part = "qkv".index(name)
            cols = pl.ds(part * width, width)
            return part, qkv_hbm.at[:, cols], w_qkv.at[:, cols]
        if name == "o":
            return 3, out_hbm, w_out
        if name == "s":
            return 4, vec_hbm, w_vec
        j = int(name[1])
        if name[0] == "f":
            return 5 + j, fc_hbm.at[j], fc_own.at[:, pl.ds(j * width, width)]
        return 5 + PIECES + j, proj_hbm.at[j], w_proj.at[pl.ds(j * shard, shard)]

    along = [("seq", k) for k in reversed(range(folds))]

    def shard_rows(full, d):
        return full.at[pl.ds(pl.multiple_of(d * shard, 8), shard)]

    def put(src, dst, s_sem, r_sem, device):
        return pltpu.make_async_remote_copy(
            src_ref=src, dst_ref=dst, send_sem=s_sem, recv_sem=r_sem, device_id=device, device_id_type=MESH
        )

    def gather_stage(name, t):
        n, full, own = array(name)
        names = along + (across[::-1] if name[0] in ORDER_ONE else across)
        deltas = [at.delta(x) for x in names]
        if t == 0:
            place = shard_rows(full, at.me)
            put(own, place, ask_send.at[n, 0], ask_recv.at[n, 0], at.partner(names[0])).start()
            put(own, place, side_send.at[n, 0], side_recv.at[n, 0], sibling).start()
            pltpu.make_async_copy(own, place, own_sem.at[n]).start()
            return
        some = full.at[pl.ds(0, shard << (t - 1))]
        put(some, some, ask_send.at[n, t - 1], ask_recv.at[n, t - 1], sibling).wait_recv()
        if t == folds:
            pltpu.make_async_copy(own, shard_rows(full, at.me), own_sem.at[n]).wait()

        def held(t, shift):
            if t < folds:
                return [shard_rows(full, at.me + shift + spread(j, deltas[:t])) for j in range(1 << t)]
            size = seq_n * shard
            return [
                full.at[pl.ds(pl.multiple_of((at.dp * seq_n + shift + spread(j, deltas[folds:t])) * shard, 8), size)]
                for j in range(1 << (t - folds))
            ]

        if t < len(names):
            for j, place in enumerate(held(t, 0)):
                src = own if j == 0 and t < folds else place
                put(src, place, ask_send.at[n, t], ask_recv.at[n, t], at.partner(names[t])).start()
        for place in held(t - 1, deltas[t - 1]):
            put(place, place, side_send.at[n, t], side_recv.at[n, t], sibling).start()

    def gathered(name):
        n, full, own = array(name)
        for t in range(stages):
            some = full.at[pl.ds(0, shard << max(t - 1, 0))]
            put(some, some, side_send.at[n, t], side_recv.at[n, t], sibling).wait_recv()

    def gather_drain(name):
        n, full, own = array(name)
        for t in range(stages - 1):
            some = full.at[pl.ds(0, shard << t)]
            put(some, some, ask_send.at[n, t], ask_recv.at[n, t], sibling).wait_send()
        for t in range(stages):
            some = full.at[pl.ds(0, shard << max(t - 1, 0))]
            put(some, some, side_send.at[n, t], side_recv.at[n, t], sibling).wait_send()

    slot_here = lax.div(at.quarter, 2) * at.parts + lax.rem(at.seq, at.parts)

    def incoming(which, i):
        src, dst = ((x_ref, x_in), (cot_ref, cot))[which]
        to_seq = at.core * at.seqs + i
        mine = (to_seq == at.seq) & (at.quarter_core == at.core)
        remote = put(
            src.at[i],
            dst.at[slot_here],
            in_send.at[which, i],
            in_recv.at[which, at.seq],
            (at.pair * 2 + at.quarter_core, to_seq),
        )
        local = pltpu.make_async_copy(src.at[i], dst.at[slot_here], in_own.at[which])
        return mine, remote, local

    def incoming_start(which):
        for i in range(at.seqs):
            mine, remote, local = incoming(which, i)
            pl.when(jnp.logical_not(mine))(remote.start)
            pl.when(mine)(local.start)

    def incoming_wait(which):
        src, dst = ((x_ref, x_in), (cot_ref, cot))[which]
        for i in range(at.seqs):
            mine, remote, local = incoming(which, i)
            pl.when(jnp.logical_not(mine))(remote.wait_send)
            pl.when(mine)(local.wait)
        for z in range(seq_n):
            comes = (at.core_of(z // at.parts) == at.core) & jnp.logical_not(
                (at.seq == z) & (at.source_core == at.core)
            )
            arrival = put(src.at[0], dst.at[0], in_send.at[which, 0], in_recv.at[which, z], sibling)
            pl.when(comes)(arrival.wait_recv)

    def load_piece(j):
        slot = 2 * lax.rem(j, 2)
        for k in range(PIECES):

            def ready(k=k):
                gathered(f"f{k}")
                gathered(f"p{k}")

            pl.when(j == k)(ready)
        weight_copy(slot, fc_hbm.at[j]).start()
        weight_copy(slot + 1, proj_hbm.at[j]).start()

    def after(slot):
        for op in AFTER[slot]:
            if op == "U":
                unsort_units()
                continue
            if op in "XC":
                incoming_start("XC".index(op))
                continue
            if op[0] == "g":
                gather_stage(op[1:-1], int(op[-1]))
                continue
            name, kind, t = op[1:], op[1], int(op[-1])
            if kind == "s":
                red = vector_reduction()
            else:
                c = 2 * int(name[1]) + (kind == "p") if kind in "fp" else 2 * PIECES + "oqkv".index(kind)
                red = reduction(int(kind in ORDER_ONE), int(c))
            if t < stages:
                red.stage(t)
                continue
            total = red.finish()
            if kind == "f":
                fc_sum[:, int(name[1]) * width : (int(name[1]) + 1) * width] = total
            elif kind == "p":
                proj_out[int(name[1]) * shard : (int(name[1]) + 1) * shard] = total
            elif kind == "o":
                wout_out[...] = total
            elif kind == "s":
                square = jnp.concatenate([total, jnp.zeros((128 - shard, 128), jnp.float32)], 0).T
                pairs_qv = jnp.where(at.me < n_dev // 2, square[10:12], square[12:14])
                line_fc, line_qv = square[6:7], pairs_qv[:1]
                for j in range(1, PIECES):
                    line_fc = line_fc + pltpu.roll(square[6 + j : 7 + j], j * shard, 1)
                line_qv = line_qv + pltpu.roll(pairs_qv[1:2], shard, 1)
                small_out[...] = jnp.concatenate([square[:6], line_fc, line_qv], 0)
            else:
                part = "qkv".index(kind)
                qkv_out[:, part * width : (part + 1) * width] = total

    def after_each(prefix, i, count):
        for k in range(count):
            pl.when(i == k)(functools.partial(after, f"{prefix}{k}"))

    period = PIECES * shard
    group = period * 128 // math.gcd(period, 128)
    lane = lax.broadcasted_iota(jnp.int32, (1, PIECES * 128), 1)
    entry = lax.rem(lane, 128)
    source = lax.div(entry, shard) * period + lax.div(lane, 128) * shard + lax.rem(entry, shard)
    per_piece = group // PIECES
    source = jnp.where(entry < per_piece, source, -1)
    sorter = (lax.broadcasted_iota(jnp.int32, (group, 1), 0) == source).astype(jnp.float32)
    lane_one = lax.broadcasted_iota(jnp.int32, (1, 128), 1)
    groups = PIECES * width // group

    def sort_units():
        pieces = [[jnp.zeros((shard, 128), jnp.float32) for _ in range(width // 128)] for _ in range(PIECES)]
        for g in range(groups):
            moved = dot(w_fc[:, g * group : (g + 1) * group], sorter.astype(jnp.bfloat16), NN)
            block, shift = divmod(g * per_piece, 128)
            for j in range(PIECES):
                turned = moved[:, j * 128 : (j + 1) * 128]
                if shift:
                    turned = pltpu.roll(turned, shift, 1)
                    if shift + per_piece > 128:
                        pieces[j][block + 1] = pieces[j][block + 1] + jnp.where(lane_one < shift, turned, 0.0)
                    turned = jnp.where(lane_one >= shift, turned, 0.0)
                pieces[j][block] = pieces[j][block] + turned
        for j in range(PIECES):
            fc_own[:, j * width : (j + 1) * width] = jnp.concatenate(pieces[j], 1).astype(jnp.bfloat16)

    def unsort_units():
        stacked = []
        for g in range(groups):
            block, shift = divmod(g * per_piece, 128)
            parts = []
            for j in range(PIECES):
                first = j * width + block * 128
                part = fc_sum[:, first : first + 128]
                if shift:
                    part = pltpu.roll(part, 128 - shift, 1)
                    if shift + per_piece > 128:
                        beyond = pltpu.roll(fc_sum[:, first + 128 : first + 256], 128 - shift, 1)
                        part = jnp.where(lane_one < 128 - shift, part, beyond)
                parts.append(jnp.where(lane_one < per_piece, part, 0.0))
            stacked.append(jnp.concatenate(parts, 1))
        moved = lax.dot_general(
            jnp.concatenate(stacked, 0), sorter, NT, precision=lax.Precision.HIGHEST, preferred_element_type=jnp.float32
        )
        for g in range(groups):
            fc_out[:, g * group : (g + 1) * group] = moved[g * shard : (g + 1) * shard]

    after("start")
    ask_start = put(start_ref, start_other, start_sem.at[0], start_sem.at[1], sibling)
    ask_start.start()
    ask_start.wait()
    seq_here = at.seq - at.source_core * at.seqs
    numbers = jnp.where(at.source_core == at.core, start_ref[seq_here], start_other[seq_here])
    spot = lax.broadcasted_iota(jnp.int32, numbers.shape, 1)
    first_seen = jnp.where((spot > 0) & (numbers == pltpu.roll(numbers, 1, 1)), 0, spot)
    for k in range(log2(numbers.shape[1])):
        earlier = pltpu.roll(first_seen, 1 << k, 1)
        first_seen = jnp.maximum(first_seen, jnp.where(spot >= 1 << k, earlier, 0))
    down = lax.broadcasted_iota(jnp.int32, (half, 1), 0)
    along_row = lax.broadcasted_iota(jnp.int32, (1, half), 1)
    key_firsts = [at.core * half, (1 - at.core) * half, (3 - at.core) * half, (2 + at.core) * half]
    for slot in range(2):
        low, high = [first_seen[:, k * half : (k + 1) * half] for k in ((0, 1), (3, 2))[slot]]
        seen_from = jnp.where(at.core == 0, low, high)
        place = key_firsts[2 * slot] + along_row
        for tile in range(2 * slot + 2):
            key = key_firsts[tile] + down
            bias[tile * half : (tile + 1) * half, slot * half : (slot + 1) * half] = jnp.where(
                (key >= seen_from) & (key <= place), 0.0, masked_score
            )
    sort_units()
    vecs[...] = jnp.zeros_like(vecs)
    resacc[...] = jnp.zeros_like(resacc)
    gact[...] = jnp.zeros_like(gact)
    after("B0")
    after("B1")

    incoming_wait(0)
    gathered("s")
    vec_copy = pltpu.make_async_copy(vec_hbm, vec_low, vec_sem)
    vec_copy.start()
    vec_copy.wait()
    columns = vec_low[...].astype(jnp.float32)
    vec[...] = columns.T[:16]
    odd_shard = lax.rem(lax.div(lax.broadcasted_iota(jnp.int32, (1, width), 1), shard), 2) == 1
    for part in range(2):
        doubled = [columns[d * shard : (d + 1) * shard] for d in range(part * n_dev // 2, (part + 1) * n_dev // 2) for _ in range(2)]
        lines = jnp.concatenate(doubled, 0).T
        vec[14 + part : 15 + part] = jnp.where(odd_shard, lines[11:12], lines[10:11])

    def first_norm(here, totals):
        normed, _ = normalised(token_block(x_in, here))
        act[here] = (normed * vec[0:1] + vec[1:2]).astype(jnp.bfloat16)
        return totals

    by_rows(first_norm)
    after("L1")

    def weight_here(name, slot):
        gathered(name)
        copy = weight_copy(slot, array(name)[1])
        copy.start()
        copy.wait()

    weight_here("k", 1)
    qkv[:, width : 2 * width] = dot(act[...], wbuf[1], NN).astype(jnp.bfloat16)

    def exchange_kv(part):
        cols, far = pl.ds((part + 1) * width, width), pl.ds(part * width, width)
        return put(qkv.at[:, cols], kv_other.at[:, far], kv_sem.at[2 * part], kv_sem.at[2 * part + 1], sibling)

    exchange_kv(0).start()
    after("FK")
    weight_here("v", 2)
    qkv[:, 2 * width :] = (dot(act[...], wbuf[2], NN) + vec[15:16]).astype(jnp.bfloat16)
    exchange_kv(1).start()
    after("FV")
    weight_here("q", 0)
    qkv[:, :width] = (dot(act[...], wbuf[0], NN) + vec[14:15]).astype(jnp.bfloat16)
    after("FQ")
    exchange_kv(0).wait()
    exchange_kv(1).wait()
    pairs = width // (2 * HEAD_DIM)

    def load_out():
        gathered("o")
        weight_copy(3, out_hbm).start()

    def heads_forward(i, carry):
        pl.when(i == pairs - 1)(load_out)
        at_q = pl.ds(pl.multiple_of(i * 128, 128), 128)
        at_k = pl.ds(pl.multiple_of(width + i * 128, 128), 128)
        at_v = pl.ds(pl.multiple_of(2 * width + i * 128, 128), 128)
        by_core(
            attend_kernel,
            qkv.at[:, at_q],
            qkv.at[:, at_k],
            qkv.at[:, at_v],
            kv_other.at[:, at_q],
            kv_other.at[:, at_k],
            bias,
            mixed.at[:, at_q],
            lse.at[pl.ds(i, 1)],
        )
        after_each("E", i, 6)
        return carry

    lax.fori_loop(0, pairs, heads_forward, 0)
    weight_copy(3, out_hbm).wait()
    resid[...] = dot(mixed[...], wbuf[3], NN)
    after("O")
    load_piece(jnp.int32(0))
    incoming_wait(1)

    def second_norm(here, totals):
        middle = token_block(x_in, here) + branch_scale * (resid[here] + vec[2:3])
        resid[here] = middle
        normed, _ = normalised(middle)
        act[here] = (normed * vec[3:4] + vec[4:5]).astype(jnp.bfloat16)
        grad_mlp = (branch_scale * token_block(cot, here)).astype(jnp.bfloat16)
        gm[here] = grad_mlp
        return [totals[0] + eights(grad_mlp.astype(jnp.float32))]

    (vecs[5:6],) = by_rows(second_norm, 1)
    after("L2")

    def piece(j, carry):
        slot = 2 * lax.rem(j, 2)
        weight_copy(slot, fc_hbm.at[j]).wait()
        weight_copy(slot + 1, proj_hbm.at[j]).wait()
        fc, proj = wbuf.at[slot], wbuf.at[slot + 1]
        bias_fc = vec[pl.ds(6 + j, 1)]

        def some(r, total):
            here = pl.ds(pl.multiple_of(r * half, 16), half)
            u = dot(act[here], fc[...], NN) + bias_fc
            bent = jnp.tanh(gelu_root * (u + gelu_coeff * u * u * u))
            hidden = (0.5 * u * (1.0 + bent)).astype(jnp.bfloat16)
            inner = gelu_root * (1.0 + 3.0 * gelu_coeff * u * u)
            slope = 0.5 * (1.0 + bent) + 0.5 * u * (1.0 - bent * bent) * inner
            a3[here] = hidden
            resacc[here] += dot(hidden, proj[...], NN)
            grad_u = (dot(gm[here], proj[...], NT) * slope).astype(jnp.bfloat16)
            gh[here] = grad_u
            gact[here] += dot(grad_u, fc[...], NT)
            return total + jnp.sum(grad_u.astype(jnp.float32), 0, keepdims=True)

        total = lax.fori_loop(0, 2, some, jnp.zeros((1, width), jnp.float32))
        vecs[pl.ds(6 + j, 1)] = total
        after_each("M", j, PIECES)
        pl.when(j + 1 < PIECES)(lambda: load_piece(j + 1))
        for kind, (left, right) in enumerate(((act, gh), (a3, gm))):
            c = 2 * j + kind
            red = reduction(kind, c)
            pl.when(c >= gbuf.shape[0])(
                lambda red=red, c=c, kind=kind: reduction(kind, c - gbuf.shape[0]).copy(0).wait_send()
            )
            gbuf[lax.rem(c, gbuf.shape[0])] = dot(left[...], right[...], TN).astype(jnp.bfloat16)
            red.start()
        after_each("D", j, PIECES)
        return carry

    lax.fori_loop(0, PIECES, piece, 0)
    for slot in range(3):
        weight_copy(slot, qkv_hbm.at[:, pl.ds(slot * width, width)]).start()
    weight_copy(3, out_hbm).start()

    def token_copies(which, j):
        slot, rest = j // at.parts, j % at.parts
        quarter = at.core + slot * (3 - 2 * at.core)
        to_seq = quarter * at.parts + rest
        mine = (to_seq == at.seq) & (at.source_core == at.core)
        place = at.seq - at.source_core * at.seqs
        out = (result_out, input_out)[which]
        remote = pltpu.make_async_remote_copy(
            src_ref=tok.at[which, j],
            dst_ref=out.at[place],
            send_sem=tok_send.at[which, j],
            recv_sem=tok_recv.at[which, place],
            device_id=(at.pair * 2 + at.source_core, to_seq),
            device_id_type=MESH,
        )
        local = pltpu.make_async_copy(tok.at[which, j], out.at[place], tok_own.at[which])
        return mine, remote, local

    def tokens_store(which, here, value):
        blk = tok.shape[2]
        place = pl.ds(pl.multiple_of(lax.rem(here.start, blk), step), step)
        tok[which, lax.div(here.start, blk), place] = value.astype(jnp.bfloat16)

    def tokens_start(which):
        for j in range(seq_n // 2):
            mine, remote, local = token_copies(which, j)
            pl.when(jnp.logical_not(mine))(remote.start)
            pl.when(mine)(local.start)

    def tokens_wait(which):
        for j in range(seq_n // 2):
            mine, remote, local = token_copies(which, j)
            pl.when(jnp.logical_not(mine))(remote.wait_send)
            pl.when(mine)(local.wait)
        for i in range(at.seqs):
            comes = jnp.logical_not((at.core * at.seqs + i == at.seq) & (at.quarter_core == at.core))
            arrival = pltpu.make_async_remote_copy(
                src_ref=tok.at[which, 0],
                dst_ref=(result_out, input_out)[which].at[i],
                send_sem=tok_send.at[which, 0],
                recv_sem=tok_recv.at[which, i],
                device_id=sibling,
                device_id_type=MESH,
            )
            pl.when(comes)(arrival.wait_recv)

    def result(here, totals):
        tokens_store(0, here, resid[here] + branch_scale * (resacc[here] + vec[5:6]))
        return totals

    by_rows(result)
    tokens_start(0)
    after("T")

    def second_back(here, totals):
        normed, inverse = normalised(resid[here])
        grad_two = gact[here]
        grad_mid = token_block(cot, here) + norm_spread(grad_two, normed, inverse, vec[3:4])
        gact[here] = grad_mid
        grad_branch = (branch_scale * grad_mid).astype(jnp.bfloat16)
        act[here] = grad_branch
        return [
            totals[0] + eights(grad_branch.astype(jnp.float32)),
            totals[1] + eights(grad_two * normed),
            totals[2] + eights(grad_two),
        ]

    vecs[2:3], vecs[3:4], vecs[4:5] = by_rows(second_back, 3)

    c_out = 2 * PIECES
    reduction(0, c_out - gbuf.shape[0]).copy(0).wait_send()
    gbuf[c_out % gbuf.shape[0]] = dot(mixed[...], act[...], TN).astype(jnp.bfloat16)
    reduction(1, c_out).start()
    after("A")
    weight_copy(3, out_hbm).wait()
    gm[...] = dot(act[...], wbuf[3], NT).astype(jnp.bfloat16)
    after("B")

    def away_copies(part):
        half_cols = width // 2
        for k in range(2):
            cols = pl.ds(k * width + part * half_cols, half_cols)
            n = 2 * (2 * part + k)
            yield put(away.at[:, cols], back.at[:, cols], swap_sem.at[n], swap_sem.at[n + 1], sibling)

    def exchange_away(part):
        for copy in away_copies(part):
            copy.start()

    def heads(i, carry):
        at_q = pl.ds(pl.multiple_of(i * 128, 128), 128)
        at_k = pl.ds(pl.multiple_of(width + i * 128, 128), 128)
        at_v = pl.ds(pl.multiple_of(2 * width + i * 128, 128), 128)
        by_core(
            attend_back_kernel,
            qkv.at[:, at_q],
            qkv.at[:, at_k],
            qkv.at[:, at_v],
            kv_other.at[:, at_q],
            kv_other.at[:, at_k],
            gm.at[:, at_q],
            bias,
            lse.at[pl.ds(i, 1)],
            gqkv.at[:, at_q],
            gqkv.at[:, at_k],
            gqkv.at[:, at_v],
            away.at[:, at_q],
            away.at[:, at_k],
            gk_sum,
            gv_sum,
        )
        pl.when(i == pairs // 2 - 1)(functools.partial(exchange_away, 0))
        after_each("H", i, 6)
        return carry

    lax.fori_loop(0, pairs, heads, 0)

    exchange_away(1)
    by_rows(first_norm)

    def grad_of(part):
        c = c_out + 1 + part
        kind = part % 2
        here = pl.ds(part * width, width)
        reduction(kind, c - gbuf.shape[0]).copy(0).wait_send()
        gbuf[c % gbuf.shape[0]] = dot(act[...], gqkv[:, here], TN).astype(jnp.bfloat16)
        reduction(kind, c).start()

    grad_of(0)
    after("Q")
    for part in range(2):
        for copy in away_copies(part):
            copy.wait()

    def meet(here, totals):
        for part in (1, 2):
            near, far = pl.ds(part * width, width), pl.ds((part - 1) * width, width)
            gqkv[here, near] = (gqkv[here, near].astype(jnp.float32) + back[here, far].astype(jnp.float32)).astype(
                jnp.bfloat16
            )
        return [
            totals[0] + eights(gqkv[here, pl.ds(0, width)].astype(jnp.float32)),
            totals[1] + eights(gqkv[here, pl.ds(2 * width, width)].astype(jnp.float32)),
        ]

    first, third = by_rows(meet, 2)
    for row, value in ((10, first), (11, first), (12, third), (13, third)):
        vecs[row : row + 1] = value
    grad_of(1)
    after("K")
    grad_of(2)
    after("V")
    for part in range(3):
        weight_copy(part, qkv_hbm.at[:, pl.ds(part * width, width)]).wait()
    grad_one = dot(gqkv[:, pl.ds(0, width)], wbuf[0], NT)
    grad_one = grad_one + dot(gqkv[:, pl.ds(width, width)], wbuf[1], NT)
    resacc[...] = grad_one + dot(gqkv[:, pl.ds(2 * width, width)], wbuf[2], NT)
    after("G")

    def first_back(here, totals):
        normed, inverse = normalised(token_block(x_in, here))
        grad_one = resacc[here]
        tokens_store(1, here, gact[here] + norm_spread(grad_one, normed, inverse, vec[0:1]))
        return [totals[0] + eights(grad_one * normed), totals[1] + eights(grad_one)]

    vecs[0:1], vecs[1:2] = by_rows(first_back, 2)
    tokens_start(1)
    columns = vecs[...].T
    small_src[...] = columns
    lane = lax.broadcasted_iota(jnp.int32, (1, 128), 1)
    even, odd = (lane == 10) | (lane == 12), (lane == 11) | (lane == 13)
    for d in range(n_dev):
        start = 2 * shard * (d % (n_dev // 2))
        kept = columns[d * shard : (d + 1) * shard]
        kept = jnp.where(even, columns[start : start + shard], kept)
        kept = jnp.where(odd, columns[start + shard : start + 2 * shard], kept)
        small_src[d * shard : (d + 1) * shard] = kept
    vector_reduction().start()
    after("N")
    for c in range(GRADS):
        red = reduction(0, c)
        for t in range(0 if c >= GRADS - gbuf.shape[0] else 1, stages):
            red.copy(t).wait_send()
    for t in range(stages):
        vector_reduction().copy(t).wait_send()
    for name in ["s", "q", "k", "v", "o"] + [f"{x}{j}" for x in "fp" for j in range(PIECES)]:
        gather_drain(name)
    tokens_wait(0)
    tokens_wait(1)


def whole(mesh_shape, x, cot, start, shards):
    dp_n, seq_n = mesh_shape
    seqs, blk, width = x.shape
    rows = blk * (seq_n // 2)
    n_dev = dp_n * seq_n
    stages = log2(n_dev)
    shard = width // n_dev
    vmem = pl.BlockSpec(memory_space=pltpu.VMEM)
    hbm = pl.BlockSpec(memory_space=ANY)
    DMA = pltpu.SemaphoreType.DMA
    low, full = jnp.bfloat16, jnp.float32
    slots = 4
    arrays = 5 + 2 * PIECES

    def buffers(lead, cols, dtype):
        turns, folds = log2(dp_n) - 1, log2(seq_n)
        parts = [(seq_n >> (m + 1), shard, cols) for m in range(folds)]
        return (
            [pltpu.VMEM(lead + (width // 2 >> t, cols), dtype) for t in range(turns + 1)]
            + [pltpu.VMEM(lead + p, dtype) for p in parts] * 2
            + [pltpu.VMEM(lead + p, full) for p in parts]
        )

    token = jax.ShapeDtypeStruct((seq_n // 2, blk, width), low)
    grads = [(shard, PIECES * width), (PIECES * shard, width), (shard, 3 * width), (shard, width), (8, 128)]
    gathers = [(width, 3 * width), (width, width), (PIECES, width, width), (PIECES, width, width), (width, 128)]
    out = pl.pallas_call(
        functools.partial(whole_kernel, dp_n, seq_n),
        out_shape=[token, token]
        + [jax.ShapeDtypeStruct(s, full) for s in grads]
        + [jax.ShapeDtypeStruct(s, low) for s in gathers],
        in_specs=[hbm] * 2 + [vmem] * 6,
        out_specs=[hbm] * 2 + [vmem] * 5 + [hbm] * 5,
        scratch_shapes=[
            pltpu.VMEM((4, width, width), low),
            pltpu.VMEM((slots, width, width), low),
            pltpu.VMEM((rows, width), low),
            pltpu.VMEM((rows, width), low),
            pltpu.VMEM((rows, width), low),
            pltpu.VMEM((rows, width), low),
            pltpu.VMEM((rows, width), full),
            pltpu.VMEM((rows, width), full),
            pltpu.VMEM((rows, 3 * width), low),
            pltpu.VMEM((rows, 2 * width), low),
            pltpu.VMEM((rows, 2 * width), low),
            pltpu.VMEM((2, seq_n // 2, blk, width), low),
            pltpu.VMEM((128, width), full),
            pltpu.VMEM((2 * rows, 128), full),
            pltpu.VMEM((2 * rows, 128), full),
            pltpu.VMEM((seq_n // 2, blk, width), low),
            pltpu.VMEM((seq_n // 2, blk, width), low),
            pltpu.VMEM(start.shape, start.dtype),
            pltpu.VMEM((rows, width), full),
            pltpu.VMEM((rows, width), low),
            pltpu.VMEM((rows, 3 * width), low),
            pltpu.VMEM((rows, 2 * width), low),
            pltpu.VMEM((width // 128, 2, rows), full),
            pltpu.VMEM((2 * rows, rows), full),
            pltpu.VMEM((width, 128), low),
            pltpu.VMEM((16, width), full),
            pltpu.VMEM((shard, PIECES * width), low),
            pltpu.VMEM((shard, PIECES * width), full),
        ]
        + buffers((GRADS,), width, low)
        + buffers((), 128, full)
        + [
            pltpu.VMEM((width, 128), full),
            DMA((GRADS, stages)),
            DMA((GRADS, stages)),
            DMA((stages,)),
            DMA((stages,)),
            DMA((4,)),
            DMA((8,)),
            DMA((2, seq_n // 2)),
            DMA((2, seq_n // 2)),
            DMA((2,)),
            DMA((arrays, stages - 1)),
            DMA((arrays, stages - 1)),
            DMA((arrays, stages)),
            DMA((arrays, stages)),
            DMA((arrays,)),
            DMA((2, seqs)),
            DMA((2, seq_n)),
            DMA((2,)),
            DMA((2,)),
            DMA((4,)),
            DMA,
        ],
        compiler_params=pltpu.CompilerParams(
            collective_id=4, has_side_effects=True, vmem_limit_bytes=64 * 1024 * 1024 - 65536
        ),
        name="whole",
    )(x, cot, start, *shards)
    return out[:7]


def normalised(rows):
    center = rows - jnp.mean(rows, -1, keepdims=True)
    inverse = lax.rsqrt(jnp.mean(center * center, -1, keepdims=True) + norm_eps)
    return center * inverse, inverse


def norm_spread(grad_in, normed, inverse, gain):
    scaled = grad_in * gain
    return inverse * (
        scaled
        - jnp.mean(scaled, -1, keepdims=True)
        - normed * jnp.mean(scaled * normed, -1, keepdims=True)
    )


def packed(vectors, row_unit, dtype):
    flat = jnp.concatenate(vectors, -1)
    size = flat.shape[-1]
    rows = -(-size // (128 * row_unit)) * row_unit
    flat = jnp.pad(flat, [(0, 0)] * (flat.ndim - 1) + [(0, rows * 128 - size)])
    return flat.reshape(flat.shape[:-1] + (rows, 128)).astype(dtype)


def unpacked(rows, sizes):
    flat = rows.reshape(rows.shape[0], -1)
    out, first = [], 0
    for size in sizes:
        out.append(flat[:, first : first + size].reshape(-1))
        first += size
    return out


def block(mesh_shape, *args):
    (
        block_input,
        segments,
        cotangent,
        ln1_gain,
        ln1_bias,
        w_qkv,
        b_qv,
        w_out,
        b_out,
        ln2_gain,
        ln2_bias,
        w_fc,
        b_fc,
        w_proj,
        b_proj,
    ) = args
    dp_n, seq_n = mesh_shape
    n_dev = dp_n * seq_n
    micro_count, seq_count, stretch, width = block_input.shape
    seq_len = segments.shape[2]
    seqs = micro_count * seq_count
    assert 2 * seqs == seq_n and seq_n % 4 == 0
    at = Place(dp_n, seq_n)
    vectors = (ln1_gain, ln1_bias, b_qv, b_out, ln2_gain, ln2_bias, b_fc, b_proj)
    sizes = [v.shape[0] for v in vectors]
    gathered = gather_all(
        mesh_shape,
        block_input.reshape(seqs, stretch, width),
        cotangent.reshape(seqs, stretch, width),
        segments.reshape(seqs, seq_len),
        (w_qkv, w_out, w_fc, w_proj, packed(vectors, 16, jnp.bfloat16)),
    )
    x_rows, cot_rows, seg_other, weight_qkv, weight_out, weight_fc, weight_proj, small = gathered
    rows = seq_len // 2
    half = rows // 2
    x_rows = x_rows.reshape(rows, width).astype(jnp.float32)
    grad_out = cot_rows.reshape(rows, width).astype(jnp.float32)
    weight_qkv, weight_out, weight_fc, weight_proj = [
        w.reshape(-1, w.shape[-1]) for w in (weight_qkv, weight_out, weight_fc, weight_proj)
    ]
    gain_one, bias_one, bias_qv, bias_out, gain_two, bias_two, bias_fc, bias_proj = [
        v.astype(jnp.float32) for v in unpacked(small, sizes)
    ]

    seg_all = jnp.where(at.source_core == at.core, segments.reshape(seqs, seq_len), seg_other)
    seg = lax.dynamic_index_in_dim(seg_all, at.seq - at.source_core * seqs, 0, keepdims=False)
    quarter = jnp.arange(half, dtype=jnp.int32)
    own_first = [at.core * half, (3 - at.core) * half]
    other_first = [(1 - at.core) * half, (2 + at.core) * half]
    firsts = [own_first[0], other_first[0], own_first[1], other_first[1]]
    key_place = jnp.concatenate([f + quarter for f in firsts])
    key_seg = jnp.concatenate([lax.dynamic_slice_in_dim(seg, f, half, 0) for f in firsts])
    query_place = jnp.concatenate([key_place[:half], key_place[2 * half : 3 * half]])
    query_seg = jnp.concatenate([key_seg[:half], key_seg[2 * half : 3 * half]])
    visible = (key_seg[:, None] == query_seg[None, :]) & (key_place[:, None] <= query_place[None, :])
    bias = jnp.where(visible, 0.0, masked_score).astype(jnp.float32)

    normed_out, normed_one, inverse_one = layer_norm(x_rows, gain_one, bias_one)
    act_one = normed_out.astype(jnp.bfloat16)
    bias_full = jnp.concatenate([bias_qv[:width], jnp.zeros((width,), jnp.float32), bias_qv[width:]])
    qkv = (jnp.dot(act_one, weight_qkv, preferred_element_type=jnp.float32) + bias_full).astype(jnp.bfloat16)
    kv_other = swap(mesh_shape, qkv, (width, 2 * width), 2)
    mixed_out, lse = attend(qkv, kv_other, bias)
    resid_mid = x_rows + branch_scale * (
        jnp.dot(mixed_out, weight_out, preferred_element_type=jnp.float32) + bias_out
    )

    normed_out, normed_two, inverse_two = layer_norm(resid_mid, gain_two, bias_two)
    act_two = normed_out.astype(jnp.bfloat16)
    hidden = jnp.dot(act_two, weight_fc, preferred_element_type=jnp.float32) + bias_fc
    act_three = gelu_tanh(hidden).astype(jnp.bfloat16)
    result = resid_mid + branch_scale * (
        jnp.dot(act_three, weight_proj, preferred_element_type=jnp.float32) + bias_proj
    )
    grad_mlp = (branch_scale * grad_out).astype(jnp.bfloat16)
    grad_bproj = jnp.sum(grad_mlp.astype(jnp.float32), 0)
    grad_wproj = dot(act_three, grad_mlp, TN)
    grad_act3 = dot(grad_mlp, weight_proj, NT)
    grad_hidden = (grad_act3 * gelu_slope(hidden)).astype(jnp.bfloat16)
    grad_bfc = jnp.sum(grad_hidden.astype(jnp.float32), 0)
    grad_wfc = dot(act_two, grad_hidden, TN)
    grad_act2 = dot(grad_hidden, weight_fc, NT)
    grad_norm2, grad_gain2, grad_bias2 = norm_back(grad_act2, normed_two, inverse_two, gain_two)
    grad_mid = grad_out + grad_norm2

    grad_branch = (branch_scale * grad_mid).astype(jnp.bfloat16)
    grad_bout = jnp.sum(grad_branch.astype(jnp.float32), 0)
    grad_wout = dot(mixed_out, grad_branch, TN)
    grad_mixed = dot(grad_branch, weight_out, NT).astype(jnp.bfloat16)
    grad_q, grad_k, grad_v, away_k, away_v = attend_back(qkv, kv_other, grad_mixed, bias, lse)
    back = swap(mesh_shape, jnp.concatenate([away_k, away_v], 1), (0, 2 * width), 3)
    key_value = jnp.concatenate([grad_k, grad_v], 1).astype(jnp.float32) + back.astype(jnp.float32)
    grad_qkv = jnp.concatenate([grad_q, key_value.astype(jnp.bfloat16)], 1)
    grad_wide = grad_qkv.astype(jnp.float32)
    grad_bqv = jnp.concatenate([jnp.sum(grad_wide[:, :width], 0), jnp.sum(grad_wide[:, 2 * width :], 0)])
    grad_wqkv = dot(act_one, grad_qkv, TN)
    grad_act1 = dot(grad_qkv, weight_qkv, NT)
    grad_norm1, grad_gain1, grad_bias1 = norm_back(grad_act1, normed_one, inverse_one, gain_one)
    grad_input = grad_mid + grad_norm1

    vec_grads = (grad_gain1, grad_bias1, grad_bqv, grad_bout, grad_gain2, grad_bias2, grad_bfc, grad_bproj)
    token_block = (seq_n // 2, stretch, width)
    parts = [
        g.astype(jnp.bfloat16).reshape((n_dev, -1, g.shape[-1]))
        for g in (grad_wqkv, grad_wout, grad_wfc, grad_wproj)
    ] + [packed([v.reshape(n_dev, -1) for v in vec_grads], 8, jnp.float32)]
    (result, grad_input), totals = reduce_all(
        mesh_shape,
        [result.astype(jnp.bfloat16).reshape(token_block), grad_input.astype(jnp.bfloat16).reshape(token_block)],
        parts,
    )
    owned = unpacked(totals[4].reshape(1, -1), sizes)
    shape = block_input.shape
    return (
        result.reshape(shape),
        grad_input.reshape(shape),
        owned[0],
        owned[1],
        totals[0],
        owned[2],
        totals[1],
        owned[3],
        owned[4],
        owned[5],
        totals[2],
        owned[6],
        totals[3],
        owned[7],
    )


def settle_kernel(*refs):
    half = len(refs) // 2
    for src, dst in zip(refs[:half], refs[half:]):
        dst[...] = src[...]


def settle(arrays):
    vmem = pl.BlockSpec(memory_space=pltpu.VMEM)
    return pl.pallas_call(
        settle_kernel,
        out_shape=[jax.ShapeDtypeStruct(a.shape, a.dtype) for a in arrays],
        in_specs=[vmem] * len(arrays),
        out_specs=[vmem] * len(arrays),
        name="settle",
    )(*arrays)


def fused_block(mesh_shape, *args):
    (
        block_input,
        segments,
        cotangent,
        ln1_gain,
        ln1_bias,
        w_qkv,
        b_qv,
        w_out,
        b_out,
        ln2_gain,
        ln2_bias,
        w_fc,
        b_fc,
        w_proj,
        b_proj,
    ) = args
    dp_n, seq_n = mesh_shape
    n_dev = dp_n * seq_n
    micro_count, seq_count, stretch, width = block_input.shape
    seq_len = segments.shape[2]
    seqs = micro_count * seq_count
    assert 2 * seqs == seq_n and seq_n % 4 == 0 and w_fc.shape[1] == PIECES * width
    at = Place(dp_n, seq_n)
    shard = width // n_dev
    vectors = [ln1_gain, ln1_bias, b_out, ln2_gain, ln2_bias, b_proj]
    vectors += [b_fc[j * shard : (j + 1) * shard] for j in range(PIECES)] + [b_qv[:shard], b_qv[shard:]]
    lane = lax.broadcasted_iota(jnp.int32, (shard, 128), 1)
    columns = jnp.zeros((shard, 128), jnp.bfloat16)
    for k, vector in enumerate(vectors):
        columns = jnp.where(lane == k, vector[:, None], columns)
    result, grad_input, grad_fc, grad_proj, grad_qkv, grad_out, lines = whole(
        mesh_shape,
        block_input.reshape(seqs, stretch, width),
        cotangent.reshape(seqs, stretch, width),
        segments.reshape(seqs, 1, seq_len),
        (w_qkv, w_out, w_fc, w_proj, columns),
    )
    result, grad_input, grad_fc, grad_proj, grad_qkv, grad_out = settle(
        (result, grad_input, grad_fc, grad_proj, grad_qkv, grad_out)
    )
    shape = block_input.shape
    return (
        result.reshape(shape),
        grad_input.reshape(shape),
        lines[0, :shard],
        lines[1, :shard],
        grad_qkv,
        lines[7, : 2 * shard],
        grad_out,
        lines[2, :shard],
        lines[3, :shard],
        lines[4, :shard],
        grad_fc,
        lines[6, : PIECES * shard],
        grad_proj,
        lines[5, :shard],
    )


def whole_block(mesh_shape, *args):
    aligned = args[5].shape[0] % 8 == 0 and mesh_shape[1] == 4
    return (fused_block if aligned else block)(mesh_shape, *args)


def solution(mesh):
    both = ("dp", "seq")
    tokens, vector, matrix = P(None, "dp", "seq", None), P(both), P(both, None)
    return jax.shard_map(
        functools.partial(whole_block, (mesh.shape["dp"], mesh.shape["seq"])),
        mesh=mesh,
        in_specs=(
            tokens,
            P(None, "dp", None),
            tokens,
            vector,
            vector,
            matrix,
            vector,
            matrix,
            vector,
            vector,
            vector,
            matrix,
            vector,
            matrix,
            vector,
        ),
        out_specs=(
            tokens,
            tokens,
            vector,
            vector,
            matrix,
            vector,
            matrix,
            vector,
            vector,
            vector,
            matrix,
            vector,
            matrix,
            vector,
        ),
        check_vma=False,
    )
```
